32 devices in a mesh: fsdp: 4 (over z), ctx: 2 (over x), tp: 4 (over y, core).
Axes of the slice: x: 2, y: 2, z: 4, core: 2. Of those that a mesh axis runs over, the one named last changes fastest.
Arguments:
- layer_input: bfloat16 [4, 2048, 768], P('fsdp', 'ctx'), may hold values from -6 to 6
- segments: int32 [4, 2048], P('fsdp', 'ctx'), may hold values from 0 to 3, never falling along the last dimension, each value on 1 to 1024 neighbouring positions
- routes: int32 [4, 2048, 2], P('fsdp', 'ctx'), may hold values from 0 to 3, all different within a row; in each aligned block of 1024 rows (0 to 1023, 1024 to 2047, ..., all dimensions but the last counted through in order) at most 1024 rows name the same one
- cotangent: bfloat16 [4, 2048, 768], P('fsdp', 'ctx'), may hold values from -6 to 6
- gains: float32 [2, 768], P(None, ('fsdp', 'ctx')), may hold values from 0.5 to 1.5
- attention_in: float32 [768, 3, 768], P(('fsdp', 'ctx'), None, 'tp'), as said below
- attention_out: float32 [768, 768], P('tp', ('fsdp', 'ctx')), may hold values from -0.3125 to 0.3125
- router_weight: float32 [768, 4], P(('fsdp', 'ctx')), may hold values from -0.21875 to 0.21875
- shared_in: float32 [768, 2, 2048], P(('fsdp', 'ctx'), None, 'tp'), may hold values from -0.21875 to 0.21875
- shared_down: float32 [2048, 768], P('tp', ('fsdp', 'ctx')), may hold values from -0.125 to 0.125
- expert_in: float32 [4, 768, 2, 2048], P('fsdp', 'ctx', None, 'tp'), may hold values from -0.21875 to 0.21875
- expert_down: float32 [4, 2048, 768], P('fsdp', 'tp', 'ctx'), may hold values from -0.125 to 0.125
- model_stats: float32 [6, 768], P(None, ('fsdp', 'ctx')), as said below
- head_stats: float32 [3, 768], P(None, 'tp'), as said below
- value_columns: float32 [768], P('tp'), as said below
- hidden_stats: float32 [3, 2048], P(None, 'tp'), as said below
- router_state: float32 [768, 4], P(('fsdp', 'ctx')), as said below
- expert_model_stats: float32 [4, 2, 768], P('fsdp', None, 'ctx'), as said below
- expert_hidden_stats: float32 [4, 3, 2048], P('fsdp', None, 'tp'), as said below
Outputs:
- layer_output: bfloat16 [4, 2048, 768], P('fsdp', 'ctx')
- input_grad: float32 [4, 2048, 768], P('fsdp', 'ctx')
- grad_gains: float32 [2, 768], P(None, ('fsdp', 'ctx'))
- grad_attention_in: float32 [768, 3, 768], P(('fsdp', 'ctx'), None, 'tp')
- grad_attention_out: float32 [768, 768], P('tp', ('fsdp', 'ctx'))
- grad_router: float32 [768, 4], P(('fsdp', 'ctx'))
- grad_shared_in: float32 [768, 2, 2048], P(('fsdp', 'ctx'), None, 'tp')
- grad_shared_down: float32 [2048, 768], P('tp', ('fsdp', 'ctx'))
- grad_expert_in: float32 [4, 768, 2, 2048], P('fsdp', 'ctx', None, 'tp')
- grad_expert_down: float32 [4, 2048, 768], P('fsdp', 'tp', 'ctx')
- new_gains: float32 [2, 768], P(None, ('fsdp', 'ctx'))
- new_attention_in: float32 [768, 3, 768], P(('fsdp', 'ctx'), None, 'tp')
- new_attention_out: float32 [768, 768], P('tp', ('fsdp', 'ctx'))
- new_router: float32 [768, 4], P(('fsdp', 'ctx'))
- new_shared_in: float32 [768, 2, 2048], P(('fsdp', 'ctx'), None, 'tp')
- new_shared_down: float32 [2048, 768], P('tp', ('fsdp', 'ctx'))
- new_expert_in: float32 [4, 768, 2, 2048], P('fsdp', 'ctx', None, 'tp')
- new_expert_down: float32 [4, 2048, 768], P('fsdp', 'tp', 'ctx')
- new_model_stats: float32 [6, 768], P(None, ('fsdp', 'ctx'))
- new_head_stats: float32 [3, 768], P(None, 'tp')
- new_value_columns: float32 [768], P('tp')
- new_hidden_stats: float32 [3, 2048], P(None, 'tp')
- new_router_state: float32 [768, 4], P(('fsdp', 'ctx'))
- new_expert_model_stats: float32 [4, 2, 768], P('fsdp', None, 'ctx')
- new_expert_hidden_stats: float32 [4, 3, 2048], P('fsdp', None, 'tp')
- update_rms: float32 [8], replicated
The draws below stay inside these ranges and needn't reach their ends.
Inputs may be any that keep to these rules, and one draw needn't show every extreme that they name: `routes`: each row names two different experts. In each aligned block of 1024 rows (the rows of one device) no expert is named by more than 1024 rows, and in some block one expert is named by exactly 1024. `segments`: within each sequence the ids never fall; each document spans 1 to 1024 positions and one spans exactly that many. `attention_in`: finite real values. `model_stats`: Positive. `head_stats`: Positive. `value_columns`: Positive. `hidden_stats`: Positive. `router_state`: Positive. `expert_model_stats`: Positive. `expert_hidden_stats`: Positive.
All inputs are finite; a program needn't handle non-finite values.
Results may differ from the reference program's by a relative error of at most 0.015.
The reference program's roundings to bfloat16 on the way count: a program that leaves them out, or rounds other values in their place, can miss the bound.
Values may be sent and summed in bfloat16 or wider, within the bound.
A program may use at most 256 MiB of HBM per device.

```python
import math
from functools import partial
import jax
import jax.numpy as jnp
import numpy as np
from jax import lax

D = 768
HEADS = 12
HD = 64
FF = 2048
FE = 2048
WINDOW = 1024
DOCS = 4
BLK = 1024
HH = 768
EXPERTS = 4
LEN = 2048
SEQS = 4
TOKENS = 8192
CAP = 1024


def spread_states(key, shape, base_scale):
    unit_draw = jax.random.uniform(key, shape, jnp.float32, 0.0, 1.0)
    level = 0.5 * jnp.exp(unit_draw * 1.386294)
    return level * base_scale


def keys_counted():
    return max(2, min(WINDOW, LEN // DOCS) // 2)


def draw_attention_in(key, part):
    unit_normal = jax.random.truncated_normal(key, -6.0, 6.0, (D, 3, HH), jnp.float32)
    part_scale = jnp.array([1.0, 1.0, 32.0 ** 0.5], jnp.float32)[None, :, None]
    return unit_normal * D ** (-0.5) * part_scale


def draw_model_stats(key, part):
    base_scale = jnp.array([0.5, 0.5, 0.16, 0.25, 72.0 / keys_counted(), 0.25], jnp.float32)[:, None] * TOKENS
    return spread_states(key, (6, D), base_scale)


def draw_head_stats(key, part):
    base_scale = jnp.array([150.0, 150.0, 72.0], jnp.float32)[:, None] * (TOKENS / keys_counted())
    return spread_states(key, (3, HH), base_scale)


def draw_value_columns(key, part):
    return spread_states(key, (HH,), 4.7 * TOKENS / keys_counted())


def draw_hidden_stats(key, part):
    base_scale = jnp.array([0.25, 0.25, 0.25], jnp.float32)[:, None] * TOKENS
    return spread_states(key, (3, FF), base_scale)


def draw_router_state(key, part):
    return spread_states(key, (D, EXPERTS), 16.0 * TOKENS)


def draw_expert_model_stats(key, part):
    return spread_states(key, (EXPERTS, 2, D), 0.12 * TOKENS / EXPERTS)


def draw_expert_hidden_stats(key, part):
    return spread_states(key, (EXPERTS, 3, FE), 0.12 * TOKENS / EXPERTS)


def shard_levels(key, dims, split, low, largest):
    def one(dim, shards_of):
        draws = jax.random.uniform(jax.random.fold_in(jax.random.fold_in(key, 6), dim), (shards_of,), jnp.float32, low / len(split), largest / len(split))
        return jnp.repeat(jnp.exp(draws), dims[dim] // shards_of).reshape((-1,) + (1,) * (len(dims) - dim - 1))

    gain = one(*split[0])
    for cut in split[1:]:
        gain = gain * one(*cut)
    return gain


def split_up(amount, total, reach, skew):
    loads = [(1 << 20) // math.isqrt(rank ** skew) + 1 for rank in range(2, amount + 1)]
    rest, holding = total - reach - (amount - 1), [1] * (amount - 1)
    while rest > 0:
        movable = [i for i in range(amount - 1) if holding[i] < reach]
        whole, left = sum([loads[i] for i in movable]), rest
        for i in movable:
            addition = min(reach - holding[i], max(1, left * loads[i] // whole), rest)
            holding[i] = holding[i] + addition
            rest = rest - addition
    return np.array([reach] + holding)


def uneven(own_key, count, total, bound, lean):
    if count == 2:
        one = jax.random.randint(own_key, (), max(1, total - bound), min(bound, total - 1) + 1)
        return jnp.stack([one, total - one])
    sizes = jnp.asarray(split_up(count, total, bound, lean), jnp.int32)
    pairs = (count - 1) // 2
    giver, taker = sizes[1:1 + 2 * pairs:2], sizes[2:2 + 2 * pairs:2]
    margin = jnp.minimum(giver - 1, bound - taker)
    moved = jax.random.randint(jax.random.fold_in(own_key, 1), (pairs,), 0, 1 << 20) % (margin + 1)
    sizes = sizes.at[1:1 + 2 * pairs:2].set(giver - moved).at[2:2 + 2 * pairs:2].set(taker + moved)
    return sizes[jax.random.permutation(jax.random.fold_in(own_key, 2), count)]


def routed_block(key, own, number, rows, amount, top, most, slope):
    order = jax.random.permutation(key, amount)
    heavy_load, common = shares(amount, rows * top, most, slope, True), shares(amount, rows * top, most, slope, False)
    places = jnp.arange(amount)

    def named(lengths, offset_by):
        used = int((lengths > 0).sum())
        fixed = max(1, used // 4)
        moved = fixed + (places - fixed + offset_by * (used - fixed)) % max(1, amount - fixed)
        return jnp.zeros((amount,), jnp.int32).at[order[jnp.where(places < fixed, places, moved)]].set(jnp.asarray(lengths, jnp.int32))

    lengths = jnp.where(number % 4 == 0, named(heavy_load, number // 4), named(common, number - number // 4 - 1))
    mixed = jax.random.permutation(jax.random.fold_in(own, 3), amount)
    giver, receiver = mixed[0:amount // 2 * 2:2], mixed[1:amount // 2 * 2:2]
    room = jnp.minimum(lengths[giver] - 1, most - lengths[receiver]) // 2
    room = jnp.where((giver == order[0]) | (receiver == order[0]) | (lengths[receiver] == 0), 0, jnp.maximum(room, 0))
    moved = jax.random.randint(jax.random.fold_in(own, 4), (amount // 2,), 0, 1 << 20) % (room + 1)
    lengths = lengths.at[giver].add(-moved).at[receiver].add(moved)
    members = jnp.searchsorted(jnp.cumsum(lengths), jnp.arange(rows * top), side="right").astype(jnp.int32)
    listing = members.reshape(top, rows).T
    listing = listing[jax.random.permutation(jax.random.fold_in(own, 1), rows)]
    offset_by = jax.random.randint(jax.random.fold_in(own, 2), (rows, 1), 0, top)
    return jnp.take_along_axis(listing, (jnp.arange(top)[None, :] + offset_by) % top, axis=1)


def shares(count, total, bound, skew, full):
    weights = [(1 << 20) // math.isqrt(grade ** skew) + 1 for grade in range(1, count + 1)]
    largest = bound if full else min(bound, max(-(-total // count), total * weights[0] // sum(weights)))
    least = 1 if total - largest >= count - 1 else 0
    given, rest = [largest] + [least] * (count - 1), total - largest - least * (count - 1)
    while rest > 0:
        movable = [i for i in range(1, count) if given[i] < largest] or [i for i in range(1, count) if given[i] < bound]
        pool, remaining = sum([weights[i] for i in movable]), rest
        for i in movable:
            extra = min(bound - given[i], max(1, remaining * weights[i] // pool), rest)
            given[i] = given[i] + extra
            rest = rest - extra
    return np.array(given)


def centred(own_key, extent, deviation, most, shards=(), kind=jnp.bfloat16):
    entries = deviation * jax.random.normal(own_key, extent, jnp.float32)
    if shards:
        entries = entries * shard_levels(own_key, extent, shards, -0.22, 0.18)
    return jnp.clip(entries, -most, most).astype(kind)


def setup_inputs(seed: int = 0) -> dict:
    splits = jax.random.split(jax.random.key(seed), 20)
    layer_input = centred(splits[0], (SEQS, LEN, D), 1.0, 6.0, ((0, 4), (1, 2)))
    segments = jax.vmap(lambda own: jnp.searchsorted(jnp.cumsum(uneven(own, DOCS, LEN, LEN // 2, 1)), jnp.arange(LEN), side="right"))(jax.random.split(splits[1], SEQS)).reshape((SEQS, LEN)).astype(jnp.int32)
    routes_keys = jax.random.split(jax.random.fold_in(splits[2], 1), SEQS * LEN // BLK)
    routes_turns = jax.random.permutation(jax.random.fold_in(splits[2], 3), SEQS * LEN // BLK)
    routes = jax.vmap(lambda own, number: routed_block(jax.random.fold_in(splits[2], 2), own, number, BLK, EXPERTS, 2, CAP, 2))(routes_keys, routes_turns).reshape((SEQS, LEN, 2))
    cotangent = centred(splits[3], (SEQS, LEN, D), 1.0, 6.0, ((0, 4), (1, 2)))
    gains = jnp.clip(1.0 + 0.1 * jax.random.normal(splits[4], (2, D), jnp.float32), 0.5, 1.5)
    attention_in = draw_attention_in(jax.random.fold_in(splits[19], 71), 0)
    attention_out = centred(splits[6], (HH, D), (HH // 2) ** -0.5, 0.3125, ((0, 4), (1, 8)), jnp.float32)
    router_weight = centred(splits[7], (D, EXPERTS), D ** -0.5, 0.21875, ((0, 8),), jnp.float32)
    shared_in = centred(splits[8], (D, 2, FF), D ** -0.5, 0.21875, ((0, 8), (2, 4)), jnp.float32)
    shared_down = centred(splits[9], (FF, D), FF ** -0.5, 0.125, ((0, 4), (1, 8)), jnp.float32)
    expert_in = centred(splits[10], (EXPERTS, D, 2, FE), D ** -0.5, 0.21875, ((0, 4), (1, 2), (3, 4)), jnp.float32)
    expert_down = centred(splits[11], (EXPERTS, FE, D), FE ** -0.5, 0.125, ((0, 4), (1, 4), (2, 2)), jnp.float32)
    model_stats = draw_model_stats(jax.random.fold_in(splits[19], 71), 0)
    head_stats = draw_head_stats(jax.random.fold_in(splits[19], 71), 0)
    value_columns = draw_value_columns(jax.random.fold_in(splits[19], 71), 0)
    hidden_stats = draw_hidden_stats(jax.random.fold_in(splits[19], 71), 0)
    router_state = draw_router_state(jax.random.fold_in(splits[19], 71), 0)
    expert_model_stats = draw_expert_model_stats(jax.random.fold_in(splits[19], 71), 0)
    expert_hidden_stats = draw_expert_hidden_stats(jax.random.fold_in(splits[19], 71), 0)
    return dict(layer_input=layer_input, segments=segments, routes=routes, cotangent=cotangent, gains=gains, attention_in=attention_in, attention_out=attention_out, router_weight=router_weight, shared_in=shared_in, shared_down=shared_down, expert_in=expert_in, expert_down=expert_down, model_stats=model_stats, head_stats=head_stats, value_columns=value_columns, hidden_stats=hidden_stats, router_state=router_state, expert_model_stats=expert_model_stats, expert_hidden_stats=expert_hidden_stats)


EPSILON = 1e-06
TINY_SQUARE = 1e-30
SCALE_FLOOR = 0.001
DECAY_RATE = 0.5
CLIP_LIMIT = 0.5
STEP_RATE = 0.5
FULL_PRECISION = lax.Precision.HIGHEST

@jax.custom_vjp
def low(v):
    return lax.optimization_barrier(v.astype(jnp.bfloat16)).astype(jnp.float32)

@jax.custom_vjp
def low_back(v):
    return v

def low_keep(v):
    return (low(v), None)

def low_pass(kept, grad):
    return (grad,)

def back_keep(v):
    return (v, None)

def back_low(kept, grad):
    return (low(grad),)
low.defvjp(low_keep, low_pass)
low_back.defvjp(back_keep, back_low)

def rms_norm(values, gain_vec):
    inv_rms = lax.rsqrt(lax.optimization_barrier(jnp.mean(values * values, axis=-1, keepdims=True)) + EPSILON)
    return values * inv_rms * gain_vec

def swiglu(gate_up):
    return jax.nn.silu(gate_up[:, 0]) * gate_up[:, 1]

def rope_tables(seq_len):
    half_dim = HD // 2
    frequency = 10000.0 ** (-jnp.arange(half_dim, dtype=jnp.float32) / half_dim)
    angles = jnp.arange(seq_len, dtype=jnp.float32)[:, None] * frequency[None, :]
    return (jnp.cos(angles), jnp.sin(angles))

def rotate(values, cosine, sine_tab):
    half_dim = values.shape[-1] // 2
    first_half = values[..., :half_dim]
    second_half = values[..., half_dim:]
    cos_b = cosine[:, None, :]
    sin_b = sine_tab[:, None, :]
    return jnp.concatenate([first_half * cos_b - second_half * sin_b, second_half * cos_b + first_half * sin_b], axis=-1)

def attend(queries, keys, values, seg_ids):
    seq_len = queries.shape[0]
    block_rows = min(512, seq_len)
    keys_padded = jnp.pad(keys, ((WINDOW, 0), (0, 0), (0, 0)))
    values_padded = jnp.pad(values, ((WINDOW, 0), (0, 0), (0, 0)))
    seg_padded = jnp.pad(seg_ids, (WINDOW, 0), constant_values=-1)

    def one_block(start_row):
        query_rows = lax.dynamic_slice_in_dim(queries, start_row, block_rows, 0)
        key_rows = lax.dynamic_slice_in_dim(keys_padded, start_row, block_rows + WINDOW, 0)
        value_rows = lax.dynamic_slice_in_dim(values_padded, start_row, block_rows + WINDOW, 0)
        seg_query = lax.dynamic_slice_in_dim(seg_ids, start_row, block_rows, 0)
        seg_key = lax.dynamic_slice_in_dim(seg_padded, start_row, block_rows + WINDOW, 0)
        distance = jnp.arange(block_rows)[:, None] + WINDOW - jnp.arange(block_rows + WINDOW)[None, :]
        allowed = (distance >= 0) & (distance < WINDOW) & (seg_query[:, None] == seg_key[None, :])
        scores = low_back(jnp.einsum('qhd,khd->hqk', query_rows, key_rows, precision=FULL_PRECISION) * 0.125)
        attn_probs = jax.nn.softmax(jnp.where(allowed[None], scores, -1e+30), axis=-1)
        return jnp.einsum('hqk,khd->qhd', low(attn_probs), value_rows, precision=FULL_PRECISION)
    starts = jnp.arange(seq_len // block_rows, dtype=jnp.int32) * block_rows
    return lax.map(jax.checkpoint(one_block), starts).reshape(seq_len, HEADS, HD)

def slot_tables(block_routes, experts, capacity):
    flat_routes = block_routes.reshape(-1)
    route_count = flat_routes.shape[0]
    onehot = (flat_routes[:, None] == jnp.arange(experts, dtype=jnp.int32)[None, :]).astype(jnp.int32)
    rank_in = lax.optimization_barrier(jnp.sum((jnp.cumsum(onehot, axis=0, dtype=jnp.int32) - 1) * onehot, axis=1, dtype=jnp.int32))
    slot_index = flat_routes * capacity + rank_in
    owner_route = jnp.zeros((experts * capacity,), jnp.int32).at[slot_index].set(jnp.arange(route_count, dtype=jnp.int32))
    filled = jnp.zeros((experts * capacity,), jnp.int32).at[slot_index].set(1)
    return (slot_index, owner_route, filled)

def expert_ffn(operands):
    inputs, weight_in, weight_down = operands
    gate_up = low_back(jnp.einsum('rd,dgf->rgf', inputs, weight_in, precision=FULL_PRECISION))
    hidden = low(swiglu(gate_up))
    return low_back(jnp.dot(hidden, weight_down, precision=FULL_PRECISION))

def pick_rows(table, position):
    return table[position]

def block_forward(layer_input, gains, attention_in, attention_out, router_weight, shared_in, shared_down, expert_in, expert_down, segments=None, routes=None):
    gains = low(gains)
    attention_in = low(attention_in)
    attention_out = low(attention_out)
    router_weight = low(router_weight)
    shared_in = low(shared_in)
    shared_down = low(shared_down)
    expert_in = low(expert_in)
    expert_down = low(expert_down)
    seq_count, seq_len, model_width = layer_input.shape
    token_rows = layer_input.reshape(seq_count * seq_len, model_width)
    normed_one = low(rms_norm(token_rows, gains[0]))
    projected = low_back(jnp.einsum('td,dgf->tgf', normed_one, attention_in, precision=FULL_PRECISION))
    cosine, sine_tab = rope_tables(seq_len)
    shaped = projected.reshape(seq_count, seq_len, 3, HEADS, HD)
    queries = low(rotate(shaped[:, :, 0], cosine, sine_tab))
    keys = low(rotate(shaped[:, :, 1], cosine, sine_tab))
    values = low(shaped[:, :, 2])
    attended = lax.map(lambda operands: attend(*operands), (queries, keys, values, segments))
    mixed_heads = low_back(low(attended.reshape(seq_count * seq_len, HH)))
    after_attn = token_rows + low_back(jnp.dot(mixed_heads, attention_out, precision=FULL_PRECISION))
    normed_two = low(rms_norm(after_attn, gains[1]))
    logits = low_back(jnp.dot(normed_two, router_weight, precision=FULL_PRECISION))
    route_flat = routes.reshape(-1, 2)
    picked = jnp.take_along_axis(logits, route_flat, axis=1)
    gate_probs = jax.nn.softmax(picked, axis=-1)
    shared_gate_up = low_back(jnp.einsum('td,dgf->tgf', normed_two, shared_in, precision=FULL_PRECISION))
    shared_hidden = low(swiglu(shared_gate_up))
    shared_out = jnp.dot(shared_hidden, shared_down, precision=FULL_PRECISION)
    block_routes = routes.reshape(-1, BLK, 2)
    block_count = block_routes.shape[0]
    slot_index, owner_route, filled = jax.vmap(partial(slot_tables, experts=EXPERTS, capacity=CAP))(block_routes)
    token_blocks = normed_two.reshape(block_count, BLK, model_width)
    sent_rows = jax.vmap(pick_rows)(token_blocks, owner_route // 2) * filled[:, :, None].astype(jnp.float32)
    per_expert = sent_rows.reshape(block_count, EXPERTS, CAP, model_width).transpose(1, 0, 2, 3).reshape(EXPERTS, block_count * CAP, model_width)
    expert_outs = lax.map(jax.checkpoint(expert_ffn), (per_expert, expert_in, expert_down))
    returned_rows = expert_outs.reshape(EXPERTS, block_count, CAP, model_width).transpose(1, 0, 2, 3).reshape(block_count, EXPERTS * CAP, model_width)
    route_out = jax.vmap(pick_rows)(returned_rows, slot_index).reshape(-1, 2, model_width)
    mixed_out = after_attn + shared_out + lax.optimization_barrier(jnp.sum(gate_probs[:, :, None] * route_out, axis=1))
    return mixed_out.reshape(seq_count, seq_len, model_width)

def factored(grad_mats, rows_old, cols_old):
    squares = grad_mats * grad_mats + TINY_SQUARE
    rows_new = DECAY_RATE * rows_old + (1.0 - DECAY_RATE) * lax.optimization_barrier(jnp.mean(squares, axis=2))
    cols_new = DECAY_RATE * cols_old + (1.0 - DECAY_RATE) * lax.optimization_barrier(jnp.mean(squares, axis=1))
    second_moment = rows_new[:, :, None] * cols_new[:, None, :] / lax.optimization_barrier(jnp.mean(rows_new, axis=1))[:, None, None]
    return (grad_mats * lax.rsqrt(second_moment), rows_new, cols_new)

def apply_step(weight, update):
    update_root = jnp.sqrt(jnp.mean(update * update))
    param_scale = jnp.maximum(SCALE_FLOOR, jnp.sqrt(jnp.mean(weight * weight)))
    return (weight - STEP_RATE * param_scale * update / jnp.maximum(1.0, update_root / CLIP_LIMIT), update_root)

def reference(layer_input, segments, routes, cotangent, gains, attention_in, attention_out, router_weight, shared_in, shared_down, expert_in, expert_down, model_stats, head_stats, value_columns, hidden_stats, router_state, expert_model_stats, expert_hidden_stats):
    forward_fn = partial(block_forward, segments=segments, routes=routes)
    mixed_out, pullback = jax.vjp(forward_fn, layer_input.astype(jnp.float32), gains, attention_in, attention_out, router_weight, shared_in, shared_down, expert_in, expert_down)
    gradients = pullback(cotangent.astype(jnp.float32))
    input_grad, grad_gains, grad_attn_in, grad_attn_out, grad_router, grad_shared_in, grad_shared_down, grad_expert_in, grad_expert_down = gradients
    gain_state = DECAY_RATE * model_stats[0:2] + (1.0 - DECAY_RATE) * (grad_gains * grad_gains + TINY_SQUARE)
    update_gains = grad_gains * lax.rsqrt(gain_state)
    router_new = DECAY_RATE * router_state + (1.0 - DECAY_RATE) * (grad_router * grad_router + TINY_SQUARE)
    update_router = grad_router * lax.rsqrt(router_new)
    attn_cols_old = jnp.concatenate([head_stats[0:2], value_columns[None]], axis=0).reshape(1, 3 * HH)
    update_attn_in, rows_attn_in, cols_attn_in = factored(grad_attn_in.reshape(1, D, 3 * HH), model_stats[2][None], attn_cols_old)
    update_attn_out, rows_attn_out, cols_attn_out = factored(grad_attn_out[None], head_stats[2][None], model_stats[4][None])
    update_shared_in, rows_shared_in, cols_shared_in = factored(grad_shared_in.reshape(1, D, 2 * FF), model_stats[3][None], hidden_stats[0:2].reshape(1, 2 * FF))
    update_shared_down, rows_shared_down, cols_shared_down = factored(grad_shared_down[None], hidden_stats[2][None], model_stats[5][None])
    update_expert_in, rows_expert_in, cols_expert_in = factored(grad_expert_in.reshape(EXPERTS, D, 2 * FE), expert_model_stats[:, 0], expert_hidden_stats[:, 0:2].reshape(EXPERTS, 2 * FE))
    update_expert_down, rows_expert_down, cols_expert_down = factored(grad_expert_down, expert_hidden_stats[:, 2], expert_model_stats[:, 1])
    new_gains, root_gains = apply_step(gains, update_gains)
    new_attn_in, root_attn_in = apply_step(attention_in, update_attn_in.reshape(D, 3, HH))
    new_attn_out, root_attn_out = apply_step(attention_out, update_attn_out[0])
    new_router, root_router = apply_step(router_weight, update_router)
    new_shared_in, root_shared_in = apply_step(shared_in, update_shared_in.reshape(D, 2, FF))
    new_shared_down, root_shared_down = apply_step(shared_down, update_shared_down[0])
    new_expert_in, root_expert_in = apply_step(expert_in, update_expert_in.reshape(EXPERTS, D, 2, FE))
    new_expert_down, root_expert_down = apply_step(expert_down, update_expert_down)
    new_model_stats = jnp.concatenate([gain_state, rows_attn_in, rows_shared_in, cols_attn_out, cols_shared_down], axis=0)
    attn_cols_new = cols_attn_in.reshape(3, HH)
    new_head_stats = jnp.concatenate([attn_cols_new[0:2], rows_attn_out], axis=0)
    new_value_columns = attn_cols_new[2]
    new_hidden_stats = jnp.concatenate([cols_shared_in.reshape(2, FF), rows_shared_down], axis=0)
    new_expert_model_stats = jnp.stack([rows_expert_in, cols_expert_down], axis=1)
    new_expert_hidden_stats = jnp.concatenate([cols_expert_in.reshape(EXPERTS, 2, FE), rows_expert_down[:, None]], axis=1)
    update_rms = jnp.stack([root_gains, root_attn_in, root_attn_out, root_router, root_shared_in, root_shared_down, root_expert_in, root_expert_down])
    return (mixed_out.astype(jnp.bfloat16), input_grad, grad_gains, grad_attn_in, grad_attn_out, grad_router, grad_shared_in, grad_shared_down, grad_expert_in, grad_expert_down, new_gains, new_attn_in, new_attn_out, new_router, new_shared_in, new_shared_down, new_expert_in, new_expert_down, new_model_stats, new_head_stats, new_value_columns, new_hidden_stats, router_new, new_expert_model_stats, new_expert_hidden_stats, update_rms)
```

```python
import jax
import jax.numpy as jnp
from jax import lax
from jax.sharding import PartitionSpec as P

D = 768
HD = 64
FF = 2048
FE = 2048
WINDOW = 1024
HH = 768


EPSILON = 1e-06
TINY_SQUARE = 1e-30
SCALE_FLOOR = 0.001
DECAY_RATE = 0.5
CLIP_LIMIT = 0.5
STEP_RATE = 0.5


def from_behind(value, axis, steps):
    count = lax.axis_size(axis)
    leading, last = (max(0, -steps), min(count, count - steps))
    return lax.ppermute(value, axis, [(source, source + steps) for source in range(leading, last)])


def rms_norm(values, gain_vec):
    inv_rms = lax.rsqrt(jnp.mean(values * values, axis=-1, keepdims=True) + EPSILON)
    return values * inv_rms * gain_vec


def swiglu(gate_up):
    return jax.nn.silu(gate_up[:, 0]) * gate_up[:, 1]


def rotate(values, cosine, sine_tab):
    half_dim = values.shape[-1] // 2
    first_half = values[..., :half_dim]
    second_half = values[..., half_dim:]
    cos_b = cosine[:, None, :]
    sin_b = sine_tab[:, None, :]
    return jnp.concatenate(
        [first_half * cos_b - second_half * sin_b, second_half * cos_b + first_half * sin_b],
        axis=-1,
    )


def slot_tables(block_routes, experts, capacity):
    flat_routes = block_routes.reshape(-1)
    route_count = flat_routes.shape[0]
    onehot = (flat_routes[:, None] == jnp.arange(experts, dtype=jnp.int32)[None, :]).astype(
        jnp.int32
    )
    rank_in = jnp.sum(
        (jnp.cumsum(onehot, axis=0, dtype=jnp.int32) - 1) * onehot, axis=1, dtype=jnp.int32
    )
    slot_index = flat_routes * capacity + rank_in
    owner_route = (
        jnp.zeros((experts * capacity,), jnp.int32)
        .at[slot_index]
        .set(jnp.arange(route_count, dtype=jnp.int32))
    )
    filled = jnp.zeros((experts * capacity,), jnp.int32).at[slot_index].set(1)
    return (slot_index, owner_route, filled)


def block_view(queries, keys_ext, values_ext, seg_own, seg_ext, start_row, base_pos):
    block_len = queries.shape[0]
    block_rows = min(512, block_len)
    query_rows = lax.dynamic_slice_in_dim(queries, start_row, block_rows, 0)
    key_rows = lax.dynamic_slice_in_dim(
        keys_ext, start_row + block_len - WINDOW, block_rows + WINDOW, 0
    )
    value_rows = lax.dynamic_slice_in_dim(
        values_ext, start_row + block_len - WINDOW, block_rows + WINDOW, 0
    )
    scores = (
        jnp.einsum("qhd,khd->hqk", query_rows, key_rows, preferred_element_type=jnp.float32) * 0.125
    )
    query_pos = start_row + jnp.arange(block_rows, dtype=jnp.int32)
    key_pos = start_row - WINDOW + jnp.arange(block_rows + WINDOW, dtype=jnp.int32)
    distance = query_pos[:, None] - key_pos[None, :]
    seg_query = lax.dynamic_slice_in_dim(seg_own, start_row, block_rows, 0)
    seg_key = lax.dynamic_slice_in_dim(
        seg_ext, start_row + block_len - WINDOW, block_rows + WINDOW, 0
    )
    allowed = (
        (distance >= 0)
        & (distance < WINDOW)
        & (seg_query[:, None] == seg_key[None, :])
        & (key_pos[None, :] + base_pos >= 0)
    )
    return (query_rows, key_rows, value_rows, jnp.where(allowed[None], scores, -1e30), allowed)


def factored_update(
    grad_mat, rows_old, cols_old, row_sums, col_sums, row_total, col_total, old_total, square_total
):
    rows_new = DECAY_RATE * rows_old + (1.0 - DECAY_RATE) * row_sums / col_total
    cols_new = DECAY_RATE * cols_old + (1.0 - DECAY_RATE) * col_sums / row_total
    mean_rows = (DECAY_RATE * old_total + (1.0 - DECAY_RATE) * square_total / col_total) / row_total
    second_moment = rows_new[:, None] * cols_new[None, :] / mean_rows
    return (grad_mat * lax.rsqrt(second_moment), rows_new, cols_new)


def apply_update(weight, update, update_root, square_sum, elements):
    param_scale = jnp.maximum(SCALE_FLOOR, jnp.sqrt(square_sum / elements))
    return weight - STEP_RATE * param_scale * update / jnp.maximum(1.0, update_root / CLIP_LIMIT)


def swiglu_experts(gate_up):
    return jax.nn.silu(gate_up[:, :, 0]) * gate_up[:, :, 1]


def gather_packed(pieces, axes):
    flat = jnp.concatenate([piece.reshape(-1) for piece, _ in pieces])
    full = lax.all_gather(flat, axes, axis=0, tiled=False)
    count = full.shape[0]
    results = []
    offset = 0
    for piece, dim in pieces:
        size = piece.size
        part = full[:, offset : offset + size].reshape((count,) + piece.shape)
        offset += size
        part = jnp.moveaxis(part, 0, dim)
        shape = list(piece.shape)
        shape[dim] *= count
        results.append(part.reshape(shape))
    return results


def scatter_packed(pieces, axes, count):
    columns = []
    local_shapes = []
    for grad, dim in pieces:
        shape = grad.shape
        split = shape[:dim] + (count, shape[dim] // count) + shape[dim + 1 :]
        local_shapes.append(shape[:dim] + (shape[dim] // count,) + shape[dim + 1 :])
        part = jnp.moveaxis(grad.reshape(split), dim, 0)
        columns.append(part.reshape(count, -1))
    packed = jnp.concatenate(columns, axis=1)
    width = packed.shape[1]
    rows = -(-width // 1024) * 8
    packed = jnp.pad(packed, ((0, 0), (0, rows * 128 - width))).reshape(count * rows, 128)
    own = lax.psum_scatter(packed, axes, scatter_dimension=0, tiled=True).reshape(-1)
    results = []
    offset = 0
    for local_shape in local_shapes:
        size = 1
        for extent in local_shape:
            size *= extent
        results.append(own[offset : offset + size].reshape(local_shape))
        offset += size
    return results


def experts_dense(normed_two, grad_out, weights, expert_in_all, expert_down_all):
    gate_up = jnp.einsum(
        "td,edgf->etgf", normed_two, expert_in_all, preferred_element_type=jnp.float32
    )
    act, act_back = jax.vjp(swiglu_experts, gate_up)
    hidden = act.astype(jnp.bfloat16)
    outs = jnp.einsum("etf,efd->etd", hidden, expert_down_all, preferred_element_type=jnp.float32)
    weights_e = weights.T[:, :, None]
    combined = jnp.sum(weights_e * outs, axis=0)
    gate_dots = jnp.sum(outs * grad_out[None], axis=-1).T
    grad_outs = (weights_e * grad_out[None]).astype(jnp.bfloat16)
    grad_hidden = jnp.einsum(
        "etd,efd->etf", grad_outs, expert_down_all, preferred_element_type=jnp.float32
    )
    grad_gate_up = act_back(grad_hidden)[0].astype(jnp.bfloat16)
    grad_down = jnp.einsum("etf,etd->efd", hidden, grad_outs, preferred_element_type=jnp.float32)
    grad_in = jnp.einsum(
        "td,etgf->edgf", normed_two, grad_gate_up, preferred_element_type=jnp.float32
    )
    grad_rows = jnp.einsum(
        "etgf,edgf->td", grad_gate_up, expert_in_all, preferred_element_type=jnp.float32
    )
    return combined, gate_dots, grad_rows, grad_in, grad_down


def experts_routed(
    normed_two, grad_out, route_rows, gate_probs, expert_in_low, expert_down_low, capacity
):
    block_len, model_width = normed_two.shape
    experts = lax.axis_size("fsdp")
    slot_index, owner_route, filled = slot_tables(route_rows, experts, capacity)
    fill_mask = filled.astype(jnp.bfloat16)[:, None]
    send_rows = (normed_two[owner_route // 2] * fill_mask).reshape(experts, capacity, model_width)
    route_grads = (
        (gate_probs[:, :, None] * grad_out[:, None, :])
        .astype(jnp.bfloat16)
        .reshape(2 * block_len, model_width)
    )
    grad_rows_sent = (route_grads[owner_route] * fill_mask).reshape(experts, capacity, model_width)
    exchange = lambda rows: lax.all_to_all(rows, "fsdp", split_axis=0, concat_axis=0, tiled=True)
    received = exchange(send_rows).reshape(experts * capacity, model_width)
    grad_received = exchange(grad_rows_sent).reshape(experts * capacity, model_width)
    gate_up = jnp.einsum("rd,dgf->rgf", received, expert_in_low, preferred_element_type=jnp.float32)
    act, act_back = jax.vjp(swiglu, gate_up)
    hidden = act.astype(jnp.bfloat16)
    outs = jnp.dot(hidden, expert_down_low, preferred_element_type=jnp.float32)
    grad_hidden = jnp.einsum(
        "rd,fd->rf", grad_received, expert_down_low, preferred_element_type=jnp.float32
    )
    grad_gate_up = act_back(grad_hidden)[0].astype(jnp.bfloat16)
    grad_in = jnp.einsum("rd,rgf->dgf", received, grad_gate_up, preferred_element_type=jnp.float32)
    grad_down = jnp.einsum("rf,rd->fd", hidden, grad_received, preferred_element_type=jnp.float32)
    grad_expert_rows = jnp.einsum(
        "rgf,dgf->rd", grad_gate_up, expert_in_low, preferred_element_type=jnp.float32
    )
    returned = exchange(outs.reshape(experts, capacity, model_width))
    route_out = returned.reshape(experts * capacity, model_width)[slot_index].reshape(
        block_len, 2, model_width
    )
    grad_returned = exchange(grad_expert_rows.reshape(experts, capacity, model_width))
    grad_routes = grad_returned.reshape(experts * capacity, model_width)[slot_index].reshape(
        block_len, 2, model_width
    )
    combined = jnp.sum(gate_probs[:, :, None] * route_out, axis=1)
    gate_dots = jnp.sum(grad_out[:, None, :] * route_out, axis=-1)
    grad_rows = jnp.sum(grad_routes, axis=1)
    own_in = lax.psum_scatter(grad_in[None], "ctx", scatter_dimension=1, tiled=True)
    own_down = lax.psum_scatter(grad_down[None], "ctx", scatter_dimension=2, tiled=True)
    return combined, gate_dots, grad_rows, own_in, own_down


def local(
    layer_input,
    segments,
    routes,
    cotangent,
    gains,
    attention_in,
    attention_out,
    router_weight,
    shared_in,
    shared_down,
    expert_in,
    expert_down,
    model_stats,
    head_stats,
    value_columns,
    hidden_stats,
    router_state,
    expert_model_stats,
    expert_hidden_stats,
):
    block_len = layer_input.shape[1]
    model_width = layer_input.shape[2]
    experts = router_weight.shape[1]
    dense_experts = experts <= 4
    capacity = min(block_len, 4 * block_len // experts)
    ctx_index = lax.axis_index("ctx")
    tp_index = lax.axis_index("tp")
    fsdp_index = lax.axis_index("fsdp")
    shard_index = lax.axis_index(("fsdp", "ctx"))
    shard_count = lax.axis_size(("fsdp", "ctx"))
    ctx_count = lax.axis_size("ctx")
    base_pos = ctx_index * block_len
    low = lambda v: v.astype(jnp.bfloat16)
    gain_low, attn_in_low = gather_packed(
        [(low(gains), 1), (low(attention_in), 0)], ("fsdp", "ctx")
    )
    later = [
        (low(attention_out), 1),
        (low(router_weight), 0),
        (low(shared_in), 0),
        (low(shared_down), 1),
    ]
    if dense_experts:
        later += [(low(expert_in), 0), (low(expert_down), 0)]
    later_full = gather_packed(later, ("fsdp", "ctx"))
    attn_out_low, router_low, shared_in_low, shared_down_low = later_full[:4]
    if dense_experts:
        fe_local = expert_down.shape[1]
        expert_in_all = later_full[4].reshape(experts, model_width, 2, fe_local)
        expert_down_all = (
            later_full[5]
            .reshape(experts, ctx_count, fe_local, model_width // ctx_count)
            .transpose(0, 2, 1, 3)
            .reshape(experts, fe_local, model_width)
        )
    else:
        expert_in_low = lax.all_gather(low(expert_in), "ctx", axis=1, tiled=True)[0]
        expert_down_low = lax.all_gather(low(expert_down), "ctx", axis=2, tiled=True)[0]
    residual = layer_input[0].astype(jnp.float32)
    gain_one = gain_low[0].astype(jnp.float32)
    gain_two = gain_low[1].astype(jnp.float32)
    normed_one, norm_one_back = jax.vjp(rms_norm, residual, gain_one)
    normed_one = normed_one.astype(jnp.bfloat16)
    projected = jnp.einsum(
        "td,dgf->tgf", normed_one, attn_in_low, preferred_element_type=jnp.float32
    )
    local_cols = projected.shape[2]
    local_heads = local_cols // HD
    half_dim = HD // 2
    frequency = 10000.0 ** (-jnp.arange(half_dim, dtype=jnp.float32) / half_dim)
    angles = (base_pos + jnp.arange(block_len, dtype=jnp.int32)).astype(jnp.float32)[
        :, None
    ] * frequency[None, :]
    cosine = jnp.cos(angles)
    sine_tab = jnp.sin(angles)
    queries = rotate(projected[:, 0].reshape(block_len, local_heads, HD), cosine, sine_tab).astype(
        jnp.bfloat16
    )
    keys_own = rotate(projected[:, 1].reshape(block_len, local_heads, HD), cosine, sine_tab).astype(
        jnp.bfloat16
    )
    values_own = projected[:, 2].reshape(block_len, local_heads, HD).astype(jnp.bfloat16)
    seg_own = segments[0].astype(jnp.bfloat16)
    keys_prev, values_prev, seg_prev = from_behind((keys_own, values_own, seg_own), "ctx", 1)
    keys_ext = jnp.concatenate([keys_prev, keys_own], axis=0)
    values_ext = jnp.concatenate([values_prev, values_own], axis=0)
    seg_ext = jnp.concatenate([seg_prev, seg_own], axis=0)
    block_rows = min(512, block_len)
    block_total = block_len // block_rows
    starts = jnp.arange(block_total, dtype=jnp.int32) * block_rows

    def forward_block(start_row):
        query_rows, key_rows, value_rows, masked, allowed = block_view(
            queries, keys_ext, values_ext, seg_own, seg_ext, start_row, base_pos
        )
        row_max = jnp.max(masked, axis=-1, keepdims=True)
        exp_terms = jnp.where(allowed[None], jnp.exp(masked - row_max), 0.0)
        row_total = jnp.sum(exp_terms, axis=-1, keepdims=True)
        attn_probs = (exp_terms / row_total).astype(jnp.bfloat16)
        attended = jnp.einsum(
            "hqk,khd->qhd", attn_probs, value_rows, preferred_element_type=jnp.float32
        )
        return (attended, row_max + jnp.log(row_total))

    attended, log_totals = lax.map(forward_block, starts)
    mixed_heads = attended.reshape(block_len, local_cols).astype(jnp.bfloat16)
    attn_total = lax.psum(
        jnp.dot(mixed_heads, attn_out_low, preferred_element_type=jnp.float32), "tp"
    )
    after_attn = residual + attn_total
    normed_two, norm_two_back = jax.vjp(rms_norm, after_attn, gain_two)
    normed_two = normed_two.astype(jnp.bfloat16)
    logits = jnp.dot(normed_two, router_low, preferred_element_type=jnp.float32)
    route_rows = routes[0]
    onehot = (route_rows[:, :, None] == jnp.arange(experts, dtype=jnp.int32)[None, None, :]).astype(
        jnp.float32
    )
    picked = jnp.sum(onehot * logits[:, None, :], axis=-1)
    gate_probs = jax.nn.softmax(picked, axis=-1)
    upstream = cotangent[0]
    grad_out = upstream.astype(jnp.float32)
    if dense_experts:
        weights = jnp.sum(gate_probs[:, :, None] * onehot, axis=1)
        combined, dots_e, grad_rows, grad_expert_in, grad_expert_down = experts_dense(
            normed_two, grad_out, weights, expert_in_all, expert_down_all
        )
        gate_dots = jnp.sum(onehot * dots_e[:, None, :], axis=-1)
    else:
        combined, gate_dots, grad_rows, own_expert_in, own_expert_down = experts_routed(
            normed_two,
            grad_out,
            route_rows,
            gate_probs,
            expert_in_low,
            expert_down_low,
            capacity,
        )
    shared_gate_up = jnp.einsum(
        "td,dgf->tgf", normed_two, shared_in_low, preferred_element_type=jnp.float32
    )
    shared_act, shared_act_back = jax.vjp(swiglu, shared_gate_up)
    shared_hidden = shared_act.astype(jnp.bfloat16)
    shared_out = jnp.dot(shared_hidden, shared_down_low, preferred_element_type=jnp.float32)
    grad_shared_hidden = jnp.einsum(
        "td,fd->tf", upstream, shared_down_low, preferred_element_type=jnp.float32
    )
    grad_shared_gate_up = shared_act_back(grad_shared_hidden)[0].astype(jnp.bfloat16)
    partial_two = (
        jnp.einsum(
            "tgf,dgf->td", grad_shared_gate_up, shared_in_low, preferred_element_type=jnp.float32
        )
        + grad_rows
    )
    branch_total, grad_normed_part, gate_total = lax.psum(
        (shared_out + combined, partial_two, gate_dots), "tp"
    )
    layer_out = after_attn + branch_total
    grad_picked = gate_probs * (
        gate_total - jnp.sum(gate_probs * gate_total, axis=-1, keepdims=True)
    )
    grad_logits = jnp.sum(grad_picked[:, :, None] * onehot, axis=1).astype(jnp.bfloat16)
    grad_shared_in = jnp.einsum(
        "td,tgf->dgf", normed_two, grad_shared_gate_up, preferred_element_type=jnp.float32
    )
    grad_shared_down = jnp.einsum(
        "tf,td->fd", shared_hidden, upstream, preferred_element_type=jnp.float32
    )
    grad_router = jnp.einsum(
        "td,te->de", normed_two, grad_logits, preferred_element_type=jnp.float32
    )
    grad_normed_two = grad_normed_part + jnp.einsum(
        "te,de->td", grad_logits, router_low, preferred_element_type=jnp.float32
    )
    grad_after, grad_gain_two = norm_two_back(grad_normed_two)
    grad_after = grad_after + grad_out
    grad_attn_low = grad_after.astype(jnp.bfloat16)
    grad_attn_out = jnp.einsum(
        "tc,td->cd", mixed_heads, grad_attn_low, preferred_element_type=jnp.float32
    )
    first_grads = [
        (grad_attn_out, 1),
        (grad_router, 0),
        (grad_shared_in, 0),
        (grad_shared_down, 1),
        (grad_gain_two, 0),
    ]
    if dense_experts:
        fe_local = expert_down.shape[1]
        first_grads += [
            (grad_expert_in.reshape(shard_count * expert_in.shape[1], 2, fe_local), 0),
            (
                grad_expert_down.reshape(experts, fe_local, ctx_count, model_width // ctx_count)
                .transpose(0, 2, 1, 3)
                .reshape(shard_count * fe_local, model_width // ctx_count),
                0,
            ),
        ]
    first_own = scatter_packed(first_grads, ("fsdp", "ctx"), shard_count)
    own_attn_out, own_router, own_shared_in, own_shared_down, own_gain_two = first_own[:5]
    if dense_experts:
        own_expert_in = first_own[5][None]
        own_expert_down = first_own[6][None]
    grad_heads = (
        jnp.einsum("td,cd->tc", grad_attn_low, attn_out_low, preferred_element_type=jnp.float32)
        .astype(jnp.bfloat16)
        .reshape(block_len, local_heads, HD)
    )

    def backward_block(block_number, running):
        grad_keys, grad_values, grad_queries = running
        start_row = block_number * block_rows
        query_rows, key_rows, value_rows, masked, allowed = block_view(
            queries, keys_ext, values_ext, seg_own, seg_ext, start_row, base_pos
        )
        log_total = lax.dynamic_index_in_dim(log_totals, block_number, 0, keepdims=False)
        attn_probs = jnp.where(allowed[None], jnp.exp(masked - log_total), 0.0)
        grad_block = lax.dynamic_slice_in_dim(grad_heads, start_row, block_rows, 0)
        grad_probs = jnp.einsum(
            "qhd,khd->hqk", grad_block, value_rows, preferred_element_type=jnp.float32
        )
        inner_sum = jnp.sum(attn_probs * grad_probs, axis=-1, keepdims=True)
        grad_scores = (attn_probs * (grad_probs - inner_sum)).astype(jnp.bfloat16)
        grad_query_rows = (
            jnp.einsum("hqk,khd->qhd", grad_scores, key_rows, preferred_element_type=jnp.float32)
            * 0.125
        )
        grad_key_rows = (
            jnp.einsum("hqk,qhd->khd", grad_scores, query_rows, preferred_element_type=jnp.float32)
            * 0.125
        )
        grad_value_rows = jnp.einsum(
            "hqk,qhd->khd",
            attn_probs.astype(jnp.bfloat16),
            grad_block,
            preferred_element_type=jnp.float32,
        )
        key_offset = start_row + block_len - WINDOW
        grad_keys = lax.dynamic_update_slice_in_dim(
            grad_keys,
            lax.dynamic_slice_in_dim(grad_keys, key_offset, block_rows + WINDOW, 0) + grad_key_rows,
            key_offset,
            0,
        )
        grad_values = lax.dynamic_update_slice_in_dim(
            grad_values,
            lax.dynamic_slice_in_dim(grad_values, key_offset, block_rows + WINDOW, 0)
            + grad_value_rows,
            key_offset,
            0,
        )
        grad_queries = lax.dynamic_update_slice_in_dim(grad_queries, grad_query_rows, start_row, 0)
        return (grad_keys, grad_values, grad_queries)

    zero_ext = jnp.zeros((2 * block_len, local_heads, HD), jnp.float32)
    zero_own = jnp.zeros((block_len, local_heads, HD), jnp.float32)
    grad_keys, grad_values, grad_queries = lax.fori_loop(
        0, block_total, backward_block, (zero_ext, zero_ext, zero_own)
    )
    rim_keys, rim_values = (
        from_behind(grad_keys[:block_len].astype(jnp.bfloat16), "ctx", -1).astype(jnp.float32),
        from_behind(grad_values[:block_len].astype(jnp.bfloat16), "ctx", -1).astype(jnp.float32),
    )
    grad_keys_own = grad_keys[block_len:] + rim_keys
    grad_values_own = grad_values[block_len:] + rim_values
    grad_query_raw = rotate(grad_queries, cosine, -sine_tab)
    grad_key_raw = rotate(grad_keys_own, cosine, -sine_tab)
    grad_projected = (
        jnp.stack([grad_query_raw, grad_key_raw, grad_values_own], axis=1)
        .reshape(block_len, 3, local_cols)
        .astype(jnp.bfloat16)
    )
    grad_attn_in = jnp.einsum(
        "td,tgf->dgf", normed_one, grad_projected, preferred_element_type=jnp.float32
    )
    partial_one = jnp.einsum(
        "tgf,dgf->td", grad_projected, attn_in_low, preferred_element_type=jnp.float32
    )
    grad_residual, grad_gain_one = norm_one_back(lax.psum(partial_one, "tp"))
    input_grad = grad_after + grad_residual
    own_attn_in, own_gain_one = scatter_packed(
        [(grad_attn_in, 0), (grad_gain_one, 0)], ("fsdp", "ctx"), shard_count
    )
    own_gains = jnp.stack([own_gain_one, own_gain_two])
    lead_tp = (tp_index == 0).astype(jnp.float32)
    first_shard = (shard_index == 0).astype(jnp.float32)
    first_ctx = (ctx_index == 0).astype(jnp.float32)
    d_local = gains.shape[1]
    ff_local = shared_down.shape[0]
    fe_local = expert_down.shape[1]
    d_quarter = expert_in.shape[1]
    square_attn_in = own_attn_in * own_attn_in + TINY_SQUARE
    square_attn_out = own_attn_out * own_attn_out + TINY_SQUARE
    square_shared_in = own_shared_in * own_shared_in + TINY_SQUARE
    square_shared_down = own_shared_down * own_shared_down + TINY_SQUARE
    square_expert_in = own_expert_in[0] * own_expert_in[0] + TINY_SQUARE
    square_expert_down = own_expert_down[0] * own_expert_down[0] + TINY_SQUARE
    model_part = lax.dynamic_update_slice(
        jnp.zeros((4, D), jnp.float32),
        jnp.stack(
            [
                jnp.sum(square_attn_in, axis=(1, 2)),
                jnp.sum(square_shared_in, axis=(1, 2)),
                jnp.sum(square_attn_out, axis=0),
                jnp.sum(square_shared_down, axis=0),
            ]
        ),
        (0, shard_index * d_local),
    )
    head_part = lax.dynamic_update_slice(
        jnp.zeros((4, HH), jnp.float32),
        jnp.concatenate(
            [jnp.sum(square_attn_in, axis=0), jnp.sum(square_attn_out, axis=1)[None]], axis=0
        ),
        (0, tp_index * local_cols),
    )
    hidden_part = lax.dynamic_update_slice(
        jnp.zeros((3, FF), jnp.float32),
        jnp.concatenate(
            [jnp.sum(square_shared_in, axis=0), jnp.sum(square_shared_down, axis=1)[None]], axis=0
        ),
        (0, tp_index * ff_local),
    )
    expert_model_part = lax.dynamic_update_slice(
        jnp.zeros((experts, 2, D), jnp.float32),
        jnp.stack([jnp.sum(square_expert_in, axis=(1, 2)), jnp.sum(square_expert_down, axis=0)])[
            None
        ],
        (fsdp_index, 0, ctx_index * d_quarter),
    )
    expert_hidden_part = lax.dynamic_update_slice(
        jnp.zeros((experts, 3, FE), jnp.float32),
        jnp.concatenate(
            [jnp.sum(square_expert_in, axis=0), jnp.sum(square_expert_down, axis=1)[None]], axis=0
        )[None],
        (fsdp_index, 0, tp_index * fe_local),
    )
    scalar_part = jnp.stack(
        [
            lead_tp * jnp.sum(gains * gains),
            jnp.sum(attention_in * attention_in),
            jnp.sum(attention_out * attention_out),
            lead_tp * jnp.sum(router_weight * router_weight),
            jnp.sum(shared_in * shared_in),
            jnp.sum(shared_down * shared_down),
            jnp.sum(expert_in * expert_in),
            jnp.sum(expert_down * expert_down),
            lead_tp * jnp.sum(model_stats[2]),
            first_shard * jnp.sum(head_stats[2]),
            lead_tp * jnp.sum(model_stats[3]),
            first_shard * jnp.sum(hidden_stats[2]),
        ]
    )
    expert_old_part = lax.dynamic_update_slice(
        jnp.zeros((2, experts), jnp.float32),
        jnp.stack(
            [
                lead_tp * jnp.sum(expert_model_stats[0, 0]),
                first_ctx * jnp.sum(expert_hidden_stats[0, 2]),
            ]
        )[:, None],
        (0, fsdp_index),
    )
    global_sums = lax.psum(
        (
            model_part,
            head_part,
            hidden_part,
            expert_model_part,
            expert_hidden_part,
            scalar_part,
            expert_old_part,
        ),
        ("fsdp", "ctx", "tp"),
    )
    (
        model_sum,
        head_sum,
        hidden_sum,
        expert_model_sum,
        expert_hidden_sum,
        scalar_sum,
        expert_old_sum,
    ) = global_sums
    shard_start = shard_index * d_local
    gain_state = DECAY_RATE * model_stats[0:2] + (1.0 - DECAY_RATE) * (
        own_gains * own_gains + TINY_SQUARE
    )
    update_gains = own_gains * lax.rsqrt(gain_state)
    router_new = DECAY_RATE * router_state + (1.0 - DECAY_RATE) * (
        own_router * own_router + TINY_SQUARE
    )
    update_router = own_router * lax.rsqrt(router_new)
    attn_cols_old = jnp.concatenate([head_stats[0:2], value_columns[None]], axis=0).reshape(-1)
    update_attn_in, rows_attn_in, cols_attn_in = factored_update(
        own_attn_in.reshape(d_local, 3 * local_cols),
        model_stats[2],
        attn_cols_old,
        lax.dynamic_slice_in_dim(model_sum[0], shard_start, d_local),
        lax.dynamic_slice_in_dim(head_sum[0:3], tp_index * local_cols, local_cols, 1).reshape(-1),
        D,
        3 * HH,
        scalar_sum[8],
        jnp.sum(model_sum[0]),
    )
    update_attn_out, rows_attn_out, cols_attn_out = factored_update(
        own_attn_out,
        head_stats[2],
        model_stats[4],
        lax.dynamic_slice_in_dim(head_sum[3], tp_index * local_cols, local_cols),
        lax.dynamic_slice_in_dim(model_sum[2], shard_start, d_local),
        HH,
        D,
        scalar_sum[9],
        jnp.sum(head_sum[3]),
    )
    update_shared_in, rows_shared_in, cols_shared_in = factored_update(
        own_shared_in.reshape(d_local, 2 * ff_local),
        model_stats[3],
        hidden_stats[0:2].reshape(-1),
        lax.dynamic_slice_in_dim(model_sum[1], shard_start, d_local),
        lax.dynamic_slice_in_dim(hidden_sum[0:2], tp_index * ff_local, ff_local, 1).reshape(-1),
        D,
        2 * FF,
        scalar_sum[10],
        jnp.sum(model_sum[1]),
    )
    update_shared_down, rows_shared_down, cols_shared_down = factored_update(
        own_shared_down,
        hidden_stats[2],
        model_stats[5],
        lax.dynamic_slice_in_dim(hidden_sum[2], tp_index * ff_local, ff_local),
        lax.dynamic_slice_in_dim(model_sum[3], shard_start, d_local),
        FF,
        D,
        scalar_sum[11],
        jnp.sum(hidden_sum[2]),
    )
    own_expert_model = lax.dynamic_index_in_dim(expert_model_sum, fsdp_index, 0, keepdims=False)
    own_expert_hidden = lax.dynamic_index_in_dim(expert_hidden_sum, fsdp_index, 0, keepdims=False)
    old_expert_totals = lax.dynamic_index_in_dim(expert_old_sum, fsdp_index, 1, keepdims=False)
    update_expert_in, rows_expert_in, cols_expert_in = factored_update(
        own_expert_in[0].reshape(d_quarter, 2 * fe_local),
        expert_model_stats[0, 0],
        expert_hidden_stats[0, 0:2].reshape(-1),
        lax.dynamic_slice_in_dim(own_expert_model[0], ctx_index * d_quarter, d_quarter),
        lax.dynamic_slice_in_dim(own_expert_hidden[0:2], tp_index * fe_local, fe_local, 1).reshape(
            -1
        ),
        D,
        2 * FE,
        old_expert_totals[0],
        jnp.sum(own_expert_model[0]),
    )
    update_expert_down, rows_expert_down, cols_expert_down = factored_update(
        own_expert_down[0],
        expert_hidden_stats[0, 2],
        expert_model_stats[0, 1],
        lax.dynamic_slice_in_dim(own_expert_hidden[2], tp_index * fe_local, fe_local),
        lax.dynamic_slice_in_dim(own_expert_model[1], ctx_index * d_quarter, d_quarter),
        FE,
        D,
        old_expert_totals[1],
        jnp.sum(own_expert_hidden[2]),
    )
    clip_part = jnp.stack(
        [
            lead_tp * jnp.sum(update_gains * update_gains),
            jnp.sum(update_attn_in * update_attn_in),
            jnp.sum(update_attn_out * update_attn_out),
            lead_tp * jnp.sum(update_router * update_router),
            jnp.sum(update_shared_in * update_shared_in),
            jnp.sum(update_shared_down * update_shared_down),
            jnp.sum(update_expert_in * update_expert_in),
            jnp.sum(update_expert_down * update_expert_down),
        ]
    )
    clip_total = lax.psum(clip_part, ("fsdp", "ctx", "tp"))
    elements = jnp.array(
        [
            2 * D,
            D * 3 * HH,
            HH * D,
            D * experts,
            D * 2 * FF,
            FF * D,
            experts * D * 2 * FE,
            experts * FE * D,
        ],
        jnp.float32,
    )
    update_roots = jnp.sqrt(clip_total / elements)
    new_gains = apply_update(gains, update_gains, update_roots[0], scalar_sum[0], elements[0])
    new_attn_in = apply_update(
        attention_in,
        update_attn_in.reshape(attention_in.shape),
        update_roots[1],
        scalar_sum[1],
        elements[1],
    )
    new_attn_out = apply_update(
        attention_out, update_attn_out, update_roots[2], scalar_sum[2], elements[2]
    )
    new_router = apply_update(
        router_weight, update_router, update_roots[3], scalar_sum[3], elements[3]
    )
    new_shared_in = apply_update(
        shared_in,
        update_shared_in.reshape(shared_in.shape),
        update_roots[4],
        scalar_sum[4],
        elements[4],
    )
    new_shared_down = apply_update(
        shared_down, update_shared_down, update_roots[5], scalar_sum[5], elements[5]
    )
    new_expert_in = apply_update(
        expert_in,
        update_expert_in.reshape(expert_in.shape),
        update_roots[6],
        scalar_sum[6],
        elements[6],
    )
    new_expert_down = apply_update(
        expert_down,
        update_expert_down.reshape(expert_down.shape),
        update_roots[7],
        scalar_sum[7],
        elements[7],
    )
    new_model_stats = jnp.concatenate(
        [gain_state, jnp.stack([rows_attn_in, rows_shared_in, cols_attn_out, cols_shared_down])],
        axis=0,
    )
    attn_cols_new = cols_attn_in.reshape(3, local_cols)
    new_head_stats = jnp.concatenate([attn_cols_new[0:2], rows_attn_out[None]], axis=0)
    new_value_columns = attn_cols_new[2]
    new_hidden_stats = jnp.concatenate(
        [cols_shared_in.reshape(2, ff_local), rows_shared_down[None]], axis=0
    )
    new_expert_model_stats = jnp.stack([rows_expert_in, cols_expert_down])[None]
    new_expert_hidden_stats = jnp.concatenate(
        [cols_expert_in.reshape(2, fe_local), rows_expert_down[None]], axis=0
    )[None]
    return (
        layer_out.astype(jnp.bfloat16)[None],
        input_grad[None],
        own_gains,
        own_attn_in,
        own_attn_out,
        own_router,
        own_shared_in,
        own_shared_down,
        own_expert_in,
        own_expert_down,
        new_gains,
        new_attn_in,
        new_attn_out,
        new_router,
        new_shared_in,
        new_shared_down,
        new_expert_in,
        new_expert_down,
        new_model_stats,
        new_head_stats,
        new_value_columns,
        new_hidden_stats,
        router_new,
        new_expert_model_stats,
        new_expert_hidden_stats,
        update_roots,
    )


def solution(mesh):
    in_specs = (
        P("fsdp", "ctx", None),
        P("fsdp", "ctx"),
        P("fsdp", "ctx", None),
        P("fsdp", "ctx", None),
        P(None, ("fsdp", "ctx")),
        P(("fsdp", "ctx"), None, "tp"),
        P("tp", ("fsdp", "ctx")),
        P(("fsdp", "ctx"), None),
        P(("fsdp", "ctx"), None, "tp"),
        P("tp", ("fsdp", "ctx")),
        P("fsdp", "ctx", None, "tp"),
        P("fsdp", "tp", "ctx"),
        P(None, ("fsdp", "ctx")),
        P(None, "tp"),
        P("tp"),
        P(None, "tp"),
        P(("fsdp", "ctx"), None),
        P("fsdp", None, "ctx"),
        P("fsdp", None, "tp"),
    )
    out_specs = (
        P("fsdp", "ctx", None),
        P("fsdp", "ctx", None),
        P(None, ("fsdp", "ctx")),
        P(("fsdp", "ctx"), None, "tp"),
        P("tp", ("fsdp", "ctx")),
        P(("fsdp", "ctx"), None),
        P(("fsdp", "ctx"), None, "tp"),
        P("tp", ("fsdp", "ctx")),
        P("fsdp", "ctx", None, "tp"),
        P("fsdp", "tp", "ctx"),
        P(None, ("fsdp", "ctx")),
        P(("fsdp", "ctx"), None, "tp"),
        P("tp", ("fsdp", "ctx")),
        P(("fsdp", "ctx"), None),
        P(("fsdp", "ctx"), None, "tp"),
        P("tp", ("fsdp", "ctx")),
        P("fsdp", "ctx", None, "tp"),
        P("fsdp", "tp", "ctx"),
        P(None, ("fsdp", "ctx")),
        P(None, "tp"),
        P("tp"),
        P(None, "tp"),
        P(("fsdp", "ctx"), None),
        P("fsdp", None, "ctx"),
        P("fsdp", None, "tp"),
        P(),
    )
    return jax.shard_map(local, mesh=mesh, in_specs=in_specs, out_specs=out_specs, check_vma=False)
```

```python
import jax
import jax.numpy as jnp
from jax import lax
from jax.sharding import PartitionSpec as P

D = 768
HD = 64
FF = 2048
FE = 2048
WINDOW = 1024
HH = 768


EPSILON = 1e-06
TINY_SQUARE = 1e-30
SCALE_FLOOR = 0.001
DECAY_RATE = 0.5
CLIP_LIMIT = 0.5
STEP_RATE = 0.5


def from_behind(value, axis, steps):
    count = lax.axis_size(axis)
    leading, last = (max(0, -steps), min(count, count - steps))
    return lax.ppermute(value, axis, [(source, source + steps) for source in range(leading, last)])


def rms_norm(values, gain_vec):
    inv_rms = lax.rsqrt(jnp.mean(values * values, axis=-1, keepdims=True) + EPSILON)
    return values * inv_rms * gain_vec


def swiglu(gate_up):
    return jax.nn.silu(gate_up[:, 0]) * gate_up[:, 1]


def rotate(values, cosine, sine_tab):
    half_dim = values.shape[-1] // 2
    first_half = values[..., :half_dim]
    second_half = values[..., half_dim:]
    cos_b = cosine[:, None, :]
    sin_b = sine_tab[:, None, :]
    return jnp.concatenate(
        [first_half * cos_b - second_half * sin_b, second_half * cos_b + first_half * sin_b],
        axis=-1,
    )


def slot_tables(block_routes, experts, capacity):
    flat_routes = block_routes.reshape(-1)
    route_count = flat_routes.shape[0]
    onehot = (flat_routes[:, None] == jnp.arange(experts, dtype=jnp.int32)[None, :]).astype(
        jnp.int32
    )
    rank_in = jnp.sum(
        (jnp.cumsum(onehot, axis=0, dtype=jnp.int32) - 1) * onehot, axis=1, dtype=jnp.int32
    )
    slot_index = flat_routes * capacity + rank_in
    owner_route = (
        jnp.zeros((experts * capacity,), jnp.int32)
        .at[slot_index]
        .set(jnp.arange(route_count, dtype=jnp.int32))
    )
    filled = jnp.zeros((experts * capacity,), jnp.int32).at[slot_index].set(1)
    return (slot_index, owner_route, filled)


def block_view(queries, keys_ext, values_ext, seg_own, seg_ext, start_row, base_pos):
    block_len = queries.shape[0]
    block_rows = min(512, block_len)
    query_rows = lax.dynamic_slice_in_dim(queries, start_row, block_rows, 0)
    key_rows = lax.dynamic_slice_in_dim(
        keys_ext, start_row + block_len - WINDOW, block_rows + WINDOW, 0
    )
    value_rows = lax.dynamic_slice_in_dim(
        values_ext, start_row + block_len - WINDOW, block_rows + WINDOW, 0
    )
    scores = (
        jnp.einsum("qhd,khd->hqk", query_rows, key_rows, preferred_element_type=jnp.float32) * 0.125
    )
    query_pos = start_row + jnp.arange(block_rows, dtype=jnp.int32)
    key_pos = start_row - WINDOW + jnp.arange(block_rows + WINDOW, dtype=jnp.int32)
    distance = query_pos[:, None] - key_pos[None, :]
    seg_query = lax.dynamic_slice_in_dim(seg_own, start_row, block_rows, 0)
    seg_key = lax.dynamic_slice_in_dim(
        seg_ext, start_row + block_len - WINDOW, block_rows + WINDOW, 0
    )
    allowed = (
        (distance >= 0)
        & (distance < WINDOW)
        & (seg_query[:, None] == seg_key[None, :])
        & (key_pos[None, :] + base_pos >= 0)
    )
    return (query_rows, key_rows, value_rows, jnp.where(allowed[None], scores, -1e30), allowed)


def factored_update(
    grad_mat, rows_old, cols_old, row_sums, col_sums, row_total, col_total, old_total, square_total
):
    rows_new = DECAY_RATE * rows_old + (1.0 - DECAY_RATE) * row_sums / col_total
    cols_new = DECAY_RATE * cols_old + (1.0 - DECAY_RATE) * col_sums / row_total
    mean_rows = (DECAY_RATE * old_total + (1.0 - DECAY_RATE) * square_total / col_total) / row_total
    second_moment = rows_new[:, None] * cols_new[None, :] / mean_rows
    return (grad_mat * lax.rsqrt(second_moment), rows_new, cols_new)


def apply_update(weight, update, update_root, square_sum, elements):
    param_scale = jnp.maximum(SCALE_FLOOR, jnp.sqrt(square_sum / elements))
    return weight - STEP_RATE * param_scale * update / jnp.maximum(1.0, update_root / CLIP_LIMIT)


def swiglu_experts(gate_up):
    return jax.nn.silu(gate_up[:, :, 0]) * gate_up[:, :, 1]


def gather_packed(pieces, axes):
    flat = jnp.concatenate([piece.reshape(-1) for piece, _ in pieces])
    full = lax.all_gather(flat, axes, axis=0, tiled=False)
    count = full.shape[0]
    results = []
    offset = 0
    for piece, dim in pieces:
        size = piece.size
        part = full[:, offset : offset + size].reshape((count,) + piece.shape)
        offset += size
        part = jnp.moveaxis(part, 0, dim)
        shape = list(piece.shape)
        shape[dim] *= count
        results.append(part.reshape(shape))
    return results


def scatter_packed(pieces, axes, count):
    columns = []
    local_shapes = []
    for grad, dim in pieces:
        shape = grad.shape
        split = shape[:dim] + (count, shape[dim] // count) + shape[dim + 1 :]
        local_shapes.append(shape[:dim] + (shape[dim] // count,) + shape[dim + 1 :])
        part = jnp.moveaxis(grad.reshape(split), dim, 0)
        columns.append(part.reshape(count, -1))
    packed = jnp.concatenate(columns, axis=1)
    width = packed.shape[1]
    rows = -(-width // 1024) * 8
    packed = jnp.pad(packed, ((0, 0), (0, rows * 128 - width))).reshape(count * rows, 128)
    own = lax.psum_scatter(packed, axes, scatter_dimension=0, tiled=True).reshape(-1)
    results = []
    offset = 0
    for local_shape in local_shapes:
        size = 1
        for extent in local_shape:
            size *= extent
        results.append(own[offset : offset + size].reshape(local_shape))
        offset += size
    return results


def experts_dense(normed_two, grad_out, weights, expert_in_all, expert_down_all):
    gate_up = jnp.einsum(
        "td,edgf->etgf", normed_two, expert_in_all, preferred_element_type=jnp.float32
    )
    act, act_back = jax.vjp(swiglu_experts, gate_up)
    hidden = act.astype(jnp.bfloat16)
    outs = jnp.einsum("etf,efd->etd", hidden, expert_down_all, preferred_element_type=jnp.float32)
    weights_e = weights.T[:, :, None]
    combined = jnp.sum(weights_e * outs, axis=0)
    gate_dots = jnp.sum(outs * grad_out[None], axis=-1).T
    grad_outs = (weights_e * grad_out[None]).astype(jnp.bfloat16)
    grad_hidden = jnp.einsum(
        "etd,efd->etf", grad_outs, expert_down_all, preferred_element_type=jnp.float32
    )
    grad_gate_up = act_back(grad_hidden)[0].astype(jnp.bfloat16)
    grad_down = jnp.einsum("etf,etd->efd", hidden, grad_outs, preferred_element_type=jnp.float32)
    grad_in = jnp.einsum(
        "td,etgf->edgf", normed_two, grad_gate_up, preferred_element_type=jnp.float32
    )
    grad_rows = jnp.einsum(
        "etgf,edgf->td", grad_gate_up, expert_in_all, preferred_element_type=jnp.float32
    )
    return combined, gate_dots, grad_rows, grad_in, grad_down


def experts_routed(
    normed_two, grad_out, route_rows, gate_probs, expert_in_low, expert_down_low, capacity
):
    block_len, model_width = normed_two.shape
    experts = lax.axis_size("fsdp")
    slot_index, owner_route, filled = slot_tables(route_rows, experts, capacity)
    fill_mask = filled.astype(jnp.bfloat16)[:, None]
    route_grads = (
        (gate_probs[:, :, None] * grad_out[:, None, :])
        .astype(jnp.bfloat16)
        .reshape(2 * block_len, model_width)
    )
    send_rows = jnp.concatenate(
        [normed_two[owner_route // 2] * fill_mask, route_grads[owner_route] * fill_mask], axis=1
    ).reshape(experts, capacity, 2 * model_width)
    exchange = lambda rows: lax.all_to_all(rows, "fsdp", split_axis=0, concat_axis=0, tiled=True)
    received_both = exchange(send_rows).reshape(experts * capacity, 2 * model_width)
    received = received_both[:, :model_width]
    grad_received = received_both[:, model_width:]
    gate_up = jnp.einsum("rd,dgf->rgf", received, expert_in_low, preferred_element_type=jnp.float32)
    act, act_back = jax.vjp(swiglu, gate_up)
    hidden = act.astype(jnp.bfloat16)
    outs = jnp.dot(hidden, expert_down_low, preferred_element_type=jnp.float32)
    grad_hidden = jnp.einsum(
        "rd,fd->rf", grad_received, expert_down_low, preferred_element_type=jnp.float32
    )
    grad_gate_up = act_back(grad_hidden)[0].astype(jnp.bfloat16)
    grad_in = jnp.einsum("rd,rgf->dgf", received, grad_gate_up, preferred_element_type=jnp.float32)
    grad_down = jnp.einsum("rf,rd->fd", hidden, grad_received, preferred_element_type=jnp.float32)
    grad_expert_rows = jnp.einsum(
        "rgf,dgf->rd", grad_gate_up, expert_in_low, preferred_element_type=jnp.float32
    )
    returned = exchange(
        jnp.concatenate([outs, grad_expert_rows], axis=1).reshape(
            experts, capacity, 2 * model_width
        )
    ).reshape(experts * capacity, 2 * model_width)[slot_index]
    route_out = returned[:, :model_width].reshape(block_len, 2, model_width)
    grad_routes = returned[:, model_width:].reshape(block_len, 2, model_width)
    combined = jnp.sum(gate_probs[:, :, None] * route_out, axis=1)
    gate_dots = jnp.sum(grad_out[:, None, :] * route_out, axis=-1)
    grad_rows = jnp.sum(grad_routes, axis=1)
    return combined, gate_dots, grad_rows, grad_in, grad_down


def local(
    layer_input,
    segments,
    routes,
    cotangent,
    gains,
    attention_in,
    attention_out,
    router_weight,
    shared_in,
    shared_down,
    expert_in,
    expert_down,
    model_stats,
    head_stats,
    value_columns,
    hidden_stats,
    router_state,
    expert_model_stats,
    expert_hidden_stats,
):
    block_len = layer_input.shape[1]
    model_width = layer_input.shape[2]
    experts = router_weight.shape[1]
    dense_experts = False
    capacity = min(block_len, 4 * block_len // experts)
    ctx_index = lax.axis_index("ctx")
    tp_index = lax.axis_index("tp")
    fsdp_index = lax.axis_index("fsdp")
    shard_index = lax.axis_index(("fsdp", "ctx"))
    shard_count = lax.axis_size(("fsdp", "ctx"))
    ctx_count = lax.axis_size("ctx")
    base_pos = ctx_index * block_len
    low = lambda v: v.astype(jnp.bfloat16)
    gain_low, attn_in_low = gather_packed(
        [(low(gains), 1), (low(attention_in), 0)], ("fsdp", "ctx")
    )
    later = [
        (low(attention_out), 1),
        (low(router_weight), 0),
        (low(shared_in), 0),
        (low(shared_down), 1),
    ]
    if dense_experts:
        later += [(low(expert_in), 0), (low(expert_down), 0)]
    later_full = gather_packed(later, ("fsdp", "ctx"))
    attn_out_low, router_low, shared_in_low, shared_down_low = later_full[:4]
    if dense_experts:
        fe_local = expert_down.shape[1]
        expert_in_all = later_full[4].reshape(experts, model_width, 2, fe_local)
        expert_down_all = (
            later_full[5]
            .reshape(experts, ctx_count, fe_local, model_width // ctx_count)
            .transpose(0, 2, 1, 3)
            .reshape(experts, fe_local, model_width)
        )
    else:
        expert_in_low = lax.all_gather(low(expert_in), "ctx", axis=1, tiled=True)[0]
        expert_down_low = lax.all_gather(low(expert_down), "ctx", axis=2, tiled=True)[0]
    residual = layer_input[0].astype(jnp.float32)
    gain_one = gain_low[0].astype(jnp.float32)
    gain_two = gain_low[1].astype(jnp.float32)
    normed_one, norm_one_back = jax.vjp(rms_norm, residual, gain_one)
    normed_one = normed_one.astype(jnp.bfloat16)
    projected = jnp.einsum(
        "td,dgf->tgf", normed_one, attn_in_low, preferred_element_type=jnp.float32
    )
    local_cols = projected.shape[2]
    local_heads = local_cols // HD
    half_dim = HD // 2
    frequency = 10000.0 ** (-jnp.arange(half_dim, dtype=jnp.float32) / half_dim)
    angles = (base_pos + jnp.arange(block_len, dtype=jnp.int32)).astype(jnp.float32)[
        :, None
    ] * frequency[None, :]
    cosine = jnp.cos(angles)
    sine_tab = jnp.sin(angles)
    queries = rotate(projected[:, 0].reshape(block_len, local_heads, HD), cosine, sine_tab).astype(
        jnp.bfloat16
    )
    keys_own = rotate(projected[:, 1].reshape(block_len, local_heads, HD), cosine, sine_tab).astype(
        jnp.bfloat16
    )
    values_own = projected[:, 2].reshape(block_len, local_heads, HD).astype(jnp.bfloat16)
    seg_own = segments[0].astype(jnp.bfloat16)
    keys_prev, values_prev, seg_prev = from_behind((keys_own, values_own, seg_own), "ctx", 1)
    keys_ext = jnp.concatenate([keys_prev, keys_own], axis=0)
    values_ext = jnp.concatenate([values_prev, values_own], axis=0)
    seg_ext = jnp.concatenate([seg_prev, seg_own], axis=0)
    block_rows = min(512, block_len)
    block_total = block_len // block_rows
    starts = jnp.arange(block_total, dtype=jnp.int32) * block_rows

    def forward_block(start_row):
        query_rows, key_rows, value_rows, masked, allowed = block_view(
            queries, keys_ext, values_ext, seg_own, seg_ext, start_row, base_pos
        )
        row_max = jnp.max(masked, axis=-1, keepdims=True)
        exp_terms = jnp.where(allowed[None], jnp.exp(masked - row_max), 0.0)
        row_total = jnp.sum(exp_terms, axis=-1, keepdims=True)
        attn_probs = (exp_terms / row_total).astype(jnp.bfloat16)
        attended = jnp.einsum(
            "hqk,khd->qhd", attn_probs, value_rows, preferred_element_type=jnp.float32
        )
        return (attended, row_max + jnp.log(row_total))

    attended, log_totals = lax.map(forward_block, starts)
    mixed_heads = attended.reshape(block_len, local_cols).astype(jnp.bfloat16)
    attn_total = lax.psum(
        jnp.dot(mixed_heads, attn_out_low, preferred_element_type=jnp.float32), "tp"
    )
    after_attn = residual + attn_total
    normed_two, norm_two_back = jax.vjp(rms_norm, after_attn, gain_two)
    normed_two = normed_two.astype(jnp.bfloat16)
    logits = jnp.dot(normed_two, router_low, preferred_element_type=jnp.float32)
    route_rows = routes[0]
    onehot = (route_rows[:, :, None] == jnp.arange(experts, dtype=jnp.int32)[None, None, :]).astype(
        jnp.float32
    )
    picked = jnp.sum(onehot * logits[:, None, :], axis=-1)
    gate_probs = jax.nn.softmax(picked, axis=-1)
    upstream = cotangent[0]
    grad_out = upstream.astype(jnp.float32)
    if dense_experts:
        weights = jnp.sum(gate_probs[:, :, None] * onehot, axis=1)
        combined, dots_e, grad_rows, grad_expert_in, grad_expert_down = experts_dense(
            normed_two, grad_out, weights, expert_in_all, expert_down_all
        )
        gate_dots = jnp.sum(onehot * dots_e[:, None, :], axis=-1)
    else:
        combined, gate_dots, grad_rows, grad_expert_in, grad_expert_down = experts_routed(
            normed_two,
            grad_out,
            route_rows,
            gate_probs,
            expert_in_low,
            expert_down_low,
            capacity,
        )
    shared_gate_up = jnp.einsum(
        "td,dgf->tgf", normed_two, shared_in_low, preferred_element_type=jnp.float32
    )
    shared_act, shared_act_back = jax.vjp(swiglu, shared_gate_up)
    shared_hidden = shared_act.astype(jnp.bfloat16)
    shared_out = jnp.dot(shared_hidden, shared_down_low, preferred_element_type=jnp.float32)
    grad_shared_hidden = jnp.einsum(
        "td,fd->tf", upstream, shared_down_low, preferred_element_type=jnp.float32
    )
    grad_shared_gate_up = shared_act_back(grad_shared_hidden)[0].astype(jnp.bfloat16)
    partial_two = (
        jnp.einsum(
            "tgf,dgf->td", grad_shared_gate_up, shared_in_low, preferred_element_type=jnp.float32
        )
        + grad_rows
    )
    branch_total, grad_normed_part, gate_total = lax.psum(
        (shared_out + combined, partial_two, gate_dots), "tp"
    )
    layer_out = after_attn + branch_total
    grad_picked = gate_probs * (
        gate_total - jnp.sum(gate_probs * gate_total, axis=-1, keepdims=True)
    )
    grad_logits = jnp.sum(grad_picked[:, :, None] * onehot, axis=1).astype(jnp.bfloat16)
    grad_shared_in = jnp.einsum(
        "td,tgf->dgf", normed_two, grad_shared_gate_up, preferred_element_type=jnp.float32
    )
    grad_shared_down = jnp.einsum(
        "tf,td->fd", shared_hidden, upstream, preferred_element_type=jnp.float32
    )
    grad_router = jnp.einsum(
        "td,te->de", normed_two, grad_logits, preferred_element_type=jnp.float32
    )
    grad_normed_two = grad_normed_part + jnp.einsum(
        "te,de->td", grad_logits, router_low, preferred_element_type=jnp.float32
    )
    grad_after, grad_gain_two = norm_two_back(grad_normed_two)
    grad_after = grad_after + grad_out
    grad_attn_low = grad_after.astype(jnp.bfloat16)
    grad_attn_out = jnp.einsum(
        "tc,td->cd", mixed_heads, grad_attn_low, preferred_element_type=jnp.float32
    )
    first_grads = [
        (grad_attn_out, 1),
        (grad_router, 0),
        (grad_shared_in, 0),
        (grad_shared_down, 1),
        (grad_gain_two, 0),
    ]
    if dense_experts:
        fe_local = expert_down.shape[1]
        first_grads += [
            (grad_expert_in.reshape(shard_count * expert_in.shape[1], 2, fe_local), 0),
            (
                grad_expert_down.reshape(experts, fe_local, ctx_count, model_width // ctx_count)
                .transpose(0, 2, 1, 3)
                .reshape(shard_count * fe_local, model_width // ctx_count),
                0,
            ),
        ]
    if not dense_experts:
        own_expert_in = lax.psum_scatter(grad_expert_in[None], "ctx", scatter_dimension=1, tiled=True)
        own_expert_down = lax.psum_scatter(
            grad_expert_down[None], "ctx", scatter_dimension=2, tiled=True
        )
    first_own = scatter_packed(first_grads, ("fsdp", "ctx"), shard_count)
    own_attn_out, own_router, own_shared_in, own_shared_down, own_gain_two = first_own[:5]
    if dense_experts:
        own_expert_in = first_own[5][None]
        own_expert_down = first_own[6][None]
    grad_heads = (
        jnp.einsum("td,cd->tc", grad_attn_low, attn_out_low, preferred_element_type=jnp.float32)
        .astype(jnp.bfloat16)
        .reshape(block_len, local_heads, HD)
    )

    def backward_block(block_number, running):
        grad_keys, grad_values, grad_queries = running
        start_row = block_number * block_rows
        query_rows, key_rows, value_rows, masked, allowed = block_view(
            queries, keys_ext, values_ext, seg_own, seg_ext, start_row, base_pos
        )
        log_total = lax.dynamic_index_in_dim(log_totals, block_number, 0, keepdims=False)
        attn_probs = jnp.where(allowed[None], jnp.exp(masked - log_total), 0.0)
        grad_block = lax.dynamic_slice_in_dim(grad_heads, start_row, block_rows, 0)
        grad_probs = jnp.einsum(
            "qhd,khd->hqk", grad_block, value_rows, preferred_element_type=jnp.float32
        )
        inner_sum = jnp.sum(attn_probs * grad_probs, axis=-1, keepdims=True)
        grad_scores = (attn_probs * (grad_probs - inner_sum)).astype(jnp.bfloat16)
        grad_query_rows = (
            jnp.einsum("hqk,khd->qhd", grad_scores, key_rows, preferred_element_type=jnp.float32)
            * 0.125
        )
        grad_key_rows = (
            jnp.einsum("hqk,qhd->khd", grad_scores, query_rows, preferred_element_type=jnp.float32)
            * 0.125
        )
        grad_value_rows = jnp.einsum(
            "hqk,qhd->khd",
            attn_probs.astype(jnp.bfloat16),
            grad_block,
            preferred_element_type=jnp.float32,
        )
        key_offset = start_row + block_len - WINDOW
        grad_keys = lax.dynamic_update_slice_in_dim(
            grad_keys,
            lax.dynamic_slice_in_dim(grad_keys, key_offset, block_rows + WINDOW, 0) + grad_key_rows,
            key_offset,
            0,
        )
        grad_values = lax.dynamic_update_slice_in_dim(
            grad_values,
            lax.dynamic_slice_in_dim(grad_values, key_offset, block_rows + WINDOW, 0)
            + grad_value_rows,
            key_offset,
            0,
        )
        grad_queries = lax.dynamic_update_slice_in_dim(grad_queries, grad_query_rows, start_row, 0)
        return (grad_keys, grad_values, grad_queries)

    zero_ext = jnp.zeros((2 * block_len, local_heads, HD), jnp.float32)
    zero_own = jnp.zeros((block_len, local_heads, HD), jnp.float32)
    grad_keys, grad_values, grad_queries = lax.fori_loop(
        0, block_total, backward_block, (zero_ext, zero_ext, zero_own)
    )
    rim_keys, rim_values = (
        from_behind(grad_keys[:block_len].astype(jnp.bfloat16), "ctx", -1).astype(jnp.float32),
        from_behind(grad_values[:block_len].astype(jnp.bfloat16), "ctx", -1).astype(jnp.float32),
    )
    grad_keys_own = grad_keys[block_len:] + rim_keys
    grad_values_own = grad_values[block_len:] + rim_values
    grad_query_raw = rotate(grad_queries, cosine, -sine_tab)
    grad_key_raw = rotate(grad_keys_own, cosine, -sine_tab)
    grad_projected = (
        jnp.stack([grad_query_raw, grad_key_raw, grad_values_own], axis=1)
        .reshape(block_len, 3, local_cols)
        .astype(jnp.bfloat16)
    )
    grad_attn_in = jnp.einsum(
        "td,tgf->dgf", normed_one, grad_projected, preferred_element_type=jnp.float32
    )
    partial_one = jnp.einsum(
        "tgf,dgf->td", grad_projected, attn_in_low, preferred_element_type=jnp.float32
    )
    grad_residual, grad_gain_one = norm_one_back(lax.psum(partial_one, "tp"))
    input_grad = grad_after + grad_residual
    own_attn_in, own_gain_one = scatter_packed(
        [(grad_attn_in, 0), (grad_gain_one, 0)], ("fsdp", "ctx"), shard_count
    )
    own_gains = jnp.stack([own_gain_one, own_gain_two])
    lead_tp = (tp_index == 0).astype(jnp.float32)
    first_shard = (shard_index == 0).astype(jnp.float32)
    first_ctx = (ctx_index == 0).astype(jnp.float32)
    d_local = gains.shape[1]
    ff_local = shared_down.shape[0]
    fe_local = expert_down.shape[1]
    d_quarter = expert_in.shape[1]
    square_attn_in = own_attn_in * own_attn_in + TINY_SQUARE
    square_attn_out = own_attn_out * own_attn_out + TINY_SQUARE
    square_shared_in = own_shared_in * own_shared_in + TINY_SQUARE
    square_shared_down = own_shared_down * own_shared_down + TINY_SQUARE
    square_expert_in = own_expert_in[0] * own_expert_in[0] + TINY_SQUARE
    square_expert_down = own_expert_down[0] * own_expert_down[0] + TINY_SQUARE
    model_part = lax.dynamic_update_slice(
        jnp.zeros((4, D), jnp.float32),
        jnp.stack(
            [
                jnp.sum(square_attn_in, axis=(1, 2)),
                jnp.sum(square_shared_in, axis=(1, 2)),
                jnp.sum(square_attn_out, axis=0),
                jnp.sum(square_shared_down, axis=0),
            ]
        ),
        (0, shard_index * d_local),
    )
    head_part = lax.dynamic_update_slice(
        jnp.zeros((4, HH), jnp.float32),
        jnp.concatenate(
            [jnp.sum(square_attn_in, axis=0), jnp.sum(square_attn_out, axis=1)[None]], axis=0
        ),
        (0, tp_index * local_cols),
    )
    hidden_part = lax.dynamic_update_slice(
        jnp.zeros((3, FF), jnp.float32),
        jnp.concatenate(
            [jnp.sum(square_shared_in, axis=0), jnp.sum(square_shared_down, axis=1)[None]], axis=0
        ),
        (0, tp_index * ff_local),
    )
    expert_model_part = lax.dynamic_update_slice(
        jnp.zeros((experts, 2, D), jnp.float32),
        jnp.stack([jnp.sum(square_expert_in, axis=(1, 2)), jnp.sum(square_expert_down, axis=0)])[
            None
        ],
        (fsdp_index, 0, ctx_index * d_quarter),
    )
    expert_hidden_part = lax.dynamic_update_slice(
        jnp.zeros((experts, 3, FE), jnp.float32),
        jnp.concatenate(
            [jnp.sum(square_expert_in, axis=0), jnp.sum(square_expert_down, axis=1)[None]], axis=0
        )[None],
        (fsdp_index, 0, tp_index * fe_local),
    )
    scalar_part = jnp.stack(
        [
            lead_tp * jnp.sum(gains * gains),
            jnp.sum(attention_in * attention_in),
            jnp.sum(attention_out * attention_out),
            lead_tp * jnp.sum(router_weight * router_weight),
            jnp.sum(shared_in * shared_in),
            jnp.sum(shared_down * shared_down),
            jnp.sum(expert_in * expert_in),
            jnp.sum(expert_down * expert_down),
            lead_tp * jnp.sum(model_stats[2]),
            first_shard * jnp.sum(head_stats[2]),
            lead_tp * jnp.sum(model_stats[3]),
            first_shard * jnp.sum(hidden_stats[2]),
        ]
    )
    expert_old_part = lax.dynamic_update_slice(
        jnp.zeros((2, experts), jnp.float32),
        jnp.stack(
            [
                lead_tp * jnp.sum(expert_model_stats[0, 0]),
                first_ctx * jnp.sum(expert_hidden_stats[0, 2]),
            ]
        )[:, None],
        (0, fsdp_index),
    )
    global_sums = lax.psum(
        (
            model_part,
            head_part,
            hidden_part,
            expert_model_part,
            expert_hidden_part,
            scalar_part,
            expert_old_part,
        ),
        ("fsdp", "ctx", "tp"),
    )
    (
        model_sum,
        head_sum,
        hidden_sum,
        expert_model_sum,
        expert_hidden_sum,
        scalar_sum,
        expert_old_sum,
    ) = global_sums
    shard_start = shard_index * d_local
    gain_state = DECAY_RATE * model_stats[0:2] + (1.0 - DECAY_RATE) * (
        own_gains * own_gains + TINY_SQUARE
    )
    update_gains = own_gains * lax.rsqrt(gain_state)
    router_new = DECAY_RATE * router_state + (1.0 - DECAY_RATE) * (
        own_router * own_router + TINY_SQUARE
    )
    update_router = own_router * lax.rsqrt(router_new)
    attn_cols_old = jnp.concatenate([head_stats[0:2], value_columns[None]], axis=0).reshape(-1)
    update_attn_in, rows_attn_in, cols_attn_in = factored_update(
        own_attn_in.reshape(d_local, 3 * local_cols),
        model_stats[2],
        attn_cols_old,
        lax.dynamic_slice_in_dim(model_sum[0], shard_start, d_local),
        lax.dynamic_slice_in_dim(head_sum[0:3], tp_index * local_cols, local_cols, 1).reshape(-1),
        D,
        3 * HH,
        scalar_sum[8],
        jnp.sum(model_sum[0]),
    )
    update_attn_out, rows_attn_out, cols_attn_out = factored_update(
        own_attn_out,
        head_stats[2],
        model_stats[4],
        lax.dynamic_slice_in_dim(head_sum[3], tp_index * local_cols, local_cols),
        lax.dynamic_slice_in_dim(model_sum[2], shard_start, d_local),
        HH,
        D,
        scalar_sum[9],
        jnp.sum(head_sum[3]),
    )
    update_shared_in, rows_shared_in, cols_shared_in = factored_update(
        own_shared_in.reshape(d_local, 2 * ff_local),
        model_stats[3],
        hidden_stats[0:2].reshape(-1),
        lax.dynamic_slice_in_dim(model_sum[1], shard_start, d_local),
        lax.dynamic_slice_in_dim(hidden_sum[0:2], tp_index * ff_local, ff_local, 1).reshape(-1),
        D,
        2 * FF,
        scalar_sum[10],
        jnp.sum(model_sum[1]),
    )
    update_shared_down, rows_shared_down, cols_shared_down = factored_update(
        own_shared_down,
        hidden_stats[2],
        model_stats[5],
        lax.dynamic_slice_in_dim(hidden_sum[2], tp_index * ff_local, ff_local),
        lax.dynamic_slice_in_dim(model_sum[3], shard_start, d_local),
        FF,
        D,
        scalar_sum[11],
        jnp.sum(hidden_sum[2]),
    )
    own_expert_model = lax.dynamic_index_in_dim(expert_model_sum, fsdp_index, 0, keepdims=False)
    own_expert_hidden = lax.dynamic_index_in_dim(expert_hidden_sum, fsdp_index, 0, keepdims=False)
    old_expert_totals = lax.dynamic_index_in_dim(expert_old_sum, fsdp_index, 1, keepdims=False)
    update_expert_in, rows_expert_in, cols_expert_in = factored_update(
        own_expert_in[0].reshape(d_quarter, 2 * fe_local),
        expert_model_stats[0, 0],
        expert_hidden_stats[0, 0:2].reshape(-1),
        lax.dynamic_slice_in_dim(own_expert_model[0], ctx_index * d_quarter, d_quarter),
        lax.dynamic_slice_in_dim(own_expert_hidden[0:2], tp_index * fe_local, fe_local, 1).reshape(
            -1
        ),
        D,
        2 * FE,
        old_expert_totals[0],
        jnp.sum(own_expert_model[0]),
    )
    update_expert_down, rows_expert_down, cols_expert_down = factored_update(
        own_expert_down[0],
        expert_hidden_stats[0, 2],
        expert_model_stats[0, 1],
        lax.dynamic_slice_in_dim(own_expert_hidden[2], tp_index * fe_local, fe_local),
        lax.dynamic_slice_in_dim(own_expert_model[1], ctx_index * d_quarter, d_quarter),
        FE,
        D,
        old_expert_totals[1],
        jnp.sum(own_expert_hidden[2]),
    )
    clip_part = jnp.stack(
        [
            lead_tp * jnp.sum(update_gains * update_gains),
            jnp.sum(update_attn_in * update_attn_in),
            jnp.sum(update_attn_out * update_attn_out),
            lead_tp * jnp.sum(update_router * update_router),
            jnp.sum(update_shared_in * update_shared_in),
            jnp.sum(update_shared_down * update_shared_down),
            jnp.sum(update_expert_in * update_expert_in),
            jnp.sum(update_expert_down * update_expert_down),
        ]
    )
    clip_total = lax.psum(clip_part, ("fsdp", "ctx", "tp"))
    elements = jnp.array(
        [
            2 * D,
            D * 3 * HH,
            HH * D,
            D * experts,
            D * 2 * FF,
            FF * D,
            experts * D * 2 * FE,
            experts * FE * D,
        ],
        jnp.float32,
    )
    update_roots = jnp.sqrt(clip_total / elements)
    new_gains = apply_update(gains, update_gains, update_roots[0], scalar_sum[0], elements[0])
    new_attn_in = apply_update(
        attention_in,
        update_attn_in.reshape(attention_in.shape),
        update_roots[1],
        scalar_sum[1],
        elements[1],
    )
    new_attn_out = apply_update(
        attention_out, update_attn_out, update_roots[2], scalar_sum[2], elements[2]
    )
    new_router = apply_update(
        router_weight, update_router, update_roots[3], scalar_sum[3], elements[3]
    )
    new_shared_in = apply_update(
        shared_in,
        update_shared_in.reshape(shared_in.shape),
        update_roots[4],
        scalar_sum[4],
        elements[4],
    )
    new_shared_down = apply_update(
        shared_down, update_shared_down, update_roots[5], scalar_sum[5], elements[5]
    )
    new_expert_in = apply_update(
        expert_in,
        update_expert_in.reshape(expert_in.shape),
        update_roots[6],
        scalar_sum[6],
        elements[6],
    )
    new_expert_down = apply_update(
        expert_down,
        update_expert_down.reshape(expert_down.shape),
        update_roots[7],
        scalar_sum[7],
        elements[7],
    )
    new_model_stats = jnp.concatenate(
        [gain_state, jnp.stack([rows_attn_in, rows_shared_in, cols_attn_out, cols_shared_down])],
        axis=0,
    )
    attn_cols_new = cols_attn_in.reshape(3, local_cols)
    new_head_stats = jnp.concatenate([attn_cols_new[0:2], rows_attn_out[None]], axis=0)
    new_value_columns = attn_cols_new[2]
    new_hidden_stats = jnp.concatenate(
        [cols_shared_in.reshape(2, ff_local), rows_shared_down[None]], axis=0
    )
    new_expert_model_stats = jnp.stack([rows_expert_in, cols_expert_down])[None]
    new_expert_hidden_stats = jnp.concatenate(
        [cols_expert_in.reshape(2, fe_local), rows_expert_down[None]], axis=0
    )[None]
    return (
        layer_out.astype(jnp.bfloat16)[None],
        input_grad[None],
        own_gains,
        own_attn_in,
        own_attn_out,
        own_router,
        own_shared_in,
        own_shared_down,
        own_expert_in,
        own_expert_down,
        new_gains,
        new_attn_in,
        new_attn_out,
        new_router,
        new_shared_in,
        new_shared_down,
        new_expert_in,
        new_expert_down,
        new_model_stats,
        new_head_stats,
        new_value_columns,
        new_hidden_stats,
        router_new,
        new_expert_model_stats,
        new_expert_hidden_stats,
        update_roots,
    )


def solution(mesh):
    in_specs = (
        P("fsdp", "ctx", None),
        P("fsdp", "ctx"),
        P("fsdp", "ctx", None),
        P("fsdp", "ctx", None),
        P(None, ("fsdp", "ctx")),
        P(("fsdp", "ctx"), None, "tp"),
        P("tp", ("fsdp", "ctx")),
        P(("fsdp", "ctx"), None),
        P(("fsdp", "ctx"), None, "tp"),
        P("tp", ("fsdp", "ctx")),
        P("fsdp", "ctx", None, "tp"),
        P("fsdp", "tp", "ctx"),
        P(None, ("fsdp", "ctx")),
        P(None, "tp"),
        P("tp"),
        P(None, "tp"),
        P(("fsdp", "ctx"), None),
        P("fsdp", None, "ctx"),
        P("fsdp", None, "tp"),
    )
    out_specs = (
        P("fsdp", "ctx", None),
        P("fsdp", "ctx", None),
        P(None, ("fsdp", "ctx")),
        P(("fsdp", "ctx"), None, "tp"),
        P("tp", ("fsdp", "ctx")),
        P(("fsdp", "ctx"), None),
        P(("fsdp", "ctx"), None, "tp"),
        P("tp", ("fsdp", "ctx")),
        P("fsdp", "ctx", None, "tp"),
        P("fsdp", "tp", "ctx"),
        P(None, ("fsdp", "ctx")),
        P(("fsdp", "ctx"), None, "tp"),
        P("tp", ("fsdp", "ctx")),
        P(("fsdp", "ctx"), None),
        P(("fsdp", "ctx"), None, "tp"),
        P("tp", ("fsdp", "ctx")),
        P("fsdp", "ctx", None, "tp"),
        P("fsdp", "tp", "ctx"),
        P(None, ("fsdp", "ctx")),
        P(None, "tp"),
        P("tp"),
        P(None, "tp"),
        P(("fsdp", "ctx"), None),
        P("fsdp", None, "ctx"),
        P("fsdp", None, "tp"),
        P(),
    )
    return jax.shard_map(local, mesh=mesh, in_specs=in_specs, out_specs=out_specs, check_vma=False)
```

```python
import jax
import jax.numpy as jnp
from jax import lax
from jax.sharding import PartitionSpec as P
from jax.experimental import pallas as pl
from jax.experimental.pallas import tpu as pltpu

D = 768
HD = 64
FF = 2048
FE = 2048
WINDOW = 1024
HH = 768


EPSILON = 1e-06
TINY_SQUARE = 1e-30
SCALE_FLOOR = 0.001
DECAY_RATE = 0.5
CLIP_LIMIT = 0.5
STEP_RATE = 0.5


def from_behind(value, axis, steps):
    count = lax.axis_size(axis)
    leading, last = (max(0, -steps), min(count, count - steps))
    return lax.ppermute(value, axis, [(source, source + steps) for source in range(leading, last)])


def rms_norm(values, gain_vec):
    inv_rms = lax.rsqrt(jnp.mean(values * values, axis=-1, keepdims=True) + EPSILON)
    return values * inv_rms * gain_vec


def swiglu(gate_up):
    return jax.nn.silu(gate_up[:, 0]) * gate_up[:, 1]


def rotate(values, cosine, sine_tab):
    half_dim = values.shape[-1] // 2
    first_half = values[..., :half_dim]
    second_half = values[..., half_dim:]
    cos_b = cosine[:, None, :]
    sin_b = sine_tab[:, None, :]
    return jnp.concatenate(
        [first_half * cos_b - second_half * sin_b, second_half * cos_b + first_half * sin_b],
        axis=-1,
    )


def slot_tables(block_routes, experts, capacity):
    flat_routes = block_routes.reshape(-1)
    route_count = flat_routes.shape[0]
    onehot = (flat_routes[:, None] == jnp.arange(experts, dtype=jnp.int32)[None, :]).astype(
        jnp.int32
    )
    rank_in = jnp.sum(
        (jnp.cumsum(onehot, axis=0, dtype=jnp.int32) - 1) * onehot, axis=1, dtype=jnp.int32
    )
    slot_index = flat_routes * capacity + rank_in
    owner_route = (
        jnp.zeros((experts * capacity,), jnp.int32)
        .at[slot_index]
        .set(jnp.arange(route_count, dtype=jnp.int32))
    )
    filled = jnp.zeros((experts * capacity,), jnp.int32).at[slot_index].set(1)
    return (slot_index, owner_route, filled)


def block_view(queries, keys_ext, values_ext, seg_own, seg_ext, start_row, base_pos):
    block_len = queries.shape[0]
    block_rows = min(512, block_len)
    query_rows = lax.dynamic_slice_in_dim(queries, start_row, block_rows, 0)
    key_rows = lax.dynamic_slice_in_dim(
        keys_ext, start_row + block_len - WINDOW, block_rows + WINDOW, 0
    )
    value_rows = lax.dynamic_slice_in_dim(
        values_ext, start_row + block_len - WINDOW, block_rows + WINDOW, 0
    )
    scores = (
        jnp.einsum("qhd,khd->hqk", query_rows, key_rows, preferred_element_type=jnp.float32) * 0.125
    )
    query_pos = start_row + jnp.arange(block_rows, dtype=jnp.int32)
    key_pos = start_row - WINDOW + jnp.arange(block_rows + WINDOW, dtype=jnp.int32)
    distance = query_pos[:, None] - key_pos[None, :]
    seg_query = lax.dynamic_slice_in_dim(seg_own, start_row, block_rows, 0)
    seg_key = lax.dynamic_slice_in_dim(
        seg_ext, start_row + block_len - WINDOW, block_rows + WINDOW, 0
    )
    allowed = (
        (distance >= 0)
        & (distance < WINDOW)
        & (seg_query[:, None] == seg_key[None, :])
        & (key_pos[None, :] + base_pos >= 0)
    )
    return (query_rows, key_rows, value_rows, jnp.where(allowed[None], scores, -1e30), allowed)


def factored_update(
    grad_mat, rows_old, cols_old, row_sums, col_sums, row_total, col_total, old_total, square_total
):
    rows_new = DECAY_RATE * rows_old + (1.0 - DECAY_RATE) * row_sums / col_total
    cols_new = DECAY_RATE * cols_old + (1.0 - DECAY_RATE) * col_sums / row_total
    mean_rows = (DECAY_RATE * old_total + (1.0 - DECAY_RATE) * square_total / col_total) / row_total
    second_moment = rows_new[:, None] * cols_new[None, :] / mean_rows
    return (grad_mat * lax.rsqrt(second_moment), rows_new, cols_new)


def apply_update(weight, update, update_root, square_sum, elements):
    param_scale = jnp.maximum(SCALE_FLOOR, jnp.sqrt(square_sum / elements))
    return weight - STEP_RATE * param_scale * update / jnp.maximum(1.0, update_root / CLIP_LIMIT)


def butterfly_partners():
    partners = []
    here = [lax.axis_index(name) for name in ("fsdp", "ctx", "tp")]
    for axis_number, name in enumerate(("fsdp", "ctx", "tp")):
        size = lax.axis_size(name)
        step = 1
        while step < size:
            bit = (here[axis_number] // step) % 2
            other = list(here)
            other[axis_number] = here[axis_number] + step * (1 - 2 * bit)
            partners.append(tuple(other))
            step *= 2
    return partners


def butterfly_kernel(x_ref, o_ref, stage, inbox, send_sems, recv_sems):
    partners = butterfly_partners()
    barrier = pltpu.get_barrier_semaphore()
    for partner in partners:
        pl.semaphore_signal(
            barrier, 1, device_id=partner, device_id_type=pl.DeviceIdType.MESH
        )
    pl.semaphore_wait(barrier, len(partners))
    acc = x_ref[...]
    for round_number, partner in enumerate(partners):
        stage[round_number] = acc
        copy = pltpu.make_async_remote_copy(
            src_ref=stage.at[round_number],
            dst_ref=inbox.at[round_number],
            send_sem=send_sems.at[round_number],
            recv_sem=recv_sems.at[round_number],
            device_id=partner,
            device_id_type=pl.DeviceIdType.MESH,
        )
        copy.start()
        copy.wait()
        acc = stage[round_number] + inbox[round_number]
    o_ref[...] = acc


def butterfly_sum(values, collective_id):
    flat = jnp.concatenate([v.reshape(-1).astype(jnp.float32) for v in values])
    size = flat.shape[0]
    rows = -(-size // 1024) * 8
    block = jnp.pad(flat, (0, rows * 128 - size)).reshape(rows, 128)
    rounds = sum(
        max(1, lax.axis_size(name)).bit_length() - 1 for name in ("fsdp", "ctx", "tp")
    )
    total = pl.pallas_call(
        butterfly_kernel,
        out_shape=jax.ShapeDtypeStruct((rows, 128), jnp.float32),
        in_specs=[pl.BlockSpec(memory_space=pltpu.VMEM)],
        out_specs=pl.BlockSpec(memory_space=pltpu.VMEM),
        scratch_shapes=[
            pltpu.VMEM((rounds, rows, 128), jnp.float32),
            pltpu.VMEM((rounds, rows, 128), jnp.float32),
            pltpu.SemaphoreType.DMA((rounds,)),
            pltpu.SemaphoreType.DMA((rounds,)),
        ],
        compiler_params=pltpu.CompilerParams(collective_id=collective_id, has_side_effects=True),
    )(block).reshape(-1)
    results = []
    offset = 0
    for v in values:
        results.append(total[offset : offset + v.size].reshape(v.shape))
        offset += v.size
    return results


def swiglu_experts(gate_up):
    return jax.nn.silu(gate_up[:, :, 0]) * gate_up[:, :, 1]


def gather_packed(pieces, axes):
    flat = jnp.concatenate([piece.reshape(-1) for piece, _ in pieces])
    full = lax.all_gather(flat, axes, axis=0, tiled=False)
    count = full.shape[0]
    results = []
    offset = 0
    for piece, dim in pieces:
        size = piece.size
        part = full[:, offset : offset + size].reshape((count,) + piece.shape)
        offset += size
        part = jnp.moveaxis(part, 0, dim)
        shape = list(piece.shape)
        shape[dim] *= count
        results.append(part.reshape(shape))
    return results


def scatter_packed(pieces, axes, count):
    columns = []
    local_shapes = []
    for grad, dim in pieces:
        shape = grad.shape
        split = shape[:dim] + (count, shape[dim] // count) + shape[dim + 1 :]
        local_shapes.append(shape[:dim] + (shape[dim] // count,) + shape[dim + 1 :])
        part = jnp.moveaxis(grad.reshape(split), dim, 0)
        columns.append(part.reshape(count, -1))
    packed = jnp.concatenate(columns, axis=1)
    width = packed.shape[1]
    rows = -(-width // 1024) * 8
    packed = jnp.pad(packed, ((0, 0), (0, rows * 128 - width))).reshape(count * rows, 128)
    own = lax.psum_scatter(packed, axes, scatter_dimension=0, tiled=True).reshape(-1)
    results = []
    offset = 0
    for local_shape in local_shapes:
        size = 1
        for extent in local_shape:
            size *= extent
        results.append(own[offset : offset + size].reshape(local_shape))
        offset += size
    return results


def experts_dense(normed_two, grad_out, weights, expert_in_all, expert_down_all):
    gate_up = jnp.einsum(
        "td,edgf->etgf", normed_two, expert_in_all, preferred_element_type=jnp.float32
    )
    act, act_back = jax.vjp(swiglu_experts, gate_up)
    hidden = act.astype(jnp.bfloat16)
    outs = jnp.einsum("etf,efd->etd", hidden, expert_down_all, preferred_element_type=jnp.float32)
    weights_e = weights.T[:, :, None]
    combined = jnp.sum(weights_e * outs, axis=0)
    gate_dots = jnp.sum(outs * grad_out[None], axis=-1).T
    grad_outs = (weights_e * grad_out[None]).astype(jnp.bfloat16)
    grad_hidden = jnp.einsum(
        "etd,efd->etf", grad_outs, expert_down_all, preferred_element_type=jnp.float32
    )
    grad_gate_up = act_back(grad_hidden)[0].astype(jnp.bfloat16)
    grad_down = jnp.einsum("etf,etd->efd", hidden, grad_outs, preferred_element_type=jnp.float32)
    grad_in = jnp.einsum(
        "td,etgf->edgf", normed_two, grad_gate_up, preferred_element_type=jnp.float32
    )
    grad_rows = jnp.einsum(
        "etgf,edgf->td", grad_gate_up, expert_in_all, preferred_element_type=jnp.float32
    )
    return combined, gate_dots, grad_rows, grad_in, grad_down


def experts_routed(
    normed_two, grad_out, route_rows, gate_probs, expert_in_low, expert_down_low, capacity
):
    block_len, model_width = normed_two.shape
    experts = lax.axis_size("fsdp")
    slot_index, owner_route, filled = slot_tables(route_rows, experts, capacity)
    fill_mask = filled.astype(jnp.bfloat16)[:, None]
    route_grads = (
        (gate_probs[:, :, None] * grad_out[:, None, :])
        .astype(jnp.bfloat16)
        .reshape(2 * block_len, model_width)
    )
    send_rows = jnp.concatenate(
        [normed_two[owner_route // 2] * fill_mask, route_grads[owner_route] * fill_mask], axis=1
    ).reshape(experts, capacity, 2 * model_width)
    exchange = lambda rows: lax.all_to_all(rows, "fsdp", split_axis=0, concat_axis=0, tiled=True)
    received_both = exchange(send_rows).reshape(experts * capacity, 2 * model_width)
    received = received_both[:, :model_width]
    grad_received = received_both[:, model_width:]
    gate_up = jnp.einsum("rd,dgf->rgf", received, expert_in_low, preferred_element_type=jnp.float32)
    act, act_back = jax.vjp(swiglu, gate_up)
    hidden = act.astype(jnp.bfloat16)
    outs = jnp.dot(hidden, expert_down_low, preferred_element_type=jnp.float32)
    grad_hidden = jnp.einsum(
        "rd,fd->rf", grad_received, expert_down_low, preferred_element_type=jnp.float32
    )
    grad_gate_up = act_back(grad_hidden)[0].astype(jnp.bfloat16)
    grad_in = jnp.einsum("rd,rgf->dgf", received, grad_gate_up, preferred_element_type=jnp.float32)
    grad_down = jnp.einsum("rf,rd->fd", hidden, grad_received, preferred_element_type=jnp.float32)
    grad_expert_rows = jnp.einsum(
        "rgf,dgf->rd", grad_gate_up, expert_in_low, preferred_element_type=jnp.float32
    )
    returned = exchange(
        jnp.concatenate([outs, grad_expert_rows], axis=1).reshape(
            experts, capacity, 2 * model_width
        )
    ).reshape(experts * capacity, 2 * model_width)[slot_index]
    route_out = returned[:, :model_width].reshape(block_len, 2, model_width)
    grad_routes = returned[:, model_width:].reshape(block_len, 2, model_width)
    combined = jnp.sum(gate_probs[:, :, None] * route_out, axis=1)
    gate_dots = jnp.sum(grad_out[:, None, :] * route_out, axis=-1)
    grad_rows = jnp.sum(grad_routes, axis=1)
    return combined, gate_dots, grad_rows, grad_in, grad_down


def local(
    layer_input,
    segments,
    routes,
    cotangent,
    gains,
    attention_in,
    attention_out,
    router_weight,
    shared_in,
    shared_down,
    expert_in,
    expert_down,
    model_stats,
    head_stats,
    value_columns,
    hidden_stats,
    router_state,
    expert_model_stats,
    expert_hidden_stats,
):
    block_len = layer_input.shape[1]
    model_width = layer_input.shape[2]
    experts = router_weight.shape[1]
    dense_experts = False
    capacity = min(block_len, 4 * block_len // experts)
    ctx_index = lax.axis_index("ctx")
    tp_index = lax.axis_index("tp")
    fsdp_index = lax.axis_index("fsdp")
    shard_index = lax.axis_index(("fsdp", "ctx"))
    shard_count = lax.axis_size(("fsdp", "ctx"))
    ctx_count = lax.axis_size("ctx")
    base_pos = ctx_index * block_len
    low = lambda v: v.astype(jnp.bfloat16)
    gain_low, attn_in_low = gather_packed(
        [(low(gains), 1), (low(attention_in), 0)], ("fsdp", "ctx")
    )
    later = [
        (low(attention_out), 1),
        (low(router_weight), 0),
        (low(shared_in), 0),
        (low(shared_down), 1),
    ]
    if dense_experts:
        later += [(low(expert_in), 0), (low(expert_down), 0)]
    later_full = gather_packed(later, ("fsdp", "ctx"))
    attn_out_low, router_low, shared_in_low, shared_down_low = later_full[:4]
    if dense_experts:
        fe_local = expert_down.shape[1]
        expert_in_all = later_full[4].reshape(experts, model_width, 2, fe_local)
        expert_down_all = (
            later_full[5]
            .reshape(experts, ctx_count, fe_local, model_width // ctx_count)
            .transpose(0, 2, 1, 3)
            .reshape(experts, fe_local, model_width)
        )
    else:
        expert_in_low = lax.all_gather(low(expert_in), "ctx", axis=1, tiled=True)[0]
        expert_down_low = lax.all_gather(low(expert_down), "ctx", axis=2, tiled=True)[0]
    residual = layer_input[0].astype(jnp.float32)
    gain_one = gain_low[0].astype(jnp.float32)
    gain_two = gain_low[1].astype(jnp.float32)
    normed_one, norm_one_back = jax.vjp(rms_norm, residual, gain_one)
    normed_one = normed_one.astype(jnp.bfloat16)
    projected = jnp.einsum(
        "td,dgf->tgf", normed_one, attn_in_low, preferred_element_type=jnp.float32
    )
    local_cols = projected.shape[2]
    local_heads = local_cols // HD
    half_dim = HD // 2
    frequency = 10000.0 ** (-jnp.arange(half_dim, dtype=jnp.float32) / half_dim)
    angles = (base_pos + jnp.arange(block_len, dtype=jnp.int32)).astype(jnp.float32)[
        :, None
    ] * frequency[None, :]
    cosine = jnp.cos(angles)
    sine_tab = jnp.sin(angles)
    queries = rotate(projected[:, 0].reshape(block_len, local_heads, HD), cosine, sine_tab).astype(
        jnp.bfloat16
    )
    keys_own = rotate(projected[:, 1].reshape(block_len, local_heads, HD), cosine, sine_tab).astype(
        jnp.bfloat16
    )
    values_own = projected[:, 2].reshape(block_len, local_heads, HD).astype(jnp.bfloat16)
    seg_own = segments[0].astype(jnp.bfloat16)
    keys_prev, values_prev, seg_prev = from_behind((keys_own, values_own, seg_own), "ctx", 1)
    keys_ext = jnp.concatenate([keys_prev, keys_own], axis=0)
    values_ext = jnp.concatenate([values_prev, values_own], axis=0)
    seg_ext = jnp.concatenate([seg_prev, seg_own], axis=0)
    block_rows = min(512, block_len)
    block_total = block_len // block_rows
    starts = jnp.arange(block_total, dtype=jnp.int32) * block_rows

    def forward_block(start_row):
        query_rows, key_rows, value_rows, masked, allowed = block_view(
            queries, keys_ext, values_ext, seg_own, seg_ext, start_row, base_pos
        )
        row_max = jnp.max(masked, axis=-1, keepdims=True)
        exp_terms = jnp.where(allowed[None], jnp.exp(masked - row_max), 0.0)
        row_total = jnp.sum(exp_terms, axis=-1, keepdims=True)
        attn_probs = (exp_terms / row_total).astype(jnp.bfloat16)
        attended = jnp.einsum(
            "hqk,khd->qhd", attn_probs, value_rows, preferred_element_type=jnp.float32
        )
        return (attended, row_max + jnp.log(row_total))

    attended, log_totals = lax.map(forward_block, starts)
    mixed_heads = attended.reshape(block_len, local_cols).astype(jnp.bfloat16)
    attn_total = lax.psum(
        jnp.dot(mixed_heads, attn_out_low, preferred_element_type=jnp.float32), "tp"
    )
    after_attn = residual + attn_total
    normed_two, norm_two_back = jax.vjp(rms_norm, after_attn, gain_two)
    normed_two = normed_two.astype(jnp.bfloat16)
    logits = jnp.dot(normed_two, router_low, preferred_element_type=jnp.float32)
    route_rows = routes[0]
    onehot = (route_rows[:, :, None] == jnp.arange(experts, dtype=jnp.int32)[None, None, :]).astype(
        jnp.float32
    )
    picked = jnp.sum(onehot * logits[:, None, :], axis=-1)
    gate_probs = jax.nn.softmax(picked, axis=-1)
    upstream = cotangent[0]
    grad_out = upstream.astype(jnp.float32)
    if dense_experts:
        weights = jnp.sum(gate_probs[:, :, None] * onehot, axis=1)
        combined, dots_e, grad_rows, grad_expert_in, grad_expert_down = experts_dense(
            normed_two, grad_out, weights, expert_in_all, expert_down_all
        )
        gate_dots = jnp.sum(onehot * dots_e[:, None, :], axis=-1)
    else:
        combined, gate_dots, grad_rows, grad_expert_in, grad_expert_down = experts_routed(
            normed_two,
            grad_out,
            route_rows,
            gate_probs,
            expert_in_low,
            expert_down_low,
            capacity,
        )
    shared_gate_up = jnp.einsum(
        "td,dgf->tgf", normed_two, shared_in_low, preferred_element_type=jnp.float32
    )
    shared_act, shared_act_back = jax.vjp(swiglu, shared_gate_up)
    shared_hidden = shared_act.astype(jnp.bfloat16)
    shared_out = jnp.dot(shared_hidden, shared_down_low, preferred_element_type=jnp.float32)
    grad_shared_hidden = jnp.einsum(
        "td,fd->tf", upstream, shared_down_low, preferred_element_type=jnp.float32
    )
    grad_shared_gate_up = shared_act_back(grad_shared_hidden)[0].astype(jnp.bfloat16)
    partial_two = (
        jnp.einsum(
            "tgf,dgf->td", grad_shared_gate_up, shared_in_low, preferred_element_type=jnp.float32
        )
        + grad_rows
    )
    branch_total, grad_normed_part, gate_total = lax.psum(
        (shared_out + combined, partial_two, gate_dots), "tp"
    )
    layer_out = after_attn + branch_total
    grad_picked = gate_probs * (
        gate_total - jnp.sum(gate_probs * gate_total, axis=-1, keepdims=True)
    )
    grad_logits = jnp.sum(grad_picked[:, :, None] * onehot, axis=1).astype(jnp.bfloat16)
    grad_shared_in = jnp.einsum(
        "td,tgf->dgf", normed_two, grad_shared_gate_up, preferred_element_type=jnp.float32
    )
    grad_shared_down = jnp.einsum(
        "tf,td->fd", shared_hidden, upstream, preferred_element_type=jnp.float32
    )
    grad_router = jnp.einsum(
        "td,te->de", normed_two, grad_logits, preferred_element_type=jnp.float32
    )
    grad_normed_two = grad_normed_part + jnp.einsum(
        "te,de->td", grad_logits, router_low, preferred_element_type=jnp.float32
    )
    grad_after, grad_gain_two = norm_two_back(grad_normed_two)
    grad_after = grad_after + grad_out
    grad_attn_low = grad_after.astype(jnp.bfloat16)
    grad_attn_out = jnp.einsum(
        "tc,td->cd", mixed_heads, grad_attn_low, preferred_element_type=jnp.float32
    )
    first_grads = [
        (grad_attn_out, 1),
        (grad_router, 0),
        (grad_shared_in, 0),
        (grad_shared_down, 1),
        (grad_gain_two, 0),
    ]
    if dense_experts:
        fe_local = expert_down.shape[1]
        first_grads += [
            (grad_expert_in.reshape(shard_count * expert_in.shape[1], 2, fe_local), 0),
            (
                grad_expert_down.reshape(experts, fe_local, ctx_count, model_width // ctx_count)
                .transpose(0, 2, 1, 3)
                .reshape(shard_count * fe_local, model_width // ctx_count),
                0,
            ),
        ]
    if not dense_experts:
        own_expert_in = lax.psum_scatter(grad_expert_in[None], "ctx", scatter_dimension=1, tiled=True)
        own_expert_down = lax.psum_scatter(
            grad_expert_down[None], "ctx", scatter_dimension=2, tiled=True
        )
    first_own = scatter_packed(first_grads, ("fsdp", "ctx"), shard_count)
    own_attn_out, own_router, own_shared_in, own_shared_down, own_gain_two = first_own[:5]
    if dense_experts:
        own_expert_in = first_own[5][None]
        own_expert_down = first_own[6][None]
    grad_heads = (
        jnp.einsum("td,cd->tc", grad_attn_low, attn_out_low, preferred_element_type=jnp.float32)
        .astype(jnp.bfloat16)
        .reshape(block_len, local_heads, HD)
    )

    def backward_block(block_number, running):
        grad_keys, grad_values, grad_queries = running
        start_row = block_number * block_rows
        query_rows, key_rows, value_rows, masked, allowed = block_view(
            queries, keys_ext, values_ext, seg_own, seg_ext, start_row, base_pos
        )
        log_total = lax.dynamic_index_in_dim(log_totals, block_number, 0, keepdims=False)
        attn_probs = jnp.where(allowed[None], jnp.exp(masked - log_total), 0.0)
        grad_block = lax.dynamic_slice_in_dim(grad_heads, start_row, block_rows, 0)
        grad_probs = jnp.einsum(
            "qhd,khd->hqk", grad_block, value_rows, preferred_element_type=jnp.float32
        )
        inner_sum = jnp.sum(attn_probs * grad_probs, axis=-1, keepdims=True)
        grad_scores = (attn_probs * (grad_probs - inner_sum)).astype(jnp.bfloat16)
        grad_query_rows = (
            jnp.einsum("hqk,khd->qhd", grad_scores, key_rows, preferred_element_type=jnp.float32)
            * 0.125
        )
        grad_key_rows = (
            jnp.einsum("hqk,qhd->khd", grad_scores, query_rows, preferred_element_type=jnp.float32)
            * 0.125
        )
        grad_value_rows = jnp.einsum(
            "hqk,qhd->khd",
            attn_probs.astype(jnp.bfloat16),
            grad_block,
            preferred_element_type=jnp.float32,
        )
        key_offset = start_row + block_len - WINDOW
        grad_keys = lax.dynamic_update_slice_in_dim(
            grad_keys,
            lax.dynamic_slice_in_dim(grad_keys, key_offset, block_rows + WINDOW, 0) + grad_key_rows,
            key_offset,
            0,
        )
        grad_values = lax.dynamic_update_slice_in_dim(
            grad_values,
            lax.dynamic_slice_in_dim(grad_values, key_offset, block_rows + WINDOW, 0)
            + grad_value_rows,
            key_offset,
            0,
        )
        grad_queries = lax.dynamic_update_slice_in_dim(grad_queries, grad_query_rows, start_row, 0)
        return (grad_keys, grad_values, grad_queries)

    zero_ext = jnp.zeros((2 * block_len, local_heads, HD), jnp.float32)
    zero_own = jnp.zeros((block_len, local_heads, HD), jnp.float32)
    grad_keys, grad_values, grad_queries = lax.fori_loop(
        0, block_total, backward_block, (zero_ext, zero_ext, zero_own)
    )
    rim_keys, rim_values = (
        from_behind(grad_keys[:block_len].astype(jnp.bfloat16), "ctx", -1).astype(jnp.float32),
        from_behind(grad_values[:block_len].astype(jnp.bfloat16), "ctx", -1).astype(jnp.float32),
    )
    grad_keys_own = grad_keys[block_len:] + rim_keys
    grad_values_own = grad_values[block_len:] + rim_values
    grad_query_raw = rotate(grad_queries, cosine, -sine_tab)
    grad_key_raw = rotate(grad_keys_own, cosine, -sine_tab)
    grad_projected = (
        jnp.stack([grad_query_raw, grad_key_raw, grad_values_own], axis=1)
        .reshape(block_len, 3, local_cols)
        .astype(jnp.bfloat16)
    )
    grad_attn_in = jnp.einsum(
        "td,tgf->dgf", normed_one, grad_projected, preferred_element_type=jnp.float32
    )
    partial_one = jnp.einsum(
        "tgf,dgf->td", grad_projected, attn_in_low, preferred_element_type=jnp.float32
    )
    grad_residual, grad_gain_one = norm_one_back(lax.psum(partial_one, "tp"))
    input_grad = grad_after + grad_residual
    own_attn_in, own_gain_one = scatter_packed(
        [(grad_attn_in, 0), (grad_gain_one, 0)], ("fsdp", "ctx"), shard_count
    )
    own_gains = jnp.stack([own_gain_one, own_gain_two])
    lead_tp = (tp_index == 0).astype(jnp.float32)
    first_shard = (shard_index == 0).astype(jnp.float32)
    first_ctx = (ctx_index == 0).astype(jnp.float32)
    d_local = gains.shape[1]
    ff_local = shared_down.shape[0]
    fe_local = expert_down.shape[1]
    d_quarter = expert_in.shape[1]
    square_attn_in = own_attn_in * own_attn_in + TINY_SQUARE
    square_attn_out = own_attn_out * own_attn_out + TINY_SQUARE
    square_shared_in = own_shared_in * own_shared_in + TINY_SQUARE
    square_shared_down = own_shared_down * own_shared_down + TINY_SQUARE
    square_expert_in = own_expert_in[0] * own_expert_in[0] + TINY_SQUARE
    square_expert_down = own_expert_down[0] * own_expert_down[0] + TINY_SQUARE
    model_part = lax.dynamic_update_slice(
        jnp.zeros((4, D), jnp.float32),
        jnp.stack(
            [
                jnp.sum(square_attn_in, axis=(1, 2)),
                jnp.sum(square_shared_in, axis=(1, 2)),
                jnp.sum(square_attn_out, axis=0),
                jnp.sum(square_shared_down, axis=0),
            ]
        ),
        (0, shard_index * d_local),
    )
    head_part = lax.dynamic_update_slice(
        jnp.zeros((4, HH), jnp.float32),
        jnp.concatenate(
            [jnp.sum(square_attn_in, axis=0), jnp.sum(square_attn_out, axis=1)[None]], axis=0
        ),
        (0, tp_index * local_cols),
    )
    hidden_part = lax.dynamic_update_slice(
        jnp.zeros((3, FF), jnp.float32),
        jnp.concatenate(
            [jnp.sum(square_shared_in, axis=0), jnp.sum(square_shared_down, axis=1)[None]], axis=0
        ),
        (0, tp_index * ff_local),
    )
    expert_model_part = lax.dynamic_update_slice(
        jnp.zeros((experts, 2, D), jnp.float32),
        jnp.stack([jnp.sum(square_expert_in, axis=(1, 2)), jnp.sum(square_expert_down, axis=0)])[
            None
        ],
        (fsdp_index, 0, ctx_index * d_quarter),
    )
    expert_hidden_part = lax.dynamic_update_slice(
        jnp.zeros((experts, 3, FE), jnp.float32),
        jnp.concatenate(
            [jnp.sum(square_expert_in, axis=0), jnp.sum(square_expert_down, axis=1)[None]], axis=0
        )[None],
        (fsdp_index, 0, tp_index * fe_local),
    )
    scalar_part = jnp.stack(
        [
            lead_tp * jnp.sum(gains * gains),
            jnp.sum(attention_in * attention_in),
            jnp.sum(attention_out * attention_out),
            lead_tp * jnp.sum(router_weight * router_weight),
            jnp.sum(shared_in * shared_in),
            jnp.sum(shared_down * shared_down),
            jnp.sum(expert_in * expert_in),
            jnp.sum(expert_down * expert_down),
            lead_tp * jnp.sum(model_stats[2]),
            first_shard * jnp.sum(head_stats[2]),
            lead_tp * jnp.sum(model_stats[3]),
            first_shard * jnp.sum(hidden_stats[2]),
        ]
    )
    expert_old_part = lax.dynamic_update_slice(
        jnp.zeros((2, experts), jnp.float32),
        jnp.stack(
            [
                lead_tp * jnp.sum(expert_model_stats[0, 0]),
                first_ctx * jnp.sum(expert_hidden_stats[0, 2]),
            ]
        )[:, None],
        (0, fsdp_index),
    )
    global_sums = butterfly_sum(
        [
            model_part,
            head_part,
            hidden_part,
            expert_model_part,
            expert_hidden_part,
            scalar_part,
            expert_old_part,
        ],
        1,
    )
    (
        model_sum,
        head_sum,
        hidden_sum,
        expert_model_sum,
        expert_hidden_sum,
        scalar_sum,
        expert_old_sum,
    ) = global_sums
    shard_start = shard_index * d_local
    gain_state = DECAY_RATE * model_stats[0:2] + (1.0 - DECAY_RATE) * (
        own_gains * own_gains + TINY_SQUARE
    )
    update_gains = own_gains * lax.rsqrt(gain_state)
    router_new = DECAY_RATE * router_state + (1.0 - DECAY_RATE) * (
        own_router * own_router + TINY_SQUARE
    )
    update_router = own_router * lax.rsqrt(router_new)
    attn_cols_old = jnp.concatenate([head_stats[0:2], value_columns[None]], axis=0).reshape(-1)
    update_attn_in, rows_attn_in, cols_attn_in = factored_update(
        own_attn_in.reshape(d_local, 3 * local_cols),
        model_stats[2],
        attn_cols_old,
        lax.dynamic_slice_in_dim(model_sum[0], shard_start, d_local),
        lax.dynamic_slice_in_dim(head_sum[0:3], tp_index * local_cols, local_cols, 1).reshape(-1),
        D,
        3 * HH,
        scalar_sum[8],
        jnp.sum(model_sum[0]),
    )
    update_attn_out, rows_attn_out, cols_attn_out = factored_update(
        own_attn_out,
        head_stats[2],
        model_stats[4],
        lax.dynamic_slice_in_dim(head_sum[3], tp_index * local_cols, local_cols),
        lax.dynamic_slice_in_dim(model_sum[2], shard_start, d_local),
        HH,
        D,
        scalar_sum[9],
        jnp.sum(head_sum[3]),
    )
    update_shared_in, rows_shared_in, cols_shared_in = factored_update(
        own_shared_in.reshape(d_local, 2 * ff_local),
        model_stats[3],
        hidden_stats[0:2].reshape(-1),
        lax.dynamic_slice_in_dim(model_sum[1], shard_start, d_local),
        lax.dynamic_slice_in_dim(hidden_sum[0:2], tp_index * ff_local, ff_local, 1).reshape(-1),
        D,
        2 * FF,
        scalar_sum[10],
        jnp.sum(model_sum[1]),
    )
    update_shared_down, rows_shared_down, cols_shared_down = factored_update(
        own_shared_down,
        hidden_stats[2],
        model_stats[5],
        lax.dynamic_slice_in_dim(hidden_sum[2], tp_index * ff_local, ff_local),
        lax.dynamic_slice_in_dim(model_sum[3], shard_start, d_local),
        FF,
        D,
        scalar_sum[11],
        jnp.sum(hidden_sum[2]),
    )
    own_expert_model = lax.dynamic_index_in_dim(expert_model_sum, fsdp_index, 0, keepdims=False)
    own_expert_hidden = lax.dynamic_index_in_dim(expert_hidden_sum, fsdp_index, 0, keepdims=False)
    old_expert_totals = lax.dynamic_index_in_dim(expert_old_sum, fsdp_index, 1, keepdims=False)
    update_expert_in, rows_expert_in, cols_expert_in = factored_update(
        own_expert_in[0].reshape(d_quarter, 2 * fe_local),
        expert_model_stats[0, 0],
        expert_hidden_stats[0, 0:2].reshape(-1),
        lax.dynamic_slice_in_dim(own_expert_model[0], ctx_index * d_quarter, d_quarter),
        lax.dynamic_slice_in_dim(own_expert_hidden[0:2], tp_index * fe_local, fe_local, 1).reshape(
            -1
        ),
        D,
        2 * FE,
        old_expert_totals[0],
        jnp.sum(own_expert_model[0]),
    )
    update_expert_down, rows_expert_down, cols_expert_down = factored_update(
        own_expert_down[0],
        expert_hidden_stats[0, 2],
        expert_model_stats[0, 1],
        lax.dynamic_slice_in_dim(own_expert_hidden[2], tp_index * fe_local, fe_local),
        lax.dynamic_slice_in_dim(own_expert_model[1], ctx_index * d_quarter, d_quarter),
        FE,
        D,
        old_expert_totals[1],
        jnp.sum(own_expert_hidden[2]),
    )
    clip_part = jnp.stack(
        [
            lead_tp * jnp.sum(update_gains * update_gains),
            jnp.sum(update_attn_in * update_attn_in),
            jnp.sum(update_attn_out * update_attn_out),
            lead_tp * jnp.sum(update_router * update_router),
            jnp.sum(update_shared_in * update_shared_in),
            jnp.sum(update_shared_down * update_shared_down),
            jnp.sum(update_expert_in * update_expert_in),
            jnp.sum(update_expert_down * update_expert_down),
        ]
    )
    clip_total = butterfly_sum([clip_part], 2)[0]
    elements = jnp.array(
        [
            2 * D,
            D * 3 * HH,
            HH * D,
            D * experts,
            D * 2 * FF,
            FF * D,
            experts * D * 2 * FE,
            experts * FE * D,
        ],
        jnp.float32,
    )
    update_roots = jnp.sqrt(clip_total / elements)
    new_gains = apply_update(gains, update_gains, update_roots[0], scalar_sum[0], elements[0])
    new_attn_in = apply_update(
        attention_in,
        update_attn_in.reshape(attention_in.shape),
        update_roots[1],
        scalar_sum[1],
        elements[1],
    )
    new_attn_out = apply_update(
        attention_out, update_attn_out, update_roots[2], scalar_sum[2], elements[2]
    )
    new_router = apply_update(
        router_weight, update_router, update_roots[3], scalar_sum[3], elements[3]
    )
    new_shared_in = apply_update(
        shared_in,
        update_shared_in.reshape(shared_in.shape),
        update_roots[4],
        scalar_sum[4],
        elements[4],
    )
    new_shared_down = apply_update(
        shared_down, update_shared_down, update_roots[5], scalar_sum[5], elements[5]
    )
    new_expert_in = apply_update(
        expert_in,
        update_expert_in.reshape(expert_in.shape),
        update_roots[6],
        scalar_sum[6],
        elements[6],
    )
    new_expert_down = apply_update(
        expert_down,
        update_expert_down.reshape(expert_down.shape),
        update_roots[7],
        scalar_sum[7],
        elements[7],
    )
    new_model_stats = jnp.concatenate(
        [gain_state, jnp.stack([rows_attn_in, rows_shared_in, cols_attn_out, cols_shared_down])],
        axis=0,
    )
    attn_cols_new = cols_attn_in.reshape(3, local_cols)
    new_head_stats = jnp.concatenate([attn_cols_new[0:2], rows_attn_out[None]], axis=0)
    new_value_columns = attn_cols_new[2]
    new_hidden_stats = jnp.concatenate(
        [cols_shared_in.reshape(2, ff_local), rows_shared_down[None]], axis=0
    )
    new_expert_model_stats = jnp.stack([rows_expert_in, cols_expert_down])[None]
    new_expert_hidden_stats = jnp.concatenate(
        [cols_expert_in.reshape(2, fe_local), rows_expert_down[None]], axis=0
    )[None]
    return (
        layer_out.astype(jnp.bfloat16)[None],
        input_grad[None],
        own_gains,
        own_attn_in,
        own_attn_out,
        own_router,
        own_shared_in,
        own_shared_down,
        own_expert_in,
        own_expert_down,
        new_gains,
        new_attn_in,
        new_attn_out,
        new_router,
        new_shared_in,
        new_shared_down,
        new_expert_in,
        new_expert_down,
        new_model_stats,
        new_head_stats,
        new_value_columns,
        new_hidden_stats,
        router_new,
        new_expert_model_stats,
        new_expert_hidden_stats,
        update_roots,
    )


def solution(mesh):
    in_specs = (
        P("fsdp", "ctx", None),
        P("fsdp", "ctx"),
        P("fsdp", "ctx", None),
        P("fsdp", "ctx", None),
        P(None, ("fsdp", "ctx")),
        P(("fsdp", "ctx"), None, "tp"),
        P("tp", ("fsdp", "ctx")),
        P(("fsdp", "ctx"), None),
        P(("fsdp", "ctx"), None, "tp"),
        P("tp", ("fsdp", "ctx")),
        P("fsdp", "ctx", None, "tp"),
        P("fsdp", "tp", "ctx"),
        P(None, ("fsdp", "ctx")),
        P(None, "tp"),
        P("tp"),
        P(None, "tp"),
        P(("fsdp", "ctx"), None),
        P("fsdp", None, "ctx"),
        P("fsdp", None, "tp"),
    )
    out_specs = (
        P("fsdp", "ctx", None),
        P("fsdp", "ctx", None),
        P(None, ("fsdp", "ctx")),
        P(("fsdp", "ctx"), None, "tp"),
        P("tp", ("fsdp", "ctx")),
        P(("fsdp", "ctx"), None),
        P(("fsdp", "ctx"), None, "tp"),
        P("tp", ("fsdp", "ctx")),
        P("fsdp", "ctx", None, "tp"),
        P("fsdp", "tp", "ctx"),
        P(None, ("fsdp", "ctx")),
        P(("fsdp", "ctx"), None, "tp"),
        P("tp", ("fsdp", "ctx")),
        P(("fsdp", "ctx"), None),
        P(("fsdp", "ctx"), None, "tp"),
        P("tp", ("fsdp", "ctx")),
        P("fsdp", "ctx", None, "tp"),
        P("fsdp", "tp", "ctx"),
        P(None, ("fsdp", "ctx")),
        P(None, "tp"),
        P("tp"),
        P(None, "tp"),
        P(("fsdp", "ctx"), None),
        P("fsdp", None, "ctx"),
        P("fsdp", None, "tp"),
        P(),
    )
    return jax.shard_map(local, mesh=mesh, in_specs=in_specs, out_specs=out_specs, check_vma=False)
```

```python
import jax
import jax.numpy as jnp
from jax import lax
from jax.sharding import PartitionSpec as P
from jax.experimental import pallas as pl
from jax.experimental.pallas import tpu as pltpu

D = 768
HD = 64
FF = 2048
FE = 2048
WINDOW = 1024
HH = 768


EPSILON = 1e-06
TINY_SQUARE = 1e-30
SCALE_FLOOR = 0.001
DECAY_RATE = 0.5
CLIP_LIMIT = 0.5
STEP_RATE = 0.5


def from_behind(value, axis, steps):
    count = lax.axis_size(axis)
    leading, last = (max(0, -steps), min(count, count - steps))
    return lax.ppermute(value, axis, [(source, source + steps) for source in range(leading, last)])


def rms_norm(values, gain_vec):
    inv_rms = lax.rsqrt(jnp.mean(values * values, axis=-1, keepdims=True) + EPSILON)
    return values * inv_rms * gain_vec


def swiglu(gate_up):
    return jax.nn.silu(gate_up[:, 0]) * gate_up[:, 1]


def rotate(values, cosine, sine_tab):
    half_dim = values.shape[-1] // 2
    first_half = values[..., :half_dim]
    second_half = values[..., half_dim:]
    cos_b = cosine[:, None, :]
    sin_b = sine_tab[:, None, :]
    return jnp.concatenate(
        [first_half * cos_b - second_half * sin_b, second_half * cos_b + first_half * sin_b],
        axis=-1,
    )


def slot_tables(block_routes, experts, capacity):
    flat_routes = block_routes.reshape(-1)
    route_count = flat_routes.shape[0]
    onehot = (flat_routes[:, None] == jnp.arange(experts, dtype=jnp.int32)[None, :]).astype(
        jnp.int32
    )
    rank_in = jnp.sum(
        (jnp.cumsum(onehot, axis=0, dtype=jnp.int32) - 1) * onehot, axis=1, dtype=jnp.int32
    )
    slot_index = flat_routes * capacity + rank_in
    owner_route = (
        jnp.zeros((experts * capacity,), jnp.int32)
        .at[slot_index]
        .set(jnp.arange(route_count, dtype=jnp.int32))
    )
    filled = jnp.zeros((experts * capacity,), jnp.int32).at[slot_index].set(1)
    return (slot_index, owner_route, filled)


def block_view(queries, keys_ext, values_ext, seg_own, seg_ext, start_row, base_pos):
    block_len = queries.shape[0]
    block_rows = min(512, block_len)
    query_rows = lax.dynamic_slice_in_dim(queries, start_row, block_rows, 0)
    key_rows = lax.dynamic_slice_in_dim(
        keys_ext, start_row + block_len - WINDOW, block_rows + WINDOW, 0
    )
    value_rows = lax.dynamic_slice_in_dim(
        values_ext, start_row + block_len - WINDOW, block_rows + WINDOW, 0
    )
    scores = (
        jnp.einsum("qhd,khd->hqk", query_rows, key_rows, preferred_element_type=jnp.float32) * 0.125
    )
    query_pos = start_row + jnp.arange(block_rows, dtype=jnp.int32)
    key_pos = start_row - WINDOW + jnp.arange(block_rows + WINDOW, dtype=jnp.int32)
    distance = query_pos[:, None] - key_pos[None, :]
    seg_query = lax.dynamic_slice_in_dim(seg_own, start_row, block_rows, 0)
    seg_key = lax.dynamic_slice_in_dim(
        seg_ext, start_row + block_len - WINDOW, block_rows + WINDOW, 0
    )
    allowed = (
        (distance >= 0)
        & (distance < WINDOW)
        & (seg_query[:, None] == seg_key[None, :])
        & (key_pos[None, :] + base_pos >= 0)
    )
    return (query_rows, key_rows, value_rows, jnp.where(allowed[None], scores, -1e30), allowed)


def factored_update(
    grad_mat, rows_old, cols_old, row_sums, col_sums, row_total, col_total, old_total, square_total
):
    rows_new = DECAY_RATE * rows_old + (1.0 - DECAY_RATE) * row_sums / col_total
    cols_new = DECAY_RATE * cols_old + (1.0 - DECAY_RATE) * col_sums / row_total
    mean_rows = (DECAY_RATE * old_total + (1.0 - DECAY_RATE) * square_total / col_total) / row_total
    second_moment = rows_new[:, None] * cols_new[None, :] / mean_rows
    return (grad_mat * lax.rsqrt(second_moment), rows_new, cols_new)


def apply_update(weight, update, update_root, square_sum, elements):
    param_scale = jnp.maximum(SCALE_FLOOR, jnp.sqrt(square_sum / elements))
    return weight - STEP_RATE * param_scale * update / jnp.maximum(1.0, update_root / CLIP_LIMIT)


def butterfly_partners():
    partners = []
    here = [lax.axis_index(name) for name in ("fsdp", "ctx", "tp")]
    for axis_number, name in enumerate(("fsdp", "ctx", "tp")):
        size = lax.axis_size(name)
        step = 1
        while step < size:
            bit = (here[axis_number] // step) % 2
            other = list(here)
            other[axis_number] = here[axis_number] + step * (1 - 2 * bit)
            partners.append(tuple(other))
            step *= 2
    return partners


def butterfly_kernel(x_ref, o_ref, stage, inbox, send_sems, recv_sems):
    partners = butterfly_partners()
    barrier = pltpu.get_barrier_semaphore()
    for partner in partners:
        pl.semaphore_signal(
            barrier, 1, device_id=partner, device_id_type=pl.DeviceIdType.MESH
        )
    pl.semaphore_wait(barrier, len(partners))
    acc = x_ref[...]
    for round_number, partner in enumerate(partners):
        stage[round_number] = acc
        copy = pltpu.make_async_remote_copy(
            src_ref=stage.at[round_number],
            dst_ref=inbox.at[round_number],
            send_sem=send_sems.at[round_number],
            recv_sem=recv_sems.at[round_number],
            device_id=partner,
            device_id_type=pl.DeviceIdType.MESH,
        )
        copy.start()
        copy.wait()
        acc = stage[round_number] + inbox[round_number]
    o_ref[...] = acc


def butterfly_sum(values, collective_id):
    flat = jnp.concatenate([v.reshape(-1).astype(jnp.float32) for v in values])
    size = flat.shape[0]
    rows = -(-size // 1024) * 8
    block = jnp.pad(flat, (0, rows * 128 - size)).reshape(rows, 128)
    rounds = sum(
        max(1, lax.axis_size(name)).bit_length() - 1 for name in ("fsdp", "ctx", "tp")
    )
    total = pl.pallas_call(
        butterfly_kernel,
        out_shape=jax.ShapeDtypeStruct((rows, 128), jnp.float32),
        in_specs=[pl.BlockSpec(memory_space=pltpu.VMEM)],
        out_specs=pl.BlockSpec(memory_space=pltpu.VMEM),
        scratch_shapes=[
            pltpu.VMEM((rounds, rows, 128), jnp.float32),
            pltpu.VMEM((rounds, rows, 128), jnp.float32),
            pltpu.SemaphoreType.DMA((rounds,)),
            pltpu.SemaphoreType.DMA((rounds,)),
        ],
        compiler_params=pltpu.CompilerParams(collective_id=collective_id, has_side_effects=True),
    )(block).reshape(-1)
    results = []
    offset = 0
    for v in values:
        results.append(total[offset : offset + v.size].reshape(v.shape))
        offset += v.size
    return results


def swiglu_experts(gate_up):
    return jax.nn.silu(gate_up[:, :, 0]) * gate_up[:, :, 1]


def gather_packed(pieces, axes):
    flat = jnp.concatenate([piece.reshape(-1) for piece, _ in pieces])
    full = lax.all_gather(flat, axes, axis=0, tiled=False)
    count = full.shape[0]
    results = []
    offset = 0
    for piece, dim in pieces:
        size = piece.size
        part = full[:, offset : offset + size].reshape((count,) + piece.shape)
        offset += size
        part = jnp.moveaxis(part, 0, dim)
        shape = list(piece.shape)
        shape[dim] *= count
        results.append(part.reshape(shape))
    return results


def scatter_packed(pieces, axes, count):
    columns = []
    local_shapes = []
    for grad, dim in pieces:
        shape = grad.shape
        split = shape[:dim] + (count, shape[dim] // count) + shape[dim + 1 :]
        local_shapes.append(shape[:dim] + (shape[dim] // count,) + shape[dim + 1 :])
        part = jnp.moveaxis(grad.reshape(split), dim, 0)
        columns.append(part.reshape(count, -1))
    packed = jnp.concatenate(columns, axis=1)
    width = packed.shape[1]
    rows = -(-width // 1024) * 8
    packed = jnp.pad(packed, ((0, 0), (0, rows * 128 - width))).reshape(count * rows, 128)
    own = lax.psum_scatter(packed, axes, scatter_dimension=0, tiled=True).reshape(-1)
    results = []
    offset = 0
    for local_shape in local_shapes:
        size = 1
        for extent in local_shape:
            size *= extent
        results.append(own[offset : offset + size].reshape(local_shape))
        offset += size
    return results


def experts_dense(normed_two, grad_out, weights, expert_in_all, expert_down_all):
    gate_up = jnp.einsum(
        "td,edgf->etgf", normed_two, expert_in_all, preferred_element_type=jnp.float32
    )
    act, act_back = jax.vjp(swiglu_experts, gate_up)
    hidden = act.astype(jnp.bfloat16)
    outs = jnp.einsum("etf,efd->etd", hidden, expert_down_all, preferred_element_type=jnp.float32)
    weights_e = weights.T[:, :, None]
    combined = jnp.sum(weights_e * outs, axis=0)
    gate_dots = jnp.sum(outs * grad_out[None], axis=-1).T
    grad_outs = (weights_e * grad_out[None]).astype(jnp.bfloat16)
    grad_hidden = jnp.einsum(
        "etd,efd->etf", grad_outs, expert_down_all, preferred_element_type=jnp.float32
    )
    grad_gate_up = act_back(grad_hidden)[0].astype(jnp.bfloat16)
    grad_down = jnp.einsum("etf,etd->efd", hidden, grad_outs, preferred_element_type=jnp.float32)
    grad_in = jnp.einsum(
        "td,etgf->edgf", normed_two, grad_gate_up, preferred_element_type=jnp.float32
    )
    grad_rows = jnp.einsum(
        "etgf,edgf->td", grad_gate_up, expert_in_all, preferred_element_type=jnp.float32
    )
    return combined, gate_dots, grad_rows, grad_in, grad_down


def experts_routed(
    normed_two, grad_out, route_rows, gate_probs, expert_in_low, expert_down_low, capacity
):
    block_len, model_width = normed_two.shape
    experts = lax.axis_size("fsdp")
    slot_index, owner_route, filled = slot_tables(route_rows, experts, capacity)
    fill_mask = filled.astype(jnp.bfloat16)[:, None]
    route_grads = (
        (gate_probs[:, :, None] * grad_out[:, None, :])
        .astype(jnp.bfloat16)
        .reshape(2 * block_len, model_width)
    )
    send_rows = jnp.concatenate(
        [normed_two[owner_route // 2] * fill_mask, route_grads[owner_route] * fill_mask], axis=1
    ).reshape(experts, capacity, 2 * model_width)
    exchange = lambda rows: lax.all_to_all(rows, "fsdp", split_axis=0, concat_axis=0, tiled=True)
    pair_count = lax.axis_size("tp")
    swap = lambda rows: lax.ppermute(
        rows, "tp", [(index, index + 1 - 2 * (index % 2)) for index in range(pair_count)]
    )
    half = capacity // 2
    side = lax.axis_index("tp") % 2
    mine = exchange(lax.dynamic_slice_in_dim(send_rows, side * half, half, 1))
    received_both = jnp.concatenate([mine, swap(mine)], axis=1).reshape(
        experts * capacity, 2 * model_width
    )
    received = received_both[:, :model_width]
    grad_received = received_both[:, model_width:]
    gate_up = jnp.einsum("rd,dgf->rgf", received, expert_in_low, preferred_element_type=jnp.float32)
    act, act_back = jax.vjp(swiglu, gate_up)
    hidden = act.astype(jnp.bfloat16)
    outs = jnp.dot(hidden, expert_down_low, preferred_element_type=jnp.float32)
    grad_hidden = jnp.einsum(
        "rd,fd->rf", grad_received, expert_down_low, preferred_element_type=jnp.float32
    )
    grad_gate_up = act_back(grad_hidden)[0].astype(jnp.bfloat16)
    grad_in = jnp.einsum("rd,rgf->dgf", received, grad_gate_up, preferred_element_type=jnp.float32)
    grad_down = jnp.einsum("rf,rd->fd", hidden, grad_received, preferred_element_type=jnp.float32)
    grad_expert_rows = jnp.einsum(
        "rgf,dgf->rd", grad_gate_up, expert_in_low, preferred_element_type=jnp.float32
    )
    results = jnp.concatenate([outs, grad_expert_rows], axis=1).reshape(
        experts, capacity, 2 * model_width
    )
    pair_sum = results[:, :half] + swap(results[:, half:])
    held = exchange(pair_sum).reshape(experts * half, 2 * model_width)
    slot_expert = slot_index // capacity
    slot_rank = slot_index % capacity
    in_side = (slot_rank // half) == side
    local_slot = slot_expert * half + slot_rank % half
    returned = jnp.where(in_side[:, None], held[local_slot], 0.0)
    route_out = returned[:, :model_width].reshape(block_len, 2, model_width)
    grad_routes = returned[:, model_width:].reshape(block_len, 2, model_width)
    combined = jnp.sum(gate_probs[:, :, None] * route_out, axis=1)
    gate_dots = jnp.sum(grad_out[:, None, :] * route_out, axis=-1)
    grad_rows = jnp.sum(grad_routes, axis=1)
    return combined, gate_dots, grad_rows, grad_in, grad_down


def local(
    layer_input,
    segments,
    routes,
    cotangent,
    gains,
    attention_in,
    attention_out,
    router_weight,
    shared_in,
    shared_down,
    expert_in,
    expert_down,
    model_stats,
    head_stats,
    value_columns,
    hidden_stats,
    router_state,
    expert_model_stats,
    expert_hidden_stats,
):
    block_len = layer_input.shape[1]
    model_width = layer_input.shape[2]
    experts = router_weight.shape[1]
    dense_experts = False
    capacity = min(block_len, 4 * block_len // experts)
    ctx_index = lax.axis_index("ctx")
    tp_index = lax.axis_index("tp")
    fsdp_index = lax.axis_index("fsdp")
    shard_index = lax.axis_index(("fsdp", "ctx"))
    shard_count = lax.axis_size(("fsdp", "ctx"))
    ctx_count = lax.axis_size("ctx")
    base_pos = ctx_index * block_len
    low = lambda v: v.astype(jnp.bfloat16)
    gain_low, attn_in_low = gather_packed(
        [(low(gains), 1), (low(attention_in), 0)], ("fsdp", "ctx")
    )
    later = [
        (low(attention_out), 1),
        (low(router_weight), 0),
        (low(shared_in), 0),
        (low(shared_down), 1),
    ]
    if dense_experts:
        later += [(low(expert_in), 0), (low(expert_down), 0)]
    later_full = gather_packed(later, ("fsdp", "ctx"))
    attn_out_low, router_low, shared_in_low, shared_down_low = later_full[:4]
    if dense_experts:
        fe_local = expert_down.shape[1]
        expert_in_all = later_full[4].reshape(experts, model_width, 2, fe_local)
        expert_down_all = (
            later_full[5]
            .reshape(experts, ctx_count, fe_local, model_width // ctx_count)
            .transpose(0, 2, 1, 3)
            .reshape(experts, fe_local, model_width)
        )
    else:
        expert_in_low = lax.all_gather(low(expert_in), "ctx", axis=1, tiled=True)[0]
        expert_down_low = lax.all_gather(low(expert_down), "ctx", axis=2, tiled=True)[0]
    residual = layer_input[0].astype(jnp.float32)
    gain_one = gain_low[0].astype(jnp.float32)
    gain_two = gain_low[1].astype(jnp.float32)
    normed_one, norm_one_back = jax.vjp(rms_norm, residual, gain_one)
    normed_one = normed_one.astype(jnp.bfloat16)
    projected = jnp.einsum(
        "td,dgf->tgf", normed_one, attn_in_low, preferred_element_type=jnp.float32
    )
    local_cols = projected.shape[2]
    local_heads = local_cols // HD
    half_dim = HD // 2
    frequency = 10000.0 ** (-jnp.arange(half_dim, dtype=jnp.float32) / half_dim)
    angles = (base_pos + jnp.arange(block_len, dtype=jnp.int32)).astype(jnp.float32)[
        :, None
    ] * frequency[None, :]
    cosine = jnp.cos(angles)
    sine_tab = jnp.sin(angles)
    queries = rotate(projected[:, 0].reshape(block_len, local_heads, HD), cosine, sine_tab).astype(
        jnp.bfloat16
    )
    keys_own = rotate(projected[:, 1].reshape(block_len, local_heads, HD), cosine, sine_tab).astype(
        jnp.bfloat16
    )
    values_own = projected[:, 2].reshape(block_len, local_heads, HD).astype(jnp.bfloat16)
    seg_own = segments[0].astype(jnp.bfloat16)
    keys_prev, values_prev, seg_prev = from_behind((keys_own, values_own, seg_own), "ctx", 1)
    keys_ext = jnp.concatenate([keys_prev, keys_own], axis=0)
    values_ext = jnp.concatenate([values_prev, values_own], axis=0)
    seg_ext = jnp.concatenate([seg_prev, seg_own], axis=0)
    block_rows = min(512, block_len)
    block_total = block_len // block_rows
    starts = jnp.arange(block_total, dtype=jnp.int32) * block_rows

    def forward_block(start_row):
        query_rows, key_rows, value_rows, masked, allowed = block_view(
            queries, keys_ext, values_ext, seg_own, seg_ext, start_row, base_pos
        )
        row_max = jnp.max(masked, axis=-1, keepdims=True)
        exp_terms = jnp.where(allowed[None], jnp.exp(masked - row_max), 0.0)
        row_total = jnp.sum(exp_terms, axis=-1, keepdims=True)
        attn_probs = (exp_terms / row_total).astype(jnp.bfloat16)
        attended = jnp.einsum(
            "hqk,khd->qhd", attn_probs, value_rows, preferred_element_type=jnp.float32
        )
        return (attended, row_max + jnp.log(row_total))

    attended, log_totals = lax.map(forward_block, starts)
    mixed_heads = attended.reshape(block_len, local_cols).astype(jnp.bfloat16)
    attn_total = lax.psum(
        jnp.dot(mixed_heads, attn_out_low, preferred_element_type=jnp.float32), "tp"
    )
    after_attn = residual + attn_total
    normed_two, norm_two_back = jax.vjp(rms_norm, after_attn, gain_two)
    normed_two = normed_two.astype(jnp.bfloat16)
    logits = jnp.dot(normed_two, router_low, preferred_element_type=jnp.float32)
    route_rows = routes[0]
    onehot = (route_rows[:, :, None] == jnp.arange(experts, dtype=jnp.int32)[None, None, :]).astype(
        jnp.float32
    )
    picked = jnp.sum(onehot * logits[:, None, :], axis=-1)
    gate_probs = jax.nn.softmax(picked, axis=-1)
    upstream = cotangent[0]
    grad_out = upstream.astype(jnp.float32)
    if dense_experts:
        weights = jnp.sum(gate_probs[:, :, None] * onehot, axis=1)
        combined, dots_e, grad_rows, grad_expert_in, grad_expert_down = experts_dense(
            normed_two, grad_out, weights, expert_in_all, expert_down_all
        )
        gate_dots = jnp.sum(onehot * dots_e[:, None, :], axis=-1)
    else:
        combined, gate_dots, grad_rows, grad_expert_in, grad_expert_down = experts_routed(
            normed_two,
            grad_out,
            route_rows,
            gate_probs,
            expert_in_low,
            expert_down_low,
            capacity,
        )
    shared_gate_up = jnp.einsum(
        "td,dgf->tgf", normed_two, shared_in_low, preferred_element_type=jnp.float32
    )
    shared_act, shared_act_back = jax.vjp(swiglu, shared_gate_up)
    shared_hidden = shared_act.astype(jnp.bfloat16)
    shared_out = jnp.dot(shared_hidden, shared_down_low, preferred_element_type=jnp.float32)
    grad_shared_hidden = jnp.einsum(
        "td,fd->tf", upstream, shared_down_low, preferred_element_type=jnp.float32
    )
    grad_shared_gate_up = shared_act_back(grad_shared_hidden)[0].astype(jnp.bfloat16)
    partial_two = (
        jnp.einsum(
            "tgf,dgf->td", grad_shared_gate_up, shared_in_low, preferred_element_type=jnp.float32
        )
        + grad_rows
    )
    branch_total, grad_normed_part, gate_total = lax.psum(
        (shared_out + combined, partial_two, gate_dots), "tp"
    )
    layer_out = after_attn + branch_total
    grad_picked = gate_probs * (
        gate_total - jnp.sum(gate_probs * gate_total, axis=-1, keepdims=True)
    )
    grad_logits = jnp.sum(grad_picked[:, :, None] * onehot, axis=1).astype(jnp.bfloat16)
    grad_shared_in = jnp.einsum(
        "td,tgf->dgf", normed_two, grad_shared_gate_up, preferred_element_type=jnp.float32
    )
    grad_shared_down = jnp.einsum(
        "tf,td->fd", shared_hidden, upstream, preferred_element_type=jnp.float32
    )
    grad_router = jnp.einsum(
        "td,te->de", normed_two, grad_logits, preferred_element_type=jnp.float32
    )
    grad_normed_two = grad_normed_part + jnp.einsum(
        "te,de->td", grad_logits, router_low, preferred_element_type=jnp.float32
    )
    grad_after, grad_gain_two = norm_two_back(grad_normed_two)
    grad_after = grad_after + grad_out
    grad_attn_low = grad_after.astype(jnp.bfloat16)
    grad_attn_out = jnp.einsum(
        "tc,td->cd", mixed_heads, grad_attn_low, preferred_element_type=jnp.float32
    )
    first_grads = [
        (grad_attn_out, 1),
        (grad_router, 0),
        (grad_shared_in, 0),
        (grad_shared_down, 1),
        (grad_gain_two, 0),
    ]
    if dense_experts:
        fe_local = expert_down.shape[1]
        first_grads += [
            (grad_expert_in.reshape(shard_count * expert_in.shape[1], 2, fe_local), 0),
            (
                grad_expert_down.reshape(experts, fe_local, ctx_count, model_width // ctx_count)
                .transpose(0, 2, 1, 3)
                .reshape(shard_count * fe_local, model_width // ctx_count),
                0,
            ),
        ]
    if not dense_experts:
        own_expert_in = lax.psum_scatter(grad_expert_in[None], "ctx", scatter_dimension=1, tiled=True)
        own_expert_down = lax.psum_scatter(
            grad_expert_down[None], "ctx", scatter_dimension=2, tiled=True
        )
    first_own = scatter_packed(first_grads, ("fsdp", "ctx"), shard_count)
    own_attn_out, own_router, own_shared_in, own_shared_down, own_gain_two = first_own[:5]
    if dense_experts:
        own_expert_in = first_own[5][None]
        own_expert_down = first_own[6][None]
    grad_heads = (
        jnp.einsum("td,cd->tc", grad_attn_low, attn_out_low, preferred_element_type=jnp.float32)
        .astype(jnp.bfloat16)
        .reshape(block_len, local_heads, HD)
    )

    def backward_block(block_number, running):
        grad_keys, grad_values, grad_queries = running
        start_row = block_number * block_rows
        query_rows, key_rows, value_rows, masked, allowed = block_view(
            queries, keys_ext, values_ext, seg_own, seg_ext, start_row, base_pos
        )
        log_total = lax.dynamic_index_in_dim(log_totals, block_number, 0, keepdims=False)
        attn_probs = jnp.where(allowed[None], jnp.exp(masked - log_total), 0.0)
        grad_block = lax.dynamic_slice_in_dim(grad_heads, start_row, block_rows, 0)
        grad_probs = jnp.einsum(
            "qhd,khd->hqk", grad_block, value_rows, preferred_element_type=jnp.float32
        )
        inner_sum = jnp.sum(attn_probs * grad_probs, axis=-1, keepdims=True)
        grad_scores = (attn_probs * (grad_probs - inner_sum)).astype(jnp.bfloat16)
        grad_query_rows = (
            jnp.einsum("hqk,khd->qhd", grad_scores, key_rows, preferred_element_type=jnp.float32)
            * 0.125
        )
        grad_key_rows = (
            jnp.einsum("hqk,qhd->khd", grad_scores, query_rows, preferred_element_type=jnp.float32)
            * 0.125
        )
        grad_value_rows = jnp.einsum(
            "hqk,qhd->khd",
            attn_probs.astype(jnp.bfloat16),
            grad_block,
            preferred_element_type=jnp.float32,
        )
        key_offset = start_row + block_len - WINDOW
        grad_keys = lax.dynamic_update_slice_in_dim(
            grad_keys,
            lax.dynamic_slice_in_dim(grad_keys, key_offset, block_rows + WINDOW, 0) + grad_key_rows,
            key_offset,
            0,
        )
        grad_values = lax.dynamic_update_slice_in_dim(
            grad_values,
            lax.dynamic_slice_in_dim(grad_values, key_offset, block_rows + WINDOW, 0)
            + grad_value_rows,
            key_offset,
            0,
        )
        grad_queries = lax.dynamic_update_slice_in_dim(grad_queries, grad_query_rows, start_row, 0)
        return (grad_keys, grad_values, grad_queries)

    zero_ext = jnp.zeros((2 * block_len, local_heads, HD), jnp.float32)
    zero_own = jnp.zeros((block_len, local_heads, HD), jnp.float32)
    grad_keys, grad_values, grad_queries = lax.fori_loop(
        0, block_total, backward_block, (zero_ext, zero_ext, zero_own)
    )
    rim_keys, rim_values = (
        from_behind(grad_keys[:block_len].astype(jnp.bfloat16), "ctx", -1).astype(jnp.float32),
        from_behind(grad_values[:block_len].astype(jnp.bfloat16), "ctx", -1).astype(jnp.float32),
    )
    grad_keys_own = grad_keys[block_len:] + rim_keys
    grad_values_own = grad_values[block_len:] + rim_values
    grad_query_raw = rotate(grad_queries, cosine, -sine_tab)
    grad_key_raw = rotate(grad_keys_own, cosine, -sine_tab)
    grad_projected = (
        jnp.stack([grad_query_raw, grad_key_raw, grad_values_own], axis=1)
        .reshape(block_len, 3, local_cols)
        .astype(jnp.bfloat16)
    )
    grad_attn_in = jnp.einsum(
        "td,tgf->dgf", normed_one, grad_projected, preferred_element_type=jnp.float32
    )
    partial_one = jnp.einsum(
        "tgf,dgf->td", grad_projected, attn_in_low, preferred_element_type=jnp.float32
    )
    grad_residual, grad_gain_one = norm_one_back(lax.psum(partial_one, "tp"))
    input_grad = grad_after + grad_residual
    own_attn_in, own_gain_one = scatter_packed(
        [(grad_attn_in, 0), (grad_gain_one, 0)], ("fsdp", "ctx"), shard_count
    )
    own_gains = jnp.stack([own_gain_one, own_gain_two])
    lead_tp = (tp_index == 0).astype(jnp.float32)
    first_shard = (shard_index == 0).astype(jnp.float32)
    first_ctx = (ctx_index == 0).astype(jnp.float32)
    d_local = gains.shape[1]
    ff_local = shared_down.shape[0]
    fe_local = expert_down.shape[1]
    d_quarter = expert_in.shape[1]
    square_attn_in = own_attn_in * own_attn_in + TINY_SQUARE
    square_attn_out = own_attn_out * own_attn_out + TINY_SQUARE
    square_shared_in = own_shared_in * own_shared_in + TINY_SQUARE
    square_shared_down = own_shared_down * own_shared_down + TINY_SQUARE
    square_expert_in = own_expert_in[0] * own_expert_in[0] + TINY_SQUARE
    square_expert_down = own_expert_down[0] * own_expert_down[0] + TINY_SQUARE
    model_part = lax.dynamic_update_slice(
        jnp.zeros((4, D), jnp.float32),
        jnp.stack(
            [
                jnp.sum(square_attn_in, axis=(1, 2)),
                jnp.sum(square_shared_in, axis=(1, 2)),
                jnp.sum(square_attn_out, axis=0),
                jnp.sum(square_shared_down, axis=0),
            ]
        ),
        (0, shard_index * d_local),
    )
    head_part = lax.dynamic_update_slice(
        jnp.zeros((4, HH), jnp.float32),
        jnp.concatenate(
            [jnp.sum(square_attn_in, axis=0), jnp.sum(square_attn_out, axis=1)[None]], axis=0
        ),
        (0, tp_index * local_cols),
    )
    hidden_part = lax.dynamic_update_slice(
        jnp.zeros((3, FF), jnp.float32),
        jnp.concatenate(
            [jnp.sum(square_shared_in, axis=0), jnp.sum(square_shared_down, axis=1)[None]], axis=0
        ),
        (0, tp_index * ff_local),
    )
    expert_model_part = lax.dynamic_update_slice(
        jnp.zeros((experts, 2, D), jnp.float32),
        jnp.stack([jnp.sum(square_expert_in, axis=(1, 2)), jnp.sum(square_expert_down, axis=0)])[
            None
        ],
        (fsdp_index, 0, ctx_index * d_quarter),
    )
    expert_hidden_part = lax.dynamic_update_slice(
        jnp.zeros((experts, 3, FE), jnp.float32),
        jnp.concatenate(
            [jnp.sum(square_expert_in, axis=0), jnp.sum(square_expert_down, axis=1)[None]], axis=0
        )[None],
        (fsdp_index, 0, tp_index * fe_local),
    )
    scalar_part = jnp.stack(
        [
            lead_tp * jnp.sum(gains * gains),
            jnp.sum(attention_in * attention_in),
            jnp.sum(attention_out * attention_out),
            lead_tp * jnp.sum(router_weight * router_weight),
            jnp.sum(shared_in * shared_in),
            jnp.sum(shared_down * shared_down),
            jnp.sum(expert_in * expert_in),
            jnp.sum(expert_down * expert_down),
            lead_tp * jnp.sum(model_stats[2]),
            first_shard * jnp.sum(head_stats[2]),
            lead_tp * jnp.sum(model_stats[3]),
            first_shard * jnp.sum(hidden_stats[2]),
        ]
    )
    expert_old_part = lax.dynamic_update_slice(
        jnp.zeros((2, experts), jnp.float32),
        jnp.stack(
            [
                lead_tp * jnp.sum(expert_model_stats[0, 0]),
                first_ctx * jnp.sum(expert_hidden_stats[0, 2]),
            ]
        )[:, None],
        (0, fsdp_index),
    )
    global_sums = butterfly_sum(
        [
            model_part,
            head_part,
            hidden_part,
            expert_model_part,
            expert_hidden_part,
            scalar_part,
            expert_old_part,
        ],
        1,
    )
    (
        model_sum,
        head_sum,
        hidden_sum,
        expert_model_sum,
        expert_hidden_sum,
        scalar_sum,
        expert_old_sum,
    ) = global_sums
    shard_start = shard_index * d_local
    gain_state = DECAY_RATE * model_stats[0:2] + (1.0 - DECAY_RATE) * (
        own_gains * own_gains + TINY_SQUARE
    )
    update_gains = own_gains * lax.rsqrt(gain_state)
    router_new = DECAY_RATE * router_state + (1.0 - DECAY_RATE) * (
        own_router * own_router + TINY_SQUARE
    )
    update_router = own_router * lax.rsqrt(router_new)
    attn_cols_old = jnp.concatenate([head_stats[0:2], value_columns[None]], axis=0).reshape(-1)
    update_attn_in, rows_attn_in, cols_attn_in = factored_update(
        own_attn_in.reshape(d_local, 3 * local_cols),
        model_stats[2],
        attn_cols_old,
        lax.dynamic_slice_in_dim(model_sum[0], shard_start, d_local),
        lax.dynamic_slice_in_dim(head_sum[0:3], tp_index * local_cols, local_cols, 1).reshape(-1),
        D,
        3 * HH,
        scalar_sum[8],
        jnp.sum(model_sum[0]),
    )
    update_attn_out, rows_attn_out, cols_attn_out = factored_update(
        own_attn_out,
        head_stats[2],
        model_stats[4],
        lax.dynamic_slice_in_dim(head_sum[3], tp_index * local_cols, local_cols),
        lax.dynamic_slice_in_dim(model_sum[2], shard_start, d_local),
        HH,
        D,
        scalar_sum[9],
        jnp.sum(head_sum[3]),
    )
    update_shared_in, rows_shared_in, cols_shared_in = factored_update(
        own_shared_in.reshape(d_local, 2 * ff_local),
        model_stats[3],
        hidden_stats[0:2].reshape(-1),
        lax.dynamic_slice_in_dim(model_sum[1], shard_start, d_local),
        lax.dynamic_slice_in_dim(hidden_sum[0:2], tp_index * ff_local, ff_local, 1).reshape(-1),
        D,
        2 * FF,
        scalar_sum[10],
        jnp.sum(model_sum[1]),
    )
    update_shared_down, rows_shared_down, cols_shared_down = factored_update(
        own_shared_down,
        hidden_stats[2],
        model_stats[5],
        lax.dynamic_slice_in_dim(hidden_sum[2], tp_index * ff_local, ff_local),
        lax.dynamic_slice_in_dim(model_sum[3], shard_start, d_local),
        FF,
        D,
        scalar_sum[11],
        jnp.sum(hidden_sum[2]),
    )
    own_expert_model = lax.dynamic_index_in_dim(expert_model_sum, fsdp_index, 0, keepdims=False)
    own_expert_hidden = lax.dynamic_index_in_dim(expert_hidden_sum, fsdp_index, 0, keepdims=False)
    old_expert_totals = lax.dynamic_index_in_dim(expert_old_sum, fsdp_index, 1, keepdims=False)
    update_expert_in, rows_expert_in, cols_expert_in = factored_update(
        own_expert_in[0].reshape(d_quarter, 2 * fe_local),
        expert_model_stats[0, 0],
        expert_hidden_stats[0, 0:2].reshape(-1),
        lax.dynamic_slice_in_dim(own_expert_model[0], ctx_index * d_quarter, d_quarter),
        lax.dynamic_slice_in_dim(own_expert_hidden[0:2], tp_index * fe_local, fe_local, 1).reshape(
            -1
        ),
        D,
        2 * FE,
        old_expert_totals[0],
        jnp.sum(own_expert_model[0]),
    )
    update_expert_down, rows_expert_down, cols_expert_down = factored_update(
        own_expert_down[0],
        expert_hidden_stats[0, 2],
        expert_model_stats[0, 1],
        lax.dynamic_slice_in_dim(own_expert_hidden[2], tp_index * fe_local, fe_local),
        lax.dynamic_slice_in_dim(own_expert_model[1], ctx_index * d_quarter, d_quarter),
        FE,
        D,
        old_expert_totals[1],
        jnp.sum(own_expert_hidden[2]),
    )
    clip_part = jnp.stack(
        [
            lead_tp * jnp.sum(update_gains * update_gains),
            jnp.sum(update_attn_in * update_attn_in),
            jnp.sum(update_attn_out * update_attn_out),
            lead_tp * jnp.sum(update_router * update_router),
            jnp.sum(update_shared_in * update_shared_in),
            jnp.sum(update_shared_down * update_shared_down),
            jnp.sum(update_expert_in * update_expert_in),
            jnp.sum(update_expert_down * update_expert_down),
        ]
    )
    clip_total = butterfly_sum([clip_part], 2)[0]
    elements = jnp.array(
        [
            2 * D,
            D * 3 * HH,
            HH * D,
            D * experts,
            D * 2 * FF,
            FF * D,
            experts * D * 2 * FE,
            experts * FE * D,
        ],
        jnp.float32,
    )
    update_roots = jnp.sqrt(clip_total / elements)
    new_gains = apply_update(gains, update_gains, update_roots[0], scalar_sum[0], elements[0])
    new_attn_in = apply_update(
        attention_in,
        update_attn_in.reshape(attention_in.shape),
        update_roots[1],
        scalar_sum[1],
        elements[1],
    )
    new_attn_out = apply_update(
        attention_out, update_attn_out, update_roots[2], scalar_sum[2], elements[2]
    )
    new_router = apply_update(
        router_weight, update_router, update_roots[3], scalar_sum[3], elements[3]
    )
    new_shared_in = apply_update(
        shared_in,
        update_shared_in.reshape(shared_in.shape),
        update_roots[4],
        scalar_sum[4],
        elements[4],
    )
    new_shared_down = apply_update(
        shared_down, update_shared_down, update_roots[5], scalar_sum[5], elements[5]
    )
    new_expert_in = apply_update(
        expert_in,
        update_expert_in.reshape(expert_in.shape),
        update_roots[6],
        scalar_sum[6],
        elements[6],
    )
    new_expert_down = apply_update(
        expert_down,
        update_expert_down.reshape(expert_down.shape),
        update_roots[7],
        scalar_sum[7],
        elements[7],
    )
    new_model_stats = jnp.concatenate(
        [gain_state, jnp.stack([rows_attn_in, rows_shared_in, cols_attn_out, cols_shared_down])],
        axis=0,
    )
    attn_cols_new = cols_attn_in.reshape(3, local_cols)
    new_head_stats = jnp.concatenate([attn_cols_new[0:2], rows_attn_out[None]], axis=0)
    new_value_columns = attn_cols_new[2]
    new_hidden_stats = jnp.concatenate(
        [cols_shared_in.reshape(2, ff_local), rows_shared_down[None]], axis=0
    )
    new_expert_model_stats = jnp.stack([rows_expert_in, cols_expert_down])[None]
    new_expert_hidden_stats = jnp.concatenate(
        [cols_expert_in.reshape(2, fe_local), rows_expert_down[None]], axis=0
    )[None]
    return (
        layer_out.astype(jnp.bfloat16)[None],
        input_grad[None],
        own_gains,
        own_attn_in,
        own_attn_out,
        own_router,
        own_shared_in,
        own_shared_down,
        own_expert_in,
        own_expert_down,
        new_gains,
        new_attn_in,
        new_attn_out,
        new_router,
        new_shared_in,
        new_shared_down,
        new_expert_in,
        new_expert_down,
        new_model_stats,
        new_head_stats,
        new_value_columns,
        new_hidden_stats,
        router_new,
        new_expert_model_stats,
        new_expert_hidden_stats,
        update_roots,
    )


def solution(mesh):
    in_specs = (
        P("fsdp", "ctx", None),
        P("fsdp", "ctx"),
        P("fsdp", "ctx", None),
        P("fsdp", "ctx", None),
        P(None, ("fsdp", "ctx")),
        P(("fsdp", "ctx"), None, "tp"),
        P("tp", ("fsdp", "ctx")),
        P(("fsdp", "ctx"), None),
        P(("fsdp", "ctx"), None, "tp"),
        P("tp", ("fsdp", "ctx")),
        P("fsdp", "ctx", None, "tp"),
        P("fsdp", "tp", "ctx"),
        P(None, ("fsdp", "ctx")),
        P(None, "tp"),
        P("tp"),
        P(None, "tp"),
        P(("fsdp", "ctx"), None),
        P("fsdp", None, "ctx"),
        P("fsdp", None, "tp"),
    )
    out_specs = (
        P("fsdp", "ctx", None),
        P("fsdp", "ctx", None),
        P(None, ("fsdp", "ctx")),
        P(("fsdp", "ctx"), None, "tp"),
        P("tp", ("fsdp", "ctx")),
        P(("fsdp", "ctx"), None),
        P(("fsdp", "ctx"), None, "tp"),
        P("tp", ("fsdp", "ctx")),
        P("fsdp", "ctx", None, "tp"),
        P("fsdp", "tp", "ctx"),
        P(None, ("fsdp", "ctx")),
        P(("fsdp", "ctx"), None, "tp"),
        P("tp", ("fsdp", "ctx")),
        P(("fsdp", "ctx"), None),
        P(("fsdp", "ctx"), None, "tp"),
        P("tp", ("fsdp", "ctx")),
        P("fsdp", "ctx", None, "tp"),
        P("fsdp", "tp", "ctx"),
        P(None, ("fsdp", "ctx")),
        P(None, "tp"),
        P("tp"),
        P(None, "tp"),
        P(("fsdp", "ctx"), None),
        P("fsdp", None, "ctx"),
        P("fsdp", None, "tp"),
        P(),
    )
    return jax.shard_map(local, mesh=mesh, in_specs=in_specs, out_specs=out_specs, check_vma=False)
```

```python
import jax
import jax.numpy as jnp
from jax import lax
from jax.sharding import PartitionSpec as P
from jax.experimental import pallas as pl
from jax.experimental.pallas import tpu as pltpu

D = 768
HD = 64
FF = 2048
FE = 2048
WINDOW = 1024
HH = 768


EPSILON = 1e-06
TINY_SQUARE = 1e-30
SCALE_FLOOR = 0.001
DECAY_RATE = 0.5
CLIP_LIMIT = 0.5
STEP_RATE = 0.5


def from_behind(value, axis, steps):
    count = lax.axis_size(axis)
    leading, last = (max(0, -steps), min(count, count - steps))
    return lax.ppermute(value, axis, [(source, source + steps) for source in range(leading, last)])


def rms_norm(values, gain_vec):
    inv_rms = lax.rsqrt(jnp.mean(values * values, axis=-1, keepdims=True) + EPSILON)
    return values * inv_rms * gain_vec


def swiglu(gate_up):
    return jax.nn.silu(gate_up[:, 0]) * gate_up[:, 1]


def rotate(values, cosine, sine_tab):
    half_dim = values.shape[-1] // 2
    first_half = values[..., :half_dim]
    second_half = values[..., half_dim:]
    cos_b = cosine[:, None, :]
    sin_b = sine_tab[:, None, :]
    return jnp.concatenate(
        [first_half * cos_b - second_half * sin_b, second_half * cos_b + first_half * sin_b],
        axis=-1,
    )


def slot_tables(block_routes, experts, capacity):
    flat_routes = block_routes.reshape(-1)
    route_count = flat_routes.shape[0]
    onehot = (flat_routes[:, None] == jnp.arange(experts, dtype=jnp.int32)[None, :]).astype(
        jnp.int32
    )
    rank_in = jnp.sum(
        (jnp.cumsum(onehot, axis=0, dtype=jnp.int32) - 1) * onehot, axis=1, dtype=jnp.int32
    )
    slot_index = flat_routes * capacity + rank_in
    owner_route = (
        jnp.zeros((experts * capacity,), jnp.int32)
        .at[slot_index]
        .set(jnp.arange(route_count, dtype=jnp.int32))
    )
    filled = jnp.zeros((experts * capacity,), jnp.int32).at[slot_index].set(1)
    return (slot_index, owner_route, filled)


def block_view(queries, keys_ext, values_ext, seg_own, seg_ext, start_row, base_pos):
    block_len = queries.shape[0]
    block_rows = min(512, block_len)
    query_rows = lax.dynamic_slice_in_dim(queries, start_row, block_rows, 0)
    key_rows = lax.dynamic_slice_in_dim(
        keys_ext, start_row + block_len - WINDOW, block_rows + WINDOW, 0
    )
    value_rows = lax.dynamic_slice_in_dim(
        values_ext, start_row + block_len - WINDOW, block_rows + WINDOW, 0
    )
    scores = (
        jnp.einsum("qhd,khd->hqk", query_rows, key_rows, preferred_element_type=jnp.float32) * 0.125
    )
    query_pos = start_row + jnp.arange(block_rows, dtype=jnp.int32)
    key_pos = start_row - WINDOW + jnp.arange(block_rows + WINDOW, dtype=jnp.int32)
    distance = query_pos[:, None] - key_pos[None, :]
    seg_query = lax.dynamic_slice_in_dim(seg_own, start_row, block_rows, 0)
    seg_key = lax.dynamic_slice_in_dim(
        seg_ext, start_row + block_len - WINDOW, block_rows + WINDOW, 0
    )
    allowed = (
        (distance >= 0)
        & (distance < WINDOW)
        & (seg_query[:, None] == seg_key[None, :])
        & (key_pos[None, :] + base_pos >= 0)
    )
    return (query_rows, key_rows, value_rows, jnp.where(allowed[None], scores, -1e30), allowed)


def factored_update(
    grad_mat, rows_old, cols_old, row_sums, col_sums, row_total, col_total, old_total, square_total
):
    rows_new = DECAY_RATE * rows_old + (1.0 - DECAY_RATE) * row_sums / col_total
    cols_new = DECAY_RATE * cols_old + (1.0 - DECAY_RATE) * col_sums / row_total
    mean_rows = (DECAY_RATE * old_total + (1.0 - DECAY_RATE) * square_total / col_total) / row_total
    second_moment = rows_new[:, None] * cols_new[None, :] / mean_rows
    return (grad_mat * lax.rsqrt(second_moment), rows_new, cols_new)


def apply_update(weight, update, update_root, square_sum, elements):
    param_scale = jnp.maximum(SCALE_FLOOR, jnp.sqrt(square_sum / elements))
    return weight - STEP_RATE * param_scale * update / jnp.maximum(1.0, update_root / CLIP_LIMIT)


def butterfly_partners():
    partners = []
    here = [lax.axis_index(name) for name in ("fsdp", "ctx", "tp")]
    for axis_number, name in enumerate(("fsdp", "ctx", "tp")):
        size = lax.axis_size(name)
        step = 1
        while step < size:
            bit = (here[axis_number] // step) % 2
            other = list(here)
            other[axis_number] = here[axis_number] + step * (1 - 2 * bit)
            partners.append(tuple(other))
            step *= 2
    return partners


def butterfly_kernel(x_ref, o_ref, stage, inbox, send_sems, recv_sems):
    partners = butterfly_partners()
    barrier = pltpu.get_barrier_semaphore()
    for partner in partners:
        pl.semaphore_signal(
            barrier, 1, device_id=partner, device_id_type=pl.DeviceIdType.MESH
        )
    pl.semaphore_wait(barrier, len(partners))
    acc = x_ref[...]
    for round_number, partner in enumerate(partners):
        stage[round_number] = acc
        copy = pltpu.make_async_remote_copy(
            src_ref=stage.at[round_number],
            dst_ref=inbox.at[round_number],
            send_sem=send_sems.at[round_number],
            recv_sem=recv_sems.at[round_number],
            device_id=partner,
            device_id_type=pl.DeviceIdType.MESH,
        )
        copy.start()
        copy.wait()
        acc = stage[round_number] + inbox[round_number]
    o_ref[...] = acc


def butterfly_sum(values, collective_id):
    flat = jnp.concatenate([v.reshape(-1).astype(jnp.float32) for v in values])
    size = flat.shape[0]
    rows = -(-size // 1024) * 8
    block = jnp.pad(flat, (0, rows * 128 - size)).reshape(rows, 128)
    rounds = sum(
        max(1, lax.axis_size(name)).bit_length() - 1 for name in ("fsdp", "ctx", "tp")
    )
    total = pl.pallas_call(
        butterfly_kernel,
        out_shape=jax.ShapeDtypeStruct((rows, 128), jnp.float32),
        in_specs=[pl.BlockSpec(memory_space=pltpu.VMEM)],
        out_specs=pl.BlockSpec(memory_space=pltpu.VMEM),
        scratch_shapes=[
            pltpu.VMEM((rounds, rows, 128), jnp.float32),
            pltpu.VMEM((rounds, rows, 128), jnp.float32),
            pltpu.SemaphoreType.DMA((rounds,)),
            pltpu.SemaphoreType.DMA((rounds,)),
        ],
        compiler_params=pltpu.CompilerParams(collective_id=collective_id, has_side_effects=True),
    )(block).reshape(-1)
    results = []
    offset = 0
    for v in values:
        results.append(total[offset : offset + v.size].reshape(v.shape))
        offset += v.size
    return results


def swiglu_experts(gate_up):
    return jax.nn.silu(gate_up[:, :, 0]) * gate_up[:, :, 1]


def gather_packed(pieces, axes):
    flat = jnp.concatenate([piece.reshape(-1) for piece, _ in pieces])
    full = lax.all_gather(flat, axes, axis=0, tiled=False)
    count = full.shape[0]
    results = []
    offset = 0
    for piece, dim in pieces:
        size = piece.size
        part = full[:, offset : offset + size].reshape((count,) + piece.shape)
        offset += size
        part = jnp.moveaxis(part, 0, dim)
        shape = list(piece.shape)
        shape[dim] *= count
        results.append(part.reshape(shape))
    return results


def scatter_packed(pieces, axes, count):
    columns = []
    local_shapes = []
    for grad, dim in pieces:
        shape = grad.shape
        split = shape[:dim] + (count, shape[dim] // count) + shape[dim + 1 :]
        local_shapes.append(shape[:dim] + (shape[dim] // count,) + shape[dim + 1 :])
        part = jnp.moveaxis(grad.reshape(split), dim, 0)
        columns.append(part.reshape(count, -1))
    packed = jnp.concatenate(columns, axis=1)
    width = packed.shape[1]
    rows = -(-width // 1024) * 8
    packed = jnp.pad(packed, ((0, 0), (0, rows * 128 - width))).reshape(count * rows, 128)
    own = lax.psum_scatter(packed, axes, scatter_dimension=0, tiled=True).reshape(-1)
    results = []
    offset = 0
    for local_shape in local_shapes:
        size = 1
        for extent in local_shape:
            size *= extent
        results.append(own[offset : offset + size].reshape(local_shape))
        offset += size
    return results


def experts_dense(normed_two, grad_out, weights, expert_in_all, expert_down_all):
    gate_up = jnp.einsum(
        "td,edgf->etgf", normed_two, expert_in_all, preferred_element_type=jnp.float32
    )
    act, act_back = jax.vjp(swiglu_experts, gate_up)
    hidden = act.astype(jnp.bfloat16)
    outs = jnp.einsum("etf,efd->etd", hidden, expert_down_all, preferred_element_type=jnp.float32)
    weights_e = weights.T[:, :, None]
    combined = jnp.sum(weights_e * outs, axis=0)
    gate_dots = jnp.sum(outs * grad_out[None], axis=-1).T
    grad_outs = (weights_e * grad_out[None]).astype(jnp.bfloat16)
    grad_hidden = jnp.einsum(
        "etd,efd->etf", grad_outs, expert_down_all, preferred_element_type=jnp.float32
    )
    grad_gate_up = act_back(grad_hidden)[0].astype(jnp.bfloat16)
    grad_down = jnp.einsum("etf,etd->efd", hidden, grad_outs, preferred_element_type=jnp.float32)
    grad_in = jnp.einsum(
        "td,etgf->edgf", normed_two, grad_gate_up, preferred_element_type=jnp.float32
    )
    grad_rows = jnp.einsum(
        "etgf,edgf->td", grad_gate_up, expert_in_all, preferred_element_type=jnp.float32
    )
    return combined, gate_dots, grad_rows, grad_in, grad_down


def experts_routed(
    normed_two, grad_out, route_rows, gate_probs, expert_in_low, expert_down_low, capacity
):
    block_len, model_width = normed_two.shape
    experts = lax.axis_size("fsdp")
    slot_index, owner_route, filled = slot_tables(route_rows, experts, capacity)
    fill_mask = filled.astype(jnp.bfloat16)[:, None]
    route_grads = (
        (gate_probs[:, :, None] * grad_out[:, None, :])
        .astype(jnp.bfloat16)
        .reshape(2 * block_len, model_width)
    )
    send_rows = jnp.concatenate(
        [normed_two[owner_route // 2] * fill_mask, route_grads[owner_route] * fill_mask], axis=1
    ).reshape(experts, capacity, 2 * model_width)
    exchange = lambda rows: lax.all_to_all(rows, "fsdp", split_axis=0, concat_axis=0, tiled=True)
    pair_count = lax.axis_size("tp")
    swap = lambda rows: lax.ppermute(
        rows, "tp", [(index, index + 1 - 2 * (index % 2)) for index in range(pair_count)]
    )
    half = capacity // 2
    side = lax.axis_index("tp") % 2
    mine = exchange(lax.dynamic_slice_in_dim(send_rows, side * half, half, 1))
    received_both = jnp.concatenate([mine, swap(mine)], axis=1).reshape(
        experts * capacity, 2 * model_width
    )
    received = received_both[:, :model_width]
    grad_received = received_both[:, model_width:]
    gate_up = jnp.einsum("rd,dgf->rgf", received, expert_in_low, preferred_element_type=jnp.float32)
    act, act_back = jax.vjp(swiglu, gate_up)
    hidden = act.astype(jnp.bfloat16)
    outs = jnp.dot(hidden, expert_down_low, preferred_element_type=jnp.float32)
    grad_hidden = jnp.einsum(
        "rd,fd->rf", grad_received, expert_down_low, preferred_element_type=jnp.float32
    )
    grad_gate_up = act_back(grad_hidden)[0].astype(jnp.bfloat16)
    grad_in = jnp.einsum("rd,rgf->dgf", received, grad_gate_up, preferred_element_type=jnp.float32)
    grad_down = jnp.einsum("rf,rd->fd", hidden, grad_received, preferred_element_type=jnp.float32)
    grad_expert_rows = jnp.einsum(
        "rgf,dgf->rd", grad_gate_up, expert_in_low, preferred_element_type=jnp.float32
    )
    results = jnp.concatenate([outs, grad_expert_rows], axis=1).reshape(
        experts, capacity, 2 * model_width
    )
    pair_sum = results[:, :half] + swap(results[:, half:])
    held = exchange(pair_sum.astype(jnp.bfloat16)).reshape(experts * half, 2 * model_width)
    slot_expert = slot_index // capacity
    slot_rank = slot_index % capacity
    in_side = (slot_rank // half) == side
    local_slot = slot_expert * half + slot_rank % half
    returned = jnp.where(in_side[:, None], held[local_slot].astype(jnp.float32), 0.0)
    route_out = returned[:, :model_width].reshape(block_len, 2, model_width)
    grad_routes = returned[:, model_width:].reshape(block_len, 2, model_width)
    combined = jnp.sum(gate_probs[:, :, None] * route_out, axis=1)
    gate_dots = jnp.sum(grad_out[:, None, :] * route_out, axis=-1)
    grad_rows = jnp.sum(grad_routes, axis=1)
    return combined, gate_dots, grad_rows, grad_in, grad_down


def local(
    layer_input,
    segments,
    routes,
    cotangent,
    gains,
    attention_in,
    attention_out,
    router_weight,
    shared_in,
    shared_down,
    expert_in,
    expert_down,
    model_stats,
    head_stats,
    value_columns,
    hidden_stats,
    router_state,
    expert_model_stats,
    expert_hidden_stats,
):
    block_len = layer_input.shape[1]
    model_width = layer_input.shape[2]
    experts = router_weight.shape[1]
    dense_experts = False
    capacity = min(block_len, 4 * block_len // experts)
    ctx_index = lax.axis_index("ctx")
    tp_index = lax.axis_index("tp")
    fsdp_index = lax.axis_index("fsdp")
    shard_index = lax.axis_index(("fsdp", "ctx"))
    shard_count = lax.axis_size(("fsdp", "ctx"))
    ctx_count = lax.axis_size("ctx")
    base_pos = ctx_index * block_len
    low = lambda v: v.astype(jnp.bfloat16)
    gain_low, attn_in_low = gather_packed(
        [(low(gains), 1), (low(attention_in), 0)], ("fsdp", "ctx")
    )
    later = [
        (low(attention_out), 1),
        (low(router_weight), 0),
        (low(shared_in), 0),
        (low(shared_down), 1),
    ]
    if dense_experts:
        later += [(low(expert_in), 0), (low(expert_down), 0)]
    later_full = gather_packed(later, ("fsdp", "ctx"))
    attn_out_low, router_low, shared_in_low, shared_down_low = later_full[:4]
    if dense_experts:
        fe_local = expert_down.shape[1]
        expert_in_all = later_full[4].reshape(experts, model_width, 2, fe_local)
        expert_down_all = (
            later_full[5]
            .reshape(experts, ctx_count, fe_local, model_width // ctx_count)
            .transpose(0, 2, 1, 3)
            .reshape(experts, fe_local, model_width)
        )
    else:
        expert_in_low = lax.all_gather(low(expert_in), "ctx", axis=1, tiled=True)[0]
        expert_down_low = lax.all_gather(low(expert_down), "ctx", axis=2, tiled=True)[0]
    residual = layer_input[0].astype(jnp.float32)
    gain_one = gain_low[0].astype(jnp.float32)
    gain_two = gain_low[1].astype(jnp.float32)
    normed_one, norm_one_back = jax.vjp(rms_norm, residual, gain_one)
    normed_one = normed_one.astype(jnp.bfloat16)
    projected = jnp.einsum(
        "td,dgf->tgf", normed_one, attn_in_low, preferred_element_type=jnp.float32
    )
    local_cols = projected.shape[2]
    local_heads = local_cols // HD
    half_dim = HD // 2
    frequency = 10000.0 ** (-jnp.arange(half_dim, dtype=jnp.float32) / half_dim)
    angles = (base_pos + jnp.arange(block_len, dtype=jnp.int32)).astype(jnp.float32)[
        :, None
    ] * frequency[None, :]
    cosine = jnp.cos(angles)
    sine_tab = jnp.sin(angles)
    queries = rotate(projected[:, 0].reshape(block_len, local_heads, HD), cosine, sine_tab).astype(
        jnp.bfloat16
    )
    keys_own = rotate(projected[:, 1].reshape(block_len, local_heads, HD), cosine, sine_tab).astype(
        jnp.bfloat16
    )
    values_own = projected[:, 2].reshape(block_len, local_heads, HD).astype(jnp.bfloat16)
    seg_own = segments[0].astype(jnp.bfloat16)
    keys_prev, values_prev, seg_prev = from_behind((keys_own, values_own, seg_own), "ctx", 1)
    keys_ext = jnp.concatenate([keys_prev, keys_own], axis=0)
    values_ext = jnp.concatenate([values_prev, values_own], axis=0)
    seg_ext = jnp.concatenate([seg_prev, seg_own], axis=0)
    block_rows = min(512, block_len)
    block_total = block_len // block_rows
    starts = jnp.arange(block_total, dtype=jnp.int32) * block_rows

    def forward_block(start_row):
        query_rows, key_rows, value_rows, masked, allowed = block_view(
            queries, keys_ext, values_ext, seg_own, seg_ext, start_row, base_pos
        )
        row_max = jnp.max(masked, axis=-1, keepdims=True)
        exp_terms = jnp.where(allowed[None], jnp.exp(masked - row_max), 0.0)
        row_total = jnp.sum(exp_terms, axis=-1, keepdims=True)
        attn_probs = (exp_terms / row_total).astype(jnp.bfloat16)
        attended = jnp.einsum(
            "hqk,khd->qhd", attn_probs, value_rows, preferred_element_type=jnp.float32
        )
        return (attended, row_max + jnp.log(row_total))

    attended, log_totals = lax.map(forward_block, starts)
    mixed_heads = attended.reshape(block_len, local_cols).astype(jnp.bfloat16)
    attn_total = lax.psum(
        jnp.dot(mixed_heads, attn_out_low, preferred_element_type=jnp.float32), "tp"
    )
    after_attn = residual + attn_total
    normed_two, norm_two_back = jax.vjp(rms_norm, after_attn, gain_two)
    normed_two = normed_two.astype(jnp.bfloat16)
    logits = jnp.dot(normed_two, router_low, preferred_element_type=jnp.float32)
    route_rows = routes[0]
    onehot = (route_rows[:, :, None] == jnp.arange(experts, dtype=jnp.int32)[None, None, :]).astype(
        jnp.float32
    )
    picked = jnp.sum(onehot * logits[:, None, :], axis=-1)
    gate_probs = jax.nn.softmax(picked, axis=-1)
    upstream = cotangent[0]
    grad_out = upstream.astype(jnp.float32)
    if dense_experts:
        weights = jnp.sum(gate_probs[:, :, None] * onehot, axis=1)
        combined, dots_e, grad_rows, grad_expert_in, grad_expert_down = experts_dense(
            normed_two, grad_out, weights, expert_in_all, expert_down_all
        )
        gate_dots = jnp.sum(onehot * dots_e[:, None, :], axis=-1)
    else:
        combined, gate_dots, grad_rows, grad_expert_in, grad_expert_down = experts_routed(
            normed_two,
            grad_out,
            route_rows,
            gate_probs,
            expert_in_low,
            expert_down_low,
            capacity,
        )
    shared_gate_up = jnp.einsum(
        "td,dgf->tgf", normed_two, shared_in_low, preferred_element_type=jnp.float32
    )
    shared_act, shared_act_back = jax.vjp(swiglu, shared_gate_up)
    shared_hidden = shared_act.astype(jnp.bfloat16)
    shared_out = jnp.dot(shared_hidden, shared_down_low, preferred_element_type=jnp.float32)
    grad_shared_hidden = jnp.einsum(
        "td,fd->tf", upstream, shared_down_low, preferred_element_type=jnp.float32
    )
    grad_shared_gate_up = shared_act_back(grad_shared_hidden)[0].astype(jnp.bfloat16)
    partial_two = (
        jnp.einsum(
            "tgf,dgf->td", grad_shared_gate_up, shared_in_low, preferred_element_type=jnp.float32
        )
        + grad_rows
    )
    branch_total, grad_normed_part, gate_total = lax.psum(
        (shared_out + combined, partial_two, gate_dots), "tp"
    )
    layer_out = after_attn + branch_total
    grad_picked = gate_probs * (
        gate_total - jnp.sum(gate_probs * gate_total, axis=-1, keepdims=True)
    )
    grad_logits = jnp.sum(grad_picked[:, :, None] * onehot, axis=1).astype(jnp.bfloat16)
    grad_shared_in = jnp.einsum(
        "td,tgf->dgf", normed_two, grad_shared_gate_up, preferred_element_type=jnp.float32
    )
    grad_shared_down = jnp.einsum(
        "tf,td->fd", shared_hidden, upstream, preferred_element_type=jnp.float32
    )
    grad_router = jnp.einsum(
        "td,te->de", normed_two, grad_logits, preferred_element_type=jnp.float32
    )
    grad_normed_two = grad_normed_part + jnp.einsum(
        "te,de->td", grad_logits, router_low, preferred_element_type=jnp.float32
    )
    grad_after, grad_gain_two = norm_two_back(grad_normed_two)
    grad_after = grad_after + grad_out
    grad_attn_low = grad_after.astype(jnp.bfloat16)
    grad_attn_out = jnp.einsum(
        "tc,td->cd", mixed_heads, grad_attn_low, preferred_element_type=jnp.float32
    )
    first_grads = [
        (grad_attn_out, 1),
        (grad_router, 0),
        (grad_shared_in, 0),
        (grad_shared_down, 1),
        (grad_gain_two, 0),
    ]
    if dense_experts:
        fe_local = expert_down.shape[1]
        first_grads += [
            (grad_expert_in.reshape(shard_count * expert_in.shape[1], 2, fe_local), 0),
            (
                grad_expert_down.reshape(experts, fe_local, ctx_count, model_width // ctx_count)
                .transpose(0, 2, 1, 3)
                .reshape(shard_count * fe_local, model_width // ctx_count),
                0,
            ),
        ]
    if not dense_experts:
        own_expert_in = lax.psum_scatter(grad_expert_in[None], "ctx", scatter_dimension=1, tiled=True)
        own_expert_down = lax.psum_scatter(
            grad_expert_down[None], "ctx", scatter_dimension=2, tiled=True
        )
    first_own = scatter_packed(first_grads, ("fsdp", "ctx"), shard_count)
    own_attn_out, own_router, own_shared_in, own_shared_down, own_gain_two = first_own[:5]
    if dense_experts:
        own_expert_in = first_own[5][None]
        own_expert_down = first_own[6][None]
    grad_heads = (
        jnp.einsum("td,cd->tc", grad_attn_low, attn_out_low, preferred_element_type=jnp.float32)
        .astype(jnp.bfloat16)
        .reshape(block_len, local_heads, HD)
    )

    def backward_block(block_number, running):
        grad_keys, grad_values, grad_queries = running
        start_row = block_number * block_rows
        query_rows, key_rows, value_rows, masked, allowed = block_view(
            queries, keys_ext, values_ext, seg_own, seg_ext, start_row, base_pos
        )
        log_total = lax.dynamic_index_in_dim(log_totals, block_number, 0, keepdims=False)
        attn_probs = jnp.where(allowed[None], jnp.exp(masked - log_total), 0.0)
        grad_block = lax.dynamic_slice_in_dim(grad_heads, start_row, block_rows, 0)
        grad_probs = jnp.einsum(
            "qhd,khd->hqk", grad_block, value_rows, preferred_element_type=jnp.float32
        )
        inner_sum = jnp.sum(attn_probs * grad_probs, axis=-1, keepdims=True)
        grad_scores = (attn_probs * (grad_probs - inner_sum)).astype(jnp.bfloat16)
        grad_query_rows = (
            jnp.einsum("hqk,khd->qhd", grad_scores, key_rows, preferred_element_type=jnp.float32)
            * 0.125
        )
        grad_key_rows = (
            jnp.einsum("hqk,qhd->khd", grad_scores, query_rows, preferred_element_type=jnp.float32)
            * 0.125
        )
        grad_value_rows = jnp.einsum(
            "hqk,qhd->khd",
            attn_probs.astype(jnp.bfloat16),
            grad_block,
            preferred_element_type=jnp.float32,
        )
        key_offset = start_row + block_len - WINDOW
        grad_keys = lax.dynamic_update_slice_in_dim(
            grad_keys,
            lax.dynamic_slice_in_dim(grad_keys, key_offset, block_rows + WINDOW, 0) + grad_key_rows,
            key_offset,
            0,
        )
        grad_values = lax.dynamic_update_slice_in_dim(
            grad_values,
            lax.dynamic_slice_in_dim(grad_values, key_offset, block_rows + WINDOW, 0)
            + grad_value_rows,
            key_offset,
            0,
        )
        grad_queries = lax.dynamic_update_slice_in_dim(grad_queries, grad_query_rows, start_row, 0)
        return (grad_keys, grad_values, grad_queries)

    zero_ext = jnp.zeros((2 * block_len, local_heads, HD), jnp.float32)
    zero_own = jnp.zeros((block_len, local_heads, HD), jnp.float32)
    grad_keys, grad_values, grad_queries = lax.fori_loop(
        0, block_total, backward_block, (zero_ext, zero_ext, zero_own)
    )
    rim_keys, rim_values = (
        from_behind(grad_keys[:block_len].astype(jnp.bfloat16), "ctx", -1).astype(jnp.float32),
        from_behind(grad_values[:block_len].astype(jnp.bfloat16), "ctx", -1).astype(jnp.float32),
    )
    grad_keys_own = grad_keys[block_len:] + rim_keys
    grad_values_own = grad_values[block_len:] + rim_values
    grad_query_raw = rotate(grad_queries, cosine, -sine_tab)
    grad_key_raw = rotate(grad_keys_own, cosine, -sine_tab)
    grad_projected = (
        jnp.stack([grad_query_raw, grad_key_raw, grad_values_own], axis=1)
        .reshape(block_len, 3, local_cols)
        .astype(jnp.bfloat16)
    )
    grad_attn_in = jnp.einsum(
        "td,tgf->dgf", normed_one, grad_projected, preferred_element_type=jnp.float32
    )
    partial_one = jnp.einsum(
        "tgf,dgf->td", grad_projected, attn_in_low, preferred_element_type=jnp.float32
    )
    grad_residual, grad_gain_one = norm_one_back(lax.psum(partial_one, "tp"))
    input_grad = grad_after + grad_residual
    own_attn_in, own_gain_one = scatter_packed(
        [(grad_attn_in, 0), (grad_gain_one, 0)], ("fsdp", "ctx"), shard_count
    )
    own_gains = jnp.stack([own_gain_one, own_gain_two])
    lead_tp = (tp_index == 0).astype(jnp.float32)
    first_shard = (shard_index == 0).astype(jnp.float32)
    first_ctx = (ctx_index == 0).astype(jnp.float32)
    d_local = gains.shape[1]
    ff_local = shared_down.shape[0]
    fe_local = expert_down.shape[1]
    d_quarter = expert_in.shape[1]
    square_attn_in = own_attn_in * own_attn_in + TINY_SQUARE
    square_attn_out = own_attn_out * own_attn_out + TINY_SQUARE
    square_shared_in = own_shared_in * own_shared_in + TINY_SQUARE
    square_shared_down = own_shared_down * own_shared_down + TINY_SQUARE
    square_expert_in = own_expert_in[0] * own_expert_in[0] + TINY_SQUARE
    square_expert_down = own_expert_down[0] * own_expert_down[0] + TINY_SQUARE
    model_part = lax.dynamic_update_slice(
        jnp.zeros((4, D), jnp.float32),
        jnp.stack(
            [
                jnp.sum(square_attn_in, axis=(1, 2)),
                jnp.sum(square_shared_in, axis=(1, 2)),
                jnp.sum(square_attn_out, axis=0),
                jnp.sum(square_shared_down, axis=0),
            ]
        ),
        (0, shard_index * d_local),
    )
    head_part = lax.dynamic_update_slice(
        jnp.zeros((4, HH), jnp.float32),
        jnp.concatenate(
            [jnp.sum(square_attn_in, axis=0), jnp.sum(square_attn_out, axis=1)[None]], axis=0
        ),
        (0, tp_index * local_cols),
    )
    hidden_part = lax.dynamic_update_slice(
        jnp.zeros((3, FF), jnp.float32),
        jnp.concatenate(
            [jnp.sum(square_shared_in, axis=0), jnp.sum(square_shared_down, axis=1)[None]], axis=0
        ),
        (0, tp_index * ff_local),
    )
    expert_model_part = lax.dynamic_update_slice(
        jnp.zeros((experts, 2, D), jnp.float32),
        jnp.stack([jnp.sum(square_expert_in, axis=(1, 2)), jnp.sum(square_expert_down, axis=0)])[
            None
        ],
        (fsdp_index, 0, ctx_index * d_quarter),
    )
    expert_hidden_part = lax.dynamic_update_slice(
        jnp.zeros((experts, 3, FE), jnp.float32),
        jnp.concatenate(
            [jnp.sum(square_expert_in, axis=0), jnp.sum(square_expert_down, axis=1)[None]], axis=0
        )[None],
        (fsdp_index, 0, tp_index * fe_local),
    )
    scalar_part = jnp.stack(
        [
            lead_tp * jnp.sum(gains * gains),
            jnp.sum(attention_in * attention_in),
            jnp.sum(attention_out * attention_out),
            lead_tp * jnp.sum(router_weight * router_weight),
            jnp.sum(shared_in * shared_in),
            jnp.sum(shared_down * shared_down),
            jnp.sum(expert_in * expert_in),
            jnp.sum(expert_down * expert_down),
            lead_tp * jnp.sum(model_stats[2]),
            first_shard * jnp.sum(head_stats[2]),
            lead_tp * jnp.sum(model_stats[3]),
            first_shard * jnp.sum(hidden_stats[2]),
        ]
    )
    expert_old_part = lax.dynamic_update_slice(
        jnp.zeros((2, experts), jnp.float32),
        jnp.stack(
            [
                lead_tp * jnp.sum(expert_model_stats[0, 0]),
                first_ctx * jnp.sum(expert_hidden_stats[0, 2]),
            ]
        )[:, None],
        (0, fsdp_index),
    )
    global_sums = butterfly_sum(
        [
            model_part,
            head_part,
            hidden_part,
            expert_model_part,
            expert_hidden_part,
            scalar_part,
            expert_old_part,
        ],
        1,
    )
    (
        model_sum,
        head_sum,
        hidden_sum,
        expert_model_sum,
        expert_hidden_sum,
        scalar_sum,
        expert_old_sum,
    ) = global_sums
    shard_start = shard_index * d_local
    gain_state = DECAY_RATE * model_stats[0:2] + (1.0 - DECAY_RATE) * (
        own_gains * own_gains + TINY_SQUARE
    )
    update_gains = own_gains * lax.rsqrt(gain_state)
    router_new = DECAY_RATE * router_state + (1.0 - DECAY_RATE) * (
        own_router * own_router + TINY_SQUARE
    )
    update_router = own_router * lax.rsqrt(router_new)
    attn_cols_old = jnp.concatenate([head_stats[0:2], value_columns[None]], axis=0).reshape(-1)
    update_attn_in, rows_attn_in, cols_attn_in = factored_update(
        own_attn_in.reshape(d_local, 3 * local_cols),
        model_stats[2],
        attn_cols_old,
        lax.dynamic_slice_in_dim(model_sum[0], shard_start, d_local),
        lax.dynamic_slice_in_dim(head_sum[0:3], tp_index * local_cols, local_cols, 1).reshape(-1),
        D,
        3 * HH,
        scalar_sum[8],
        jnp.sum(model_sum[0]),
    )
    update_attn_out, rows_attn_out, cols_attn_out = factored_update(
        own_attn_out,
        head_stats[2],
        model_stats[4],
        lax.dynamic_slice_in_dim(head_sum[3], tp_index * local_cols, local_cols),
        lax.dynamic_slice_in_dim(model_sum[2], shard_start, d_local),
        HH,
        D,
        scalar_sum[9],
        jnp.sum(head_sum[3]),
    )
    update_shared_in, rows_shared_in, cols_shared_in = factored_update(
        own_shared_in.reshape(d_local, 2 * ff_local),
        model_stats[3],
        hidden_stats[0:2].reshape(-1),
        lax.dynamic_slice_in_dim(model_sum[1], shard_start, d_local),
        lax.dynamic_slice_in_dim(hidden_sum[0:2], tp_index * ff_local, ff_local, 1).reshape(-1),
        D,
        2 * FF,
        scalar_sum[10],
        jnp.sum(model_sum[1]),
    )
    update_shared_down, rows_shared_down, cols_shared_down = factored_update(
        own_shared_down,
        hidden_stats[2],
        model_stats[5],
        lax.dynamic_slice_in_dim(hidden_sum[2], tp_index * ff_local, ff_local),
        lax.dynamic_slice_in_dim(model_sum[3], shard_start, d_local),
        FF,
        D,
        scalar_sum[11],
        jnp.sum(hidden_sum[2]),
    )
    own_expert_model = lax.dynamic_index_in_dim(expert_model_sum, fsdp_index, 0, keepdims=False)
    own_expert_hidden = lax.dynamic_index_in_dim(expert_hidden_sum, fsdp_index, 0, keepdims=False)
    old_expert_totals = lax.dynamic_index_in_dim(expert_old_sum, fsdp_index, 1, keepdims=False)
    update_expert_in, rows_expert_in, cols_expert_in = factored_update(
        own_expert_in[0].reshape(d_quarter, 2 * fe_local),
        expert_model_stats[0, 0],
        expert_hidden_stats[0, 0:2].reshape(-1),
        lax.dynamic_slice_in_dim(own_expert_model[0], ctx_index * d_quarter, d_quarter),
        lax.dynamic_slice_in_dim(own_expert_hidden[0:2], tp_index * fe_local, fe_local, 1).reshape(
            -1
        ),
        D,
        2 * FE,
        old_expert_totals[0],
        jnp.sum(own_expert_model[0]),
    )
    update_expert_down, rows_expert_down, cols_expert_down = factored_update(
        own_expert_down[0],
        expert_hidden_stats[0, 2],
        expert_model_stats[0, 1],
        lax.dynamic_slice_in_dim(own_expert_hidden[2], tp_index * fe_local, fe_local),
        lax.dynamic_slice_in_dim(own_expert_model[1], ctx_index * d_quarter, d_quarter),
        FE,
        D,
        old_expert_totals[1],
        jnp.sum(own_expert_hidden[2]),
    )
    clip_part = jnp.stack(
        [
            lead_tp * jnp.sum(update_gains * update_gains),
            jnp.sum(update_attn_in * update_attn_in),
            jnp.sum(update_attn_out * update_attn_out),
            lead_tp * jnp.sum(update_router * update_router),
            jnp.sum(update_shared_in * update_shared_in),
            jnp.sum(update_shared_down * update_shared_down),
            jnp.sum(update_expert_in * update_expert_in),
            jnp.sum(update_expert_down * update_expert_down),
        ]
    )
    clip_total = butterfly_sum([clip_part], 2)[0]
    elements = jnp.array(
        [
            2 * D,
            D * 3 * HH,
            HH * D,
            D * experts,
            D * 2 * FF,
            FF * D,
            experts * D * 2 * FE,
            experts * FE * D,
        ],
        jnp.float32,
    )
    update_roots = jnp.sqrt(clip_total / elements)
    new_gains = apply_update(gains, update_gains, update_roots[0], scalar_sum[0], elements[0])
    new_attn_in = apply_update(
        attention_in,
        update_attn_in.reshape(attention_in.shape),
        update_roots[1],
        scalar_sum[1],
        elements[1],
    )
    new_attn_out = apply_update(
        attention_out, update_attn_out, update_roots[2], scalar_sum[2], elements[2]
    )
    new_router = apply_update(
        router_weight, update_router, update_roots[3], scalar_sum[3], elements[3]
    )
    new_shared_in = apply_update(
        shared_in,
        update_shared_in.reshape(shared_in.shape),
        update_roots[4],
        scalar_sum[4],
        elements[4],
    )
    new_shared_down = apply_update(
        shared_down, update_shared_down, update_roots[5], scalar_sum[5], elements[5]
    )
    new_expert_in = apply_update(
        expert_in,
        update_expert_in.reshape(expert_in.shape),
        update_roots[6],
        scalar_sum[6],
        elements[6],
    )
    new_expert_down = apply_update(
        expert_down,
        update_expert_down.reshape(expert_down.shape),
        update_roots[7],
        scalar_sum[7],
        elements[7],
    )
    new_model_stats = jnp.concatenate(
        [gain_state, jnp.stack([rows_attn_in, rows_shared_in, cols_attn_out, cols_shared_down])],
        axis=0,
    )
    attn_cols_new = cols_attn_in.reshape(3, local_cols)
    new_head_stats = jnp.concatenate([attn_cols_new[0:2], rows_attn_out[None]], axis=0)
    new_value_columns = attn_cols_new[2]
    new_hidden_stats = jnp.concatenate(
        [cols_shared_in.reshape(2, ff_local), rows_shared_down[None]], axis=0
    )
    new_expert_model_stats = jnp.stack([rows_expert_in, cols_expert_down])[None]
    new_expert_hidden_stats = jnp.concatenate(
        [cols_expert_in.reshape(2, fe_local), rows_expert_down[None]], axis=0
    )[None]
    return (
        layer_out.astype(jnp.bfloat16)[None],
        input_grad[None],
        own_gains,
        own_attn_in,
        own_attn_out,
        own_router,
        own_shared_in,
        own_shared_down,
        own_expert_in,
        own_expert_down,
        new_gains,
        new_attn_in,
        new_attn_out,
        new_router,
        new_shared_in,
        new_shared_down,
        new_expert_in,
        new_expert_down,
        new_model_stats,
        new_head_stats,
        new_value_columns,
        new_hidden_stats,
        router_new,
        new_expert_model_stats,
        new_expert_hidden_stats,
        update_roots,
    )


def solution(mesh):
    in_specs = (
        P("fsdp", "ctx", None),
        P("fsdp", "ctx"),
        P("fsdp", "ctx", None),
        P("fsdp", "ctx", None),
        P(None, ("fsdp", "ctx")),
        P(("fsdp", "ctx"), None, "tp"),
        P("tp", ("fsdp", "ctx")),
        P(("fsdp", "ctx"), None),
        P(("fsdp", "ctx"), None, "tp"),
        P("tp", ("fsdp", "ctx")),
        P("fsdp", "ctx", None, "tp"),
        P("fsdp", "tp", "ctx"),
        P(None, ("fsdp", "ctx")),
        P(None, "tp"),
        P("tp"),
        P(None, "tp"),
        P(("fsdp", "ctx"), None),
        P("fsdp", None, "ctx"),
        P("fsdp", None, "tp"),
    )
    out_specs = (
        P("fsdp", "ctx", None),
        P("fsdp", "ctx", None),
        P(None, ("fsdp", "ctx")),
        P(("fsdp", "ctx"), None, "tp"),
        P("tp", ("fsdp", "ctx")),
        P(("fsdp", "ctx"), None),
        P(("fsdp", "ctx"), None, "tp"),
        P("tp", ("fsdp", "ctx")),
        P("fsdp", "ctx", None, "tp"),
        P("fsdp", "tp", "ctx"),
        P(None, ("fsdp", "ctx")),
        P(("fsdp", "ctx"), None, "tp"),
        P("tp", ("fsdp", "ctx")),
        P(("fsdp", "ctx"), None),
        P(("fsdp", "ctx"), None, "tp"),
        P("tp", ("fsdp", "ctx")),
        P("fsdp", "ctx", None, "tp"),
        P("fsdp", "tp", "ctx"),
        P(None, ("fsdp", "ctx")),
        P(None, "tp"),
        P("tp"),
        P(None, "tp"),
        P(("fsdp", "ctx"), None),
        P("fsdp", None, "ctx"),
        P("fsdp", None, "tp"),
        P(),
    )
    return jax.shard_map(local, mesh=mesh, in_specs=in_specs, out_specs=out_specs, check_vma=False)
```

```python
import jax
import jax.numpy as jnp
from jax import lax
from jax.sharding import PartitionSpec as P
from jax.experimental import pallas as pl
from jax.experimental.pallas import tpu as pltpu

D = 768
HD = 64
FF = 2048
FE = 2048
WINDOW = 1024
HH = 768


EPSILON = 1e-06
TINY_SQUARE = 1e-30
SCALE_FLOOR = 0.001
DECAY_RATE = 0.5
CLIP_LIMIT = 0.5
STEP_RATE = 0.5


def from_behind(value, axis, steps):
    count = lax.axis_size(axis)
    leading, last = (max(0, -steps), min(count, count - steps))
    return lax.ppermute(value, axis, [(source, source + steps) for source in range(leading, last)])


def rms_norm(values, gain_vec):
    inv_rms = lax.rsqrt(jnp.mean(values * values, axis=-1, keepdims=True) + EPSILON)
    return values * inv_rms * gain_vec


def swiglu(gate_up):
    return jax.nn.silu(gate_up[:, 0]) * gate_up[:, 1]


def rotate(values, cosine, sine_tab):
    half_dim = values.shape[-1] // 2
    first_half = values[..., :half_dim]
    second_half = values[..., half_dim:]
    cos_b = cosine[:, None, :]
    sin_b = sine_tab[:, None, :]
    return jnp.concatenate(
        [first_half * cos_b - second_half * sin_b, second_half * cos_b + first_half * sin_b],
        axis=-1,
    )


def slot_tables(block_routes, experts, capacity):
    flat_routes = block_routes.reshape(-1)
    route_count = flat_routes.shape[0]
    onehot = (flat_routes[:, None] == jnp.arange(experts, dtype=jnp.int32)[None, :]).astype(
        jnp.int32
    )
    rank_in = jnp.sum(
        (jnp.cumsum(onehot, axis=0, dtype=jnp.int32) - 1) * onehot, axis=1, dtype=jnp.int32
    )
    slot_index = flat_routes * capacity + rank_in
    owner_route = (
        jnp.zeros((experts * capacity,), jnp.int32)
        .at[slot_index]
        .set(jnp.arange(route_count, dtype=jnp.int32))
    )
    filled = jnp.zeros((experts * capacity,), jnp.int32).at[slot_index].set(1)
    return (slot_index, owner_route, filled)


def block_view(queries, keys_ext, values_ext, seg_own, seg_ext, start_row, base_pos):
    block_len = queries.shape[0]
    block_rows = min(512, block_len)
    query_rows = lax.dynamic_slice_in_dim(queries, start_row, block_rows, 0)
    key_rows = lax.dynamic_slice_in_dim(
        keys_ext, start_row + block_len - WINDOW, block_rows + WINDOW, 0
    )
    value_rows = lax.dynamic_slice_in_dim(
        values_ext, start_row + block_len - WINDOW, block_rows + WINDOW, 0
    )
    scores = (
        jnp.einsum("qhd,khd->hqk", query_rows, key_rows, preferred_element_type=jnp.float32) * 0.125
    )
    query_pos = start_row + jnp.arange(block_rows, dtype=jnp.int32)
    key_pos = start_row - WINDOW + jnp.arange(block_rows + WINDOW, dtype=jnp.int32)
    distance = query_pos[:, None] - key_pos[None, :]
    seg_query = lax.dynamic_slice_in_dim(seg_own, start_row, block_rows, 0)
    seg_key = lax.dynamic_slice_in_dim(
        seg_ext, start_row + block_len - WINDOW, block_rows + WINDOW, 0
    )
    allowed = (
        (distance >= 0)
        & (distance < WINDOW)
        & (seg_query[:, None] == seg_key[None, :])
        & (key_pos[None, :] + base_pos >= 0)
    )
    return (query_rows, key_rows, value_rows, jnp.where(allowed[None], scores, -1e30), allowed)


def factored_update(
    grad_mat, rows_old, cols_old, row_sums, col_sums, row_total, col_total, old_total, square_total
):
    rows_new = DECAY_RATE * rows_old + (1.0 - DECAY_RATE) * row_sums / col_total
    cols_new = DECAY_RATE * cols_old + (1.0 - DECAY_RATE) * col_sums / row_total
    mean_rows = (DECAY_RATE * old_total + (1.0 - DECAY_RATE) * square_total / col_total) / row_total
    second_moment = rows_new[:, None] * cols_new[None, :] / mean_rows
    return (grad_mat * lax.rsqrt(second_moment), rows_new, cols_new)


def apply_update(weight, update, update_root, square_sum, elements):
    param_scale = jnp.maximum(SCALE_FLOOR, jnp.sqrt(square_sum / elements))
    return weight - STEP_RATE * param_scale * update / jnp.maximum(1.0, update_root / CLIP_LIMIT)


def butterfly_partners():
    partners = []
    here = [lax.axis_index(name) for name in ("fsdp", "ctx", "tp")]
    for axis_number, name in enumerate(("fsdp", "ctx", "tp")):
        size = lax.axis_size(name)
        step = 1
        while step < size:
            bit = (here[axis_number] // step) % 2
            other = list(here)
            other[axis_number] = here[axis_number] + step * (1 - 2 * bit)
            partners.append(tuple(other))
            step *= 2
    return partners


def butterfly_kernel(x_ref, o_ref, stage, inbox, send_sems, recv_sems):
    partners = butterfly_partners()
    barrier = pltpu.get_barrier_semaphore()
    for partner in partners:
        pl.semaphore_signal(
            barrier, 1, device_id=partner, device_id_type=pl.DeviceIdType.MESH
        )
    pl.semaphore_wait(barrier, len(partners))
    acc = x_ref[...]
    for round_number, partner in enumerate(partners):
        stage[round_number] = acc
        copy = pltpu.make_async_remote_copy(
            src_ref=stage.at[round_number],
            dst_ref=inbox.at[round_number],
            send_sem=send_sems.at[round_number],
            recv_sem=recv_sems.at[round_number],
            device_id=partner,
            device_id_type=pl.DeviceIdType.MESH,
        )
        copy.start()
        copy.wait()
        acc = stage[round_number] + inbox[round_number]
    o_ref[...] = acc


def butterfly_sum(values, collective_id):
    flat = jnp.concatenate([v.reshape(-1).astype(jnp.float32) for v in values])
    size = flat.shape[0]
    rows = -(-size // 1024) * 8
    block = jnp.pad(flat, (0, rows * 128 - size)).reshape(rows, 128)
    rounds = sum(
        max(1, lax.axis_size(name)).bit_length() - 1 for name in ("fsdp", "ctx", "tp")
    )
    total = pl.pallas_call(
        butterfly_kernel,
        out_shape=jax.ShapeDtypeStruct((rows, 128), jnp.float32),
        in_specs=[pl.BlockSpec(memory_space=pltpu.VMEM)],
        out_specs=pl.BlockSpec(memory_space=pltpu.VMEM),
        scratch_shapes=[
            pltpu.VMEM((rounds, rows, 128), jnp.float32),
            pltpu.VMEM((rounds, rows, 128), jnp.float32),
            pltpu.SemaphoreType.DMA((rounds,)),
            pltpu.SemaphoreType.DMA((rounds,)),
        ],
        compiler_params=pltpu.CompilerParams(collective_id=collective_id, has_side_effects=True),
    )(block).reshape(-1)
    results = []
    offset = 0
    for v in values:
        results.append(total[offset : offset + v.size].reshape(v.shape))
        offset += v.size
    return results


def halving_kernel(x_ref, o_ref, stage_one, stage_two, inbox_one, inbox_two, inbox_three, sems):
    rows = o_ref.shape[0]
    chunk = 64
    fsdp_here = lax.axis_index("fsdp")
    ctx_here = lax.axis_index("ctx")
    tp_here = lax.axis_index("tp")
    bit_low = fsdp_here % 2
    bit_high = (fsdp_here // 2) % 2
    partners = [
        (fsdp_here, 1 - ctx_here, tp_here),
        (fsdp_here + 1 - 2 * bit_low, ctx_here, tp_here),
        (fsdp_here + 2 - 4 * bit_high, ctx_here, tp_here),
    ]
    barrier = pltpu.get_barrier_semaphore()
    for partner in partners:
        pl.semaphore_signal(barrier, 1, device_id=partner, device_id_type=pl.DeviceIdType.MESH)
    pl.semaphore_wait(barrier, len(partners))

    def swap(src, dst, number, partner):
        copy = pltpu.make_async_remote_copy(
            src_ref=src,
            dst_ref=dst,
            send_sem=sems.at[0, number],
            recv_sem=sems.at[1, number],
            device_id=partner,
            device_id_type=pl.DeviceIdType.MESH,
        )
        copy.start()
        copy.wait()

    swap(x_ref.at[:, pl.ds(1 - ctx_here, 1)], inbox_one, 0, partners[0])

    @pl.loop(0, rows // chunk)
    def _(step):
        part = pl.ds(pl.multiple_of(step * chunk, chunk), chunk)
        for high in range(2):
            for low in range(2):
                stage_one[high, low, part] = (
                    x_ref[2 * high + low, ctx_here, part] + inbox_one[2 * high + low, 0, part]
                )

    swap(stage_one.at[:, pl.ds(1 - bit_low, 1)], inbox_two, 1, partners[1])

    @pl.loop(0, rows // chunk)
    def _(step):
        part = pl.ds(pl.multiple_of(step * chunk, chunk), chunk)
        for high in range(2):
            stage_two[high, part] = stage_one[high, bit_low, part] + inbox_two[high, 0, part]

    swap(stage_two.at[pl.ds(1 - bit_high, 1)], inbox_three, 2, partners[2])

    @pl.loop(0, rows // chunk)
    def _(step):
        part = pl.ds(pl.multiple_of(step * chunk, chunk), chunk)
        o_ref[part] = stage_two[bit_high, part] + inbox_three[0, part]


def halving_scatter(packed, collective_id):
    count, width = packed.shape
    rows = -(-width // (128 * 64)) * 64
    block = jnp.pad(packed, ((0, 0), (0, rows * 128 - width))).reshape(count // 2, 2, rows, 128)
    own = pl.pallas_call(
        halving_kernel,
        out_shape=jax.ShapeDtypeStruct((rows, 128), jnp.float32),
        in_specs=[pl.BlockSpec(memory_space=pltpu.VMEM)],
        out_specs=pl.BlockSpec(memory_space=pltpu.VMEM),
        scratch_shapes=[
            pltpu.VMEM((2, 2, rows, 128), jnp.float32),
            pltpu.VMEM((2, rows, 128), jnp.float32),
            pltpu.VMEM((count // 2, 1, rows, 128), jnp.float32),
            pltpu.VMEM((2, 1, rows, 128), jnp.float32),
            pltpu.VMEM((1, rows, 128), jnp.float32),
            pltpu.SemaphoreType.DMA((2, 3)),
        ],
        compiler_params=pltpu.CompilerParams(
            collective_id=collective_id, has_side_effects=True, vmem_limit_bytes=60 * 1024 * 1024
        ),
    )(block)
    return own.reshape(-1)[:width]


def swiglu_experts(gate_up):
    return jax.nn.silu(gate_up[:, :, 0]) * gate_up[:, :, 1]


def gather_packed(pieces, axes):
    flat = jnp.concatenate([piece.reshape(-1) for piece, _ in pieces])
    full = lax.all_gather(flat, axes, axis=0, tiled=False)
    count = full.shape[0]
    results = []
    offset = 0
    for piece, dim in pieces:
        size = piece.size
        part = full[:, offset : offset + size].reshape((count,) + piece.shape)
        offset += size
        part = jnp.moveaxis(part, 0, dim)
        shape = list(piece.shape)
        shape[dim] *= count
        results.append(part.reshape(shape))
    return results


def scatter_packed(pieces, axes, count, use_kernel=False):
    columns = []
    local_shapes = []
    for grad, dim in pieces:
        shape = grad.shape
        split = shape[:dim] + (count, shape[dim] // count) + shape[dim + 1 :]
        local_shapes.append(shape[:dim] + (shape[dim] // count,) + shape[dim + 1 :])
        part = jnp.moveaxis(grad.reshape(split), dim, 0)
        columns.append(part.reshape(count, -1))
    packed = jnp.concatenate(columns, axis=1)
    if use_kernel:
        own = halving_scatter(packed, 3)
    else:
        width = packed.shape[1]
        rows = -(-width // 1024) * 8
        packed = jnp.pad(packed, ((0, 0), (0, rows * 128 - width))).reshape(count * rows, 128)
        own = lax.psum_scatter(packed, axes, scatter_dimension=0, tiled=True).reshape(-1)
    results = []
    offset = 0
    for local_shape in local_shapes:
        size = 1
        for extent in local_shape:
            size *= extent
        results.append(own[offset : offset + size].reshape(local_shape))
        offset += size
    return results


def experts_dense(normed_two, grad_out, weights, expert_in_all, expert_down_all):
    gate_up = jnp.einsum(
        "td,edgf->etgf", normed_two, expert_in_all, preferred_element_type=jnp.float32
    )
    act, act_back = jax.vjp(swiglu_experts, gate_up)
    hidden = act.astype(jnp.bfloat16)
    outs = jnp.einsum("etf,efd->etd", hidden, expert_down_all, preferred_element_type=jnp.float32)
    weights_e = weights.T[:, :, None]
    combined = jnp.sum(weights_e * outs, axis=0)
    gate_dots = jnp.sum(outs * grad_out[None], axis=-1).T
    grad_outs = (weights_e * grad_out[None]).astype(jnp.bfloat16)
    grad_hidden = jnp.einsum(
        "etd,efd->etf", grad_outs, expert_down_all, preferred_element_type=jnp.float32
    )
    grad_gate_up = act_back(grad_hidden)[0].astype(jnp.bfloat16)
    grad_down = jnp.einsum("etf,etd->efd", hidden, grad_outs, preferred_element_type=jnp.float32)
    grad_in = jnp.einsum(
        "td,etgf->edgf", normed_two, grad_gate_up, preferred_element_type=jnp.float32
    )
    grad_rows = jnp.einsum(
        "etgf,edgf->td", grad_gate_up, expert_in_all, preferred_element_type=jnp.float32
    )
    return combined, gate_dots, grad_rows, grad_in, grad_down


def experts_routed(
    normed_two, grad_out, route_rows, gate_probs, expert_in_low, expert_down_low, capacity
):
    block_len, model_width = normed_two.shape
    experts = lax.axis_size("fsdp")
    slot_index, owner_route, filled = slot_tables(route_rows, experts, capacity)
    fill_mask = filled.astype(jnp.bfloat16)[:, None]
    route_grads = (
        (gate_probs[:, :, None] * grad_out[:, None, :])
        .astype(jnp.bfloat16)
        .reshape(2 * block_len, model_width)
    )
    send_rows = jnp.concatenate(
        [normed_two[owner_route // 2] * fill_mask, route_grads[owner_route] * fill_mask], axis=1
    ).reshape(experts, capacity, 2 * model_width)
    exchange = lambda rows: lax.all_to_all(rows, "fsdp", split_axis=0, concat_axis=0, tiled=True)
    pair_count = lax.axis_size("tp")
    swap = lambda rows: lax.ppermute(
        rows, "tp", [(index, index + 1 - 2 * (index % 2)) for index in range(pair_count)]
    )
    half = capacity // 2
    side = lax.axis_index("tp") % 2
    mine = exchange(lax.dynamic_slice_in_dim(send_rows, side * half, half, 1))
    received_both = jnp.concatenate([mine, swap(mine)], axis=1).reshape(
        experts * capacity, 2 * model_width
    )
    received = received_both[:, :model_width]
    grad_received = received_both[:, model_width:]
    gate_up = jnp.einsum("rd,dgf->rgf", received, expert_in_low, preferred_element_type=jnp.float32)
    act, act_back = jax.vjp(swiglu, gate_up)
    hidden = act.astype(jnp.bfloat16)
    outs = jnp.dot(hidden, expert_down_low, preferred_element_type=jnp.float32)
    grad_hidden = jnp.einsum(
        "rd,fd->rf", grad_received, expert_down_low, preferred_element_type=jnp.float32
    )
    grad_gate_up = act_back(grad_hidden)[0].astype(jnp.bfloat16)
    grad_in = jnp.einsum("rd,rgf->dgf", received, grad_gate_up, preferred_element_type=jnp.float32)
    grad_down = jnp.einsum("rf,rd->fd", hidden, grad_received, preferred_element_type=jnp.float32)
    grad_expert_rows = jnp.einsum(
        "rgf,dgf->rd", grad_gate_up, expert_in_low, preferred_element_type=jnp.float32
    )
    results = jnp.concatenate([outs, grad_expert_rows], axis=1).reshape(
        experts, capacity, 2 * model_width
    )
    pair_sum = results[:, :half] + swap(results[:, half:])
    held = exchange(pair_sum.astype(jnp.bfloat16)).reshape(experts * half, 2 * model_width)
    slot_expert = slot_index // capacity
    slot_rank = slot_index % capacity
    in_side = (slot_rank // half) == side
    local_slot = slot_expert * half + slot_rank % half
    returned = jnp.where(in_side[:, None], held[local_slot].astype(jnp.float32), 0.0)
    route_out = returned[:, :model_width].reshape(block_len, 2, model_width)
    grad_routes = returned[:, model_width:].reshape(block_len, 2, model_width)
    combined = jnp.sum(gate_probs[:, :, None] * route_out, axis=1)
    gate_dots = jnp.sum(grad_out[:, None, :] * route_out, axis=-1)
    grad_rows = jnp.sum(grad_routes, axis=1)
    return combined, gate_dots, grad_rows, grad_in, grad_down


def local(
    layer_input,
    segments,
    routes,
    cotangent,
    gains,
    attention_in,
    attention_out,
    router_weight,
    shared_in,
    shared_down,
    expert_in,
    expert_down,
    model_stats,
    head_stats,
    value_columns,
    hidden_stats,
    router_state,
    expert_model_stats,
    expert_hidden_stats,
):
    block_len = layer_input.shape[1]
    model_width = layer_input.shape[2]
    experts = router_weight.shape[1]
    dense_experts = False
    capacity = min(block_len, 4 * block_len // experts)
    ctx_index = lax.axis_index("ctx")
    tp_index = lax.axis_index("tp")
    fsdp_index = lax.axis_index("fsdp")
    shard_index = lax.axis_index(("fsdp", "ctx"))
    shard_count = lax.axis_size(("fsdp", "ctx"))
    ctx_count = lax.axis_size("ctx")
    base_pos = ctx_index * block_len
    low = lambda v: v.astype(jnp.bfloat16)
    gain_low, attn_in_low = gather_packed(
        [(low(gains), 1), (low(attention_in), 0)], ("fsdp", "ctx")
    )
    later = [
        (low(attention_out), 1),
        (low(router_weight), 0),
        (low(shared_in), 0),
        (low(shared_down), 1),
    ]
    if dense_experts:
        later += [(low(expert_in), 0), (low(expert_down), 0)]
    later_full = gather_packed(later, ("fsdp", "ctx"))
    attn_out_low, router_low, shared_in_low, shared_down_low = later_full[:4]
    if dense_experts:
        fe_local = expert_down.shape[1]
        expert_in_all = later_full[4].reshape(experts, model_width, 2, fe_local)
        expert_down_all = (
            later_full[5]
            .reshape(experts, ctx_count, fe_local, model_width // ctx_count)
            .transpose(0, 2, 1, 3)
            .reshape(experts, fe_local, model_width)
        )
    else:
        expert_in_low = lax.all_gather(low(expert_in), "ctx", axis=1, tiled=True)[0]
        expert_down_low = lax.all_gather(low(expert_down), "ctx", axis=2, tiled=True)[0]
    residual = layer_input[0].astype(jnp.float32)
    gain_one = gain_low[0].astype(jnp.float32)
    gain_two = gain_low[1].astype(jnp.float32)
    normed_one, norm_one_back = jax.vjp(rms_norm, residual, gain_one)
    normed_one = normed_one.astype(jnp.bfloat16)
    projected = jnp.einsum(
        "td,dgf->tgf", normed_one, attn_in_low, preferred_element_type=jnp.float32
    )
    local_cols = projected.shape[2]
    local_heads = local_cols // HD
    half_dim = HD // 2
    frequency = 10000.0 ** (-jnp.arange(half_dim, dtype=jnp.float32) / half_dim)
    angles = (base_pos + jnp.arange(block_len, dtype=jnp.int32)).astype(jnp.float32)[
        :, None
    ] * frequency[None, :]
    cosine = jnp.cos(angles)
    sine_tab = jnp.sin(angles)
    queries = rotate(projected[:, 0].reshape(block_len, local_heads, HD), cosine, sine_tab).astype(
        jnp.bfloat16
    )
    keys_own = rotate(projected[:, 1].reshape(block_len, local_heads, HD), cosine, sine_tab).astype(
        jnp.bfloat16
    )
    values_own = projected[:, 2].reshape(block_len, local_heads, HD).astype(jnp.bfloat16)
    seg_own = segments[0].astype(jnp.bfloat16)
    keys_prev, values_prev, seg_prev = from_behind((keys_own, values_own, seg_own), "ctx", 1)
    keys_ext = jnp.concatenate([keys_prev, keys_own], axis=0)
    values_ext = jnp.concatenate([values_prev, values_own], axis=0)
    seg_ext = jnp.concatenate([seg_prev, seg_own], axis=0)
    block_rows = min(512, block_len)
    block_total = block_len // block_rows
    starts = jnp.arange(block_total, dtype=jnp.int32) * block_rows

    def forward_block(start_row):
        query_rows, key_rows, value_rows, masked, allowed = block_view(
            queries, keys_ext, values_ext, seg_own, seg_ext, start_row, base_pos
        )
        row_max = jnp.max(masked, axis=-1, keepdims=True)
        exp_terms = jnp.where(allowed[None], jnp.exp(masked - row_max), 0.0)
        row_total = jnp.sum(exp_terms, axis=-1, keepdims=True)
        attn_probs = (exp_terms / row_total).astype(jnp.bfloat16)
        attended = jnp.einsum(
            "hqk,khd->qhd", attn_probs, value_rows, preferred_element_type=jnp.float32
        )
        return (attended, row_max + jnp.log(row_total))

    attended, log_totals = lax.map(forward_block, starts)
    mixed_heads = attended.reshape(block_len, local_cols).astype(jnp.bfloat16)
    attn_total = lax.psum(
        jnp.dot(mixed_heads, attn_out_low, preferred_element_type=jnp.float32), "tp"
    )
    after_attn = residual + attn_total
    normed_two, norm_two_back = jax.vjp(rms_norm, after_attn, gain_two)
    normed_two = normed_two.astype(jnp.bfloat16)
    logits = jnp.dot(normed_two, router_low, preferred_element_type=jnp.float32)
    route_rows = routes[0]
    onehot = (route_rows[:, :, None] == jnp.arange(experts, dtype=jnp.int32)[None, None, :]).astype(
        jnp.float32
    )
    picked = jnp.sum(onehot * logits[:, None, :], axis=-1)
    gate_probs = jax.nn.softmax(picked, axis=-1)
    upstream = cotangent[0]
    grad_out = upstream.astype(jnp.float32)
    if dense_experts:
        weights = jnp.sum(gate_probs[:, :, None] * onehot, axis=1)
        combined, dots_e, grad_rows, grad_expert_in, grad_expert_down = experts_dense(
            normed_two, grad_out, weights, expert_in_all, expert_down_all
        )
        gate_dots = jnp.sum(onehot * dots_e[:, None, :], axis=-1)
    else:
        combined, gate_dots, grad_rows, grad_expert_in, grad_expert_down = experts_routed(
            normed_two,
            grad_out,
            route_rows,
            gate_probs,
            expert_in_low,
            expert_down_low,
            capacity,
        )
    shared_gate_up = jnp.einsum(
        "td,dgf->tgf", normed_two, shared_in_low, preferred_element_type=jnp.float32
    )
    shared_act, shared_act_back = jax.vjp(swiglu, shared_gate_up)
    shared_hidden = shared_act.astype(jnp.bfloat16)
    shared_out = jnp.dot(shared_hidden, shared_down_low, preferred_element_type=jnp.float32)
    grad_shared_hidden = jnp.einsum(
        "td,fd->tf", upstream, shared_down_low, preferred_element_type=jnp.float32
    )
    grad_shared_gate_up = shared_act_back(grad_shared_hidden)[0].astype(jnp.bfloat16)
    partial_two = (
        jnp.einsum(
            "tgf,dgf->td", grad_shared_gate_up, shared_in_low, preferred_element_type=jnp.float32
        )
        + grad_rows
    )
    branch_total, grad_normed_part, gate_total = lax.psum(
        (shared_out + combined, partial_two, gate_dots), "tp"
    )
    layer_out = after_attn + branch_total
    grad_picked = gate_probs * (
        gate_total - jnp.sum(gate_probs * gate_total, axis=-1, keepdims=True)
    )
    grad_logits = jnp.sum(grad_picked[:, :, None] * onehot, axis=1).astype(jnp.bfloat16)
    grad_shared_in = jnp.einsum(
        "td,tgf->dgf", normed_two, grad_shared_gate_up, preferred_element_type=jnp.float32
    )
    grad_shared_down = jnp.einsum(
        "tf,td->fd", shared_hidden, upstream, preferred_element_type=jnp.float32
    )
    grad_router = jnp.einsum(
        "td,te->de", normed_two, grad_logits, preferred_element_type=jnp.float32
    )
    grad_normed_two = grad_normed_part + jnp.einsum(
        "te,de->td", grad_logits, router_low, preferred_element_type=jnp.float32
    )
    grad_after, grad_gain_two = norm_two_back(grad_normed_two)
    grad_after = grad_after + grad_out
    grad_attn_low = grad_after.astype(jnp.bfloat16)
    grad_attn_out = jnp.einsum(
        "tc,td->cd", mixed_heads, grad_attn_low, preferred_element_type=jnp.float32
    )
    first_grads = [
        (grad_attn_out, 1),
        (grad_router, 0),
        (grad_shared_in, 0),
        (grad_shared_down, 1),
        (grad_gain_two, 0),
    ]
    if dense_experts:
        fe_local = expert_down.shape[1]
        first_grads += [
            (grad_expert_in.reshape(shard_count * expert_in.shape[1], 2, fe_local), 0),
            (
                grad_expert_down.reshape(experts, fe_local, ctx_count, model_width // ctx_count)
                .transpose(0, 2, 1, 3)
                .reshape(shard_count * fe_local, model_width // ctx_count),
                0,
            ),
        ]
    if not dense_experts:
        own_expert_in = lax.psum_scatter(grad_expert_in[None], "ctx", scatter_dimension=1, tiled=True)
        own_expert_down = lax.psum_scatter(
            grad_expert_down[None], "ctx", scatter_dimension=2, tiled=True
        )
    grad_heads = (
        jnp.einsum("td,cd->tc", grad_attn_low, attn_out_low, preferred_element_type=jnp.float32)
        .astype(jnp.bfloat16)
        .reshape(block_len, local_heads, HD)
    )

    def backward_block(block_number, running):
        grad_keys, grad_values, grad_queries = running
        start_row = block_number * block_rows
        query_rows, key_rows, value_rows, masked, allowed = block_view(
            queries, keys_ext, values_ext, seg_own, seg_ext, start_row, base_pos
        )
        log_total = lax.dynamic_index_in_dim(log_totals, block_number, 0, keepdims=False)
        attn_probs = jnp.where(allowed[None], jnp.exp(masked - log_total), 0.0)
        grad_block = lax.dynamic_slice_in_dim(grad_heads, start_row, block_rows, 0)
        grad_probs = jnp.einsum(
            "qhd,khd->hqk", grad_block, value_rows, preferred_element_type=jnp.float32
        )
        inner_sum = jnp.sum(attn_probs * grad_probs, axis=-1, keepdims=True)
        grad_scores = (attn_probs * (grad_probs - inner_sum)).astype(jnp.bfloat16)
        grad_query_rows = (
            jnp.einsum("hqk,khd->qhd", grad_scores, key_rows, preferred_element_type=jnp.float32)
            * 0.125
        )
        grad_key_rows = (
            jnp.einsum("hqk,qhd->khd", grad_scores, query_rows, preferred_element_type=jnp.float32)
            * 0.125
        )
        grad_value_rows = jnp.einsum(
            "hqk,qhd->khd",
            attn_probs.astype(jnp.bfloat16),
            grad_block,
            preferred_element_type=jnp.float32,
        )
        key_offset = start_row + block_len - WINDOW
        grad_keys = lax.dynamic_update_slice_in_dim(
            grad_keys,
            lax.dynamic_slice_in_dim(grad_keys, key_offset, block_rows + WINDOW, 0) + grad_key_rows,
            key_offset,
            0,
        )
        grad_values = lax.dynamic_update_slice_in_dim(
            grad_values,
            lax.dynamic_slice_in_dim(grad_values, key_offset, block_rows + WINDOW, 0)
            + grad_value_rows,
            key_offset,
            0,
        )
        grad_queries = lax.dynamic_update_slice_in_dim(grad_queries, grad_query_rows, start_row, 0)
        return (grad_keys, grad_values, grad_queries)

    zero_ext = jnp.zeros((2 * block_len, local_heads, HD), jnp.float32)
    zero_own = jnp.zeros((block_len, local_heads, HD), jnp.float32)
    grad_keys, grad_values, grad_queries = lax.fori_loop(
        0, block_total, backward_block, (zero_ext, zero_ext, zero_own)
    )
    rim_keys, rim_values = (
        from_behind(grad_keys[:block_len].astype(jnp.bfloat16), "ctx", -1).astype(jnp.float32),
        from_behind(grad_values[:block_len].astype(jnp.bfloat16), "ctx", -1).astype(jnp.float32),
    )
    grad_keys_own = grad_keys[block_len:] + rim_keys
    grad_values_own = grad_values[block_len:] + rim_values
    grad_query_raw = rotate(grad_queries, cosine, -sine_tab)
    grad_key_raw = rotate(grad_keys_own, cosine, -sine_tab)
    grad_projected = (
        jnp.stack([grad_query_raw, grad_key_raw, grad_values_own], axis=1)
        .reshape(block_len, 3, local_cols)
        .astype(jnp.bfloat16)
    )
    grad_attn_in = jnp.einsum(
        "td,tgf->dgf", normed_one, grad_projected, preferred_element_type=jnp.float32
    )
    partial_one = jnp.einsum(
        "tgf,dgf->td", grad_projected, attn_in_low, preferred_element_type=jnp.float32
    )
    grad_residual, grad_gain_one = norm_one_back(lax.psum(partial_one, "tp"))
    input_grad = grad_after + grad_residual
    halving = lax.axis_size("fsdp") == 4 and ctx_count == 2
    all_own = scatter_packed(
        first_grads + [(grad_attn_in, 0), (grad_gain_one, 0)],
        ("fsdp", "ctx"),
        shard_count,
        halving,
    )
    own_attn_out, own_router, own_shared_in, own_shared_down, own_gain_two = all_own[:5]
    own_attn_in, own_gain_one = all_own[-2:]
    if dense_experts:
        own_expert_in = all_own[5][None]
        own_expert_down = all_own[6][None]
    own_gains = jnp.stack([own_gain_one, own_gain_two])
    lead_tp = (tp_index == 0).astype(jnp.float32)
    first_shard = (shard_index == 0).astype(jnp.float32)
    first_ctx = (ctx_index == 0).astype(jnp.float32)
    d_local = gains.shape[1]
    ff_local = shared_down.shape[0]
    fe_local = expert_down.shape[1]
    d_quarter = expert_in.shape[1]
    square_attn_in = own_attn_in * own_attn_in + TINY_SQUARE
    square_attn_out = own_attn_out * own_attn_out + TINY_SQUARE
    square_shared_in = own_shared_in * own_shared_in + TINY_SQUARE
    square_shared_down = own_shared_down * own_shared_down + TINY_SQUARE
    square_expert_in = own_expert_in[0] * own_expert_in[0] + TINY_SQUARE
    square_expert_down = own_expert_down[0] * own_expert_down[0] + TINY_SQUARE
    model_part = lax.dynamic_update_slice(
        jnp.zeros((4, D), jnp.float32),
        jnp.stack(
            [
                jnp.sum(square_attn_in, axis=(1, 2)),
                jnp.sum(square_shared_in, axis=(1, 2)),
                jnp.sum(square_attn_out, axis=0),
                jnp.sum(square_shared_down, axis=0),
            ]
        ),
        (0, shard_index * d_local),
    )
    head_part = lax.dynamic_update_slice(
        jnp.zeros((4, HH), jnp.float32),
        jnp.concatenate(
            [jnp.sum(square_attn_in, axis=0), jnp.sum(square_attn_out, axis=1)[None]], axis=0
        ),
        (0, tp_index * local_cols),
    )
    hidden_part = lax.dynamic_update_slice(
        jnp.zeros((3, FF), jnp.float32),
        jnp.concatenate(
            [jnp.sum(square_shared_in, axis=0), jnp.sum(square_shared_down, axis=1)[None]], axis=0
        ),
        (0, tp_index * ff_local),
    )
    expert_model_part = lax.dynamic_update_slice(
        jnp.zeros((experts, 2, D), jnp.float32),
        jnp.stack([jnp.sum(square_expert_in, axis=(1, 2)), jnp.sum(square_expert_down, axis=0)])[
            None
        ],
        (fsdp_index, 0, ctx_index * d_quarter),
    )
    expert_hidden_part = lax.dynamic_update_slice(
        jnp.zeros((experts, 3, FE), jnp.float32),
        jnp.concatenate(
            [jnp.sum(square_expert_in, axis=0), jnp.sum(square_expert_down, axis=1)[None]], axis=0
        )[None],
        (fsdp_index, 0, tp_index * fe_local),
    )
    scalar_part = jnp.stack(
        [
            lead_tp * jnp.sum(gains * gains),
            jnp.sum(attention_in * attention_in),
            jnp.sum(attention_out * attention_out),
            lead_tp * jnp.sum(router_weight * router_weight),
            jnp.sum(shared_in * shared_in),
            jnp.sum(shared_down * shared_down),
            jnp.sum(expert_in * expert_in),
            jnp.sum(expert_down * expert_down),
            lead_tp * jnp.sum(model_stats[2]),
            first_shard * jnp.sum(head_stats[2]),
            lead_tp * jnp.sum(model_stats[3]),
            first_shard * jnp.sum(hidden_stats[2]),
        ]
    )
    expert_old_part = lax.dynamic_update_slice(
        jnp.zeros((2, experts), jnp.float32),
        jnp.stack(
            [
                lead_tp * jnp.sum(expert_model_stats[0, 0]),
                first_ctx * jnp.sum(expert_hidden_stats[0, 2]),
            ]
        )[:, None],
        (0, fsdp_index),
    )
    global_sums = butterfly_sum(
        [
            model_part,
            head_part,
            hidden_part,
            expert_model_part,
            expert_hidden_part,
            scalar_part,
            expert_old_part,
        ],
        1,
    )
    (
        model_sum,
        head_sum,
        hidden_sum,
        expert_model_sum,
        expert_hidden_sum,
        scalar_sum,
        expert_old_sum,
    ) = global_sums
    shard_start = shard_index * d_local
    gain_state = DECAY_RATE * model_stats[0:2] + (1.0 - DECAY_RATE) * (
        own_gains * own_gains + TINY_SQUARE
    )
    update_gains = own_gains * lax.rsqrt(gain_state)
    router_new = DECAY_RATE * router_state + (1.0 - DECAY_RATE) * (
        own_router * own_router + TINY_SQUARE
    )
    update_router = own_router * lax.rsqrt(router_new)
    attn_cols_old = jnp.concatenate([head_stats[0:2], value_columns[None]], axis=0).reshape(-1)
    update_attn_in, rows_attn_in, cols_attn_in = factored_update(
        own_attn_in.reshape(d_local, 3 * local_cols),
        model_stats[2],
        attn_cols_old,
        lax.dynamic_slice_in_dim(model_sum[0], shard_start, d_local),
        lax.dynamic_slice_in_dim(head_sum[0:3], tp_index * local_cols, local_cols, 1).reshape(-1),
        D,
        3 * HH,
        scalar_sum[8],
        jnp.sum(model_sum[0]),
    )
    update_attn_out, rows_attn_out, cols_attn_out = factored_update(
        own_attn_out,
        head_stats[2],
        model_stats[4],
        lax.dynamic_slice_in_dim(head_sum[3], tp_index * local_cols, local_cols),
        lax.dynamic_slice_in_dim(model_sum[2], shard_start, d_local),
        HH,
        D,
        scalar_sum[9],
        jnp.sum(head_sum[3]),
    )
    update_shared_in, rows_shared_in, cols_shared_in = factored_update(
        own_shared_in.reshape(d_local, 2 * ff_local),
        model_stats[3],
        hidden_stats[0:2].reshape(-1),
        lax.dynamic_slice_in_dim(model_sum[1], shard_start, d_local),
        lax.dynamic_slice_in_dim(hidden_sum[0:2], tp_index * ff_local, ff_local, 1).reshape(-1),
        D,
        2 * FF,
        scalar_sum[10],
        jnp.sum(model_sum[1]),
    )
    update_shared_down, rows_shared_down, cols_shared_down = factored_update(
        own_shared_down,
        hidden_stats[2],
        model_stats[5],
        lax.dynamic_slice_in_dim(hidden_sum[2], tp_index * ff_local, ff_local),
        lax.dynamic_slice_in_dim(model_sum[3], shard_start, d_local),
        FF,
        D,
        scalar_sum[11],
        jnp.sum(hidden_sum[2]),
    )
    own_expert_model = lax.dynamic_index_in_dim(expert_model_sum, fsdp_index, 0, keepdims=False)
    own_expert_hidden = lax.dynamic_index_in_dim(expert_hidden_sum, fsdp_index, 0, keepdims=False)
    old_expert_totals = lax.dynamic_index_in_dim(expert_old_sum, fsdp_index, 1, keepdims=False)
    update_expert_in, rows_expert_in, cols_expert_in = factored_update(
        own_expert_in[0].reshape(d_quarter, 2 * fe_local),
        expert_model_stats[0, 0],
        expert_hidden_stats[0, 0:2].reshape(-1),
        lax.dynamic_slice_in_dim(own_expert_model[0], ctx_index * d_quarter, d_quarter),
        lax.dynamic_slice_in_dim(own_expert_hidden[0:2], tp_index * fe_local, fe_local, 1).reshape(
            -1
        ),
        D,
        2 * FE,
        old_expert_totals[0],
        jnp.sum(own_expert_model[0]),
    )
    update_expert_down, rows_expert_down, cols_expert_down = factored_update(
        own_expert_down[0],
        expert_hidden_stats[0, 2],
        expert_model_stats[0, 1],
        lax.dynamic_slice_in_dim(own_expert_hidden[2], tp_index * fe_local, fe_local),
        lax.dynamic_slice_in_dim(own_expert_model[1], ctx_index * d_quarter, d_quarter),
        FE,
        D,
        old_expert_totals[1],
        jnp.sum(own_expert_hidden[2]),
    )
    clip_part = jnp.stack(
        [
            lead_tp * jnp.sum(update_gains * update_gains),
            jnp.sum(update_attn_in * update_attn_in),
            jnp.sum(update_attn_out * update_attn_out),
            lead_tp * jnp.sum(update_router * update_router),
            jnp.sum(update_shared_in * update_shared_in),
            jnp.sum(update_shared_down * update_shared_down),
            jnp.sum(update_expert_in * update_expert_in),
            jnp.sum(update_expert_down * update_expert_down),
        ]
    )
    clip_total = butterfly_sum([clip_part], 2)[0]
    elements = jnp.array(
        [
            2 * D,
            D * 3 * HH,
            HH * D,
            D * experts,
            D * 2 * FF,
            FF * D,
            experts * D * 2 * FE,
            experts * FE * D,
        ],
        jnp.float32,
    )
    update_roots = jnp.sqrt(clip_total / elements)
    new_gains = apply_update(gains, update_gains, update_roots[0], scalar_sum[0], elements[0])
    new_attn_in = apply_update(
        attention_in,
        update_attn_in.reshape(attention_in.shape),
        update_roots[1],
        scalar_sum[1],
        elements[1],
    )
    new_attn_out = apply_update(
        attention_out, update_attn_out, update_roots[2], scalar_sum[2], elements[2]
    )
    new_router = apply_update(
        router_weight, update_router, update_roots[3], scalar_sum[3], elements[3]
    )
    new_shared_in = apply_update(
        shared_in,
        update_shared_in.reshape(shared_in.shape),
        update_roots[4],
        scalar_sum[4],
        elements[4],
    )
    new_shared_down = apply_update(
        shared_down, update_shared_down, update_roots[5], scalar_sum[5], elements[5]
    )
    new_expert_in = apply_update(
        expert_in,
        update_expert_in.reshape(expert_in.shape),
        update_roots[6],
        scalar_sum[6],
        elements[6],
    )
    new_expert_down = apply_update(
        expert_down,
        update_expert_down.reshape(expert_down.shape),
        update_roots[7],
        scalar_sum[7],
        elements[7],
    )
    new_model_stats = jnp.concatenate(
        [gain_state, jnp.stack([rows_attn_in, rows_shared_in, cols_attn_out, cols_shared_down])],
        axis=0,
    )
    attn_cols_new = cols_attn_in.reshape(3, local_cols)
    new_head_stats = jnp.concatenate([attn_cols_new[0:2], rows_attn_out[None]], axis=0)
    new_value_columns = attn_cols_new[2]
    new_hidden_stats = jnp.concatenate(
        [cols_shared_in.reshape(2, ff_local), rows_shared_down[None]], axis=0
    )
    new_expert_model_stats = jnp.stack([rows_expert_in, cols_expert_down])[None]
    new_expert_hidden_stats = jnp.concatenate(
        [cols_expert_in.reshape(2, fe_local), rows_expert_down[None]], axis=0
    )[None]
    return (
        layer_out.astype(jnp.bfloat16)[None],
        input_grad[None],
        own_gains,
        own_attn_in,
        own_attn_out,
        own_router,
        own_shared_in,
        own_shared_down,
        own_expert_in,
        own_expert_down,
        new_gains,
        new_attn_in,
        new_attn_out,
        new_router,
        new_shared_in,
        new_shared_down,
        new_expert_in,
        new_expert_down,
        new_model_stats,
        new_head_stats,
        new_value_columns,
        new_hidden_stats,
        router_new,
        new_expert_model_stats,
        new_expert_hidden_stats,
        update_roots,
    )


def solution(mesh):
    in_specs = (
        P("fsdp", "ctx", None),
        P("fsdp", "ctx"),
        P("fsdp", "ctx", None),
        P("fsdp", "ctx", None),
        P(None, ("fsdp", "ctx")),
        P(("fsdp", "ctx"), None, "tp"),
        P("tp", ("fsdp", "ctx")),
        P(("fsdp", "ctx"), None),
        P(("fsdp", "ctx"), None, "tp"),
        P("tp", ("fsdp", "ctx")),
        P("fsdp", "ctx", None, "tp"),
        P("fsdp", "tp", "ctx"),
        P(None, ("fsdp", "ctx")),
        P(None, "tp"),
        P("tp"),
        P(None, "tp"),
        P(("fsdp", "ctx"), None),
        P("fsdp", None, "ctx"),
        P("fsdp", None, "tp"),
    )
    out_specs = (
        P("fsdp", "ctx", None),
        P("fsdp", "ctx", None),
        P(None, ("fsdp", "ctx")),
        P(("fsdp", "ctx"), None, "tp"),
        P("tp", ("fsdp", "ctx")),
        P(("fsdp", "ctx"), None),
        P(("fsdp", "ctx"), None, "tp"),
        P("tp", ("fsdp", "ctx")),
        P("fsdp", "ctx", None, "tp"),
        P("fsdp", "tp", "ctx"),
        P(None, ("fsdp", "ctx")),
        P(("fsdp", "ctx"), None, "tp"),
        P("tp", ("fsdp", "ctx")),
        P(("fsdp", "ctx"), None),
        P(("fsdp", "ctx"), None, "tp"),
        P("tp", ("fsdp", "ctx")),
        P("fsdp", "ctx", None, "tp"),
        P("fsdp", "tp", "ctx"),
        P(None, ("fsdp", "ctx")),
        P(None, "tp"),
        P("tp"),
        P(None, "tp"),
        P(("fsdp", "ctx"), None),
        P("fsdp", None, "ctx"),
        P("fsdp", None, "tp"),
        P(),
    )
    return jax.shard_map(local, mesh=mesh, in_specs=in_specs, out_specs=out_specs, check_vma=False)
```

```python
import jax
import jax.numpy as jnp
from jax import lax
from jax.sharding import PartitionSpec as P
from jax.experimental import pallas as pl
from jax.experimental.pallas import tpu as pltpu

D = 768
HD = 64
FF = 2048
FE = 2048
WINDOW = 1024
HH = 768


EPSILON = 1e-06
TINY_SQUARE = 1e-30
SCALE_FLOOR = 0.001
DECAY_RATE = 0.5
CLIP_LIMIT = 0.5
STEP_RATE = 0.5


def from_behind(value, axis, steps):
    count = lax.axis_size(axis)
    leading, last = (max(0, -steps), min(count, count - steps))
    return lax.ppermute(value, axis, [(source, source + steps) for source in range(leading, last)])


def rms_norm(values, gain_vec):
    inv_rms = lax.rsqrt(jnp.mean(values * values, axis=-1, keepdims=True) + EPSILON)
    return values * inv_rms * gain_vec


def swiglu(gate_up):
    return jax.nn.silu(gate_up[:, 0]) * gate_up[:, 1]


def rotate(values, cosine, sine_tab):
    half_dim = values.shape[-1] // 2
    first_half = values[..., :half_dim]
    second_half = values[..., half_dim:]
    cos_b = cosine[:, None, :]
    sin_b = sine_tab[:, None, :]
    return jnp.concatenate(
        [first_half * cos_b - second_half * sin_b, second_half * cos_b + first_half * sin_b],
        axis=-1,
    )


def slot_tables(block_routes, experts, capacity):
    flat_routes = block_routes.reshape(-1)
    route_count = flat_routes.shape[0]
    onehot = (flat_routes[:, None] == jnp.arange(experts, dtype=jnp.int32)[None, :]).astype(
        jnp.int32
    )
    rank_in = jnp.sum(
        (jnp.cumsum(onehot, axis=0, dtype=jnp.int32) - 1) * onehot, axis=1, dtype=jnp.int32
    )
    slot_index = flat_routes * capacity + rank_in
    owner_route = (
        jnp.zeros((experts * capacity,), jnp.int32)
        .at[slot_index]
        .set(jnp.arange(route_count, dtype=jnp.int32))
    )
    filled = jnp.zeros((experts * capacity,), jnp.int32).at[slot_index].set(1)
    return (slot_index, owner_route, filled)


def block_view(queries, keys_ext, values_ext, seg_own, seg_ext, start_row, base_pos):
    block_len = queries.shape[0]
    block_rows = min(512, block_len)
    query_rows = lax.dynamic_slice_in_dim(queries, start_row, block_rows, 0)
    key_rows = lax.dynamic_slice_in_dim(
        keys_ext, start_row + block_len - WINDOW, block_rows + WINDOW, 0
    )
    value_rows = lax.dynamic_slice_in_dim(
        values_ext, start_row + block_len - WINDOW, block_rows + WINDOW, 0
    )
    scores = (
        jnp.einsum("qhd,khd->hqk", query_rows, key_rows, preferred_element_type=jnp.float32) * 0.125
    )
    query_pos = start_row + jnp.arange(block_rows, dtype=jnp.int32)
    key_pos = start_row - WINDOW + jnp.arange(block_rows + WINDOW, dtype=jnp.int32)
    distance = query_pos[:, None] - key_pos[None, :]
    seg_query = lax.dynamic_slice_in_dim(seg_own, start_row, block_rows, 0)
    seg_key = lax.dynamic_slice_in_dim(
        seg_ext, start_row + block_len - WINDOW, block_rows + WINDOW, 0
    )
    allowed = (
        (distance >= 0)
        & (distance < WINDOW)
        & (seg_query[:, None] == seg_key[None, :])
        & (key_pos[None, :] + base_pos >= 0)
    )
    return (query_rows, key_rows, value_rows, jnp.where(allowed[None], scores, -1e30), allowed)


def factored_update(
    grad_mat, rows_old, cols_old, row_sums, col_sums, row_total, col_total, old_total, square_total
):
    rows_new = DECAY_RATE * rows_old + (1.0 - DECAY_RATE) * row_sums / col_total
    cols_new = DECAY_RATE * cols_old + (1.0 - DECAY_RATE) * col_sums / row_total
    mean_rows = (DECAY_RATE * old_total + (1.0 - DECAY_RATE) * square_total / col_total) / row_total
    second_moment = rows_new[:, None] * cols_new[None, :] / mean_rows
    return (grad_mat * lax.rsqrt(second_moment), rows_new, cols_new)


def apply_update(weight, update, update_root, square_sum, elements):
    param_scale = jnp.maximum(SCALE_FLOOR, jnp.sqrt(square_sum / elements))
    return weight - STEP_RATE * param_scale * update / jnp.maximum(1.0, update_root / CLIP_LIMIT)


def butterfly_partners():
    partners = []
    here = [lax.axis_index(name) for name in ("fsdp", "ctx", "tp")]
    for axis_number, name in enumerate(("fsdp", "ctx", "tp")):
        size = lax.axis_size(name)
        step = 1
        while step < size:
            bit = (here[axis_number] // step) % 2
            other = list(here)
            other[axis_number] = here[axis_number] + step * (1 - 2 * bit)
            partners.append(tuple(other))
            step *= 2
    return partners


def butterfly_kernel(x_ref, o_ref, stage, inbox, send_sems, recv_sems):
    partners = butterfly_partners()
    barrier = pltpu.get_barrier_semaphore()
    for partner in partners:
        pl.semaphore_signal(
            barrier, 1, device_id=partner, device_id_type=pl.DeviceIdType.MESH
        )
    pl.semaphore_wait(barrier, len(partners))
    acc = x_ref[...]
    for round_number, partner in enumerate(partners):
        stage[round_number] = acc
        copy = pltpu.make_async_remote_copy(
            src_ref=stage.at[round_number],
            dst_ref=inbox.at[round_number],
            send_sem=send_sems.at[round_number],
            recv_sem=recv_sems.at[round_number],
            device_id=partner,
            device_id_type=pl.DeviceIdType.MESH,
        )
        copy.start()
        copy.wait()
        acc = stage[round_number] + inbox[round_number]
    o_ref[...] = acc


def butterfly_sum(values, collective_id):
    flat = jnp.concatenate([v.reshape(-1).astype(jnp.float32) for v in values])
    size = flat.shape[0]
    rows = -(-size // 1024) * 8
    block = jnp.pad(flat, (0, rows * 128 - size)).reshape(rows, 128)
    rounds = sum(
        max(1, lax.axis_size(name)).bit_length() - 1 for name in ("fsdp", "ctx", "tp")
    )
    total = pl.pallas_call(
        butterfly_kernel,
        out_shape=jax.ShapeDtypeStruct((rows, 128), jnp.float32),
        in_specs=[pl.BlockSpec(memory_space=pltpu.VMEM)],
        out_specs=pl.BlockSpec(memory_space=pltpu.VMEM),
        scratch_shapes=[
            pltpu.VMEM((rounds, rows, 128), jnp.float32),
            pltpu.VMEM((rounds, rows, 128), jnp.float32),
            pltpu.SemaphoreType.DMA((rounds,)),
            pltpu.SemaphoreType.DMA((rounds,)),
        ],
        compiler_params=pltpu.CompilerParams(collective_id=collective_id, has_side_effects=True),
    )(block).reshape(-1)
    results = []
    offset = 0
    for v in values:
        results.append(total[offset : offset + v.size].reshape(v.shape))
        offset += v.size
    return results


def halving_kernel(x_ref, o_ref, stage_one, stage_two, inbox_one, inbox_two, inbox_three, sems):
    rows = o_ref.shape[0]
    chunk = 64
    fsdp_here = lax.axis_index("fsdp")
    ctx_here = lax.axis_index("ctx")
    tp_here = lax.axis_index("tp")
    bit_low = fsdp_here % 2
    bit_high = (fsdp_here // 2) % 2
    partners = [
        (fsdp_here, 1 - ctx_here, tp_here),
        (fsdp_here + 1 - 2 * bit_low, ctx_here, tp_here),
        (fsdp_here + 2 - 4 * bit_high, ctx_here, tp_here),
    ]
    barrier = pltpu.get_barrier_semaphore()
    for partner in partners:
        pl.semaphore_signal(barrier, 1, device_id=partner, device_id_type=pl.DeviceIdType.MESH)
    pl.semaphore_wait(barrier, len(partners))

    def swap(src, dst, number, partner):
        copy = pltpu.make_async_remote_copy(
            src_ref=src,
            dst_ref=dst,
            send_sem=sems.at[0, number],
            recv_sem=sems.at[1, number],
            device_id=partner,
            device_id_type=pl.DeviceIdType.MESH,
        )
        copy.start()
        copy.wait()

    swap(x_ref.at[:, pl.ds(1 - ctx_here, 1)], inbox_one, 0, partners[0])

    @pl.loop(0, rows // chunk)
    def _(step):
        part = pl.ds(pl.multiple_of(step * chunk, chunk), chunk)
        for high in range(2):
            for low in range(2):
                stage_one[high, low, part] = (
                    x_ref[2 * high + low, ctx_here, part] + inbox_one[2 * high + low, 0, part]
                )

    swap(stage_one.at[:, pl.ds(1 - bit_low, 1)], inbox_two, 1, partners[1])

    @pl.loop(0, rows // chunk)
    def _(step):
        part = pl.ds(pl.multiple_of(step * chunk, chunk), chunk)
        for high in range(2):
            stage_two[high, part] = stage_one[high, bit_low, part] + inbox_two[high, 0, part]

    swap(stage_two.at[pl.ds(1 - bit_high, 1)], inbox_three, 2, partners[2])

    @pl.loop(0, rows // chunk)
    def _(step):
        part = pl.ds(pl.multiple_of(step * chunk, chunk), chunk)
        o_ref[part] = stage_two[bit_high, part] + inbox_three[0, part]


def halving_scatter(packed, collective_id):
    count, width = packed.shape
    rows = -(-width // (128 * 64)) * 64
    block = jnp.pad(packed, ((0, 0), (0, rows * 128 - width))).reshape(count // 2, 2, rows, 128)
    own = pl.pallas_call(
        halving_kernel,
        out_shape=jax.ShapeDtypeStruct((rows, 128), jnp.float32),
        in_specs=[pl.BlockSpec(memory_space=pltpu.VMEM)],
        out_specs=pl.BlockSpec(memory_space=pltpu.VMEM),
        scratch_shapes=[
            pltpu.VMEM((2, 2, rows, 128), jnp.float32),
            pltpu.VMEM((2, rows, 128), jnp.float32),
            pltpu.VMEM((count // 2, 1, rows, 128), jnp.float32),
            pltpu.VMEM((2, 1, rows, 128), jnp.float32),
            pltpu.VMEM((1, rows, 128), jnp.float32),
            pltpu.SemaphoreType.DMA((2, 3)),
        ],
        compiler_params=pltpu.CompilerParams(
            collective_id=collective_id, has_side_effects=True, vmem_limit_bytes=60 * 1024 * 1024
        ),
    )(block)
    return own.reshape(-1)[:width]


def gather_kernel(x_ref, o_ref, inbox, send_sems, recv_sems):
    fsdp_here = lax.axis_index("fsdp")
    ctx_here = lax.axis_index("ctx")
    tp_here = lax.axis_index("tp")
    ctx_count = lax.axis_size("ctx")
    count = lax.axis_size("fsdp") * ctx_count
    me = fsdp_here * ctx_count + ctx_here
    peers = []
    for offset in range(1, count):
        other = (me + offset) % count
        peers.append((other // ctx_count, other % ctx_count, tp_here))
    barrier = pltpu.get_barrier_semaphore()
    for peer in peers:
        pl.semaphore_signal(barrier, 1, device_id=peer, device_id_type=pl.DeviceIdType.MESH)
    pl.semaphore_wait(barrier, len(peers))
    copies = []
    for number, peer in enumerate(peers):
        copy = pltpu.make_async_remote_copy(
            src_ref=x_ref,
            dst_ref=inbox.at[me],
            send_sem=send_sems.at[number],
            recv_sem=recv_sems.at[me],
            device_id=peer,
            device_id_type=pl.DeviceIdType.MESH,
        )
        copy.start()
        copies.append(copy)
    o_ref[me] = x_ref[...]
    for copy in copies:
        copy.wait_send()
    for offset in range(1, count):
        source = (me + count - offset) % count
        pltpu.make_async_remote_copy(
            src_ref=x_ref,
            dst_ref=inbox.at[source],
            send_sem=send_sems.at[0],
            recv_sem=recv_sems.at[source],
            device_id=peers[0],
            device_id_type=pl.DeviceIdType.MESH,
        ).wait_recv()
        o_ref[source] = inbox[source]


def gather_shards(flat, collective_id):
    size = flat.shape[0]
    rows = -(-size // 2048) * 16
    block = jnp.pad(flat, (0, rows * 128 - size)).reshape(rows, 128)
    count = lax.axis_size("fsdp") * lax.axis_size("ctx")
    full = pl.pallas_call(
        gather_kernel,
        out_shape=jax.ShapeDtypeStruct((count, rows, 128), flat.dtype),
        in_specs=[pl.BlockSpec(memory_space=pltpu.VMEM)],
        out_specs=pl.BlockSpec(memory_space=pltpu.VMEM),
        scratch_shapes=[
            pltpu.VMEM((count, rows, 128), flat.dtype),
            pltpu.SemaphoreType.DMA((count - 1,)),
            pltpu.SemaphoreType.DMA((count,)),
        ],
        compiler_params=pltpu.CompilerParams(collective_id=collective_id, has_side_effects=True),
    )(block)
    return full.reshape(count, rows * 128)[:, :size]


def swiglu_experts(gate_up):
    return jax.nn.silu(gate_up[:, :, 0]) * gate_up[:, :, 1]


def gather_packed(pieces, axes, use_kernel=False):
    flat = jnp.concatenate([piece.reshape(-1) for piece, _ in pieces])
    if use_kernel:
        full = gather_shards(flat, 4)
    else:
        full = lax.all_gather(flat, axes, axis=0, tiled=False)
    count = full.shape[0]
    results = []
    offset = 0
    for piece, dim in pieces:
        size = piece.size
        part = full[:, offset : offset + size].reshape((count,) + piece.shape)
        offset += size
        part = jnp.moveaxis(part, 0, dim)
        shape = list(piece.shape)
        shape[dim] *= count
        results.append(part.reshape(shape))
    return results


def scatter_packed(pieces, axes, count, use_kernel=False):
    columns = []
    local_shapes = []
    for grad, dim in pieces:
        shape = grad.shape
        split = shape[:dim] + (count, shape[dim] // count) + shape[dim + 1 :]
        local_shapes.append(shape[:dim] + (shape[dim] // count,) + shape[dim + 1 :])
        part = jnp.moveaxis(grad.reshape(split), dim, 0)
        columns.append(part.reshape(count, -1))
    packed = jnp.concatenate(columns, axis=1)
    if use_kernel:
        own = halving_scatter(packed, 3)
    else:
        width = packed.shape[1]
        rows = -(-width // 1024) * 8
        packed = jnp.pad(packed, ((0, 0), (0, rows * 128 - width))).reshape(count * rows, 128)
        own = lax.psum_scatter(packed, axes, scatter_dimension=0, tiled=True).reshape(-1)
    results = []
    offset = 0
    for local_shape in local_shapes:
        size = 1
        for extent in local_shape:
            size *= extent
        results.append(own[offset : offset + size].reshape(local_shape))
        offset += size
    return results


def experts_dense(normed_two, grad_out, weights, expert_in_all, expert_down_all):
    gate_up = jnp.einsum(
        "td,edgf->etgf", normed_two, expert_in_all, preferred_element_type=jnp.float32
    )
    act, act_back = jax.vjp(swiglu_experts, gate_up)
    hidden = act.astype(jnp.bfloat16)
    outs = jnp.einsum("etf,efd->etd", hidden, expert_down_all, preferred_element_type=jnp.float32)
    weights_e = weights.T[:, :, None]
    combined = jnp.sum(weights_e * outs, axis=0)
    gate_dots = jnp.sum(outs * grad_out[None], axis=-1).T
    grad_outs = (weights_e * grad_out[None]).astype(jnp.bfloat16)
    grad_hidden = jnp.einsum(
        "etd,efd->etf", grad_outs, expert_down_all, preferred_element_type=jnp.float32
    )
    grad_gate_up = act_back(grad_hidden)[0].astype(jnp.bfloat16)
    grad_down = jnp.einsum("etf,etd->efd", hidden, grad_outs, preferred_element_type=jnp.float32)
    grad_in = jnp.einsum(
        "td,etgf->edgf", normed_two, grad_gate_up, preferred_element_type=jnp.float32
    )
    grad_rows = jnp.einsum(
        "etgf,edgf->td", grad_gate_up, expert_in_all, preferred_element_type=jnp.float32
    )
    return combined, gate_dots, grad_rows, grad_in, grad_down


def experts_routed(
    normed_two, grad_out, route_rows, gate_probs, expert_in_low, expert_down_low, capacity
):
    block_len, model_width = normed_two.shape
    experts = lax.axis_size("fsdp")
    slot_index, owner_route, filled = slot_tables(route_rows, experts, capacity)
    fill_mask = filled.astype(jnp.bfloat16)[:, None]
    route_grads = (
        (gate_probs[:, :, None] * grad_out[:, None, :])
        .astype(jnp.bfloat16)
        .reshape(2 * block_len, model_width)
    )
    send_rows = jnp.concatenate(
        [normed_two[owner_route // 2] * fill_mask, route_grads[owner_route] * fill_mask], axis=1
    ).reshape(experts, capacity, 2 * model_width)
    exchange = lambda rows: lax.all_to_all(rows, "fsdp", split_axis=0, concat_axis=0, tiled=True)
    pair_count = lax.axis_size("tp")
    swap = lambda rows: lax.ppermute(
        rows, "tp", [(index, index + 1 - 2 * (index % 2)) for index in range(pair_count)]
    )
    half = capacity // 2
    side = lax.axis_index("tp") % 2
    mine = exchange(lax.dynamic_slice_in_dim(send_rows, side * half, half, 1))
    received_both = jnp.concatenate([mine, swap(mine)], axis=1).reshape(
        experts * capacity, 2 * model_width
    )
    received = received_both[:, :model_width]
    grad_received = received_both[:, model_width:]
    gate_up = jnp.einsum("rd,dgf->rgf", received, expert_in_low, preferred_element_type=jnp.float32)
    act, act_back = jax.vjp(swiglu, gate_up)
    hidden = act.astype(jnp.bfloat16)
    outs = jnp.dot(hidden, expert_down_low, preferred_element_type=jnp.float32)
    grad_hidden = jnp.einsum(
        "rd,fd->rf", grad_received, expert_down_low, preferred_element_type=jnp.float32
    )
    grad_gate_up = act_back(grad_hidden)[0].astype(jnp.bfloat16)
    grad_in = jnp.einsum("rd,rgf->dgf", received, grad_gate_up, preferred_element_type=jnp.float32)
    grad_down = jnp.einsum("rf,rd->fd", hidden, grad_received, preferred_element_type=jnp.float32)
    grad_expert_rows = jnp.einsum(
        "rgf,dgf->rd", grad_gate_up, expert_in_low, preferred_element_type=jnp.float32
    )
    results = jnp.concatenate([outs, grad_expert_rows], axis=1).reshape(
        experts, capacity, 2 * model_width
    )
    pair_sum = results[:, :half] + swap(results[:, half:])
    held = exchange(pair_sum.astype(jnp.bfloat16)).reshape(experts * half, 2 * model_width)
    slot_expert = slot_index // capacity
    slot_rank = slot_index % capacity
    in_side = (slot_rank // half) == side
    local_slot = slot_expert * half + slot_rank % half
    returned = jnp.where(in_side[:, None], held[local_slot].astype(jnp.float32), 0.0)
    route_out = returned[:, :model_width].reshape(block_len, 2, model_width)
    grad_routes = returned[:, model_width:].reshape(block_len, 2, model_width)
    combined = jnp.sum(gate_probs[:, :, None] * route_out, axis=1)
    gate_dots = jnp.sum(grad_out[:, None, :] * route_out, axis=-1)
    grad_rows = jnp.sum(grad_routes, axis=1)
    return combined, gate_dots, grad_rows, grad_in, grad_down


def local(
    layer_input,
    segments,
    routes,
    cotangent,
    gains,
    attention_in,
    attention_out,
    router_weight,
    shared_in,
    shared_down,
    expert_in,
    expert_down,
    model_stats,
    head_stats,
    value_columns,
    hidden_stats,
    router_state,
    expert_model_stats,
    expert_hidden_stats,
):
    block_len = layer_input.shape[1]
    model_width = layer_input.shape[2]
    experts = router_weight.shape[1]
    dense_experts = False
    capacity = min(block_len, 4 * block_len // experts)
    ctx_index = lax.axis_index("ctx")
    tp_index = lax.axis_index("tp")
    fsdp_index = lax.axis_index("fsdp")
    shard_index = lax.axis_index(("fsdp", "ctx"))
    shard_count = lax.axis_size(("fsdp", "ctx"))
    ctx_count = lax.axis_size("ctx")
    base_pos = ctx_index * block_len
    low = lambda v: v.astype(jnp.bfloat16)
    gain_low, attn_in_low = gather_packed(
        [(low(gains), 1), (low(attention_in), 0)], ("fsdp", "ctx"), shard_count <= 8
    )
    later = [
        (low(attention_out), 1),
        (low(router_weight), 0),
        (low(shared_in), 0),
        (low(shared_down), 1),
    ]
    if dense_experts:
        later += [(low(expert_in), 0), (low(expert_down), 0)]
    later_full = gather_packed(later, ("fsdp", "ctx"))
    attn_out_low, router_low, shared_in_low, shared_down_low = later_full[:4]
    if dense_experts:
        fe_local = expert_down.shape[1]
        expert_in_all = later_full[4].reshape(experts, model_width, 2, fe_local)
        expert_down_all = (
            later_full[5]
            .reshape(experts, ctx_count, fe_local, model_width // ctx_count)
            .transpose(0, 2, 1, 3)
            .reshape(experts, fe_local, model_width)
        )
    else:
        expert_in_low = lax.all_gather(low(expert_in), "ctx", axis=1, tiled=True)[0]
        expert_down_low = lax.all_gather(low(expert_down), "ctx", axis=2, tiled=True)[0]
    residual = layer_input[0].astype(jnp.float32)
    gain_one = gain_low[0].astype(jnp.float32)
    gain_two = gain_low[1].astype(jnp.float32)
    normed_one, norm_one_back = jax.vjp(rms_norm, residual, gain_one)
    normed_one = normed_one.astype(jnp.bfloat16)
    projected = jnp.einsum(
        "td,dgf->tgf", normed_one, attn_in_low, preferred_element_type=jnp.float32
    )
    local_cols = projected.shape[2]
    local_heads = local_cols // HD
    half_dim = HD // 2
    frequency = 10000.0 ** (-jnp.arange(half_dim, dtype=jnp.float32) / half_dim)
    angles = (base_pos + jnp.arange(block_len, dtype=jnp.int32)).astype(jnp.float32)[
        :, None
    ] * frequency[None, :]
    cosine = jnp.cos(angles)
    sine_tab = jnp.sin(angles)
    queries = rotate(projected[:, 0].reshape(block_len, local_heads, HD), cosine, sine_tab).astype(
        jnp.bfloat16
    )
    keys_own = rotate(projected[:, 1].reshape(block_len, local_heads, HD), cosine, sine_tab).astype(
        jnp.bfloat16
    )
    values_own = projected[:, 2].reshape(block_len, local_heads, HD).astype(jnp.bfloat16)
    seg_own = segments[0].astype(jnp.bfloat16)
    keys_prev, values_prev, seg_prev = from_behind((keys_own, values_own, seg_own), "ctx", 1)
    keys_ext = jnp.concatenate([keys_prev, keys_own], axis=0)
    values_ext = jnp.concatenate([values_prev, values_own], axis=0)
    seg_ext = jnp.concatenate([seg_prev, seg_own], axis=0)
    block_rows = min(512, block_len)
    block_total = block_len // block_rows
    starts = jnp.arange(block_total, dtype=jnp.int32) * block_rows

    def forward_block(start_row):
        query_rows, key_rows, value_rows, masked, allowed = block_view(
            queries, keys_ext, values_ext, seg_own, seg_ext, start_row, base_pos
        )
        row_max = jnp.max(masked, axis=-1, keepdims=True)
        exp_terms = jnp.where(allowed[None], jnp.exp(masked - row_max), 0.0)
        row_total = jnp.sum(exp_terms, axis=-1, keepdims=True)
        attn_probs = (exp_terms / row_total).astype(jnp.bfloat16)
        attended = jnp.einsum(
            "hqk,khd->qhd", attn_probs, value_rows, preferred_element_type=jnp.float32
        )
        return (attended, row_max + jnp.log(row_total))

    attended, log_totals = lax.map(forward_block, starts)
    mixed_heads = attended.reshape(block_len, local_cols).astype(jnp.bfloat16)
    attn_total = lax.psum(
        jnp.dot(mixed_heads, attn_out_low, preferred_element_type=jnp.float32), "tp"
    )
    after_attn = residual + attn_total
    normed_two, norm_two_back = jax.vjp(rms_norm, after_attn, gain_two)
    normed_two = normed_two.astype(jnp.bfloat16)
    logits = jnp.dot(normed_two, router_low, preferred_element_type=jnp.float32)
    route_rows = routes[0]
    onehot = (route_rows[:, :, None] == jnp.arange(experts, dtype=jnp.int32)[None, None, :]).astype(
        jnp.float32
    )
    picked = jnp.sum(onehot * logits[:, None, :], axis=-1)
    gate_probs = jax.nn.softmax(picked, axis=-1)
    upstream = cotangent[0]
    grad_out = upstream.astype(jnp.float32)
    if dense_experts:
        weights = jnp.sum(gate_probs[:, :, None] * onehot, axis=1)
        combined, dots_e, grad_rows, grad_expert_in, grad_expert_down = experts_dense(
            normed_two, grad_out, weights, expert_in_all, expert_down_all
        )
        gate_dots = jnp.sum(onehot * dots_e[:, None, :], axis=-1)
    else:
        combined, gate_dots, grad_rows, grad_expert_in, grad_expert_down = experts_routed(
            normed_two,
            grad_out,
            route_rows,
            gate_probs,
            expert_in_low,
            expert_down_low,
            capacity,
        )
    shared_gate_up = jnp.einsum(
        "td,dgf->tgf", normed_two, shared_in_low, preferred_element_type=jnp.float32
    )
    shared_act, shared_act_back = jax.vjp(swiglu, shared_gate_up)
    shared_hidden = shared_act.astype(jnp.bfloat16)
    shared_out = jnp.dot(shared_hidden, shared_down_low, preferred_element_type=jnp.float32)
    grad_shared_hidden = jnp.einsum(
        "td,fd->tf", upstream, shared_down_low, preferred_element_type=jnp.float32
    )
    grad_shared_gate_up = shared_act_back(grad_shared_hidden)[0].astype(jnp.bfloat16)
    partial_two = (
        jnp.einsum(
            "tgf,dgf->td", grad_shared_gate_up, shared_in_low, preferred_element_type=jnp.float32
        )
        + grad_rows
    )
    branch_total, grad_normed_part, gate_total = lax.psum(
        (shared_out + combined, partial_two, gate_dots), "tp"
    )
    layer_out = after_attn + branch_total
    grad_picked = gate_probs * (
        gate_total - jnp.sum(gate_probs * gate_total, axis=-1, keepdims=True)
    )
    grad_logits = jnp.sum(grad_picked[:, :, None] * onehot, axis=1).astype(jnp.bfloat16)
    grad_shared_in = jnp.einsum(
        "td,tgf->dgf", normed_two, grad_shared_gate_up, preferred_element_type=jnp.float32
    )
    grad_shared_down = jnp.einsum(
        "tf,td->fd", shared_hidden, upstream, preferred_element_type=jnp.float32
    )
    grad_router = jnp.einsum(
        "td,te->de", normed_two, grad_logits, preferred_element_type=jnp.float32
    )
    grad_normed_two = grad_normed_part + jnp.einsum(
        "te,de->td", grad_logits, router_low, preferred_element_type=jnp.float32
    )
    grad_after, grad_gain_two = norm_two_back(grad_normed_two)
    grad_after = grad_after + grad_out
    grad_attn_low = grad_after.astype(jnp.bfloat16)
    grad_attn_out = jnp.einsum(
        "tc,td->cd", mixed_heads, grad_attn_low, preferred_element_type=jnp.float32
    )
    first_grads = [
        (grad_attn_out, 1),
        (grad_router, 0),
        (grad_shared_in, 0),
        (grad_shared_down, 1),
        (grad_gain_two, 0),
    ]
    if dense_experts:
        fe_local = expert_down.shape[1]
        first_grads += [
            (grad_expert_in.reshape(shard_count * expert_in.shape[1], 2, fe_local), 0),
            (
                grad_expert_down.reshape(experts, fe_local, ctx_count, model_width // ctx_count)
                .transpose(0, 2, 1, 3)
                .reshape(shard_count * fe_local, model_width // ctx_count),
                0,
            ),
        ]
    if not dense_experts:
        own_expert_in = lax.psum_scatter(grad_expert_in[None], "ctx", scatter_dimension=1, tiled=True)
        own_expert_down = lax.psum_scatter(
            grad_expert_down[None], "ctx", scatter_dimension=2, tiled=True
        )
    grad_heads = (
        jnp.einsum("td,cd->tc", grad_attn_low, attn_out_low, preferred_element_type=jnp.float32)
        .astype(jnp.bfloat16)
        .reshape(block_len, local_heads, HD)
    )

    def backward_block(block_number, running):
        grad_keys, grad_values, grad_queries = running
        start_row = block_number * block_rows
        query_rows, key_rows, value_rows, masked, allowed = block_view(
            queries, keys_ext, values_ext, seg_own, seg_ext, start_row, base_pos
        )
        log_total = lax.dynamic_index_in_dim(log_totals, block_number, 0, keepdims=False)
        attn_probs = jnp.where(allowed[None], jnp.exp(masked - log_total), 0.0)
        grad_block = lax.dynamic_slice_in_dim(grad_heads, start_row, block_rows, 0)
        grad_probs = jnp.einsum(
            "qhd,khd->hqk", grad_block, value_rows, preferred_element_type=jnp.float32
        )
        inner_sum = jnp.sum(attn_probs * grad_probs, axis=-1, keepdims=True)
        grad_scores = (attn_probs * (grad_probs - inner_sum)).astype(jnp.bfloat16)
        grad_query_rows = (
            jnp.einsum("hqk,khd->qhd", grad_scores, key_rows, preferred_element_type=jnp.float32)
            * 0.125
        )
        grad_key_rows = (
            jnp.einsum("hqk,qhd->khd", grad_scores, query_rows, preferred_element_type=jnp.float32)
            * 0.125
        )
        grad_value_rows = jnp.einsum(
            "hqk,qhd->khd",
            attn_probs.astype(jnp.bfloat16),
            grad_block,
            preferred_element_type=jnp.float32,
        )
        key_offset = start_row + block_len - WINDOW
        grad_keys = lax.dynamic_update_slice_in_dim(
            grad_keys,
            lax.dynamic_slice_in_dim(grad_keys, key_offset, block_rows + WINDOW, 0) + grad_key_rows,
            key_offset,
            0,
        )
        grad_values = lax.dynamic_update_slice_in_dim(
            grad_values,
            lax.dynamic_slice_in_dim(grad_values, key_offset, block_rows + WINDOW, 0)
            + grad_value_rows,
            key_offset,
            0,
        )
        grad_queries = lax.dynamic_update_slice_in_dim(grad_queries, grad_query_rows, start_row, 0)
        return (grad_keys, grad_values, grad_queries)

    zero_ext = jnp.zeros((2 * block_len, local_heads, HD), jnp.float32)
    zero_own = jnp.zeros((block_len, local_heads, HD), jnp.float32)
    grad_keys, grad_values, grad_queries = lax.fori_loop(
        0, block_total, backward_block, (zero_ext, zero_ext, zero_own)
    )
    rim_keys, rim_values = (
        from_behind(grad_keys[:block_len].astype(jnp.bfloat16), "ctx", -1).astype(jnp.float32),
        from_behind(grad_values[:block_len].astype(jnp.bfloat16), "ctx", -1).astype(jnp.float32),
    )
    grad_keys_own = grad_keys[block_len:] + rim_keys
    grad_values_own = grad_values[block_len:] + rim_values
    grad_query_raw = rotate(grad_queries, cosine, -sine_tab)
    grad_key_raw = rotate(grad_keys_own, cosine, -sine_tab)
    grad_projected = (
        jnp.stack([grad_query_raw, grad_key_raw, grad_values_own], axis=1)
        .reshape(block_len, 3, local_cols)
        .astype(jnp.bfloat16)
    )
    grad_attn_in = jnp.einsum(
        "td,tgf->dgf", normed_one, grad_projected, preferred_element_type=jnp.float32
    )
    partial_one = jnp.einsum(
        "tgf,dgf->td", grad_projected, attn_in_low, preferred_element_type=jnp.float32
    )
    tp_one = lax.psum(partial_one, "tp")
    halving = lax.axis_size("fsdp") == 4 and ctx_count == 2
    all_own = scatter_packed(
        first_grads + [(grad_attn_in, 0)],
        ("fsdp", "ctx"),
        shard_count,
        halving,
    )
    own_attn_out, own_router, own_shared_in, own_shared_down, own_gain_two = all_own[:5]
    own_attn_in = all_own[-1]
    grad_residual, grad_gain_one = norm_one_back(tp_one + 0.0 * own_attn_in[0, 0, 0])
    input_grad = grad_after + grad_residual
    if dense_experts:
        own_expert_in = all_own[5][None]
        own_expert_down = all_own[6][None]
    lead_tp = (tp_index == 0).astype(jnp.float32)
    first_shard = (shard_index == 0).astype(jnp.float32)
    first_ctx = (ctx_index == 0).astype(jnp.float32)
    d_local = gains.shape[1]
    ff_local = shared_down.shape[0]
    fe_local = expert_down.shape[1]
    d_quarter = expert_in.shape[1]
    square_attn_in = own_attn_in * own_attn_in + TINY_SQUARE
    square_attn_out = own_attn_out * own_attn_out + TINY_SQUARE
    square_shared_in = own_shared_in * own_shared_in + TINY_SQUARE
    square_shared_down = own_shared_down * own_shared_down + TINY_SQUARE
    square_expert_in = own_expert_in[0] * own_expert_in[0] + TINY_SQUARE
    square_expert_down = own_expert_down[0] * own_expert_down[0] + TINY_SQUARE
    model_part = lax.dynamic_update_slice(
        jnp.zeros((4, D), jnp.float32),
        jnp.stack(
            [
                jnp.sum(square_attn_in, axis=(1, 2)),
                jnp.sum(square_shared_in, axis=(1, 2)),
                jnp.sum(square_attn_out, axis=0),
                jnp.sum(square_shared_down, axis=0),
            ]
        ),
        (0, shard_index * d_local),
    )
    head_part = lax.dynamic_update_slice(
        jnp.zeros((4, HH), jnp.float32),
        jnp.concatenate(
            [jnp.sum(square_attn_in, axis=0), jnp.sum(square_attn_out, axis=1)[None]], axis=0
        ),
        (0, tp_index * local_cols),
    )
    hidden_part = lax.dynamic_update_slice(
        jnp.zeros((3, FF), jnp.float32),
        jnp.concatenate(
            [jnp.sum(square_shared_in, axis=0), jnp.sum(square_shared_down, axis=1)[None]], axis=0
        ),
        (0, tp_index * ff_local),
    )
    expert_model_part = lax.dynamic_update_slice(
        jnp.zeros((experts, 2, D), jnp.float32),
        jnp.stack([jnp.sum(square_expert_in, axis=(1, 2)), jnp.sum(square_expert_down, axis=0)])[
            None
        ],
        (fsdp_index, 0, ctx_index * d_quarter),
    )
    expert_hidden_part = lax.dynamic_update_slice(
        jnp.zeros((experts, 3, FE), jnp.float32),
        jnp.concatenate(
            [jnp.sum(square_expert_in, axis=0), jnp.sum(square_expert_down, axis=1)[None]], axis=0
        )[None],
        (fsdp_index, 0, tp_index * fe_local),
    )
    scalar_part = jnp.stack(
        [
            lead_tp * jnp.sum(gains * gains),
            jnp.sum(attention_in * attention_in),
            jnp.sum(attention_out * attention_out),
            lead_tp * jnp.sum(router_weight * router_weight),
            jnp.sum(shared_in * shared_in),
            jnp.sum(shared_down * shared_down),
            jnp.sum(expert_in * expert_in),
            jnp.sum(expert_down * expert_down),
            lead_tp * jnp.sum(model_stats[2]),
            first_shard * jnp.sum(head_stats[2]),
            lead_tp * jnp.sum(model_stats[3]),
            first_shard * jnp.sum(hidden_stats[2]),
        ]
    )
    expert_old_part = lax.dynamic_update_slice(
        jnp.zeros((2, experts), jnp.float32),
        jnp.stack(
            [
                lead_tp * jnp.sum(expert_model_stats[0, 0]),
                first_ctx * jnp.sum(expert_hidden_stats[0, 2]),
            ]
        )[:, None],
        (0, fsdp_index),
    )
    global_sums = butterfly_sum(
        [
            model_part,
            head_part,
            hidden_part,
            expert_model_part,
            expert_hidden_part,
            scalar_part,
            expert_old_part,
            lead_tp * grad_gain_one,
        ],
        1,
    )
    (
        model_sum,
        head_sum,
        hidden_sum,
        expert_model_sum,
        expert_hidden_sum,
        scalar_sum,
        expert_old_sum,
        gain_one_sum,
    ) = global_sums
    own_gain_one = lax.dynamic_slice_in_dim(gain_one_sum, shard_index * d_local, d_local)
    own_gains = jnp.stack([own_gain_one, own_gain_two])
    shard_start = shard_index * d_local
    gain_state = DECAY_RATE * model_stats[0:2] + (1.0 - DECAY_RATE) * (
        own_gains * own_gains + TINY_SQUARE
    )
    update_gains = own_gains * lax.rsqrt(gain_state)
    router_new = DECAY_RATE * router_state + (1.0 - DECAY_RATE) * (
        own_router * own_router + TINY_SQUARE
    )
    update_router = own_router * lax.rsqrt(router_new)
    attn_cols_old = jnp.concatenate([head_stats[0:2], value_columns[None]], axis=0).reshape(-1)
    update_attn_in, rows_attn_in, cols_attn_in = factored_update(
        own_attn_in.reshape(d_local, 3 * local_cols),
        model_stats[2],
        attn_cols_old,
        lax.dynamic_slice_in_dim(model_sum[0], shard_start, d_local),
        lax.dynamic_slice_in_dim(head_sum[0:3], tp_index * local_cols, local_cols, 1).reshape(-1),
        D,
        3 * HH,
        scalar_sum[8],
        jnp.sum(model_sum[0]),
    )
    update_attn_out, rows_attn_out, cols_attn_out = factored_update(
        own_attn_out,
        head_stats[2],
        model_stats[4],
        lax.dynamic_slice_in_dim(head_sum[3], tp_index * local_cols, local_cols),
        lax.dynamic_slice_in_dim(model_sum[2], shard_start, d_local),
        HH,
        D,
        scalar_sum[9],
        jnp.sum(head_sum[3]),
    )
    update_shared_in, rows_shared_in, cols_shared_in = factored_update(
        own_shared_in.reshape(d_local, 2 * ff_local),
        model_stats[3],
        hidden_stats[0:2].reshape(-1),
        lax.dynamic_slice_in_dim(model_sum[1], shard_start, d_local),
        lax.dynamic_slice_in_dim(hidden_sum[0:2], tp_index * ff_local, ff_local, 1).reshape(-1),
        D,
        2 * FF,
        scalar_sum[10],
        jnp.sum(model_sum[1]),
    )
    update_shared_down, rows_shared_down, cols_shared_down = factored_update(
        own_shared_down,
        hidden_stats[2],
        model_stats[5],
        lax.dynamic_slice_in_dim(hidden_sum[2], tp_index * ff_local, ff_local),
        lax.dynamic_slice_in_dim(model_sum[3], shard_start, d_local),
        FF,
        D,
        scalar_sum[11],
        jnp.sum(hidden_sum[2]),
    )
    own_expert_model = lax.dynamic_index_in_dim(expert_model_sum, fsdp_index, 0, keepdims=False)
    own_expert_hidden = lax.dynamic_index_in_dim(expert_hidden_sum, fsdp_index, 0, keepdims=False)
    old_expert_totals = lax.dynamic_index_in_dim(expert_old_sum, fsdp_index, 1, keepdims=False)
    update_expert_in, rows_expert_in, cols_expert_in = factored_update(
        own_expert_in[0].reshape(d_quarter, 2 * fe_local),
        expert_model_stats[0, 0],
        expert_hidden_stats[0, 0:2].reshape(-1),
        lax.dynamic_slice_in_dim(own_expert_model[0], ctx_index * d_quarter, d_quarter),
        lax.dynamic_slice_in_dim(own_expert_hidden[0:2], tp_index * fe_local, fe_local, 1).reshape(
            -1
        ),
        D,
        2 * FE,
        old_expert_totals[0],
        jnp.sum(own_expert_model[0]),
    )
    update_expert_down, rows_expert_down, cols_expert_down = factored_update(
        own_expert_down[0],
        expert_hidden_stats[0, 2],
        expert_model_stats[0, 1],
        lax.dynamic_slice_in_dim(own_expert_hidden[2], tp_index * fe_local, fe_local),
        lax.dynamic_slice_in_dim(own_expert_model[1], ctx_index * d_quarter, d_quarter),
        FE,
        D,
        old_expert_totals[1],
        jnp.sum(own_expert_hidden[2]),
    )
    clip_part = jnp.stack(
        [
            lead_tp * jnp.sum(update_gains * update_gains),
            jnp.sum(update_attn_in * update_attn_in),
            jnp.sum(update_attn_out * update_attn_out),
            lead_tp * jnp.sum(update_router * update_router),
            jnp.sum(update_shared_in * update_shared_in),
            jnp.sum(update_shared_down * update_shared_down),
            jnp.sum(update_expert_in * update_expert_in),
            jnp.sum(update_expert_down * update_expert_down),
        ]
    )
    clip_total = butterfly_sum([clip_part], 2)[0]
    elements = jnp.array(
        [
            2 * D,
            D * 3 * HH,
            HH * D,
            D * experts,
            D * 2 * FF,
            FF * D,
            experts * D * 2 * FE,
            experts * FE * D,
        ],
        jnp.float32,
    )
    update_roots = jnp.sqrt(clip_total / elements)
    new_gains = apply_update(gains, update_gains, update_roots[0], scalar_sum[0], elements[0])
    new_attn_in = apply_update(
        attention_in,
        update_attn_in.reshape(attention_in.shape),
        update_roots[1],
        scalar_sum[1],
        elements[1],
    )
    new_attn_out = apply_update(
        attention_out, update_attn_out, update_roots[2], scalar_sum[2], elements[2]
    )
    new_router = apply_update(
        router_weight, update_router, update_roots[3], scalar_sum[3], elements[3]
    )
    new_shared_in = apply_update(
        shared_in,
        update_shared_in.reshape(shared_in.shape),
        update_roots[4],
        scalar_sum[4],
        elements[4],
    )
    new_shared_down = apply_update(
        shared_down, update_shared_down, update_roots[5], scalar_sum[5], elements[5]
    )
    new_expert_in = apply_update(
        expert_in,
        update_expert_in.reshape(expert_in.shape),
        update_roots[6],
        scalar_sum[6],
        elements[6],
    )
    new_expert_down = apply_update(
        expert_down,
        update_expert_down.reshape(expert_down.shape),
        update_roots[7],
        scalar_sum[7],
        elements[7],
    )
    new_model_stats = jnp.concatenate(
        [gain_state, jnp.stack([rows_attn_in, rows_shared_in, cols_attn_out, cols_shared_down])],
        axis=0,
    )
    attn_cols_new = cols_attn_in.reshape(3, local_cols)
    new_head_stats = jnp.concatenate([attn_cols_new[0:2], rows_attn_out[None]], axis=0)
    new_value_columns = attn_cols_new[2]
    new_hidden_stats = jnp.concatenate(
        [cols_shared_in.reshape(2, ff_local), rows_shared_down[None]], axis=0
    )
    new_expert_model_stats = jnp.stack([rows_expert_in, cols_expert_down])[None]
    new_expert_hidden_stats = jnp.concatenate(
        [cols_expert_in.reshape(2, fe_local), rows_expert_down[None]], axis=0
    )[None]
    return (
        layer_out.astype(jnp.bfloat16)[None],
        input_grad[None],
        own_gains,
        own_attn_in,
        own_attn_out,
        own_router,
        own_shared_in,
        own_shared_down,
        own_expert_in,
        own_expert_down,
        new_gains,
        new_attn_in,
        new_attn_out,
        new_router,
        new_shared_in,
        new_shared_down,
        new_expert_in,
        new_expert_down,
        new_model_stats,
        new_head_stats,
        new_value_columns,
        new_hidden_stats,
        router_new,
        new_expert_model_stats,
        new_expert_hidden_stats,
        update_roots,
    )


def solution(mesh):
    in_specs = (
        P("fsdp", "ctx", None),
        P("fsdp", "ctx"),
        P("fsdp", "ctx", None),
        P("fsdp", "ctx", None),
        P(None, ("fsdp", "ctx")),
        P(("fsdp", "ctx"), None, "tp"),
        P("tp", ("fsdp", "ctx")),
        P(("fsdp", "ctx"), None),
        P(("fsdp", "ctx"), None, "tp"),
        P("tp", ("fsdp", "ctx")),
        P("fsdp", "ctx", None, "tp"),
        P("fsdp", "tp", "ctx"),
        P(None, ("fsdp", "ctx")),
        P(None, "tp"),
        P("tp"),
        P(None, "tp"),
        P(("fsdp", "ctx"), None),
        P("fsdp", None, "ctx"),
        P("fsdp", None, "tp"),
    )
    out_specs = (
        P("fsdp", "ctx", None),
        P("fsdp", "ctx", None),
        P(None, ("fsdp", "ctx")),
        P(("fsdp", "ctx"), None, "tp"),
        P("tp", ("fsdp", "ctx")),
        P(("fsdp", "ctx"), None),
        P(("fsdp", "ctx"), None, "tp"),
        P("tp", ("fsdp", "ctx")),
        P("fsdp", "ctx", None, "tp"),
        P("fsdp", "tp", "ctx"),
        P(None, ("fsdp", "ctx")),
        P(("fsdp", "ctx"), None, "tp"),
        P("tp", ("fsdp", "ctx")),
        P(("fsdp", "ctx"), None),
        P(("fsdp", "ctx"), None, "tp"),
        P("tp", ("fsdp", "ctx")),
        P("fsdp", "ctx", None, "tp"),
        P("fsdp", "tp", "ctx"),
        P(None, ("fsdp", "ctx")),
        P(None, "tp"),
        P("tp"),
        P(None, "tp"),
        P(("fsdp", "ctx"), None),
        P("fsdp", None, "ctx"),
        P("fsdp", None, "tp"),
        P(),
    )
    return jax.shard_map(local, mesh=mesh, in_specs=in_specs, out_specs=out_specs, check_vma=False)
```

```python
import jax
import jax.numpy as jnp
from jax import lax
from jax.sharding import PartitionSpec as P
from jax.experimental import pallas as pl
from jax.experimental.pallas import tpu as pltpu

D = 768
HD = 64
FF = 2048
FE = 2048
WINDOW = 1024
HH = 768


EPSILON = 1e-06
TINY_SQUARE = 1e-30
SCALE_FLOOR = 0.001
DECAY_RATE = 0.5
CLIP_LIMIT = 0.5
STEP_RATE = 0.5


def from_behind(value, axis, steps):
    count = lax.axis_size(axis)
    leading, last = (max(0, -steps), min(count, count - steps))
    return lax.ppermute(value, axis, [(source, source + steps) for source in range(leading, last)])


def rms_norm(values, gain_vec):
    inv_rms = lax.rsqrt(jnp.mean(values * values, axis=-1, keepdims=True) + EPSILON)
    return values * inv_rms * gain_vec


def swiglu(gate_up):
    return jax.nn.silu(gate_up[:, 0]) * gate_up[:, 1]


def rotate(values, cosine, sine_tab):
    half_dim = values.shape[-1] // 2
    first_half = values[..., :half_dim]
    second_half = values[..., half_dim:]
    cos_b = cosine[:, None, :]
    sin_b = sine_tab[:, None, :]
    return jnp.concatenate(
        [first_half * cos_b - second_half * sin_b, second_half * cos_b + first_half * sin_b],
        axis=-1,
    )


def slot_tables(block_routes, experts, capacity):
    flat_routes = block_routes.reshape(-1)
    route_count = flat_routes.shape[0]
    onehot = (flat_routes[:, None] == jnp.arange(experts, dtype=jnp.int32)[None, :]).astype(
        jnp.int32
    )
    rank_in = jnp.sum(
        (jnp.cumsum(onehot, axis=0, dtype=jnp.int32) - 1) * onehot, axis=1, dtype=jnp.int32
    )
    slot_index = flat_routes * capacity + rank_in
    owner_route = (
        jnp.zeros((experts * capacity,), jnp.int32)
        .at[slot_index]
        .set(jnp.arange(route_count, dtype=jnp.int32))
    )
    filled = jnp.zeros((experts * capacity,), jnp.int32).at[slot_index].set(1)
    return (slot_index, owner_route, filled)


def block_view(queries, keys_ext, values_ext, seg_own, seg_ext, start_row, base_pos):
    block_len = queries.shape[0]
    block_rows = min(512, block_len)
    query_rows = lax.dynamic_slice_in_dim(queries, start_row, block_rows, 0)
    key_rows = lax.dynamic_slice_in_dim(
        keys_ext, start_row + block_len - WINDOW, block_rows + WINDOW, 0
    )
    value_rows = lax.dynamic_slice_in_dim(
        values_ext, start_row + block_len - WINDOW, block_rows + WINDOW, 0
    )
    scores = (
        jnp.einsum("qhd,khd->hqk", query_rows, key_rows, preferred_element_type=jnp.float32) * 0.125
    )
    query_pos = start_row + jnp.arange(block_rows, dtype=jnp.int32)
    key_pos = start_row - WINDOW + jnp.arange(block_rows + WINDOW, dtype=jnp.int32)
    distance = query_pos[:, None] - key_pos[None, :]
    seg_query = lax.dynamic_slice_in_dim(seg_own, start_row, block_rows, 0)
    seg_key = lax.dynamic_slice_in_dim(
        seg_ext, start_row + block_len - WINDOW, block_rows + WINDOW, 0
    )
    allowed = (
        (distance >= 0)
        & (distance < WINDOW)
        & (seg_query[:, None] == seg_key[None, :])
        & (key_pos[None, :] + base_pos >= 0)
    )
    return (query_rows, key_rows, value_rows, jnp.where(allowed[None], scores, -1e30), allowed)


def factored_update(
    grad_mat, rows_old, cols_old, row_sums, col_sums, row_total, col_total, old_total, square_total
):
    rows_new = DECAY_RATE * rows_old + (1.0 - DECAY_RATE) * row_sums / col_total
    cols_new = DECAY_RATE * cols_old + (1.0 - DECAY_RATE) * col_sums / row_total
    mean_rows = (DECAY_RATE * old_total + (1.0 - DECAY_RATE) * square_total / col_total) / row_total
    second_moment = rows_new[:, None] * cols_new[None, :] / mean_rows
    return (grad_mat * lax.rsqrt(second_moment), rows_new, cols_new)


def apply_update(weight, update, update_root, square_sum, elements):
    param_scale = jnp.maximum(SCALE_FLOOR, jnp.sqrt(square_sum / elements))
    return weight - STEP_RATE * param_scale * update / jnp.maximum(1.0, update_root / CLIP_LIMIT)


def butterfly_partners():
    partners = []
    here = [lax.axis_index(name) for name in ("fsdp", "ctx", "tp")]
    for axis_number, name in enumerate(("fsdp", "ctx", "tp")):
        size = lax.axis_size(name)
        step = 1
        while step < size:
            bit = (here[axis_number] // step) % 2
            other = list(here)
            other[axis_number] = here[axis_number] + step * (1 - 2 * bit)
            partners.append(tuple(other))
            step *= 2
    return partners


def butterfly_kernel(x_ref, o_ref, stage, inbox, send_sems, recv_sems):
    partners = butterfly_partners()
    barrier = pltpu.get_barrier_semaphore()
    for partner in partners:
        pl.semaphore_signal(
            barrier, 1, device_id=partner, device_id_type=pl.DeviceIdType.MESH
        )
    pl.semaphore_wait(barrier, len(partners))
    acc = x_ref[...]
    for round_number, partner in enumerate(partners):
        stage[round_number] = acc
        copy = pltpu.make_async_remote_copy(
            src_ref=stage.at[round_number],
            dst_ref=inbox.at[round_number],
            send_sem=send_sems.at[round_number],
            recv_sem=recv_sems.at[round_number],
            device_id=partner,
            device_id_type=pl.DeviceIdType.MESH,
        )
        copy.start()
        copy.wait()
        acc = stage[round_number] + inbox[round_number]
    o_ref[...] = acc


def butterfly_sum(values, collective_id):
    flat = jnp.concatenate([v.reshape(-1).astype(jnp.float32) for v in values])
    size = flat.shape[0]
    rows = -(-size // 1024) * 8
    block = jnp.pad(flat, (0, rows * 128 - size)).reshape(rows, 128)
    rounds = sum(
        max(1, lax.axis_size(name)).bit_length() - 1 for name in ("fsdp", "ctx", "tp")
    )
    total = pl.pallas_call(
        butterfly_kernel,
        out_shape=jax.ShapeDtypeStruct((rows, 128), jnp.float32),
        in_specs=[pl.BlockSpec(memory_space=pltpu.VMEM)],
        out_specs=pl.BlockSpec(memory_space=pltpu.VMEM),
        scratch_shapes=[
            pltpu.VMEM((rounds, rows, 128), jnp.float32),
            pltpu.VMEM((rounds, rows, 128), jnp.float32),
            pltpu.SemaphoreType.DMA((rounds,)),
            pltpu.SemaphoreType.DMA((rounds,)),
        ],
        compiler_params=pltpu.CompilerParams(collective_id=collective_id, has_side_effects=True),
    )(block).reshape(-1)
    results = []
    offset = 0
    for v in values:
        results.append(total[offset : offset + v.size].reshape(v.shape))
        offset += v.size
    return results


def halving_kernel(x_ref, o_ref, stage_one, stage_two, inbox_one, inbox_two, inbox_three, sems):
    rows = o_ref.shape[0]
    chunk = 64
    fsdp_here = lax.axis_index("fsdp")
    ctx_here = lax.axis_index("ctx")
    tp_here = lax.axis_index("tp")
    bit_low = fsdp_here % 2
    bit_high = (fsdp_here // 2) % 2
    partners = [
        (fsdp_here, 1 - ctx_here, tp_here),
        (fsdp_here + 1 - 2 * bit_low, ctx_here, tp_here),
        (fsdp_here + 2 - 4 * bit_high, ctx_here, tp_here),
    ]
    barrier = pltpu.get_barrier_semaphore()
    for partner in partners:
        pl.semaphore_signal(barrier, 1, device_id=partner, device_id_type=pl.DeviceIdType.MESH)
    pl.semaphore_wait(barrier, len(partners))

    def swap(src, dst, number, partner):
        copy = pltpu.make_async_remote_copy(
            src_ref=src,
            dst_ref=dst,
            send_sem=sems.at[0, number],
            recv_sem=sems.at[1, number],
            device_id=partner,
            device_id_type=pl.DeviceIdType.MESH,
        )
        copy.start()
        copy.wait()

    swap(x_ref.at[:, pl.ds(1 - ctx_here, 1)], inbox_one, 0, partners[0])

    @pl.loop(0, rows // chunk)
    def _(step):
        part = pl.ds(pl.multiple_of(step * chunk, chunk), chunk)
        for high in range(2):
            for low in range(2):
                stage_one[high, low, part] = (
                    x_ref[2 * high + low, ctx_here, part] + inbox_one[2 * high + low, 0, part]
                )

    swap(stage_one.at[:, pl.ds(1 - bit_low, 1)], inbox_two, 1, partners[1])

    @pl.loop(0, rows // chunk)
    def _(step):
        part = pl.ds(pl.multiple_of(step * chunk, chunk), chunk)
        for high in range(2):
            stage_two[high, part] = stage_one[high, bit_low, part] + inbox_two[high, 0, part]

    swap(stage_two.at[pl.ds(1 - bit_high, 1)], inbox_three, 2, partners[2])

    @pl.loop(0, rows // chunk)
    def _(step):
        part = pl.ds(pl.multiple_of(step * chunk, chunk), chunk)
        o_ref[part] = stage_two[bit_high, part] + inbox_three[0, part]


def halving_scatter(packed, collective_id):
    count, width = packed.shape
    rows = -(-width // (128 * 64)) * 64
    block = jnp.pad(packed, ((0, 0), (0, rows * 128 - width))).reshape(count // 2, 2, rows, 128)
    own = pl.pallas_call(
        halving_kernel,
        out_shape=jax.ShapeDtypeStruct((rows, 128), jnp.float32),
        in_specs=[pl.BlockSpec(memory_space=pltpu.VMEM)],
        out_specs=pl.BlockSpec(memory_space=pltpu.VMEM),
        scratch_shapes=[
            pltpu.VMEM((2, 2, rows, 128), jnp.float32),
            pltpu.VMEM((2, rows, 128), jnp.float32),
            pltpu.VMEM((count // 2, 1, rows, 128), jnp.float32),
            pltpu.VMEM((2, 1, rows, 128), jnp.float32),
            pltpu.VMEM((1, rows, 128), jnp.float32),
            pltpu.SemaphoreType.DMA((2, 3)),
        ],
        compiler_params=pltpu.CompilerParams(
            collective_id=collective_id, has_side_effects=True, vmem_limit_bytes=60 * 1024 * 1024
        ),
    )(block)
    return own.reshape(-1)[:width]


def gather_kernel(x_ref, o_ref, inbox, send_sems, recv_sems):
    fsdp_here = lax.axis_index("fsdp")
    ctx_here = lax.axis_index("ctx")
    tp_here = lax.axis_index("tp")
    ctx_count = lax.axis_size("ctx")
    count = lax.axis_size("fsdp") * ctx_count
    me = fsdp_here * ctx_count + ctx_here
    peers = []
    for offset in range(1, count):
        other = (me + offset) % count
        peers.append((other // ctx_count, other % ctx_count, tp_here))
    barrier = pltpu.get_barrier_semaphore()
    for peer in peers:
        pl.semaphore_signal(barrier, 1, device_id=peer, device_id_type=pl.DeviceIdType.MESH)
    pl.semaphore_wait(barrier, len(peers))
    copies = []
    for number, peer in enumerate(peers):
        copy = pltpu.make_async_remote_copy(
            src_ref=x_ref,
            dst_ref=inbox.at[me],
            send_sem=send_sems.at[number],
            recv_sem=recv_sems.at[me],
            device_id=peer,
            device_id_type=pl.DeviceIdType.MESH,
        )
        copy.start()
        copies.append(copy)
    o_ref[me] = x_ref[...]
    for copy in copies:
        copy.wait_send()
    for offset in range(1, count):
        source = (me + count - offset) % count
        pltpu.make_async_remote_copy(
            src_ref=x_ref,
            dst_ref=inbox.at[source],
            send_sem=send_sems.at[0],
            recv_sem=recv_sems.at[source],
            device_id=peers[0],
            device_id_type=pl.DeviceIdType.MESH,
        ).wait_recv()
        o_ref[source] = inbox[source]


def gather_shards(flat, collective_id):
    size = flat.shape[0]
    rows = -(-size // 2048) * 16
    block = jnp.pad(flat, (0, rows * 128 - size)).reshape(rows, 128)
    count = lax.axis_size("fsdp") * lax.axis_size("ctx")
    full = pl.pallas_call(
        gather_kernel,
        out_shape=jax.ShapeDtypeStruct((count, rows, 128), flat.dtype),
        in_specs=[pl.BlockSpec(memory_space=pltpu.VMEM)],
        out_specs=pl.BlockSpec(memory_space=pltpu.VMEM),
        scratch_shapes=[
            pltpu.VMEM((count, rows, 128), flat.dtype),
            pltpu.SemaphoreType.DMA((count - 1,)),
            pltpu.SemaphoreType.DMA((count,)),
        ],
        compiler_params=pltpu.CompilerParams(collective_id=collective_id, has_side_effects=True),
    )(block)
    return full.reshape(count, rows * 128)[:, :size]


def swiglu_experts(gate_up):
    return jax.nn.silu(gate_up[:, :, 0]) * gate_up[:, :, 1]


def gather_packed(pieces, axes, use_kernel=False):
    flat = jnp.concatenate([piece.reshape(-1) for piece, _ in pieces])
    if use_kernel:
        full = gather_shards(flat, 4)
    else:
        full = lax.all_gather(flat, axes, axis=0, tiled=False)
    count = full.shape[0]
    results = []
    offset = 0
    for piece, dim in pieces:
        size = piece.size
        part = full[:, offset : offset + size].reshape((count,) + piece.shape)
        offset += size
        part = jnp.moveaxis(part, 0, dim)
        shape = list(piece.shape)
        shape[dim] *= count
        results.append(part.reshape(shape))
    return results


def scatter_packed(pieces, axes, count, use_kernel=False):
    columns = []
    local_shapes = []
    for grad, dim in pieces:
        shape = grad.shape
        split = shape[:dim] + (count, shape[dim] // count) + shape[dim + 1 :]
        local_shapes.append(shape[:dim] + (shape[dim] // count,) + shape[dim + 1 :])
        part = jnp.moveaxis(grad.reshape(split), dim, 0)
        columns.append(part.reshape(count, -1))
    packed = jnp.concatenate(columns, axis=1)
    if use_kernel:
        own = halving_scatter(packed, 3)
    else:
        width = packed.shape[1]
        rows = -(-width // 1024) * 8
        packed = jnp.pad(packed, ((0, 0), (0, rows * 128 - width))).reshape(count * rows, 128)
        own = lax.psum_scatter(packed, axes, scatter_dimension=0, tiled=True).reshape(-1)
    results = []
    offset = 0
    for local_shape in local_shapes:
        size = 1
        for extent in local_shape:
            size *= extent
        results.append(own[offset : offset + size].reshape(local_shape))
        offset += size
    return results


def experts_dense(normed_two, grad_out, weights, expert_in_all, expert_down_all):
    gate_up = jnp.einsum(
        "td,edgf->etgf", normed_two, expert_in_all, preferred_element_type=jnp.float32
    )
    act, act_back = jax.vjp(swiglu_experts, gate_up)
    hidden = act.astype(jnp.bfloat16)
    outs = jnp.einsum("etf,efd->etd", hidden, expert_down_all, preferred_element_type=jnp.float32)
    weights_e = weights.T[:, :, None]
    combined = jnp.sum(weights_e * outs, axis=0)
    gate_dots = jnp.sum(outs * grad_out[None], axis=-1).T
    grad_outs = (weights_e * grad_out[None]).astype(jnp.bfloat16)
    grad_hidden = jnp.einsum(
        "etd,efd->etf", grad_outs, expert_down_all, preferred_element_type=jnp.float32
    )
    grad_gate_up = act_back(grad_hidden)[0].astype(jnp.bfloat16)
    grad_down = jnp.einsum("etf,etd->efd", hidden, grad_outs, preferred_element_type=jnp.float32)
    grad_in = jnp.einsum(
        "td,etgf->edgf", normed_two, grad_gate_up, preferred_element_type=jnp.float32
    )
    grad_rows = jnp.einsum(
        "etgf,edgf->td", grad_gate_up, expert_in_all, preferred_element_type=jnp.float32
    )
    return combined, gate_dots, grad_rows, grad_in, grad_down


def experts_routed(
    normed_two, grad_out, route_rows, gate_probs, expert_in_low, expert_down_low, capacity
):
    block_len, model_width = normed_two.shape
    experts = lax.axis_size("fsdp")
    slot_index, owner_route, filled = slot_tables(route_rows, experts, capacity)
    fill_mask = filled.astype(jnp.bfloat16)[:, None]
    route_grads = (
        (gate_probs[:, :, None] * grad_out[:, None, :])
        .astype(jnp.bfloat16)
        .reshape(2 * block_len, model_width)
    )
    send_rows = jnp.stack(
        [
            (normed_two[owner_route // 2] * fill_mask).reshape(experts, capacity, model_width),
            (route_grads[owner_route] * fill_mask).reshape(experts, capacity, model_width),
        ],
        axis=1,
    )
    exchange = lambda rows: lax.all_to_all(rows, "fsdp", split_axis=0, concat_axis=0, tiled=True)
    pair_count = lax.axis_size("tp")
    swap = lambda rows: lax.ppermute(
        rows, "tp", [(index, index + 1 - 2 * (index % 2)) for index in range(pair_count)]
    )
    half = capacity // 2
    side = lax.axis_index("tp") % 2
    mine = exchange(lax.dynamic_slice_in_dim(send_rows, side * half, half, 2))
    received_both = jnp.concatenate([mine, swap(mine)], axis=2)
    received = received_both[:, 0].reshape(experts * capacity, model_width)
    grad_received = received_both[:, 1].reshape(experts * capacity, model_width)
    gate_up = jnp.einsum("rd,dgf->rgf", received, expert_in_low, preferred_element_type=jnp.float32)
    act, act_back = jax.vjp(swiglu, gate_up)
    hidden = act.astype(jnp.bfloat16)
    outs = jnp.dot(hidden, expert_down_low, preferred_element_type=jnp.float32)
    grad_hidden = jnp.einsum(
        "rd,fd->rf", grad_received, expert_down_low, preferred_element_type=jnp.float32
    )
    grad_gate_up = act_back(grad_hidden)[0].astype(jnp.bfloat16)
    grad_in = jnp.einsum("rd,rgf->dgf", received, grad_gate_up, preferred_element_type=jnp.float32)
    grad_down = jnp.einsum("rf,rd->fd", hidden, grad_received, preferred_element_type=jnp.float32)
    grad_expert_rows = jnp.einsum(
        "rgf,dgf->rd", grad_gate_up, expert_in_low, preferred_element_type=jnp.float32
    )
    pair_sums = []
    for rows in (outs, grad_expert_rows):
        rows = rows.reshape(experts, capacity, model_width)
        pair_sums.append(rows[:, :half] + swap(rows[:, half:]))
    held = exchange(jnp.stack(pair_sums, axis=1).astype(jnp.bfloat16))
    slot_expert = slot_index // capacity
    slot_rank = slot_index % capacity
    in_side = ((slot_rank // half) == side)[:, None]
    local_slot = slot_expert * half + slot_rank % half
    picked_rows = []
    for which in range(2):
        rows = held[:, which].reshape(experts * half, model_width)[local_slot]
        picked_rows.append(
            jnp.where(in_side, rows.astype(jnp.float32), 0.0).reshape(block_len, 2, model_width)
        )
    route_out, grad_routes = picked_rows
    combined = jnp.sum(gate_probs[:, :, None] * route_out, axis=1)
    gate_dots = jnp.sum(grad_out[:, None, :] * route_out, axis=-1)
    grad_rows = jnp.sum(grad_routes, axis=1)
    return combined, gate_dots, grad_rows, grad_in, grad_down


def local(
    layer_input,
    segments,
    routes,
    cotangent,
    gains,
    attention_in,
    attention_out,
    router_weight,
    shared_in,
    shared_down,
    expert_in,
    expert_down,
    model_stats,
    head_stats,
    value_columns,
    hidden_stats,
    router_state,
    expert_model_stats,
    expert_hidden_stats,
):
    block_len = layer_input.shape[1]
    model_width = layer_input.shape[2]
    experts = router_weight.shape[1]
    dense_experts = False
    capacity = min(block_len, 4 * block_len // experts)
    ctx_index = lax.axis_index("ctx")
    tp_index = lax.axis_index("tp")
    fsdp_index = lax.axis_index("fsdp")
    shard_index = lax.axis_index(("fsdp", "ctx"))
    shard_count = lax.axis_size(("fsdp", "ctx"))
    ctx_count = lax.axis_size("ctx")
    base_pos = ctx_index * block_len
    low = lambda v: v.astype(jnp.bfloat16)
    gain_low, attn_in_low = gather_packed(
        [(low(gains), 1), (low(attention_in), 0)], ("fsdp", "ctx"), shard_count <= 8
    )
    later = [
        (low(attention_out), 1),
        (low(router_weight), 0),
        (low(shared_in), 0),
        (low(shared_down), 1),
    ]
    if dense_experts:
        later += [(low(expert_in), 0), (low(expert_down), 0)]
    later_full = gather_packed(later, ("fsdp", "ctx"))
    attn_out_low, router_low, shared_in_low, shared_down_low = later_full[:4]
    if dense_experts:
        fe_local = expert_down.shape[1]
        expert_in_all = later_full[4].reshape(experts, model_width, 2, fe_local)
        expert_down_all = (
            later_full[5]
            .reshape(experts, ctx_count, fe_local, model_width // ctx_count)
            .transpose(0, 2, 1, 3)
            .reshape(experts, fe_local, model_width)
        )
    else:
        expert_in_low = lax.all_gather(low(expert_in), "ctx", axis=1, tiled=True)[0]
        expert_down_low = lax.all_gather(low(expert_down), "ctx", axis=2, tiled=True)[0]
    residual = layer_input[0].astype(jnp.float32)
    gain_one = gain_low[0].astype(jnp.float32)
    gain_two = gain_low[1].astype(jnp.float32)
    normed_one, norm_one_back = jax.vjp(rms_norm, residual, gain_one)
    normed_one = normed_one.astype(jnp.bfloat16)
    projected = jnp.einsum(
        "td,dgf->tgf", normed_one, attn_in_low, preferred_element_type=jnp.float32
    )
    local_cols = projected.shape[2]
    local_heads = local_cols // HD
    half_dim = HD // 2
    frequency = 10000.0 ** (-jnp.arange(half_dim, dtype=jnp.float32) / half_dim)
    angles = (base_pos + jnp.arange(block_len, dtype=jnp.int32)).astype(jnp.float32)[
        :, None
    ] * frequency[None, :]
    cosine = jnp.cos(angles)
    sine_tab = jnp.sin(angles)
    queries = rotate(projected[:, 0].reshape(block_len, local_heads, HD), cosine, sine_tab).astype(
        jnp.bfloat16
    )
    keys_own = rotate(projected[:, 1].reshape(block_len, local_heads, HD), cosine, sine_tab).astype(
        jnp.bfloat16
    )
    values_own = projected[:, 2].reshape(block_len, local_heads, HD).astype(jnp.bfloat16)
    seg_own = segments[0].astype(jnp.bfloat16)
    keys_prev, values_prev, seg_prev = from_behind((keys_own, values_own, seg_own), "ctx", 1)
    keys_ext = jnp.concatenate([keys_prev, keys_own], axis=0)
    values_ext = jnp.concatenate([values_prev, values_own], axis=0)
    seg_ext = jnp.concatenate([seg_prev, seg_own], axis=0)
    block_rows = min(512, block_len)
    block_total = block_len // block_rows
    starts = jnp.arange(block_total, dtype=jnp.int32) * block_rows

    def forward_block(start_row):
        query_rows, key_rows, value_rows, masked, allowed = block_view(
            queries, keys_ext, values_ext, seg_own, seg_ext, start_row, base_pos
        )
        row_max = jnp.max(masked, axis=-1, keepdims=True)
        exp_terms = jnp.where(allowed[None], jnp.exp(masked - row_max), 0.0)
        row_total = jnp.sum(exp_terms, axis=-1, keepdims=True)
        attn_probs = (exp_terms / row_total).astype(jnp.bfloat16)
        attended = jnp.einsum(
            "hqk,khd->qhd", attn_probs, value_rows, preferred_element_type=jnp.float32
        )
        return (attended, row_max + jnp.log(row_total))

    attended, log_totals = lax.map(forward_block, starts)
    mixed_heads = attended.reshape(block_len, local_cols).astype(jnp.bfloat16)
    attn_total = lax.psum(
        jnp.dot(mixed_heads, attn_out_low, preferred_element_type=jnp.float32), "tp"
    )
    after_attn = residual + attn_total
    normed_two, norm_two_back = jax.vjp(rms_norm, after_attn, gain_two)
    normed_two = normed_two.astype(jnp.bfloat16)
    logits = jnp.dot(normed_two, router_low, preferred_element_type=jnp.float32)
    route_rows = routes[0]
    onehot = (route_rows[:, :, None] == jnp.arange(experts, dtype=jnp.int32)[None, None, :]).astype(
        jnp.float32
    )
    picked = jnp.sum(onehot * logits[:, None, :], axis=-1)
    gate_probs = jax.nn.softmax(picked, axis=-1)
    upstream = cotangent[0]
    grad_out = upstream.astype(jnp.float32)
    if dense_experts:
        weights = jnp.sum(gate_probs[:, :, None] * onehot, axis=1)
        combined, dots_e, grad_rows, grad_expert_in, grad_expert_down = experts_dense(
            normed_two, grad_out, weights, expert_in_all, expert_down_all
        )
        gate_dots = jnp.sum(onehot * dots_e[:, None, :], axis=-1)
    else:
        combined, gate_dots, grad_rows, grad_expert_in, grad_expert_down = experts_routed(
            normed_two,
            grad_out,
            route_rows,
            gate_probs,
            expert_in_low,
            expert_down_low,
            capacity,
        )
    shared_gate_up = jnp.einsum(
        "td,dgf->tgf", normed_two, shared_in_low, preferred_element_type=jnp.float32
    )
    shared_act, shared_act_back = jax.vjp(swiglu, shared_gate_up)
    shared_hidden = shared_act.astype(jnp.bfloat16)
    shared_out = jnp.dot(shared_hidden, shared_down_low, preferred_element_type=jnp.float32)
    grad_shared_hidden = jnp.einsum(
        "td,fd->tf", upstream, shared_down_low, preferred_element_type=jnp.float32
    )
    grad_shared_gate_up = shared_act_back(grad_shared_hidden)[0].astype(jnp.bfloat16)
    partial_two = (
        jnp.einsum(
            "tgf,dgf->td", grad_shared_gate_up, shared_in_low, preferred_element_type=jnp.float32
        )
        + grad_rows
    )
    branch_total, grad_normed_part, gate_total = lax.psum(
        (shared_out + combined, partial_two, gate_dots), "tp"
    )
    layer_out = after_attn + branch_total
    grad_picked = gate_probs * (
        gate_total - jnp.sum(gate_probs * gate_total, axis=-1, keepdims=True)
    )
    grad_logits = jnp.sum(grad_picked[:, :, None] * onehot, axis=1).astype(jnp.bfloat16)
    grad_shared_in = jnp.einsum(
        "td,tgf->dgf", normed_two, grad_shared_gate_up, preferred_element_type=jnp.float32
    )
    grad_shared_down = jnp.einsum(
        "tf,td->fd", shared_hidden, upstream, preferred_element_type=jnp.float32
    )
    grad_router = jnp.einsum(
        "td,te->de", normed_two, grad_logits, preferred_element_type=jnp.float32
    )
    grad_normed_two = grad_normed_part + jnp.einsum(
        "te,de->td", grad_logits, router_low, preferred_element_type=jnp.float32
    )
    grad_after, grad_gain_two = norm_two_back(grad_normed_two)
    grad_after = grad_after + grad_out
    grad_attn_low = grad_after.astype(jnp.bfloat16)
    grad_attn_out = jnp.einsum(
        "tc,td->cd", mixed_heads, grad_attn_low, preferred_element_type=jnp.float32
    )
    first_grads = [
        (grad_attn_out, 1),
        (grad_router, 0),
        (grad_shared_in, 0),
        (grad_shared_down, 1),
        (grad_gain_two, 0),
    ]
    if dense_experts:
        fe_local = expert_down.shape[1]
        first_grads += [
            (grad_expert_in.reshape(shard_count * expert_in.shape[1], 2, fe_local), 0),
            (
                grad_expert_down.reshape(experts, fe_local, ctx_count, model_width // ctx_count)
                .transpose(0, 2, 1, 3)
                .reshape(shard_count * fe_local, model_width // ctx_count),
                0,
            ),
        ]
    if not dense_experts:
        own_expert_in = lax.psum_scatter(grad_expert_in[None], "ctx", scatter_dimension=1, tiled=True)
        own_expert_down = lax.psum_scatter(
            grad_expert_down[None], "ctx", scatter_dimension=2, tiled=True
        )
    grad_heads = (
        jnp.einsum("td,cd->tc", grad_attn_low, attn_out_low, preferred_element_type=jnp.float32)
        .astype(jnp.bfloat16)
        .reshape(block_len, local_heads, HD)
    )

    def backward_block(block_number, running):
        grad_keys, grad_values, grad_queries = running
        start_row = block_number * block_rows
        query_rows, key_rows, value_rows, masked, allowed = block_view(
            queries, keys_ext, values_ext, seg_own, seg_ext, start_row, base_pos
        )
        log_total = lax.dynamic_index_in_dim(log_totals, block_number, 0, keepdims=False)
        attn_probs = jnp.where(allowed[None], jnp.exp(masked - log_total), 0.0)
        grad_block = lax.dynamic_slice_in_dim(grad_heads, start_row, block_rows, 0)
        grad_probs = jnp.einsum(
            "qhd,khd->hqk", grad_block, value_rows, preferred_element_type=jnp.float32
        )
        inner_sum = jnp.sum(attn_probs * grad_probs, axis=-1, keepdims=True)
        grad_scores = (attn_probs * (grad_probs - inner_sum)).astype(jnp.bfloat16)
        grad_query_rows = (
            jnp.einsum("hqk,khd->qhd", grad_scores, key_rows, preferred_element_type=jnp.float32)
            * 0.125
        )
        grad_key_rows = (
            jnp.einsum("hqk,qhd->khd", grad_scores, query_rows, preferred_element_type=jnp.float32)
            * 0.125
        )
        grad_value_rows = jnp.einsum(
            "hqk,qhd->khd",
            attn_probs.astype(jnp.bfloat16),
            grad_block,
            preferred_element_type=jnp.float32,
        )
        key_offset = start_row + block_len - WINDOW
        grad_keys = lax.dynamic_update_slice_in_dim(
            grad_keys,
            lax.dynamic_slice_in_dim(grad_keys, key_offset, block_rows + WINDOW, 0) + grad_key_rows,
            key_offset,
            0,
        )
        grad_values = lax.dynamic_update_slice_in_dim(
            grad_values,
            lax.dynamic_slice_in_dim(grad_values, key_offset, block_rows + WINDOW, 0)
            + grad_value_rows,
            key_offset,
            0,
        )
        grad_queries = lax.dynamic_update_slice_in_dim(grad_queries, grad_query_rows, start_row, 0)
        return (grad_keys, grad_values, grad_queries)

    zero_ext = jnp.zeros((2 * block_len, local_heads, HD), jnp.float32)
    zero_own = jnp.zeros((block_len, local_heads, HD), jnp.float32)
    grad_keys, grad_values, grad_queries = lax.fori_loop(
        0, block_total, backward_block, (zero_ext, zero_ext, zero_own)
    )
    rim_keys, rim_values = (
        from_behind(grad_keys[:block_len].astype(jnp.bfloat16), "ctx", -1).astype(jnp.float32),
        from_behind(grad_values[:block_len].astype(jnp.bfloat16), "ctx", -1).astype(jnp.float32),
    )
    grad_keys_own = grad_keys[block_len:] + rim_keys
    grad_values_own = grad_values[block_len:] + rim_values
    grad_query_raw = rotate(grad_queries, cosine, -sine_tab)
    grad_key_raw = rotate(grad_keys_own, cosine, -sine_tab)
    grad_projected = (
        jnp.stack([grad_query_raw, grad_key_raw, grad_values_own], axis=1)
        .reshape(block_len, 3, local_cols)
        .astype(jnp.bfloat16)
    )
    grad_attn_in = jnp.einsum(
        "td,tgf->dgf", normed_one, grad_projected, preferred_element_type=jnp.float32
    )
    partial_one = jnp.einsum(
        "tgf,dgf->td", grad_projected, attn_in_low, preferred_element_type=jnp.float32
    )
    tp_one = lax.psum(partial_one, "tp")
    halving = lax.axis_size("fsdp") == 4 and ctx_count == 2
    all_own = scatter_packed(
        first_grads + [(grad_attn_in, 0)],
        ("fsdp", "ctx"),
        shard_count,
        halving,
    )
    own_attn_out, own_router, own_shared_in, own_shared_down, own_gain_two = all_own[:5]
    own_attn_in = all_own[-1]
    grad_residual, grad_gain_one = norm_one_back(tp_one + 0.0 * own_attn_in[0, 0, 0])
    input_grad = grad_after + grad_residual
    if dense_experts:
        own_expert_in = all_own[5][None]
        own_expert_down = all_own[6][None]
    lead_tp = (tp_index == 0).astype(jnp.float32)
    first_shard = (shard_index == 0).astype(jnp.float32)
    first_ctx = (ctx_index == 0).astype(jnp.float32)
    d_local = gains.shape[1]
    ff_local = shared_down.shape[0]
    fe_local = expert_down.shape[1]
    d_quarter = expert_in.shape[1]
    square_attn_in = own_attn_in * own_attn_in + TINY_SQUARE
    square_attn_out = own_attn_out * own_attn_out + TINY_SQUARE
    square_shared_in = own_shared_in * own_shared_in + TINY_SQUARE
    square_shared_down = own_shared_down * own_shared_down + TINY_SQUARE
    square_expert_in = own_expert_in[0] * own_expert_in[0] + TINY_SQUARE
    square_expert_down = own_expert_down[0] * own_expert_down[0] + TINY_SQUARE
    model_part = lax.dynamic_update_slice(
        jnp.zeros((4, D), jnp.float32),
        jnp.stack(
            [
                jnp.sum(square_attn_in, axis=(1, 2)),
                jnp.sum(square_shared_in, axis=(1, 2)),
                jnp.sum(square_attn_out, axis=0),
                jnp.sum(square_shared_down, axis=0),
            ]
        ),
        (0, shard_index * d_local),
    )
    head_part = lax.dynamic_update_slice(
        jnp.zeros((4, HH), jnp.float32),
        jnp.concatenate(
            [jnp.sum(square_attn_in, axis=0), jnp.sum(square_attn_out, axis=1)[None]], axis=0
        ),
        (0, tp_index * local_cols),
    )
    hidden_part = lax.dynamic_update_slice(
        jnp.zeros((3, FF), jnp.float32),
        jnp.concatenate(
            [jnp.sum(square_shared_in, axis=0), jnp.sum(square_shared_down, axis=1)[None]], axis=0
        ),
        (0, tp_index * ff_local),
    )
    expert_model_part = lax.dynamic_update_slice(
        jnp.zeros((experts, 2, D), jnp.float32),
        jnp.stack([jnp.sum(square_expert_in, axis=(1, 2)), jnp.sum(square_expert_down, axis=0)])[
            None
        ],
        (fsdp_index, 0, ctx_index * d_quarter),
    )
    expert_hidden_part = lax.dynamic_update_slice(
        jnp.zeros((experts, 3, FE), jnp.float32),
        jnp.concatenate(
            [jnp.sum(square_expert_in, axis=0), jnp.sum(square_expert_down, axis=1)[None]], axis=0
        )[None],
        (fsdp_index, 0, tp_index * fe_local),
    )
    scalar_part = jnp.stack(
        [
            lead_tp * jnp.sum(gains * gains),
            jnp.sum(attention_in * attention_in),
            jnp.sum(attention_out * attention_out),
            lead_tp * jnp.sum(router_weight * router_weight),
            jnp.sum(shared_in * shared_in),
            jnp.sum(shared_down * shared_down),
            jnp.sum(expert_in * expert_in),
            jnp.sum(expert_down * expert_down),
            lead_tp * jnp.sum(model_stats[2]),
            first_shard * jnp.sum(head_stats[2]),
            lead_tp * jnp.sum(model_stats[3]),
            first_shard * jnp.sum(hidden_stats[2]),
        ]
    )
    expert_old_part = lax.dynamic_update_slice(
        jnp.zeros((2, experts), jnp.float32),
        jnp.stack(
            [
                lead_tp * jnp.sum(expert_model_stats[0, 0]),
                first_ctx * jnp.sum(expert_hidden_stats[0, 2]),
            ]
        )[:, None],
        (0, fsdp_index),
    )
    global_sums = butterfly_sum(
        [
            model_part,
            head_part,
            hidden_part,
            expert_model_part,
            expert_hidden_part,
            scalar_part,
            expert_old_part,
            lead_tp * grad_gain_one,
        ],
        1,
    )
    (
        model_sum,
        head_sum,
        hidden_sum,
        expert_model_sum,
        expert_hidden_sum,
        scalar_sum,
        expert_old_sum,
        gain_one_sum,
    ) = global_sums
    own_gain_one = lax.dynamic_slice_in_dim(gain_one_sum, shard_index * d_local, d_local)
    own_gains = jnp.stack([own_gain_one, own_gain_two])
    shard_start = shard_index * d_local
    gain_state = DECAY_RATE * model_stats[0:2] + (1.0 - DECAY_RATE) * (
        own_gains * own_gains + TINY_SQUARE
    )
    update_gains = own_gains * lax.rsqrt(gain_state)
    router_new = DECAY_RATE * router_state + (1.0 - DECAY_RATE) * (
        own_router * own_router + TINY_SQUARE
    )
    update_router = own_router * lax.rsqrt(router_new)
    attn_cols_old = jnp.concatenate([head_stats[0:2], value_columns[None]], axis=0).reshape(-1)
    update_attn_in, rows_attn_in, cols_attn_in = factored_update(
        own_attn_in.reshape(d_local, 3 * local_cols),
        model_stats[2],
        attn_cols_old,
        lax.dynamic_slice_in_dim(model_sum[0], shard_start, d_local),
        lax.dynamic_slice_in_dim(head_sum[0:3], tp_index * local_cols, local_cols, 1).reshape(-1),
        D,
        3 * HH,
        scalar_sum[8],
        jnp.sum(model_sum[0]),
    )
    update_attn_out, rows_attn_out, cols_attn_out = factored_update(
        own_attn_out,
        head_stats[2],
        model_stats[4],
        lax.dynamic_slice_in_dim(head_sum[3], tp_index * local_cols, local_cols),
        lax.dynamic_slice_in_dim(model_sum[2], shard_start, d_local),
        HH,
        D,
        scalar_sum[9],
        jnp.sum(head_sum[3]),
    )
    update_shared_in, rows_shared_in, cols_shared_in = factored_update(
        own_shared_in.reshape(d_local, 2 * ff_local),
        model_stats[3],
        hidden_stats[0:2].reshape(-1),
        lax.dynamic_slice_in_dim(model_sum[1], shard_start, d_local),
        lax.dynamic_slice_in_dim(hidden_sum[0:2], tp_index * ff_local, ff_local, 1).reshape(-1),
        D,
        2 * FF,
        scalar_sum[10],
        jnp.sum(model_sum[1]),
    )
    update_shared_down, rows_shared_down, cols_shared_down = factored_update(
        own_shared_down,
        hidden_stats[2],
        model_stats[5],
        lax.dynamic_slice_in_dim(hidden_sum[2], tp_index * ff_local, ff_local),
        lax.dynamic_slice_in_dim(model_sum[3], shard_start, d_local),
        FF,
        D,
        scalar_sum[11],
        jnp.sum(hidden_sum[2]),
    )
    own_expert_model = lax.dynamic_index_in_dim(expert_model_sum, fsdp_index, 0, keepdims=False)
    own_expert_hidden = lax.dynamic_index_in_dim(expert_hidden_sum, fsdp_index, 0, keepdims=False)
    old_expert_totals = lax.dynamic_index_in_dim(expert_old_sum, fsdp_index, 1, keepdims=False)
    update_expert_in, rows_expert_in, cols_expert_in = factored_update(
        own_expert_in[0].reshape(d_quarter, 2 * fe_local),
        expert_model_stats[0, 0],
        expert_hidden_stats[0, 0:2].reshape(-1),
        lax.dynamic_slice_in_dim(own_expert_model[0], ctx_index * d_quarter, d_quarter),
        lax.dynamic_slice_in_dim(own_expert_hidden[0:2], tp_index * fe_local, fe_local, 1).reshape(
            -1
        ),
        D,
        2 * FE,
        old_expert_totals[0],
        jnp.sum(own_expert_model[0]),
    )
    update_expert_down, rows_expert_down, cols_expert_down = factored_update(
        own_expert_down[0],
        expert_hidden_stats[0, 2],
        expert_model_stats[0, 1],
        lax.dynamic_slice_in_dim(own_expert_hidden[2], tp_index * fe_local, fe_local),
        lax.dynamic_slice_in_dim(own_expert_model[1], ctx_index * d_quarter, d_quarter),
        FE,
        D,
        old_expert_totals[1],
        jnp.sum(own_expert_hidden[2]),
    )
    clip_part = jnp.stack(
        [
            lead_tp * jnp.sum(update_gains * update_gains),
            jnp.sum(update_attn_in * update_attn_in),
            jnp.sum(update_attn_out * update_attn_out),
            lead_tp * jnp.sum(update_router * update_router),
            jnp.sum(update_shared_in * update_shared_in),
            jnp.sum(update_shared_down * update_shared_down),
            jnp.sum(update_expert_in * update_expert_in),
            jnp.sum(update_expert_down * update_expert_down),
        ]
    )
    clip_total = butterfly_sum([clip_part], 2)[0]
    elements = jnp.array(
        [
            2 * D,
            D * 3 * HH,
            HH * D,
            D * experts,
            D * 2 * FF,
            FF * D,
            experts * D * 2 * FE,
            experts * FE * D,
        ],
        jnp.float32,
    )
    update_roots = jnp.sqrt(clip_total / elements)
    new_gains = apply_update(gains, update_gains, update_roots[0], scalar_sum[0], elements[0])
    new_attn_in = apply_update(
        attention_in,
        update_attn_in.reshape(attention_in.shape),
        update_roots[1],
        scalar_sum[1],
        elements[1],
    )
    new_attn_out = apply_update(
        attention_out, update_attn_out, update_roots[2], scalar_sum[2], elements[2]
    )
    new_router = apply_update(
        router_weight, update_router, update_roots[3], scalar_sum[3], elements[3]
    )
    new_shared_in = apply_update(
        shared_in,
        update_shared_in.reshape(shared_in.shape),
        update_roots[4],
        scalar_sum[4],
        elements[4],
    )
    new_shared_down = apply_update(
        shared_down, update_shared_down, update_roots[5], scalar_sum[5], elements[5]
    )
    new_expert_in = apply_update(
        expert_in,
        update_expert_in.reshape(expert_in.shape),
        update_roots[6],
        scalar_sum[6],
        elements[6],
    )
    new_expert_down = apply_update(
        expert_down,
        update_expert_down.reshape(expert_down.shape),
        update_roots[7],
        scalar_sum[7],
        elements[7],
    )
    new_model_stats = jnp.concatenate(
        [gain_state, jnp.stack([rows_attn_in, rows_shared_in, cols_attn_out, cols_shared_down])],
        axis=0,
    )
    attn_cols_new = cols_attn_in.reshape(3, local_cols)
    new_head_stats = jnp.concatenate([attn_cols_new[0:2], rows_attn_out[None]], axis=0)
    new_value_columns = attn_cols_new[2]
    new_hidden_stats = jnp.concatenate(
        [cols_shared_in.reshape(2, ff_local), rows_shared_down[None]], axis=0
    )
    new_expert_model_stats = jnp.stack([rows_expert_in, cols_expert_down])[None]
    new_expert_hidden_stats = jnp.concatenate(
        [cols_expert_in.reshape(2, fe_local), rows_expert_down[None]], axis=0
    )[None]
    return (
        layer_out.astype(jnp.bfloat16)[None],
        input_grad[None],
        own_gains,
        own_attn_in,
        own_attn_out,
        own_router,
        own_shared_in,
        own_shared_down,
        own_expert_in,
        own_expert_down,
        new_gains,
        new_attn_in,
        new_attn_out,
        new_router,
        new_shared_in,
        new_shared_down,
        new_expert_in,
        new_expert_down,
        new_model_stats,
        new_head_stats,
        new_value_columns,
        new_hidden_stats,
        router_new,
        new_expert_model_stats,
        new_expert_hidden_stats,
        update_roots,
    )


def solution(mesh):
    in_specs = (
        P("fsdp", "ctx", None),
        P("fsdp", "ctx"),
        P("fsdp", "ctx", None),
        P("fsdp", "ctx", None),
        P(None, ("fsdp", "ctx")),
        P(("fsdp", "ctx"), None, "tp"),
        P("tp", ("fsdp", "ctx")),
        P(("fsdp", "ctx"), None),
        P(("fsdp", "ctx"), None, "tp"),
        P("tp", ("fsdp", "ctx")),
        P("fsdp", "ctx", None, "tp"),
        P("fsdp", "tp", "ctx"),
        P(None, ("fsdp", "ctx")),
        P(None, "tp"),
        P("tp"),
        P(None, "tp"),
        P(("fsdp", "ctx"), None),
        P("fsdp", None, "ctx"),
        P("fsdp", None, "tp"),
    )
    out_specs = (
        P("fsdp", "ctx", None),
        P("fsdp", "ctx", None),
        P(None, ("fsdp", "ctx")),
        P(("fsdp", "ctx"), None, "tp"),
        P("tp", ("fsdp", "ctx")),
        P(("fsdp", "ctx"), None),
        P(("fsdp", "ctx"), None, "tp"),
        P("tp", ("fsdp", "ctx")),
        P("fsdp", "ctx", None, "tp"),
        P("fsdp", "tp", "ctx"),
        P(None, ("fsdp", "ctx")),
        P(("fsdp", "ctx"), None, "tp"),
        P("tp", ("fsdp", "ctx")),
        P(("fsdp", "ctx"), None),
        P(("fsdp", "ctx"), None, "tp"),
        P("tp", ("fsdp", "ctx")),
        P("fsdp", "ctx", None, "tp"),
        P("fsdp", "tp", "ctx"),
        P(None, ("fsdp", "ctx")),
        P(None, "tp"),
        P("tp"),
        P(None, "tp"),
        P(("fsdp", "ctx"), None),
        P("fsdp", None, "ctx"),
        P("fsdp", None, "tp"),
        P(),
    )
    return jax.shard_map(local, mesh=mesh, in_specs=in_specs, out_specs=out_specs, check_vma=False)
```

```python
import jax
import jax.numpy as jnp
from jax import lax
from jax.sharding import PartitionSpec as P
from jax.experimental import pallas as pl
from jax.experimental.pallas import tpu as pltpu

D = 768
HD = 64
FF = 2048
FE = 2048
WINDOW = 1024
HH = 768


EPSILON = 1e-06
TINY_SQUARE = 1e-30
SCALE_FLOOR = 0.001
DECAY_RATE = 0.5
CLIP_LIMIT = 0.5
STEP_RATE = 0.5


def from_behind(value, axis, steps):
    count = lax.axis_size(axis)
    leading, last = (max(0, -steps), min(count, count - steps))
    return lax.ppermute(value, axis, [(source, source + steps) for source in range(leading, last)])


def rms_norm(values, gain_vec):
    inv_rms = lax.rsqrt(jnp.mean(values * values, axis=-1, keepdims=True) + EPSILON)
    return values * inv_rms * gain_vec


def swiglu(gate_up):
    return jax.nn.silu(gate_up[:, 0]) * gate_up[:, 1]


def rotate(values, cosine, sine_tab):
    half_dim = values.shape[-1] // 2
    first_half = values[..., :half_dim]
    second_half = values[..., half_dim:]
    cos_b = cosine[:, None, :]
    sin_b = sine_tab[:, None, :]
    return jnp.concatenate(
        [first_half * cos_b - second_half * sin_b, second_half * cos_b + first_half * sin_b],
        axis=-1,
    )


def slot_tables(block_routes, experts, capacity):
    flat_routes = block_routes.reshape(-1)
    route_count = flat_routes.shape[0]
    onehot = (flat_routes[:, None] == jnp.arange(experts, dtype=jnp.int32)[None, :]).astype(
        jnp.int32
    )
    rank_in = jnp.sum(
        (jnp.cumsum(onehot, axis=0, dtype=jnp.int32) - 1) * onehot, axis=1, dtype=jnp.int32
    )
    slot_index = flat_routes * capacity + rank_in
    owner_route = (
        jnp.zeros((experts * capacity,), jnp.int32)
        .at[slot_index]
        .set(jnp.arange(route_count, dtype=jnp.int32))
    )
    filled = jnp.zeros((experts * capacity,), jnp.int32).at[slot_index].set(1)
    return (slot_index, owner_route, filled)


def block_view(queries, keys_ext, values_ext, seg_own, seg_ext, start_row, base_pos):
    block_len = queries.shape[0]
    block_rows = min(512, block_len)
    query_rows = lax.dynamic_slice_in_dim(queries, start_row, block_rows, 0)
    key_rows = lax.dynamic_slice_in_dim(
        keys_ext, start_row + block_len - WINDOW, block_rows + WINDOW, 0
    )
    value_rows = lax.dynamic_slice_in_dim(
        values_ext, start_row + block_len - WINDOW, block_rows + WINDOW, 0
    )
    scores = (
        jnp.einsum("qhd,khd->hqk", query_rows, key_rows, preferred_element_type=jnp.float32) * 0.125
    )
    query_pos = start_row + jnp.arange(block_rows, dtype=jnp.int32)
    key_pos = start_row - WINDOW + jnp.arange(block_rows + WINDOW, dtype=jnp.int32)
    distance = query_pos[:, None] - key_pos[None, :]
    seg_query = lax.dynamic_slice_in_dim(seg_own, start_row, block_rows, 0)
    seg_key = lax.dynamic_slice_in_dim(
        seg_ext, start_row + block_len - WINDOW, block_rows + WINDOW, 0
    )
    allowed = (
        (distance >= 0)
        & (distance < WINDOW)
        & (seg_query[:, None] == seg_key[None, :])
        & (key_pos[None, :] + base_pos >= 0)
    )
    return (query_rows, key_rows, value_rows, jnp.where(allowed[None], scores, -1e30), allowed)


def factored_update(
    grad_mat, rows_old, cols_old, row_sums, col_sums, row_total, col_total, old_total, square_total
):
    rows_new = DECAY_RATE * rows_old + (1.0 - DECAY_RATE) * row_sums / col_total
    cols_new = DECAY_RATE * cols_old + (1.0 - DECAY_RATE) * col_sums / row_total
    mean_rows = (DECAY_RATE * old_total + (1.0 - DECAY_RATE) * square_total / col_total) / row_total
    second_moment = rows_new[:, None] * cols_new[None, :] / mean_rows
    return (grad_mat * lax.rsqrt(second_moment), rows_new, cols_new)


def apply_update(weight, update, update_root, square_sum, elements):
    param_scale = jnp.maximum(SCALE_FLOOR, jnp.sqrt(square_sum / elements))
    return weight - STEP_RATE * param_scale * update / jnp.maximum(1.0, update_root / CLIP_LIMIT)


def butterfly_partners():
    partners = []
    here = [lax.axis_index(name) for name in ("fsdp", "ctx", "tp")]
    for axis_number, name in enumerate(("fsdp", "ctx", "tp")):
        size = lax.axis_size(name)
        step = 1
        while step < size:
            bit = (here[axis_number] // step) % 2
            other = list(here)
            other[axis_number] = here[axis_number] + step * (1 - 2 * bit)
            partners.append(tuple(other))
            step *= 2
    return partners


def butterfly_kernel(x_ref, o_ref, stage, inbox, send_sems, recv_sems):
    partners = butterfly_partners()
    barrier = pltpu.get_barrier_semaphore()
    for partner in partners:
        pl.semaphore_signal(
            barrier, 1, device_id=partner, device_id_type=pl.DeviceIdType.MESH
        )
    pl.semaphore_wait(barrier, len(partners))
    acc = x_ref[...]
    for round_number, partner in enumerate(partners):
        stage[round_number] = acc
        copy = pltpu.make_async_remote_copy(
            src_ref=stage.at[round_number],
            dst_ref=inbox.at[round_number],
            send_sem=send_sems.at[round_number],
            recv_sem=recv_sems.at[round_number],
            device_id=partner,
            device_id_type=pl.DeviceIdType.MESH,
        )
        copy.start()
        copy.wait()
        acc = stage[round_number] + inbox[round_number]
    o_ref[...] = acc


def butterfly_sum(values, collective_id):
    flat = jnp.concatenate([v.reshape(-1).astype(jnp.float32) for v in values])
    size = flat.shape[0]
    rows = -(-size // 1024) * 8
    block = jnp.pad(flat, (0, rows * 128 - size)).reshape(rows, 128)
    rounds = sum(
        max(1, lax.axis_size(name)).bit_length() - 1 for name in ("fsdp", "ctx", "tp")
    )
    total = pl.pallas_call(
        butterfly_kernel,
        out_shape=jax.ShapeDtypeStruct((rows, 128), jnp.float32),
        in_specs=[pl.BlockSpec(memory_space=pltpu.VMEM)],
        out_specs=pl.BlockSpec(memory_space=pltpu.VMEM),
        scratch_shapes=[
            pltpu.VMEM((rounds, rows, 128), jnp.float32),
            pltpu.VMEM((rounds, rows, 128), jnp.float32),
            pltpu.SemaphoreType.DMA((rounds,)),
            pltpu.SemaphoreType.DMA((rounds,)),
        ],
        compiler_params=pltpu.CompilerParams(collective_id=collective_id, has_side_effects=True),
    )(block).reshape(-1)
    results = []
    offset = 0
    for v in values:
        results.append(total[offset : offset + v.size].reshape(v.shape))
        offset += v.size
    return results


def halving_kernel(x_ref, o_ref, stage_one, stage_two, inbox_one, inbox_two, inbox_three, sems):
    rows = o_ref.shape[0]
    chunk = 64
    fsdp_here = lax.axis_index("fsdp")
    ctx_here = lax.axis_index("ctx")
    tp_here = lax.axis_index("tp")
    bit_low = fsdp_here % 2
    bit_high = (fsdp_here // 2) % 2
    partners = [
        (fsdp_here, 1 - ctx_here, tp_here),
        (fsdp_here + 1 - 2 * bit_low, ctx_here, tp_here),
        (fsdp_here + 2 - 4 * bit_high, ctx_here, tp_here),
    ]
    barrier = pltpu.get_barrier_semaphore()
    for partner in partners:
        pl.semaphore_signal(barrier, 1, device_id=partner, device_id_type=pl.DeviceIdType.MESH)
    pl.semaphore_wait(barrier, len(partners))

    def swap(src, dst, number, partner):
        copy = pltpu.make_async_remote_copy(
            src_ref=src,
            dst_ref=dst,
            send_sem=sems.at[0, number],
            recv_sem=sems.at[1, number],
            device_id=partner,
            device_id_type=pl.DeviceIdType.MESH,
        )
        copy.start()
        copy.wait()

    swap(x_ref.at[:, pl.ds(1 - ctx_here, 1)], inbox_one, 0, partners[0])

    @pl.loop(0, rows // chunk)
    def _(step):
        part = pl.ds(pl.multiple_of(step * chunk, chunk), chunk)
        for high in range(2):
            for low in range(2):
                stage_one[high, low, part] = (
                    x_ref[2 * high + low, ctx_here, part] + inbox_one[2 * high + low, 0, part]
                )

    swap(stage_one.at[:, pl.ds(1 - bit_low, 1)], inbox_two, 1, partners[1])

    @pl.loop(0, rows // chunk)
    def _(step):
        part = pl.ds(pl.multiple_of(step * chunk, chunk), chunk)
        for high in range(2):
            stage_two[high, part] = stage_one[high, bit_low, part] + inbox_two[high, 0, part]

    swap(stage_two.at[pl.ds(1 - bit_high, 1)], inbox_three, 2, partners[2])

    @pl.loop(0, rows // chunk)
    def _(step):
        part = pl.ds(pl.multiple_of(step * chunk, chunk), chunk)
        o_ref[part] = stage_two[bit_high, part] + inbox_three[0, part]


def halving_scatter(packed, collective_id):
    count, width = packed.shape
    rows = -(-width // (128 * 64)) * 64
    block = jnp.pad(packed, ((0, 0), (0, rows * 128 - width))).reshape(count // 2, 2, rows, 128)
    own = pl.pallas_call(
        halving_kernel,
        out_shape=jax.ShapeDtypeStruct((rows, 128), jnp.float32),
        in_specs=[pl.BlockSpec(memory_space=pltpu.VMEM)],
        out_specs=pl.BlockSpec(memory_space=pltpu.VMEM),
        scratch_shapes=[
            pltpu.VMEM((2, 2, rows, 128), jnp.float32),
            pltpu.VMEM((2, rows, 128), jnp.float32),
            pltpu.VMEM((count // 2, 1, rows, 128), jnp.float32),
            pltpu.VMEM((2, 1, rows, 128), jnp.float32),
            pltpu.VMEM((1, rows, 128), jnp.float32),
            pltpu.SemaphoreType.DMA((2, 3)),
        ],
        compiler_params=pltpu.CompilerParams(
            collective_id=collective_id, has_side_effects=True, vmem_limit_bytes=60 * 1024 * 1024
        ),
    )(block)
    return own.reshape(-1)[:width]


def gather_kernel(x_ref, o_ref, inbox, send_sems, recv_sems):
    fsdp_here = lax.axis_index("fsdp")
    ctx_here = lax.axis_index("ctx")
    tp_here = lax.axis_index("tp")
    ctx_count = lax.axis_size("ctx")
    count = lax.axis_size("fsdp") * ctx_count
    me = fsdp_here * ctx_count + ctx_here
    peers = []
    for offset in range(1, count):
        other = (me + offset) % count
        peers.append((other // ctx_count, other % ctx_count, tp_here))
    barrier = pltpu.get_barrier_semaphore()
    for peer in peers:
        pl.semaphore_signal(barrier, 1, device_id=peer, device_id_type=pl.DeviceIdType.MESH)
    pl.semaphore_wait(barrier, len(peers))
    copies = []
    for number, peer in enumerate(peers):
        copy = pltpu.make_async_remote_copy(
            src_ref=x_ref,
            dst_ref=inbox.at[me],
            send_sem=send_sems.at[number],
            recv_sem=recv_sems.at[me],
            device_id=peer,
            device_id_type=pl.DeviceIdType.MESH,
        )
        copy.start()
        copies.append(copy)
    o_ref[me] = x_ref[...]
    for copy in copies:
        copy.wait_send()
    for offset in range(1, count):
        source = (me + count - offset) % count
        pltpu.make_async_remote_copy(
            src_ref=x_ref,
            dst_ref=inbox.at[source],
            send_sem=send_sems.at[0],
            recv_sem=recv_sems.at[source],
            device_id=peers[0],
            device_id_type=pl.DeviceIdType.MESH,
        ).wait_recv()
        o_ref[source] = inbox[source]


def gather_shards(flat, collective_id):
    size = flat.shape[0]
    rows = -(-size // 2048) * 16
    block = jnp.pad(flat, (0, rows * 128 - size)).reshape(rows, 128)
    count = lax.axis_size("fsdp") * lax.axis_size("ctx")
    full = pl.pallas_call(
        gather_kernel,
        out_shape=jax.ShapeDtypeStruct((count, rows, 128), flat.dtype),
        in_specs=[pl.BlockSpec(memory_space=pltpu.VMEM)],
        out_specs=pl.BlockSpec(memory_space=pltpu.VMEM),
        scratch_shapes=[
            pltpu.VMEM((count, rows, 128), flat.dtype),
            pltpu.SemaphoreType.DMA((count - 1,)),
            pltpu.SemaphoreType.DMA((count,)),
        ],
        compiler_params=pltpu.CompilerParams(collective_id=collective_id, has_side_effects=True),
    )(block)
    return full.reshape(count, rows * 128)[:, :size]


def swiglu_experts(gate_up):
    return jax.nn.silu(gate_up[:, :, 0]) * gate_up[:, :, 1]


def gather_packed(pieces, axes, use_kernel=False):
    flat = jnp.concatenate([piece.reshape(-1) for piece, _ in pieces])
    if use_kernel:
        full = gather_shards(flat, 4)
    else:
        full = lax.all_gather(flat, axes, axis=0, tiled=False)
    count = full.shape[0]
    results = []
    offset = 0
    for piece, dim in pieces:
        size = piece.size
        part = full[:, offset : offset + size].reshape((count,) + piece.shape)
        offset += size
        part = jnp.moveaxis(part, 0, dim)
        shape = list(piece.shape)
        shape[dim] *= count
        results.append(part.reshape(shape))
    return results


def scatter_packed(pieces, axes, count, use_kernel=False):
    columns = []
    local_shapes = []
    for grad, dim in pieces:
        shape = grad.shape
        split = shape[:dim] + (count, shape[dim] // count) + shape[dim + 1 :]
        local_shapes.append(shape[:dim] + (shape[dim] // count,) + shape[dim + 1 :])
        part = jnp.moveaxis(grad.reshape(split), dim, 0)
        columns.append(part.reshape(count, -1))
    packed = jnp.concatenate(columns, axis=1)
    if use_kernel:
        own = halving_scatter(packed, 3)
    else:
        width = packed.shape[1]
        rows = -(-width // 1024) * 8
        packed = jnp.pad(packed, ((0, 0), (0, rows * 128 - width))).reshape(count * rows, 128)
        own = lax.psum_scatter(packed, axes, scatter_dimension=0, tiled=True).reshape(-1)
    results = []
    offset = 0
    for local_shape in local_shapes:
        size = 1
        for extent in local_shape:
            size *= extent
        results.append(own[offset : offset + size].reshape(local_shape))
        offset += size
    return results


def experts_dense(normed_two, grad_out, weights, expert_in_all, expert_down_all):
    gate_up = jnp.einsum(
        "td,edgf->etgf", normed_two, expert_in_all, preferred_element_type=jnp.float32
    )
    act, act_back = jax.vjp(swiglu_experts, gate_up)
    hidden = act.astype(jnp.bfloat16)
    outs = jnp.einsum("etf,efd->etd", hidden, expert_down_all, preferred_element_type=jnp.float32)
    weights_e = weights.T[:, :, None]
    combined = jnp.sum(weights_e * outs, axis=0)
    gate_dots = jnp.sum(outs * grad_out[None], axis=-1).T
    grad_outs = (weights_e * grad_out[None]).astype(jnp.bfloat16)
    grad_hidden = jnp.einsum(
        "etd,efd->etf", grad_outs, expert_down_all, preferred_element_type=jnp.float32
    )
    grad_gate_up = act_back(grad_hidden)[0].astype(jnp.bfloat16)
    grad_down = jnp.einsum("etf,etd->efd", hidden, grad_outs, preferred_element_type=jnp.float32)
    grad_in = jnp.einsum(
        "td,etgf->edgf", normed_two, grad_gate_up, preferred_element_type=jnp.float32
    )
    grad_rows = jnp.einsum(
        "etgf,edgf->td", grad_gate_up, expert_in_all, preferred_element_type=jnp.float32
    )
    return combined, gate_dots, grad_rows, grad_in, grad_down


def experts_routed(
    normed_two, grad_out, route_rows, gate_probs, expert_in_low, expert_down_low, capacity
):
    block_len, model_width = normed_two.shape
    experts = lax.axis_size("fsdp")
    slot_index, owner_route, filled = slot_tables(route_rows, experts, capacity)
    fill_mask = filled.astype(jnp.bfloat16)[:, None]
    route_grads = (
        (gate_probs[:, :, None] * grad_out[:, None, :])
        .astype(jnp.bfloat16)
        .reshape(2 * block_len, model_width)
    )
    send_rows = jnp.stack(
        [
            (normed_two[owner_route // 2] * fill_mask).reshape(experts, capacity, model_width),
            (route_grads[owner_route] * fill_mask).reshape(experts, capacity, model_width),
        ],
        axis=1,
    )
    exchange = lambda rows: lax.all_to_all(rows, "fsdp", split_axis=0, concat_axis=0, tiled=True)
    pair_count = lax.axis_size("tp")
    swap = lambda rows: lax.ppermute(
        rows, "tp", [(index, index + 1 - 2 * (index % 2)) for index in range(pair_count)]
    )
    half = capacity // 2
    side = lax.axis_index("tp") % 2
    mine = exchange(lax.dynamic_slice_in_dim(send_rows, side * half, half, 2))
    received_both = jnp.concatenate([mine, swap(mine)], axis=2)
    received = received_both[:, 0].reshape(experts * capacity, model_width)
    grad_received = received_both[:, 1].reshape(experts * capacity, model_width)
    gate_up = jnp.einsum("rd,dgf->rgf", received, expert_in_low, preferred_element_type=jnp.float32)
    act, act_back = jax.vjp(swiglu, gate_up)
    hidden = act.astype(jnp.bfloat16)
    outs = jnp.dot(hidden, expert_down_low, preferred_element_type=jnp.float32)
    grad_hidden = jnp.einsum(
        "rd,fd->rf", grad_received, expert_down_low, preferred_element_type=jnp.float32
    )
    grad_gate_up = act_back(grad_hidden)[0].astype(jnp.bfloat16)
    grad_in = jnp.einsum("rd,rgf->dgf", received, grad_gate_up, preferred_element_type=jnp.float32)
    grad_down = jnp.einsum("rf,rd->fd", hidden, grad_received, preferred_element_type=jnp.float32)
    grad_expert_rows = jnp.einsum(
        "rgf,dgf->rd", grad_gate_up, expert_in_low, preferred_element_type=jnp.float32
    )
    pair_sums = []
    for rows in (outs, grad_expert_rows):
        rows = rows.reshape(experts, capacity, model_width)
        pair_sums.append(rows[:, :half] + swap(rows[:, half:]))
    held = exchange(jnp.stack(pair_sums, axis=1).astype(jnp.bfloat16))
    slot_expert = slot_index // capacity
    slot_rank = slot_index % capacity
    in_side = ((slot_rank // half) == side)[:, None]
    local_slot = slot_expert * half + slot_rank % half
    picked_rows = []
    for which in range(2):
        rows = held[:, which].reshape(experts * half, model_width)[local_slot]
        picked_rows.append(
            jnp.where(in_side, rows.astype(jnp.float32), 0.0).reshape(block_len, 2, model_width)
        )
    route_out, grad_routes = picked_rows
    combined = jnp.sum(gate_probs[:, :, None] * route_out, axis=1)
    gate_dots = jnp.sum(grad_out[:, None, :] * route_out, axis=-1)
    grad_rows = jnp.sum(grad_routes, axis=1)
    return combined, gate_dots, grad_rows, grad_in, grad_down


def local(
    layer_input,
    segments,
    routes,
    cotangent,
    gains,
    attention_in,
    attention_out,
    router_weight,
    shared_in,
    shared_down,
    expert_in,
    expert_down,
    model_stats,
    head_stats,
    value_columns,
    hidden_stats,
    router_state,
    expert_model_stats,
    expert_hidden_stats,
):
    block_len = layer_input.shape[1]
    model_width = layer_input.shape[2]
    experts = router_weight.shape[1]
    dense_experts = False
    capacity = min(block_len, 4 * block_len // experts)
    ctx_index = lax.axis_index("ctx")
    tp_index = lax.axis_index("tp")
    fsdp_index = lax.axis_index("fsdp")
    shard_index = lax.axis_index(("fsdp", "ctx"))
    shard_count = lax.axis_size(("fsdp", "ctx"))
    ctx_count = lax.axis_size("ctx")
    base_pos = ctx_index * block_len
    low = lambda v: v.astype(jnp.bfloat16)
    dense_pieces = [
        (low(gains), 1),
        (low(attention_in), 0),
        (low(attention_out), 1),
        (low(router_weight), 0),
        (low(shared_in), 0),
        (low(shared_down), 1),
    ]
    if shard_count <= 8:
        dense_full = gather_packed(dense_pieces, ("fsdp", "ctx"), True)
    else:
        dense_full = gather_packed(dense_pieces[:2], ("fsdp", "ctx")) + gather_packed(
            dense_pieces[2:], ("fsdp", "ctx")
        )
    gain_low, attn_in_low, attn_out_low, router_low, shared_in_low, shared_down_low = dense_full
    if ctx_count == 2:
        flip = lambda v: lax.ppermute(v, "ctx", [(0, 1), (1, 0)])
        in_pair = [low(expert_in), flip(low(expert_in))]
        down_pair = [low(expert_down), flip(low(expert_down))]
        if_first = lambda pair, axis: jnp.where(
            ctx_index == 0,
            jnp.concatenate(pair, axis=axis),
            jnp.concatenate(pair[::-1], axis=axis),
        )
        expert_in_low = if_first(in_pair, 1)[0]
        expert_down_low = if_first(down_pair, 2)[0]
    else:
        expert_in_low = lax.all_gather(low(expert_in), "ctx", axis=1, tiled=True)[0]
        expert_down_low = lax.all_gather(low(expert_down), "ctx", axis=2, tiled=True)[0]
    residual = layer_input[0].astype(jnp.float32)
    gain_one = gain_low[0].astype(jnp.float32)
    gain_two = gain_low[1].astype(jnp.float32)
    normed_one, norm_one_back = jax.vjp(rms_norm, residual, gain_one)
    normed_one = normed_one.astype(jnp.bfloat16)
    projected = jnp.einsum(
        "td,dgf->tgf", normed_one, attn_in_low, preferred_element_type=jnp.float32
    )
    local_cols = projected.shape[2]
    local_heads = local_cols // HD
    half_dim = HD // 2
    frequency = 10000.0 ** (-jnp.arange(half_dim, dtype=jnp.float32) / half_dim)
    angles = (base_pos + jnp.arange(block_len, dtype=jnp.int32)).astype(jnp.float32)[
        :, None
    ] * frequency[None, :]
    cosine = jnp.cos(angles)
    sine_tab = jnp.sin(angles)
    queries = rotate(projected[:, 0].reshape(block_len, local_heads, HD), cosine, sine_tab).astype(
        jnp.bfloat16
    )
    keys_own = rotate(projected[:, 1].reshape(block_len, local_heads, HD), cosine, sine_tab).astype(
        jnp.bfloat16
    )
    values_own = projected[:, 2].reshape(block_len, local_heads, HD).astype(jnp.bfloat16)
    seg_own = segments[0].astype(jnp.bfloat16)
    keys_prev, values_prev, seg_prev = from_behind((keys_own, values_own, seg_own), "ctx", 1)
    keys_ext = jnp.concatenate([keys_prev, keys_own], axis=0)
    values_ext = jnp.concatenate([values_prev, values_own], axis=0)
    seg_ext = jnp.concatenate([seg_prev, seg_own], axis=0)
    block_rows = min(512, block_len)
    block_total = block_len // block_rows
    starts = jnp.arange(block_total, dtype=jnp.int32) * block_rows

    def forward_block(start_row):
        query_rows, key_rows, value_rows, masked, allowed = block_view(
            queries, keys_ext, values_ext, seg_own, seg_ext, start_row, base_pos
        )
        row_max = jnp.max(masked, axis=-1, keepdims=True)
        exp_terms = jnp.where(allowed[None], jnp.exp(masked - row_max), 0.0)
        row_total = jnp.sum(exp_terms, axis=-1, keepdims=True)
        attn_probs = (exp_terms / row_total).astype(jnp.bfloat16)
        attended = jnp.einsum(
            "hqk,khd->qhd", attn_probs, value_rows, preferred_element_type=jnp.float32
        )
        return (attended, row_max + jnp.log(row_total))

    attended, log_totals = lax.map(forward_block, starts)
    mixed_heads = attended.reshape(block_len, local_cols).astype(jnp.bfloat16)
    attn_total = lax.psum(
        jnp.dot(mixed_heads, attn_out_low, preferred_element_type=jnp.float32), "tp"
    )
    after_attn = residual + attn_total
    normed_two, norm_two_back = jax.vjp(rms_norm, after_attn, gain_two)
    normed_two = normed_two.astype(jnp.bfloat16)
    logits = jnp.dot(normed_two, router_low, preferred_element_type=jnp.float32)
    route_rows = routes[0]
    onehot = (route_rows[:, :, None] == jnp.arange(experts, dtype=jnp.int32)[None, None, :]).astype(
        jnp.float32
    )
    picked = jnp.sum(onehot * logits[:, None, :], axis=-1)
    gate_probs = jax.nn.softmax(picked, axis=-1)
    upstream = cotangent[0]
    grad_out = upstream.astype(jnp.float32)
    if dense_experts:
        weights = jnp.sum(gate_probs[:, :, None] * onehot, axis=1)
        combined, dots_e, grad_rows, grad_expert_in, grad_expert_down = experts_dense(
            normed_two, grad_out, weights, expert_in_all, expert_down_all
        )
        gate_dots = jnp.sum(onehot * dots_e[:, None, :], axis=-1)
    else:
        combined, gate_dots, grad_rows, grad_expert_in, grad_expert_down = experts_routed(
            normed_two,
            grad_out,
            route_rows,
            gate_probs,
            expert_in_low,
            expert_down_low,
            capacity,
        )
    shared_gate_up = jnp.einsum(
        "td,dgf->tgf", normed_two, shared_in_low, preferred_element_type=jnp.float32
    )
    shared_act, shared_act_back = jax.vjp(swiglu, shared_gate_up)
    shared_hidden = shared_act.astype(jnp.bfloat16)
    shared_out = jnp.dot(shared_hidden, shared_down_low, preferred_element_type=jnp.float32)
    grad_shared_hidden = jnp.einsum(
        "td,fd->tf", upstream, shared_down_low, preferred_element_type=jnp.float32
    )
    grad_shared_gate_up = shared_act_back(grad_shared_hidden)[0].astype(jnp.bfloat16)
    partial_two = (
        jnp.einsum(
            "tgf,dgf->td", grad_shared_gate_up, shared_in_low, preferred_element_type=jnp.float32
        )
        + grad_rows
    )
    branch_total, grad_normed_part, gate_total = lax.psum(
        (shared_out + combined, partial_two, gate_dots), "tp"
    )
    layer_out = after_attn + branch_total
    grad_picked = gate_probs * (
        gate_total - jnp.sum(gate_probs * gate_total, axis=-1, keepdims=True)
    )
    grad_logits = jnp.sum(grad_picked[:, :, None] * onehot, axis=1).astype(jnp.bfloat16)
    grad_shared_in = jnp.einsum(
        "td,tgf->dgf", normed_two, grad_shared_gate_up, preferred_element_type=jnp.float32
    )
    grad_shared_down = jnp.einsum(
        "tf,td->fd", shared_hidden, upstream, preferred_element_type=jnp.float32
    )
    grad_router = jnp.einsum(
        "td,te->de", normed_two, grad_logits, preferred_element_type=jnp.float32
    )
    grad_normed_two = grad_normed_part + jnp.einsum(
        "te,de->td", grad_logits, router_low, preferred_element_type=jnp.float32
    )
    grad_after, grad_gain_two = norm_two_back(grad_normed_two)
    grad_after = grad_after + grad_out
    grad_attn_low = grad_after.astype(jnp.bfloat16)
    grad_attn_out = jnp.einsum(
        "tc,td->cd", mixed_heads, grad_attn_low, preferred_element_type=jnp.float32
    )
    first_grads = [
        (grad_attn_out, 1),
        (grad_router, 0),
        (grad_shared_in, 0),
        (grad_shared_down, 1),
        (grad_gain_two, 0),
    ]
    if dense_experts:
        fe_local = expert_down.shape[1]
        first_grads += [
            (grad_expert_in.reshape(shard_count * expert_in.shape[1], 2, fe_local), 0),
            (
                grad_expert_down.reshape(experts, fe_local, ctx_count, model_width // ctx_count)
                .transpose(0, 2, 1, 3)
                .reshape(shard_count * fe_local, model_width // ctx_count),
                0,
            ),
        ]
    if not dense_experts:
        own_expert_in = lax.psum_scatter(grad_expert_in[None], "ctx", scatter_dimension=1, tiled=True)
        own_expert_down = lax.psum_scatter(
            grad_expert_down[None], "ctx", scatter_dimension=2, tiled=True
        )
    grad_heads = (
        jnp.einsum("td,cd->tc", grad_attn_low, attn_out_low, preferred_element_type=jnp.float32)
        .astype(jnp.bfloat16)
        .reshape(block_len, local_heads, HD)
    )

    def backward_block(block_number, running):
        grad_keys, grad_values, grad_queries = running
        start_row = block_number * block_rows
        query_rows, key_rows, value_rows, masked, allowed = block_view(
            queries, keys_ext, values_ext, seg_own, seg_ext, start_row, base_pos
        )
        log_total = lax.dynamic_index_in_dim(log_totals, block_number, 0, keepdims=False)
        attn_probs = jnp.where(allowed[None], jnp.exp(masked - log_total), 0.0)
        grad_block = lax.dynamic_slice_in_dim(grad_heads, start_row, block_rows, 0)
        grad_probs = jnp.einsum(
            "qhd,khd->hqk", grad_block, value_rows, preferred_element_type=jnp.float32
        )
        inner_sum = jnp.sum(attn_probs * grad_probs, axis=-1, keepdims=True)
        grad_scores = (attn_probs * (grad_probs - inner_sum)).astype(jnp.bfloat16)
        grad_query_rows = (
            jnp.einsum("hqk,khd->qhd", grad_scores, key_rows, preferred_element_type=jnp.float32)
            * 0.125
        )
        grad_key_rows = (
            jnp.einsum("hqk,qhd->khd", grad_scores, query_rows, preferred_element_type=jnp.float32)
            * 0.125
        )
        grad_value_rows = jnp.einsum(
            "hqk,qhd->khd",
            attn_probs.astype(jnp.bfloat16),
            grad_block,
            preferred_element_type=jnp.float32,
        )
        key_offset = start_row + block_len - WINDOW
        grad_keys = lax.dynamic_update_slice_in_dim(
            grad_keys,
            lax.dynamic_slice_in_dim(grad_keys, key_offset, block_rows + WINDOW, 0) + grad_key_rows,
            key_offset,
            0,
        )
        grad_values = lax.dynamic_update_slice_in_dim(
            grad_values,
            lax.dynamic_slice_in_dim(grad_values, key_offset, block_rows + WINDOW, 0)
            + grad_value_rows,
            key_offset,
            0,
        )
        grad_queries = lax.dynamic_update_slice_in_dim(grad_queries, grad_query_rows, start_row, 0)
        return (grad_keys, grad_values, grad_queries)

    zero_ext = jnp.zeros((2 * block_len, local_heads, HD), jnp.float32)
    zero_own = jnp.zeros((block_len, local_heads, HD), jnp.float32)
    grad_keys, grad_values, grad_queries = lax.fori_loop(
        0, block_total, backward_block, (zero_ext, zero_ext, zero_own)
    )
    rim_keys, rim_values = (
        from_behind(grad_keys[:block_len].astype(jnp.bfloat16), "ctx", -1).astype(jnp.float32),
        from_behind(grad_values[:block_len].astype(jnp.bfloat16), "ctx", -1).astype(jnp.float32),
    )
    grad_keys_own = grad_keys[block_len:] + rim_keys
    grad_values_own = grad_values[block_len:] + rim_values
    grad_query_raw = rotate(grad_queries, cosine, -sine_tab)
    grad_key_raw = rotate(grad_keys_own, cosine, -sine_tab)
    grad_projected = (
        jnp.stack([grad_query_raw, grad_key_raw, grad_values_own], axis=1)
        .reshape(block_len, 3, local_cols)
        .astype(jnp.bfloat16)
    )
    grad_attn_in = jnp.einsum(
        "td,tgf->dgf", normed_one, grad_projected, preferred_element_type=jnp.float32
    )
    partial_one = jnp.einsum(
        "tgf,dgf->td", grad_projected, attn_in_low, preferred_element_type=jnp.float32
    )
    tp_one = lax.psum(partial_one, "tp")
    halving = lax.axis_size("fsdp") == 4 and ctx_count == 2
    all_own = scatter_packed(
        first_grads + [(grad_attn_in, 0)],
        ("fsdp", "ctx"),
        shard_count,
        halving,
    )
    own_attn_out, own_router, own_shared_in, own_shared_down, own_gain_two = all_own[:5]
    own_attn_in = all_own[-1]
    grad_residual, grad_gain_one = norm_one_back(tp_one + 0.0 * own_attn_in[0, 0, 0])
    input_grad = grad_after + grad_residual
    if dense_experts:
        own_expert_in = all_own[5][None]
        own_expert_down = all_own[6][None]
    lead_tp = (tp_index == 0).astype(jnp.float32)
    first_shard = (shard_index == 0).astype(jnp.float32)
    first_ctx = (ctx_index == 0).astype(jnp.float32)
    d_local = gains.shape[1]
    ff_local = shared_down.shape[0]
    fe_local = expert_down.shape[1]
    d_quarter = expert_in.shape[1]
    square_attn_in = own_attn_in * own_attn_in + TINY_SQUARE
    square_attn_out = own_attn_out * own_attn_out + TINY_SQUARE
    square_shared_in = own_shared_in * own_shared_in + TINY_SQUARE
    square_shared_down = own_shared_down * own_shared_down + TINY_SQUARE
    square_expert_in = own_expert_in[0] * own_expert_in[0] + TINY_SQUARE
    square_expert_down = own_expert_down[0] * own_expert_down[0] + TINY_SQUARE
    model_part = lax.dynamic_update_slice(
        jnp.zeros((4, D), jnp.float32),
        jnp.stack(
            [
                jnp.sum(square_attn_in, axis=(1, 2)),
                jnp.sum(square_shared_in, axis=(1, 2)),
                jnp.sum(square_attn_out, axis=0),
                jnp.sum(square_shared_down, axis=0),
            ]
        ),
        (0, shard_index * d_local),
    )
    head_part = lax.dynamic_update_slice(
        jnp.zeros((4, HH), jnp.float32),
        jnp.concatenate(
            [jnp.sum(square_attn_in, axis=0), jnp.sum(square_attn_out, axis=1)[None]], axis=0
        ),
        (0, tp_index * local_cols),
    )
    hidden_part = lax.dynamic_update_slice(
        jnp.zeros((3, FF), jnp.float32),
        jnp.concatenate(
            [jnp.sum(square_shared_in, axis=0), jnp.sum(square_shared_down, axis=1)[None]], axis=0
        ),
        (0, tp_index * ff_local),
    )
    expert_model_part = lax.dynamic_update_slice(
        jnp.zeros((experts, 2, D), jnp.float32),
        jnp.stack([jnp.sum(square_expert_in, axis=(1, 2)), jnp.sum(square_expert_down, axis=0)])[
            None
        ],
        (fsdp_index, 0, ctx_index * d_quarter),
    )
    expert_hidden_part = lax.dynamic_update_slice(
        jnp.zeros((experts, 3, FE), jnp.float32),
        jnp.concatenate(
            [jnp.sum(square_expert_in, axis=0), jnp.sum(square_expert_down, axis=1)[None]], axis=0
        )[None],
        (fsdp_index, 0, tp_index * fe_local),
    )
    scalar_part = jnp.stack(
        [
            lead_tp * jnp.sum(gains * gains),
            jnp.sum(attention_in * attention_in),
            jnp.sum(attention_out * attention_out),
            lead_tp * jnp.sum(router_weight * router_weight),
            jnp.sum(shared_in * shared_in),
            jnp.sum(shared_down * shared_down),
            jnp.sum(expert_in * expert_in),
            jnp.sum(expert_down * expert_down),
            lead_tp * jnp.sum(model_stats[2]),
            first_shard * jnp.sum(head_stats[2]),
            lead_tp * jnp.sum(model_stats[3]),
            first_shard * jnp.sum(hidden_stats[2]),
        ]
    )
    expert_old_part = lax.dynamic_update_slice(
        jnp.zeros((2, experts), jnp.float32),
        jnp.stack(
            [
                lead_tp * jnp.sum(expert_model_stats[0, 0]),
                first_ctx * jnp.sum(expert_hidden_stats[0, 2]),
            ]
        )[:, None],
        (0, fsdp_index),
    )
    global_sums = butterfly_sum(
        [
            model_part,
            head_part,
            hidden_part,
            expert_model_part,
            expert_hidden_part,
            scalar_part,
            expert_old_part,
            lead_tp * grad_gain_one,
        ],
        1,
    )
    (
        model_sum,
        head_sum,
        hidden_sum,
        expert_model_sum,
        expert_hidden_sum,
        scalar_sum,
        expert_old_sum,
        gain_one_sum,
    ) = global_sums
    own_gain_one = lax.dynamic_slice_in_dim(gain_one_sum, shard_index * d_local, d_local)
    own_gains = jnp.stack([own_gain_one, own_gain_two])
    shard_start = shard_index * d_local
    gain_state = DECAY_RATE * model_stats[0:2] + (1.0 - DECAY_RATE) * (
        own_gains * own_gains + TINY_SQUARE
    )
    update_gains = own_gains * lax.rsqrt(gain_state)
    router_new = DECAY_RATE * router_state + (1.0 - DECAY_RATE) * (
        own_router * own_router + TINY_SQUARE
    )
    update_router = own_router * lax.rsqrt(router_new)
    attn_cols_old = jnp.concatenate([head_stats[0:2], value_columns[None]], axis=0).reshape(-1)
    update_attn_in, rows_attn_in, cols_attn_in = factored_update(
        own_attn_in.reshape(d_local, 3 * local_cols),
        model_stats[2],
        attn_cols_old,
        lax.dynamic_slice_in_dim(model_sum[0], shard_start, d_local),
        lax.dynamic_slice_in_dim(head_sum[0:3], tp_index * local_cols, local_cols, 1).reshape(-1),
        D,
        3 * HH,
        scalar_sum[8],
        jnp.sum(model_sum[0]),
    )
    update_attn_out, rows_attn_out, cols_attn_out = factored_update(
        own_attn_out,
        head_stats[2],
        model_stats[4],
        lax.dynamic_slice_in_dim(head_sum[3], tp_index * local_cols, local_cols),
        lax.dynamic_slice_in_dim(model_sum[2], shard_start, d_local),
        HH,
        D,
        scalar_sum[9],
        jnp.sum(head_sum[3]),
    )
    update_shared_in, rows_shared_in, cols_shared_in = factored_update(
        own_shared_in.reshape(d_local, 2 * ff_local),
        model_stats[3],
        hidden_stats[0:2].reshape(-1),
        lax.dynamic_slice_in_dim(model_sum[1], shard_start, d_local),
        lax.dynamic_slice_in_dim(hidden_sum[0:2], tp_index * ff_local, ff_local, 1).reshape(-1),
        D,
        2 * FF,
        scalar_sum[10],
        jnp.sum(model_sum[1]),
    )
    update_shared_down, rows_shared_down, cols_shared_down = factored_update(
        own_shared_down,
        hidden_stats[2],
        model_stats[5],
        lax.dynamic_slice_in_dim(hidden_sum[2], tp_index * ff_local, ff_local),
        lax.dynamic_slice_in_dim(model_sum[3], shard_start, d_local),
        FF,
        D,
        scalar_sum[11],
        jnp.sum(hidden_sum[2]),
    )
    own_expert_model = lax.dynamic_index_in_dim(expert_model_sum, fsdp_index, 0, keepdims=False)
    own_expert_hidden = lax.dynamic_index_in_dim(expert_hidden_sum, fsdp_index, 0, keepdims=False)
    old_expert_totals = lax.dynamic_index_in_dim(expert_old_sum, fsdp_index, 1, keepdims=False)
    update_expert_in, rows_expert_in, cols_expert_in = factored_update(
        own_expert_in[0].reshape(d_quarter, 2 * fe_local),
        expert_model_stats[0, 0],
        expert_hidden_stats[0, 0:2].reshape(-1),
        lax.dynamic_slice_in_dim(own_expert_model[0], ctx_index * d_quarter, d_quarter),
        lax.dynamic_slice_in_dim(own_expert_hidden[0:2], tp_index * fe_local, fe_local, 1).reshape(
            -1
        ),
        D,
        2 * FE,
        old_expert_totals[0],
        jnp.sum(own_expert_model[0]),
    )
    update_expert_down, rows_expert_down, cols_expert_down = factored_update(
        own_expert_down[0],
        expert_hidden_stats[0, 2],
        expert_model_stats[0, 1],
        lax.dynamic_slice_in_dim(own_expert_hidden[2], tp_index * fe_local, fe_local),
        lax.dynamic_slice_in_dim(own_expert_model[1], ctx_index * d_quarter, d_quarter),
        FE,
        D,
        old_expert_totals[1],
        jnp.sum(own_expert_hidden[2]),
    )
    clip_part = jnp.stack(
        [
            lead_tp * jnp.sum(update_gains * update_gains),
            jnp.sum(update_attn_in * update_attn_in),
            jnp.sum(update_attn_out * update_attn_out),
            lead_tp * jnp.sum(update_router * update_router),
            jnp.sum(update_shared_in * update_shared_in),
            jnp.sum(update_shared_down * update_shared_down),
            jnp.sum(update_expert_in * update_expert_in),
            jnp.sum(update_expert_down * update_expert_down),
        ]
    )
    clip_total = butterfly_sum([clip_part], 2)[0]
    elements = jnp.array(
        [
            2 * D,
            D * 3 * HH,
            HH * D,
            D * experts,
            D * 2 * FF,
            FF * D,
            experts * D * 2 * FE,
            experts * FE * D,
        ],
        jnp.float32,
    )
    update_roots = jnp.sqrt(clip_total / elements)
    new_gains = apply_update(gains, update_gains, update_roots[0], scalar_sum[0], elements[0])
    new_attn_in = apply_update(
        attention_in,
        update_attn_in.reshape(attention_in.shape),
        update_roots[1],
        scalar_sum[1],
        elements[1],
    )
    new_attn_out = apply_update(
        attention_out, update_attn_out, update_roots[2], scalar_sum[2], elements[2]
    )
    new_router = apply_update(
        router_weight, update_router, update_roots[3], scalar_sum[3], elements[3]
    )
    new_shared_in = apply_update(
        shared_in,
        update_shared_in.reshape(shared_in.shape),
        update_roots[4],
        scalar_sum[4],
        elements[4],
    )
    new_shared_down = apply_update(
        shared_down, update_shared_down, update_roots[5], scalar_sum[5], elements[5]
    )
    new_expert_in = apply_update(
        expert_in,
        update_expert_in.reshape(expert_in.shape),
        update_roots[6],
        scalar_sum[6],
        elements[6],
    )
    new_expert_down = apply_update(
        expert_down,
        update_expert_down.reshape(expert_down.shape),
        update_roots[7],
        scalar_sum[7],
        elements[7],
    )
    new_model_stats = jnp.concatenate(
        [gain_state, jnp.stack([rows_attn_in, rows_shared_in, cols_attn_out, cols_shared_down])],
        axis=0,
    )
    attn_cols_new = cols_attn_in.reshape(3, local_cols)
    new_head_stats = jnp.concatenate([attn_cols_new[0:2], rows_attn_out[None]], axis=0)
    new_value_columns = attn_cols_new[2]
    new_hidden_stats = jnp.concatenate(
        [cols_shared_in.reshape(2, ff_local), rows_shared_down[None]], axis=0
    )
    new_expert_model_stats = jnp.stack([rows_expert_in, cols_expert_down])[None]
    new_expert_hidden_stats = jnp.concatenate(
        [cols_expert_in.reshape(2, fe_local), rows_expert_down[None]], axis=0
    )[None]
    return (
        layer_out.astype(jnp.bfloat16)[None],
        input_grad[None],
        own_gains,
        own_attn_in,
        own_attn_out,
        own_router,
        own_shared_in,
        own_shared_down,
        own_expert_in,
        own_expert_down,
        new_gains,
        new_attn_in,
        new_attn_out,
        new_router,
        new_shared_in,
        new_shared_down,
        new_expert_in,
        new_expert_down,
        new_model_stats,
        new_head_stats,
        new_value_columns,
        new_hidden_stats,
        router_new,
        new_expert_model_stats,
        new_expert_hidden_stats,
        update_roots,
    )


def solution(mesh):
    in_specs = (
        P("fsdp", "ctx", None),
        P("fsdp", "ctx"),
        P("fsdp", "ctx", None),
        P("fsdp", "ctx", None),
        P(None, ("fsdp", "ctx")),
        P(("fsdp", "ctx"), None, "tp"),
        P("tp", ("fsdp", "ctx")),
        P(("fsdp", "ctx"), None),
        P(("fsdp", "ctx"), None, "tp"),
        P("tp", ("fsdp", "ctx")),
        P("fsdp", "ctx", None, "tp"),
        P("fsdp", "tp", "ctx"),
        P(None, ("fsdp", "ctx")),
        P(None, "tp"),
        P("tp"),
        P(None, "tp"),
        P(("fsdp", "ctx"), None),
        P("fsdp", None, "ctx"),
        P("fsdp", None, "tp"),
    )
    out_specs = (
        P("fsdp", "ctx", None),
        P("fsdp", "ctx", None),
        P(None, ("fsdp", "ctx")),
        P(("fsdp", "ctx"), None, "tp"),
        P("tp", ("fsdp", "ctx")),
        P(("fsdp", "ctx"), None),
        P(("fsdp", "ctx"), None, "tp"),
        P("tp", ("fsdp", "ctx")),
        P("fsdp", "ctx", None, "tp"),
        P("fsdp", "tp", "ctx"),
        P(None, ("fsdp", "ctx")),
        P(("fsdp", "ctx"), None, "tp"),
        P("tp", ("fsdp", "ctx")),
        P(("fsdp", "ctx"), None),
        P(("fsdp", "ctx"), None, "tp"),
        P("tp", ("fsdp", "ctx")),
        P("fsdp", "ctx", None, "tp"),
        P("fsdp", "tp", "ctx"),
        P(None, ("fsdp", "ctx")),
        P(None, "tp"),
        P("tp"),
        P(None, "tp"),
        P(("fsdp", "ctx"), None),
        P("fsdp", None, "ctx"),
        P("fsdp", None, "tp"),
        P(),
    )
    return jax.shard_map(local, mesh=mesh, in_specs=in_specs, out_specs=out_specs, check_vma=False)
```

```python
import jax
import jax.numpy as jnp
from jax import lax
from jax.sharding import PartitionSpec as P
from jax.experimental import pallas as pl
from jax.experimental.pallas import tpu as pltpu

D = 768
HD = 64
FF = 2048
FE = 2048
WINDOW = 1024
HH = 768


EPSILON = 1e-06
TINY_SQUARE = 1e-30
SCALE_FLOOR = 0.001
DECAY_RATE = 0.5
CLIP_LIMIT = 0.5
STEP_RATE = 0.5


def from_behind(value, axis, steps):
    count = lax.axis_size(axis)
    leading, last = (max(0, -steps), min(count, count - steps))
    return lax.ppermute(value, axis, [(source, source + steps) for source in range(leading, last)])


def rms_norm(values, gain_vec):
    inv_rms = lax.rsqrt(jnp.mean(values * values, axis=-1, keepdims=True) + EPSILON)
    return values * inv_rms * gain_vec


def swiglu(gate_up):
    return jax.nn.silu(gate_up[:, 0]) * gate_up[:, 1]


def rotate(values, cosine, sine_tab):
    half_dim = values.shape[-1] // 2
    first_half = values[..., :half_dim]
    second_half = values[..., half_dim:]
    cos_b = cosine[:, None, :]
    sin_b = sine_tab[:, None, :]
    return jnp.concatenate(
        [first_half * cos_b - second_half * sin_b, second_half * cos_b + first_half * sin_b],
        axis=-1,
    )


def slot_tables(block_routes, experts, capacity):
    flat_routes = block_routes.reshape(-1)
    route_count = flat_routes.shape[0]
    onehot = (flat_routes[:, None] == jnp.arange(experts, dtype=jnp.int32)[None, :]).astype(
        jnp.int32
    )
    rank_in = jnp.sum(
        (jnp.cumsum(onehot, axis=0, dtype=jnp.int32) - 1) * onehot, axis=1, dtype=jnp.int32
    )
    slot_index = flat_routes * capacity + rank_in
    owner_route = (
        jnp.zeros((experts * capacity,), jnp.int32)
        .at[slot_index]
        .set(jnp.arange(route_count, dtype=jnp.int32))
    )
    filled = jnp.zeros((experts * capacity,), jnp.int32).at[slot_index].set(1)
    return (slot_index, owner_route, filled)


def block_view(queries, keys_ext, values_ext, seg_own, seg_ext, start_row, base_pos):
    block_len = queries.shape[0]
    block_rows = min(512, block_len)
    query_rows = lax.dynamic_slice_in_dim(queries, start_row, block_rows, 0)
    key_rows = lax.dynamic_slice_in_dim(
        keys_ext, start_row + block_len - WINDOW, block_rows + WINDOW, 0
    )
    value_rows = lax.dynamic_slice_in_dim(
        values_ext, start_row + block_len - WINDOW, block_rows + WINDOW, 0
    )
    scores = (
        jnp.einsum("qhd,khd->hqk", query_rows, key_rows, preferred_element_type=jnp.float32) * 0.125
    )
    query_pos = start_row + jnp.arange(block_rows, dtype=jnp.int32)
    key_pos = start_row - WINDOW + jnp.arange(block_rows + WINDOW, dtype=jnp.int32)
    distance = query_pos[:, None] - key_pos[None, :]
    seg_query = lax.dynamic_slice_in_dim(seg_own, start_row, block_rows, 0)
    seg_key = lax.dynamic_slice_in_dim(
        seg_ext, start_row + block_len - WINDOW, block_rows + WINDOW, 0
    )
    allowed = (
        (distance >= 0)
        & (distance < WINDOW)
        & (seg_query[:, None] == seg_key[None, :])
        & (key_pos[None, :] + base_pos >= 0)
    )
    return (query_rows, key_rows, value_rows, jnp.where(allowed[None], scores, -1e30), allowed)


def factored_update(
    grad_mat, rows_old, cols_old, row_sums, col_sums, row_total, col_total, old_total, square_total
):
    rows_new = DECAY_RATE * rows_old + (1.0 - DECAY_RATE) * row_sums / col_total
    cols_new = DECAY_RATE * cols_old + (1.0 - DECAY_RATE) * col_sums / row_total
    mean_rows = (DECAY_RATE * old_total + (1.0 - DECAY_RATE) * square_total / col_total) / row_total
    second_moment = rows_new[:, None] * cols_new[None, :] / mean_rows
    return (grad_mat * lax.rsqrt(second_moment), rows_new, cols_new)


def apply_update(weight, update, update_root, square_sum, elements):
    param_scale = jnp.maximum(SCALE_FLOOR, jnp.sqrt(square_sum / elements))
    return weight - STEP_RATE * param_scale * update / jnp.maximum(1.0, update_root / CLIP_LIMIT)


def butterfly_partners():
    partners = []
    here = [lax.axis_index(name) for name in ("fsdp", "ctx", "tp")]
    for axis_number, name in enumerate(("fsdp", "ctx", "tp")):
        size = lax.axis_size(name)
        step = 1
        while step < size:
            bit = (here[axis_number] // step) % 2
            other = list(here)
            other[axis_number] = here[axis_number] + step * (1 - 2 * bit)
            partners.append(tuple(other))
            step *= 2
    return partners


def butterfly_kernel(x_ref, o_ref, stage, inbox, send_sems, recv_sems):
    partners = butterfly_partners()
    barrier = pltpu.get_barrier_semaphore()
    for partner in partners:
        pl.semaphore_signal(
            barrier, 1, device_id=partner, device_id_type=pl.DeviceIdType.MESH
        )
    pl.semaphore_wait(barrier, len(partners))
    acc = x_ref[...]
    for round_number, partner in enumerate(partners):
        stage[round_number] = acc
        copy = pltpu.make_async_remote_copy(
            src_ref=stage.at[round_number],
            dst_ref=inbox.at[round_number],
            send_sem=send_sems.at[round_number],
            recv_sem=recv_sems.at[round_number],
            device_id=partner,
            device_id_type=pl.DeviceIdType.MESH,
        )
        copy.start()
        copy.wait()
        acc = stage[round_number] + inbox[round_number]
    o_ref[...] = acc


def butterfly_sum(values, collective_id):
    flat = jnp.concatenate([v.reshape(-1).astype(jnp.float32) for v in values])
    size = flat.shape[0]
    rows = -(-size // 1024) * 8
    block = jnp.pad(flat, (0, rows * 128 - size)).reshape(rows, 128)
    rounds = sum(
        max(1, lax.axis_size(name)).bit_length() - 1 for name in ("fsdp", "ctx", "tp")
    )
    total = pl.pallas_call(
        butterfly_kernel,
        out_shape=jax.ShapeDtypeStruct((rows, 128), jnp.float32),
        in_specs=[pl.BlockSpec(memory_space=pltpu.VMEM)],
        out_specs=pl.BlockSpec(memory_space=pltpu.VMEM),
        scratch_shapes=[
            pltpu.VMEM((rounds, rows, 128), jnp.float32),
            pltpu.VMEM((rounds, rows, 128), jnp.float32),
            pltpu.SemaphoreType.DMA((rounds,)),
            pltpu.SemaphoreType.DMA((rounds,)),
        ],
        compiler_params=pltpu.CompilerParams(collective_id=collective_id, has_side_effects=True),
    )(block).reshape(-1)
    results = []
    offset = 0
    for v in values:
        results.append(total[offset : offset + v.size].reshape(v.shape))
        offset += v.size
    return results


def halving_kernel(
    x_ref, o_ref, stage_a, stage_a2, stage_b, stage_b2, in_a1, in_a2, in_a3, in_b1, in_b2, in_b3, sems
):
    rows = o_ref.shape[0] // 2
    chunk = 64
    fsdp_here = lax.axis_index("fsdp")
    ctx_here = lax.axis_index("ctx")
    tp_here = lax.axis_index("tp")
    bit_low = fsdp_here % 2
    bit_high = (fsdp_here // 2) % 2
    partners = [
        (fsdp_here, 1 - ctx_here, tp_here),
        (fsdp_here + 1 - 2 * bit_low, ctx_here, tp_here),
        (fsdp_here + 2 - 4 * bit_high, ctx_here, tp_here),
    ]
    barrier = pltpu.get_barrier_semaphore()
    for partner in partners:
        pl.semaphore_signal(barrier, 1, device_id=partner, device_id_type=pl.DeviceIdType.MESH)
    pl.semaphore_wait(barrier, len(partners))
    first, second = pl.ds(0, rows), pl.ds(rows, rows)

    def swap_pair(sources, targets, number, partner_pair):
        copies = []
        for index in range(2):
            copy = pltpu.make_async_remote_copy(
                src_ref=sources[index],
                dst_ref=targets[index],
                send_sem=sems.at[0, 2 * number + index],
                recv_sem=sems.at[1, 2 * number + index],
                device_id=partner_pair[index],
                device_id_type=pl.DeviceIdType.MESH,
            )
            copy.start()
            copies.append(copy)
        for copy in copies:
            copy.wait()

    def each_chunk(body):
        @pl.loop(0, rows // chunk)
        def _(step):
            body(pl.ds(pl.multiple_of(step * chunk, chunk), chunk))

    swap_pair(
        [
            x_ref.at[:, :, pl.ds(1 - ctx_here, 1), first],
            x_ref.at[:, pl.ds(1 - bit_low, 1), :, second],
        ],
        [in_a1, in_b1],
        0,
        [partners[0], partners[1]],
    )

    def round_one(part):
        shifted = pl.ds(part.start + rows, chunk)
        for high in range(2):
            for other in range(2):
                stage_a[high, other, part] = (
                    x_ref[high, other, ctx_here, part] + in_a1[high, other, 0, part]
                )
                stage_b[high, other, part] = (
                    x_ref[high, bit_low, other, shifted] + in_b1[high, 0, other, part]
                )

    each_chunk(round_one)
    swap_pair(
        [stage_a.at[:, pl.ds(1 - bit_low, 1)], stage_b.at[:, pl.ds(1 - ctx_here, 1)]],
        [in_a2, in_b2],
        1,
        [partners[1], partners[0]],
    )

    def round_two(part):
        for high in range(2):
            stage_a2[high, part] = stage_a[high, bit_low, part] + in_a2[high, 0, part]
            stage_b2[high, part] = stage_b[high, ctx_here, part] + in_b2[high, 0, part]

    each_chunk(round_two)
    swap_pair(
        [stage_a2.at[pl.ds(1 - bit_high, 1)], stage_b2.at[pl.ds(1 - bit_high, 1)]],
        [in_a3, in_b3],
        2,
        [partners[2], partners[2]],
    )

    def round_three(part):
        o_ref[part] = stage_a2[bit_high, part] + in_a3[0, part]
        o_ref[pl.ds(part.start + rows, chunk)] = stage_b2[bit_high, part] + in_b3[0, part]

    each_chunk(round_three)


def halving_scatter(packed, collective_id):
    count, width = packed.shape
    rows = -(-width // (128 * 128)) * 64
    block = jnp.pad(packed, ((0, 0), (0, 2 * rows * 128 - width))).reshape(
        2, 2, 2, 2 * rows, 128
    )
    own = pl.pallas_call(
        halving_kernel,
        out_shape=jax.ShapeDtypeStruct((2 * rows, 128), jnp.float32),
        in_specs=[pl.BlockSpec(memory_space=pltpu.VMEM)],
        out_specs=pl.BlockSpec(memory_space=pltpu.VMEM),
        scratch_shapes=[
            pltpu.VMEM((2, 2, rows, 128), jnp.float32),
            pltpu.VMEM((2, rows, 128), jnp.float32),
            pltpu.VMEM((2, 2, rows, 128), jnp.float32),
            pltpu.VMEM((2, rows, 128), jnp.float32),
            pltpu.VMEM((2, 2, 1, rows, 128), jnp.float32),
            pltpu.VMEM((2, 1, rows, 128), jnp.float32),
            pltpu.VMEM((1, rows, 128), jnp.float32),
            pltpu.VMEM((2, 1, 2, rows, 128), jnp.float32),
            pltpu.VMEM((2, 1, rows, 128), jnp.float32),
            pltpu.VMEM((1, rows, 128), jnp.float32),
            pltpu.SemaphoreType.DMA((2, 6)),
        ],
        compiler_params=pltpu.CompilerParams(
            collective_id=collective_id, has_side_effects=True, vmem_limit_bytes=60 * 1024 * 1024
        ),
    )(block)
    return own.reshape(-1)[:width]

def gather_kernel(x_ref, o_ref, inbox, send_sems, recv_sems):
    fsdp_here = lax.axis_index("fsdp")
    ctx_here = lax.axis_index("ctx")
    tp_here = lax.axis_index("tp")
    ctx_count = lax.axis_size("ctx")
    count = lax.axis_size("fsdp") * ctx_count
    me = fsdp_here * ctx_count + ctx_here
    peers = []
    for offset in range(1, count):
        other = (me + offset) % count
        peers.append((other // ctx_count, other % ctx_count, tp_here))
    barrier = pltpu.get_barrier_semaphore()
    for peer in peers:
        pl.semaphore_signal(barrier, 1, device_id=peer, device_id_type=pl.DeviceIdType.MESH)
    pl.semaphore_wait(barrier, len(peers))
    copies = []
    for number, peer in enumerate(peers):
        copy = pltpu.make_async_remote_copy(
            src_ref=x_ref,
            dst_ref=inbox.at[me],
            send_sem=send_sems.at[number],
            recv_sem=recv_sems.at[me],
            device_id=peer,
            device_id_type=pl.DeviceIdType.MESH,
        )
        copy.start()
        copies.append(copy)
    o_ref[me] = x_ref[...]
    for copy in copies:
        copy.wait_send()
    for offset in range(1, count):
        source = (me + count - offset) % count
        pltpu.make_async_remote_copy(
            src_ref=x_ref,
            dst_ref=inbox.at[source],
            send_sem=send_sems.at[0],
            recv_sem=recv_sems.at[source],
            device_id=peers[0],
            device_id_type=pl.DeviceIdType.MESH,
        ).wait_recv()
        o_ref[source] = inbox[source]


def gather_shards(flat, collective_id):
    size = flat.shape[0]
    rows = -(-size // 2048) * 16
    block = jnp.pad(flat, (0, rows * 128 - size)).reshape(rows, 128)
    count = lax.axis_size("fsdp") * lax.axis_size("ctx")
    full = pl.pallas_call(
        gather_kernel,
        out_shape=jax.ShapeDtypeStruct((count, rows, 128), flat.dtype),
        in_specs=[pl.BlockSpec(memory_space=pltpu.VMEM)],
        out_specs=pl.BlockSpec(memory_space=pltpu.VMEM),
        scratch_shapes=[
            pltpu.VMEM((count, rows, 128), flat.dtype),
            pltpu.SemaphoreType.DMA((count - 1,)),
            pltpu.SemaphoreType.DMA((count,)),
        ],
        compiler_params=pltpu.CompilerParams(collective_id=collective_id, has_side_effects=True),
    )(block)
    return full.reshape(count, rows * 128)[:, :size]


def swiglu_experts(gate_up):
    return jax.nn.silu(gate_up[:, :, 0]) * gate_up[:, :, 1]


def gather_packed(pieces, axes, use_kernel=False):
    flat = jnp.concatenate([piece.reshape(-1) for piece, _ in pieces])
    if use_kernel:
        full = gather_shards(flat, 4)
    else:
        full = lax.all_gather(flat, axes, axis=0, tiled=False)
    count = full.shape[0]
    results = []
    offset = 0
    for piece, dim in pieces:
        size = piece.size
        part = full[:, offset : offset + size].reshape((count,) + piece.shape)
        offset += size
        part = jnp.moveaxis(part, 0, dim)
        shape = list(piece.shape)
        shape[dim] *= count
        results.append(part.reshape(shape))
    return results


def scatter_packed(pieces, axes, count, use_kernel=False):
    columns = []
    local_shapes = []
    for grad, dim in pieces:
        shape = grad.shape
        split = shape[:dim] + (count, shape[dim] // count) + shape[dim + 1 :]
        local_shapes.append(shape[:dim] + (shape[dim] // count,) + shape[dim + 1 :])
        part = jnp.moveaxis(grad.reshape(split), dim, 0)
        columns.append(part.reshape(count, -1))
    packed = jnp.concatenate(columns, axis=1)
    if use_kernel:
        own = halving_scatter(packed, 3)
    else:
        width = packed.shape[1]
        rows = -(-width // 1024) * 8
        packed = jnp.pad(packed, ((0, 0), (0, rows * 128 - width))).reshape(count * rows, 128)
        own = lax.psum_scatter(packed, axes, scatter_dimension=0, tiled=True).reshape(-1)
    results = []
    offset = 0
    for local_shape in local_shapes:
        size = 1
        for extent in local_shape:
            size *= extent
        results.append(own[offset : offset + size].reshape(local_shape))
        offset += size
    return results


def experts_dense(normed_two, grad_out, weights, expert_in_all, expert_down_all):
    gate_up = jnp.einsum(
        "td,edgf->etgf", normed_two, expert_in_all, preferred_element_type=jnp.float32
    )
    act, act_back = jax.vjp(swiglu_experts, gate_up)
    hidden = act.astype(jnp.bfloat16)
    outs = jnp.einsum("etf,efd->etd", hidden, expert_down_all, preferred_element_type=jnp.float32)
    weights_e = weights.T[:, :, None]
    combined = jnp.sum(weights_e * outs, axis=0)
    gate_dots = jnp.sum(outs * grad_out[None], axis=-1).T
    grad_outs = (weights_e * grad_out[None]).astype(jnp.bfloat16)
    grad_hidden = jnp.einsum(
        "etd,efd->etf", grad_outs, expert_down_all, preferred_element_type=jnp.float32
    )
    grad_gate_up = act_back(grad_hidden)[0].astype(jnp.bfloat16)
    grad_down = jnp.einsum("etf,etd->efd", hidden, grad_outs, preferred_element_type=jnp.float32)
    grad_in = jnp.einsum(
        "td,etgf->edgf", normed_two, grad_gate_up, preferred_element_type=jnp.float32
    )
    grad_rows = jnp.einsum(
        "etgf,edgf->td", grad_gate_up, expert_in_all, preferred_element_type=jnp.float32
    )
    return combined, gate_dots, grad_rows, grad_in, grad_down


def experts_routed(
    normed_two, grad_out, route_rows, gate_probs, expert_in_low, expert_down_low, capacity
):
    block_len, model_width = normed_two.shape
    experts = lax.axis_size("fsdp")
    slot_index, owner_route, filled = slot_tables(route_rows, experts, capacity)
    fill_mask = filled.astype(jnp.bfloat16)[:, None]
    route_grads = (
        (gate_probs[:, :, None] * grad_out[:, None, :])
        .astype(jnp.bfloat16)
        .reshape(2 * block_len, model_width)
    )
    send_rows = jnp.stack(
        [
            (normed_two[owner_route // 2] * fill_mask).reshape(experts, capacity, model_width),
            (route_grads[owner_route] * fill_mask).reshape(experts, capacity, model_width),
        ],
        axis=1,
    )
    exchange = lambda rows: lax.all_to_all(rows, "fsdp", split_axis=0, concat_axis=0, tiled=True)
    pair_count = lax.axis_size("tp")
    swap = lambda rows: lax.ppermute(
        rows, "tp", [(index, index + 1 - 2 * (index % 2)) for index in range(pair_count)]
    )
    half = capacity // 2
    side = lax.axis_index("tp") % 2
    mine = exchange(lax.dynamic_slice_in_dim(send_rows, side * half, half, 2))
    received_both = jnp.concatenate([mine, swap(mine)], axis=2)
    received = received_both[:, 0].reshape(experts * capacity, model_width)
    grad_received = received_both[:, 1].reshape(experts * capacity, model_width)
    gate_up = jnp.einsum("rd,dgf->rgf", received, expert_in_low, preferred_element_type=jnp.float32)
    act, act_back = jax.vjp(swiglu, gate_up)
    hidden = act.astype(jnp.bfloat16)
    outs = jnp.dot(hidden, expert_down_low, preferred_element_type=jnp.float32)
    grad_hidden = jnp.einsum(
        "rd,fd->rf", grad_received, expert_down_low, preferred_element_type=jnp.float32
    )
    grad_gate_up = act_back(grad_hidden)[0].astype(jnp.bfloat16)
    grad_in = jnp.einsum("rd,rgf->dgf", received, grad_gate_up, preferred_element_type=jnp.float32)
    grad_down = jnp.einsum("rf,rd->fd", hidden, grad_received, preferred_element_type=jnp.float32)
    grad_expert_rows = jnp.einsum(
        "rgf,dgf->rd", grad_gate_up, expert_in_low, preferred_element_type=jnp.float32
    )
    pair_sums = []
    for rows in (outs, grad_expert_rows):
        rows = rows.reshape(experts, capacity, model_width)
        pair_sums.append(rows[:, :half] + swap(rows[:, half:]))
    held = exchange(jnp.stack(pair_sums, axis=1).astype(jnp.bfloat16))
    slot_expert = slot_index // capacity
    slot_rank = slot_index % capacity
    in_side = ((slot_rank // half) == side)[:, None]
    local_slot = slot_expert * half + slot_rank % half
    picked_rows = []
    for which in range(2):
        rows = held[:, which].reshape(experts * half, model_width)[local_slot]
        picked_rows.append(
            jnp.where(in_side, rows.astype(jnp.float32), 0.0).reshape(block_len, 2, model_width)
        )
    route_out, grad_routes = picked_rows
    combined = jnp.sum(gate_probs[:, :, None] * route_out, axis=1)
    gate_dots = jnp.sum(grad_out[:, None, :] * route_out, axis=-1)
    grad_rows = jnp.sum(grad_routes, axis=1)
    return combined, gate_dots, grad_rows, grad_in, grad_down


def local(
    layer_input,
    segments,
    routes,
    cotangent,
    gains,
    attention_in,
    attention_out,
    router_weight,
    shared_in,
    shared_down,
    expert_in,
    expert_down,
    model_stats,
    head_stats,
    value_columns,
    hidden_stats,
    router_state,
    expert_model_stats,
    expert_hidden_stats,
):
    block_len = layer_input.shape[1]
    model_width = layer_input.shape[2]
    experts = router_weight.shape[1]
    dense_experts = False
    capacity = min(block_len, 4 * block_len // experts)
    ctx_index = lax.axis_index("ctx")
    tp_index = lax.axis_index("tp")
    fsdp_index = lax.axis_index("fsdp")
    shard_index = lax.axis_index(("fsdp", "ctx"))
    shard_count = lax.axis_size(("fsdp", "ctx"))
    ctx_count = lax.axis_size("ctx")
    base_pos = ctx_index * block_len
    low = lambda v: v.astype(jnp.bfloat16)
    gain_low, attn_in_low = gather_packed(
        [(low(gains), 1), (low(attention_in), 0)], ("fsdp", "ctx"), shard_count <= 8
    )
    later = [
        (low(attention_out), 1),
        (low(router_weight), 0),
        (low(shared_in), 0),
        (low(shared_down), 1),
    ]
    if dense_experts:
        later += [(low(expert_in), 0), (low(expert_down), 0)]
    later_full = gather_packed(later, ("fsdp", "ctx"))
    attn_out_low, router_low, shared_in_low, shared_down_low = later_full[:4]
    if dense_experts:
        fe_local = expert_down.shape[1]
        expert_in_all = later_full[4].reshape(experts, model_width, 2, fe_local)
        expert_down_all = (
            later_full[5]
            .reshape(experts, ctx_count, fe_local, model_width // ctx_count)
            .transpose(0, 2, 1, 3)
            .reshape(experts, fe_local, model_width)
        )
    else:
        expert_in_low = lax.all_gather(low(expert_in), "ctx", axis=1, tiled=True)[0]
        expert_down_low = lax.all_gather(low(expert_down), "ctx", axis=2, tiled=True)[0]
    residual = layer_input[0].astype(jnp.float32)
    gain_one = gain_low[0].astype(jnp.float32)
    gain_two = gain_low[1].astype(jnp.float32)
    normed_one, norm_one_back = jax.vjp(rms_norm, residual, gain_one)
    normed_one = normed_one.astype(jnp.bfloat16)
    projected = jnp.einsum(
        "td,dgf->tgf", normed_one, attn_in_low, preferred_element_type=jnp.float32
    )
    local_cols = projected.shape[2]
    local_heads = local_cols // HD
    half_dim = HD // 2
    frequency = 10000.0 ** (-jnp.arange(half_dim, dtype=jnp.float32) / half_dim)
    angles = (base_pos + jnp.arange(block_len, dtype=jnp.int32)).astype(jnp.float32)[
        :, None
    ] * frequency[None, :]
    cosine = jnp.cos(angles)
    sine_tab = jnp.sin(angles)
    queries = rotate(projected[:, 0].reshape(block_len, local_heads, HD), cosine, sine_tab).astype(
        jnp.bfloat16
    )
    keys_own = rotate(projected[:, 1].reshape(block_len, local_heads, HD), cosine, sine_tab).astype(
        jnp.bfloat16
    )
    values_own = projected[:, 2].reshape(block_len, local_heads, HD).astype(jnp.bfloat16)
    seg_own = segments[0].astype(jnp.bfloat16)
    keys_prev, values_prev, seg_prev = from_behind((keys_own, values_own, seg_own), "ctx", 1)
    keys_ext = jnp.concatenate([keys_prev, keys_own], axis=0)
    values_ext = jnp.concatenate([values_prev, values_own], axis=0)
    seg_ext = jnp.concatenate([seg_prev, seg_own], axis=0)
    block_rows = min(512, block_len)
    block_total = block_len // block_rows
    starts = jnp.arange(block_total, dtype=jnp.int32) * block_rows

    def forward_block(start_row):
        query_rows, key_rows, value_rows, masked, allowed = block_view(
            queries, keys_ext, values_ext, seg_own, seg_ext, start_row, base_pos
        )
        row_max = jnp.max(masked, axis=-1, keepdims=True)
        exp_terms = jnp.where(allowed[None], jnp.exp(masked - row_max), 0.0)
        row_total = jnp.sum(exp_terms, axis=-1, keepdims=True)
        attn_probs = (exp_terms / row_total).astype(jnp.bfloat16)
        attended = jnp.einsum(
            "hqk,khd->qhd", attn_probs, value_rows, preferred_element_type=jnp.float32
        )
        return (attended, row_max + jnp.log(row_total))

    attended, log_totals = lax.map(forward_block, starts)
    mixed_heads = attended.reshape(block_len, local_cols).astype(jnp.bfloat16)
    attn_total = lax.psum(
        jnp.dot(mixed_heads, attn_out_low, preferred_element_type=jnp.float32), "tp"
    )
    after_attn = residual + attn_total
    normed_two, norm_two_back = jax.vjp(rms_norm, after_attn, gain_two)
    normed_two = normed_two.astype(jnp.bfloat16)
    logits = jnp.dot(normed_two, router_low, preferred_element_type=jnp.float32)
    route_rows = routes[0]
    onehot = (route_rows[:, :, None] == jnp.arange(experts, dtype=jnp.int32)[None, None, :]).astype(
        jnp.float32
    )
    picked = jnp.sum(onehot * logits[:, None, :], axis=-1)
    gate_probs = jax.nn.softmax(picked, axis=-1)
    upstream = cotangent[0]
    grad_out = upstream.astype(jnp.float32)
    if dense_experts:
        weights = jnp.sum(gate_probs[:, :, None] * onehot, axis=1)
        combined, dots_e, grad_rows, grad_expert_in, grad_expert_down = experts_dense(
            normed_two, grad_out, weights, expert_in_all, expert_down_all
        )
        gate_dots = jnp.sum(onehot * dots_e[:, None, :], axis=-1)
    else:
        combined, gate_dots, grad_rows, grad_expert_in, grad_expert_down = experts_routed(
            normed_two,
            grad_out,
            route_rows,
            gate_probs,
            expert_in_low,
            expert_down_low,
            capacity,
        )
    shared_gate_up = jnp.einsum(
        "td,dgf->tgf", normed_two, shared_in_low, preferred_element_type=jnp.float32
    )
    shared_act, shared_act_back = jax.vjp(swiglu, shared_gate_up)
    shared_hidden = shared_act.astype(jnp.bfloat16)
    shared_out = jnp.dot(shared_hidden, shared_down_low, preferred_element_type=jnp.float32)
    grad_shared_hidden = jnp.einsum(
        "td,fd->tf", upstream, shared_down_low, preferred_element_type=jnp.float32
    )
    grad_shared_gate_up = shared_act_back(grad_shared_hidden)[0].astype(jnp.bfloat16)
    partial_two = (
        jnp.einsum(
            "tgf,dgf->td", grad_shared_gate_up, shared_in_low, preferred_element_type=jnp.float32
        )
        + grad_rows
    )
    branch_total, grad_normed_part, gate_total = lax.psum(
        (shared_out + combined, partial_two, gate_dots), "tp"
    )
    layer_out = after_attn + branch_total
    grad_picked = gate_probs * (
        gate_total - jnp.sum(gate_probs * gate_total, axis=-1, keepdims=True)
    )
    grad_logits = jnp.sum(grad_picked[:, :, None] * onehot, axis=1).astype(jnp.bfloat16)
    grad_shared_in = jnp.einsum(
        "td,tgf->dgf", normed_two, grad_shared_gate_up, preferred_element_type=jnp.float32
    )
    grad_shared_down = jnp.einsum(
        "tf,td->fd", shared_hidden, upstream, preferred_element_type=jnp.float32
    )
    grad_router = jnp.einsum(
        "td,te->de", normed_two, grad_logits, preferred_element_type=jnp.float32
    )
    grad_normed_two = grad_normed_part + jnp.einsum(
        "te,de->td", grad_logits, router_low, preferred_element_type=jnp.float32
    )
    grad_after, grad_gain_two = norm_two_back(grad_normed_two)
    grad_after = grad_after + grad_out
    grad_attn_low = grad_after.astype(jnp.bfloat16)
    grad_attn_out = jnp.einsum(
        "tc,td->cd", mixed_heads, grad_attn_low, preferred_element_type=jnp.float32
    )
    first_grads = [
        (grad_attn_out, 1),
        (grad_router, 0),
        (grad_shared_in, 0),
        (grad_shared_down, 1),
        (grad_gain_two, 0),
    ]
    if dense_experts:
        fe_local = expert_down.shape[1]
        first_grads += [
            (grad_expert_in.reshape(shard_count * expert_in.shape[1], 2, fe_local), 0),
            (
                grad_expert_down.reshape(experts, fe_local, ctx_count, model_width // ctx_count)
                .transpose(0, 2, 1, 3)
                .reshape(shard_count * fe_local, model_width // ctx_count),
                0,
            ),
        ]
    if not dense_experts:
        own_expert_in = lax.psum_scatter(grad_expert_in[None], "ctx", scatter_dimension=1, tiled=True)
        own_expert_down = lax.psum_scatter(
            grad_expert_down[None], "ctx", scatter_dimension=2, tiled=True
        )
    grad_heads = (
        jnp.einsum("td,cd->tc", grad_attn_low, attn_out_low, preferred_element_type=jnp.float32)
        .astype(jnp.bfloat16)
        .reshape(block_len, local_heads, HD)
    )

    def backward_block(block_number, running):
        grad_keys, grad_values, grad_queries = running
        start_row = block_number * block_rows
        query_rows, key_rows, value_rows, masked, allowed = block_view(
            queries, keys_ext, values_ext, seg_own, seg_ext, start_row, base_pos
        )
        log_total = lax.dynamic_index_in_dim(log_totals, block_number, 0, keepdims=False)
        attn_probs = jnp.where(allowed[None], jnp.exp(masked - log_total), 0.0)
        grad_block = lax.dynamic_slice_in_dim(grad_heads, start_row, block_rows, 0)
        grad_probs = jnp.einsum(
            "qhd,khd->hqk", grad_block, value_rows, preferred_element_type=jnp.float32
        )
        inner_sum = jnp.sum(attn_probs * grad_probs, axis=-1, keepdims=True)
        grad_scores = (attn_probs * (grad_probs - inner_sum)).astype(jnp.bfloat16)
        grad_query_rows = (
            jnp.einsum("hqk,khd->qhd", grad_scores, key_rows, preferred_element_type=jnp.float32)
            * 0.125
        )
        grad_key_rows = (
            jnp.einsum("hqk,qhd->khd", grad_scores, query_rows, preferred_element_type=jnp.float32)
            * 0.125
        )
        grad_value_rows = jnp.einsum(
            "hqk,qhd->khd",
            attn_probs.astype(jnp.bfloat16),
            grad_block,
            preferred_element_type=jnp.float32,
        )
        key_offset = start_row + block_len - WINDOW
        grad_keys = lax.dynamic_update_slice_in_dim(
            grad_keys,
            lax.dynamic_slice_in_dim(grad_keys, key_offset, block_rows + WINDOW, 0) + grad_key_rows,
            key_offset,
            0,
        )
        grad_values = lax.dynamic_update_slice_in_dim(
            grad_values,
            lax.dynamic_slice_in_dim(grad_values, key_offset, block_rows + WINDOW, 0)
            + grad_value_rows,
            key_offset,
            0,
        )
        grad_queries = lax.dynamic_update_slice_in_dim(grad_queries, grad_query_rows, start_row, 0)
        return (grad_keys, grad_values, grad_queries)

    zero_ext = jnp.zeros((2 * block_len, local_heads, HD), jnp.float32)
    zero_own = jnp.zeros((block_len, local_heads, HD), jnp.float32)
    grad_keys, grad_values, grad_queries = lax.fori_loop(
        0, block_total, backward_block, (zero_ext, zero_ext, zero_own)
    )
    rim_keys, rim_values = (
        from_behind(grad_keys[:block_len].astype(jnp.bfloat16), "ctx", -1).astype(jnp.float32),
        from_behind(grad_values[:block_len].astype(jnp.bfloat16), "ctx", -1).astype(jnp.float32),
    )
    grad_keys_own = grad_keys[block_len:] + rim_keys
    grad_values_own = grad_values[block_len:] + rim_values
    grad_query_raw = rotate(grad_queries, cosine, -sine_tab)
    grad_key_raw = rotate(grad_keys_own, cosine, -sine_tab)
    grad_projected = (
        jnp.stack([grad_query_raw, grad_key_raw, grad_values_own], axis=1)
        .reshape(block_len, 3, local_cols)
        .astype(jnp.bfloat16)
    )
    grad_attn_in = jnp.einsum(
        "td,tgf->dgf", normed_one, grad_projected, preferred_element_type=jnp.float32
    )
    partial_one = jnp.einsum(
        "tgf,dgf->td", grad_projected, attn_in_low, preferred_element_type=jnp.float32
    )
    tp_one = lax.psum(partial_one, "tp")
    halving = lax.axis_size("fsdp") == 4 and ctx_count == 2
    all_own = scatter_packed(
        first_grads + [(grad_attn_in, 0)],
        ("fsdp", "ctx"),
        shard_count,
        halving,
    )
    own_attn_out, own_router, own_shared_in, own_shared_down, own_gain_two = all_own[:5]
    own_attn_in = all_own[-1]
    grad_residual, grad_gain_one = norm_one_back(tp_one + 0.0 * own_attn_in[0, 0, 0])
    input_grad = grad_after + grad_residual
    if dense_experts:
        own_expert_in = all_own[5][None]
        own_expert_down = all_own[6][None]
    lead_tp = (tp_index == 0).astype(jnp.float32)
    first_shard = (shard_index == 0).astype(jnp.float32)
    first_ctx = (ctx_index == 0).astype(jnp.float32)
    d_local = gains.shape[1]
    ff_local = shared_down.shape[0]
    fe_local = expert_down.shape[1]
    d_quarter = expert_in.shape[1]
    square_attn_in = own_attn_in * own_attn_in + TINY_SQUARE
    square_attn_out = own_attn_out * own_attn_out + TINY_SQUARE
    square_shared_in = own_shared_in * own_shared_in + TINY_SQUARE
    square_shared_down = own_shared_down * own_shared_down + TINY_SQUARE
    square_expert_in = own_expert_in[0] * own_expert_in[0] + TINY_SQUARE
    square_expert_down = own_expert_down[0] * own_expert_down[0] + TINY_SQUARE
    model_part = lax.dynamic_update_slice(
        jnp.zeros((4, D), jnp.float32),
        jnp.stack(
            [
                jnp.sum(square_attn_in, axis=(1, 2)),
                jnp.sum(square_shared_in, axis=(1, 2)),
                jnp.sum(square_attn_out, axis=0),
                jnp.sum(square_shared_down, axis=0),
            ]
        ),
        (0, shard_index * d_local),
    )
    head_part = lax.dynamic_update_slice(
        jnp.zeros((4, HH), jnp.float32),
        jnp.concatenate(
            [jnp.sum(square_attn_in, axis=0), jnp.sum(square_attn_out, axis=1)[None]], axis=0
        ),
        (0, tp_index * local_cols),
    )
    hidden_part = lax.dynamic_update_slice(
        jnp.zeros((3, FF), jnp.float32),
        jnp.concatenate(
            [jnp.sum(square_shared_in, axis=0), jnp.sum(square_shared_down, axis=1)[None]], axis=0
        ),
        (0, tp_index * ff_local),
    )
    expert_model_part = lax.dynamic_update_slice(
        jnp.zeros((experts, 2, D), jnp.float32),
        jnp.stack([jnp.sum(square_expert_in, axis=(1, 2)), jnp.sum(square_expert_down, axis=0)])[
            None
        ],
        (fsdp_index, 0, ctx_index * d_quarter),
    )
    expert_hidden_part = lax.dynamic_update_slice(
        jnp.zeros((experts, 3, FE), jnp.float32),
        jnp.concatenate(
            [jnp.sum(square_expert_in, axis=0), jnp.sum(square_expert_down, axis=1)[None]], axis=0
        )[None],
        (fsdp_index, 0, tp_index * fe_local),
    )
    scalar_part = jnp.stack(
        [
            lead_tp * jnp.sum(gains * gains),
            jnp.sum(attention_in * attention_in),
            jnp.sum(attention_out * attention_out),
            lead_tp * jnp.sum(router_weight * router_weight),
            jnp.sum(shared_in * shared_in),
            jnp.sum(shared_down * shared_down),
            jnp.sum(expert_in * expert_in),
            jnp.sum(expert_down * expert_down),
            lead_tp * jnp.sum(model_stats[2]),
            first_shard * jnp.sum(head_stats[2]),
            lead_tp * jnp.sum(model_stats[3]),
            first_shard * jnp.sum(hidden_stats[2]),
        ]
    )
    expert_old_part = lax.dynamic_update_slice(
        jnp.zeros((2, experts), jnp.float32),
        jnp.stack(
            [
                lead_tp * jnp.sum(expert_model_stats[0, 0]),
                first_ctx * jnp.sum(expert_hidden_stats[0, 2]),
            ]
        )[:, None],
        (0, fsdp_index),
    )
    global_sums = butterfly_sum(
        [
            model_part,
            head_part,
            hidden_part,
            expert_model_part,
            expert_hidden_part,
            scalar_part,
            expert_old_part,
            lead_tp * grad_gain_one,
        ],
        1,
    )
    (
        model_sum,
        head_sum,
        hidden_sum,
        expert_model_sum,
        expert_hidden_sum,
        scalar_sum,
        expert_old_sum,
        gain_one_sum,
    ) = global_sums
    own_gain_one = lax.dynamic_slice_in_dim(gain_one_sum, shard_index * d_local, d_local)
    own_gains = jnp.stack([own_gain_one, own_gain_two])
    shard_start = shard_index * d_local
    gain_state = DECAY_RATE * model_stats[0:2] + (1.0 - DECAY_RATE) * (
        own_gains * own_gains + TINY_SQUARE
    )
    update_gains = own_gains * lax.rsqrt(gain_state)
    router_new = DECAY_RATE * router_state + (1.0 - DECAY_RATE) * (
        own_router * own_router + TINY_SQUARE
    )
    update_router = own_router * lax.rsqrt(router_new)
    attn_cols_old = jnp.concatenate([head_stats[0:2], value_columns[None]], axis=0).reshape(-1)
    update_attn_in, rows_attn_in, cols_attn_in = factored_update(
        own_attn_in.reshape(d_local, 3 * local_cols),
        model_stats[2],
        attn_cols_old,
        lax.dynamic_slice_in_dim(model_sum[0], shard_start, d_local),
        lax.dynamic_slice_in_dim(head_sum[0:3], tp_index * local_cols, local_cols, 1).reshape(-1),
        D,
        3 * HH,
        scalar_sum[8],
        jnp.sum(model_sum[0]),
    )
    update_attn_out, rows_attn_out, cols_attn_out = factored_update(
        own_attn_out,
        head_stats[2],
        model_stats[4],
        lax.dynamic_slice_in_dim(head_sum[3], tp_index * local_cols, local_cols),
        lax.dynamic_slice_in_dim(model_sum[2], shard_start, d_local),
        HH,
        D,
        scalar_sum[9],
        jnp.sum(head_sum[3]),
    )
    update_shared_in, rows_shared_in, cols_shared_in = factored_update(
        own_shared_in.reshape(d_local, 2 * ff_local),
        model_stats[3],
        hidden_stats[0:2].reshape(-1),
        lax.dynamic_slice_in_dim(model_sum[1], shard_start, d_local),
        lax.dynamic_slice_in_dim(hidden_sum[0:2], tp_index * ff_local, ff_local, 1).reshape(-1),
        D,
        2 * FF,
        scalar_sum[10],
        jnp.sum(model_sum[1]),
    )
    update_shared_down, rows_shared_down, cols_shared_down = factored_update(
        own_shared_down,
        hidden_stats[2],
        model_stats[5],
        lax.dynamic_slice_in_dim(hidden_sum[2], tp_index * ff_local, ff_local),
        lax.dynamic_slice_in_dim(model_sum[3], shard_start, d_local),
        FF,
        D,
        scalar_sum[11],
        jnp.sum(hidden_sum[2]),
    )
    own_expert_model = lax.dynamic_index_in_dim(expert_model_sum, fsdp_index, 0, keepdims=False)
    own_expert_hidden = lax.dynamic_index_in_dim(expert_hidden_sum, fsdp_index, 0, keepdims=False)
    old_expert_totals = lax.dynamic_index_in_dim(expert_old_sum, fsdp_index, 1, keepdims=False)
    update_expert_in, rows_expert_in, cols_expert_in = factored_update(
        own_expert_in[0].reshape(d_quarter, 2 * fe_local),
        expert_model_stats[0, 0],
        expert_hidden_stats[0, 0:2].reshape(-1),
        lax.dynamic_slice_in_dim(own_expert_model[0], ctx_index * d_quarter, d_quarter),
        lax.dynamic_slice_in_dim(own_expert_hidden[0:2], tp_index * fe_local, fe_local, 1).reshape(
            -1
        ),
        D,
        2 * FE,
        old_expert_totals[0],
        jnp.sum(own_expert_model[0]),
    )
    update_expert_down, rows_expert_down, cols_expert_down = factored_update(
        own_expert_down[0],
        expert_hidden_stats[0, 2],
        expert_model_stats[0, 1],
        lax.dynamic_slice_in_dim(own_expert_hidden[2], tp_index * fe_local, fe_local),
        lax.dynamic_slice_in_dim(own_expert_model[1], ctx_index * d_quarter, d_quarter),
        FE,
        D,
        old_expert_totals[1],
        jnp.sum(own_expert_hidden[2]),
    )
    clip_part = jnp.stack(
        [
            lead_tp * jnp.sum(update_gains * update_gains),
            jnp.sum(update_attn_in * update_attn_in),
            jnp.sum(update_attn_out * update_attn_out),
            lead_tp * jnp.sum(update_router * update_router),
            jnp.sum(update_shared_in * update_shared_in),
            jnp.sum(update_shared_down * update_shared_down),
            jnp.sum(update_expert_in * update_expert_in),
            jnp.sum(update_expert_down * update_expert_down),
        ]
    )
    clip_total = butterfly_sum([clip_part], 2)[0]
    elements = jnp.array(
        [
            2 * D,
            D * 3 * HH,
            HH * D,
            D * experts,
            D * 2 * FF,
            FF * D,
            experts * D * 2 * FE,
            experts * FE * D,
        ],
        jnp.float32,
    )
    update_roots = jnp.sqrt(clip_total / elements)
    new_gains = apply_update(gains, update_gains, update_roots[0], scalar_sum[0], elements[0])
    new_attn_in = apply_update(
        attention_in,
        update_attn_in.reshape(attention_in.shape),
        update_roots[1],
        scalar_sum[1],
        elements[1],
    )
    new_attn_out = apply_update(
        attention_out, update_attn_out, update_roots[2], scalar_sum[2], elements[2]
    )
    new_router = apply_update(
        router_weight, update_router, update_roots[3], scalar_sum[3], elements[3]
    )
    new_shared_in = apply_update(
        shared_in,
        update_shared_in.reshape(shared_in.shape),
        update_roots[4],
        scalar_sum[4],
        elements[4],
    )
    new_shared_down = apply_update(
        shared_down, update_shared_down, update_roots[5], scalar_sum[5], elements[5]
    )
    new_expert_in = apply_update(
        expert_in,
        update_expert_in.reshape(expert_in.shape),
        update_roots[6],
        scalar_sum[6],
        elements[6],
    )
    new_expert_down = apply_update(
        expert_down,
        update_expert_down.reshape(expert_down.shape),
        update_roots[7],
        scalar_sum[7],
        elements[7],
    )
    new_model_stats = jnp.concatenate(
        [gain_state, jnp.stack([rows_attn_in, rows_shared_in, cols_attn_out, cols_shared_down])],
        axis=0,
    )
    attn_cols_new = cols_attn_in.reshape(3, local_cols)
    new_head_stats = jnp.concatenate([attn_cols_new[0:2], rows_attn_out[None]], axis=0)
    new_value_columns = attn_cols_new[2]
    new_hidden_stats = jnp.concatenate(
        [cols_shared_in.reshape(2, ff_local), rows_shared_down[None]], axis=0
    )
    new_expert_model_stats = jnp.stack([rows_expert_in, cols_expert_down])[None]
    new_expert_hidden_stats = jnp.concatenate(
        [cols_expert_in.reshape(2, fe_local), rows_expert_down[None]], axis=0
    )[None]
    return (
        layer_out.astype(jnp.bfloat16)[None],
        input_grad[None],
        own_gains,
        own_attn_in,
        own_attn_out,
        own_router,
        own_shared_in,
        own_shared_down,
        own_expert_in,
        own_expert_down,
        new_gains,
        new_attn_in,
        new_attn_out,
        new_router,
        new_shared_in,
        new_shared_down,
        new_expert_in,
        new_expert_down,
        new_model_stats,
        new_head_stats,
        new_value_columns,
        new_hidden_stats,
        router_new,
        new_expert_model_stats,
        new_expert_hidden_stats,
        update_roots,
    )


def solution(mesh):
    in_specs = (
        P("fsdp", "ctx", None),
        P("fsdp", "ctx"),
        P("fsdp", "ctx", None),
        P("fsdp", "ctx", None),
        P(None, ("fsdp", "ctx")),
        P(("fsdp", "ctx"), None, "tp"),
        P("tp", ("fsdp", "ctx")),
        P(("fsdp", "ctx"), None),
        P(("fsdp", "ctx"), None, "tp"),
        P("tp", ("fsdp", "ctx")),
        P("fsdp", "ctx", None, "tp"),
        P("fsdp", "tp", "ctx"),
        P(None, ("fsdp", "ctx")),
        P(None, "tp"),
        P("tp"),
        P(None, "tp"),
        P(("fsdp", "ctx"), None),
        P("fsdp", None, "ctx"),
        P("fsdp", None, "tp"),
    )
    out_specs = (
        P("fsdp", "ctx", None),
        P("fsdp", "ctx", None),
        P(None, ("fsdp", "ctx")),
        P(("fsdp", "ctx"), None, "tp"),
        P("tp", ("fsdp", "ctx")),
        P(("fsdp", "ctx"), None),
        P(("fsdp", "ctx"), None, "tp"),
        P("tp", ("fsdp", "ctx")),
        P("fsdp", "ctx", None, "tp"),
        P("fsdp", "tp", "ctx"),
        P(None, ("fsdp", "ctx")),
        P(("fsdp", "ctx"), None, "tp"),
        P("tp", ("fsdp", "ctx")),
        P(("fsdp", "ctx"), None),
        P(("fsdp", "ctx"), None, "tp"),
        P("tp", ("fsdp", "ctx")),
        P("fsdp", "ctx", None, "tp"),
        P("fsdp", "tp", "ctx"),
        P(None, ("fsdp", "ctx")),
        P(None, "tp"),
        P("tp"),
        P(None, "tp"),
        P(("fsdp", "ctx"), None),
        P("fsdp", None, "ctx"),
        P("fsdp", None, "tp"),
        P(),
    )
    return jax.shard_map(local, mesh=mesh, in_specs=in_specs, out_specs=out_specs, check_vma=False)
```

```python
import jax
import jax.numpy as jnp
from jax import lax
from jax.sharding import PartitionSpec as P
from jax.experimental import pallas as pl
from jax.experimental.pallas import tpu as pltpu

D = 768
HD = 64
FF = 2048
FE = 2048
WINDOW = 1024
HH = 768


EPSILON = 1e-06
TINY_SQUARE = 1e-30
SCALE_FLOOR = 0.001
DECAY_RATE = 0.5
CLIP_LIMIT = 0.5
STEP_RATE = 0.5


def from_behind(value, axis, steps):
    count = lax.axis_size(axis)
    leading, last = (max(0, -steps), min(count, count - steps))
    return lax.ppermute(value, axis, [(source, source + steps) for source in range(leading, last)])


def rms_norm(values, gain_vec):
    inv_rms = lax.rsqrt(jnp.mean(values * values, axis=-1, keepdims=True) + EPSILON)
    return values * inv_rms * gain_vec


def swiglu(gate_up):
    return jax.nn.silu(gate_up[:, 0]) * gate_up[:, 1]


def rotate(values, cosine, sine_tab):
    half_dim = values.shape[-1] // 2
    first_half = values[..., :half_dim]
    second_half = values[..., half_dim:]
    cos_b = cosine[:, None, :]
    sin_b = sine_tab[:, None, :]
    return jnp.concatenate(
        [first_half * cos_b - second_half * sin_b, second_half * cos_b + first_half * sin_b],
        axis=-1,
    )


def slot_tables(block_routes, experts, capacity):
    flat_routes = block_routes.reshape(-1)
    route_count = flat_routes.shape[0]
    onehot = (flat_routes[:, None] == jnp.arange(experts, dtype=jnp.int32)[None, :]).astype(
        jnp.int32
    )
    rank_in = jnp.sum(
        (jnp.cumsum(onehot, axis=0, dtype=jnp.int32) - 1) * onehot, axis=1, dtype=jnp.int32
    )
    slot_index = flat_routes * capacity + rank_in
    owner_route = (
        jnp.zeros((experts * capacity,), jnp.int32)
        .at[slot_index]
        .set(jnp.arange(route_count, dtype=jnp.int32))
    )
    filled = jnp.zeros((experts * capacity,), jnp.int32).at[slot_index].set(1)
    return (slot_index, owner_route, filled)


def block_view(queries, keys_ext, values_ext, seg_own, seg_ext, start_row, base_pos):
    block_len = queries.shape[0]
    block_rows = min(512, block_len)
    query_rows = lax.dynamic_slice_in_dim(queries, start_row, block_rows, 0)
    key_rows = lax.dynamic_slice_in_dim(
        keys_ext, start_row + block_len - WINDOW, block_rows + WINDOW, 0
    )
    value_rows = lax.dynamic_slice_in_dim(
        values_ext, start_row + block_len - WINDOW, block_rows + WINDOW, 0
    )
    scores = (
        jnp.einsum("qhd,khd->hqk", query_rows, key_rows, preferred_element_type=jnp.float32) * 0.125
    )
    query_pos = start_row + jnp.arange(block_rows, dtype=jnp.int32)
    key_pos = start_row - WINDOW + jnp.arange(block_rows + WINDOW, dtype=jnp.int32)
    distance = query_pos[:, None] - key_pos[None, :]
    seg_query = lax.dynamic_slice_in_dim(seg_own, start_row, block_rows, 0)
    seg_key = lax.dynamic_slice_in_dim(
        seg_ext, start_row + block_len - WINDOW, block_rows + WINDOW, 0
    )
    allowed = (
        (distance >= 0)
        & (distance < WINDOW)
        & (seg_query[:, None] == seg_key[None, :])
        & (key_pos[None, :] + base_pos >= 0)
    )
    return (query_rows, key_rows, value_rows, jnp.where(allowed[None], scores, -1e30), allowed)


def factored_update(
    grad_mat, rows_old, cols_old, row_sums, col_sums, row_total, col_total, old_total, square_total
):
    rows_new = DECAY_RATE * rows_old + (1.0 - DECAY_RATE) * row_sums / col_total
    cols_new = DECAY_RATE * cols_old + (1.0 - DECAY_RATE) * col_sums / row_total
    mean_rows = (DECAY_RATE * old_total + (1.0 - DECAY_RATE) * square_total / col_total) / row_total
    second_moment = rows_new[:, None] * cols_new[None, :] / mean_rows
    return (grad_mat * lax.rsqrt(second_moment), rows_new, cols_new)


def apply_update(weight, update, update_root, square_sum, elements):
    param_scale = jnp.maximum(SCALE_FLOOR, jnp.sqrt(square_sum / elements))
    return weight - STEP_RATE * param_scale * update / jnp.maximum(1.0, update_root / CLIP_LIMIT)


def butterfly_partners():
    partners = []
    here = [lax.axis_index(name) for name in ("fsdp", "ctx", "tp")]
    for axis_number, name in enumerate(("fsdp", "ctx", "tp")):
        size = lax.axis_size(name)
        step = 1
        while step < size:
            bit = (here[axis_number] // step) % 2
            other = list(here)
            other[axis_number] = here[axis_number] + step * (1 - 2 * bit)
            partners.append(tuple(other))
            step *= 2
    return partners


def butterfly_kernel(x_ref, o_ref, stage, inbox, send_sems, recv_sems):
    partners = butterfly_partners()
    barrier = pltpu.get_barrier_semaphore()
    for partner in partners:
        pl.semaphore_signal(
            barrier, 1, device_id=partner, device_id_type=pl.DeviceIdType.MESH
        )
    pl.semaphore_wait(barrier, len(partners))
    acc = x_ref[...]
    for round_number, partner in enumerate(partners):
        stage[round_number] = acc
        copy = pltpu.make_async_remote_copy(
            src_ref=stage.at[round_number],
            dst_ref=inbox.at[round_number],
            send_sem=send_sems.at[round_number],
            recv_sem=recv_sems.at[round_number],
            device_id=partner,
            device_id_type=pl.DeviceIdType.MESH,
        )
        copy.start()
        copy.wait()
        acc = stage[round_number] + inbox[round_number]
    o_ref[...] = acc


def butterfly_sum(values, collective_id):
    flat = jnp.concatenate([v.reshape(-1).astype(jnp.float32) for v in values])
    size = flat.shape[0]
    rows = -(-size // 1024) * 8
    block = jnp.pad(flat, (0, rows * 128 - size)).reshape(rows, 128)
    rounds = sum(
        max(1, lax.axis_size(name)).bit_length() - 1 for name in ("fsdp", "ctx", "tp")
    )
    total = pl.pallas_call(
        butterfly_kernel,
        out_shape=jax.ShapeDtypeStruct((rows, 128), jnp.float32),
        in_specs=[pl.BlockSpec(memory_space=pltpu.VMEM)],
        out_specs=pl.BlockSpec(memory_space=pltpu.VMEM),
        scratch_shapes=[
            pltpu.VMEM((rounds, rows, 128), jnp.float32),
            pltpu.VMEM((rounds, rows, 128), jnp.float32),
            pltpu.SemaphoreType.DMA((rounds,)),
            pltpu.SemaphoreType.DMA((rounds,)),
        ],
        compiler_params=pltpu.CompilerParams(collective_id=collective_id, has_side_effects=True),
    )(block).reshape(-1)
    results = []
    offset = 0
    for v in values:
        results.append(total[offset : offset + v.size].reshape(v.shape))
        offset += v.size
    return results


def halving_kernel(
    x_ref, o_ref, stage_a, stage_a2, stage_b, stage_b2, in_a1, in_a2, in_a3, in_b1, in_b2, in_b3, sems
):
    rows = o_ref.shape[0] // 2
    chunk = 64
    fsdp_here = lax.axis_index("fsdp")
    ctx_here = lax.axis_index("ctx")
    tp_here = lax.axis_index("tp")
    bit_low = fsdp_here % 2
    bit_high = (fsdp_here // 2) % 2
    partners = [
        (fsdp_here, 1 - ctx_here, tp_here),
        (fsdp_here + 1 - 2 * bit_low, ctx_here, tp_here),
        (fsdp_here + 2 - 4 * bit_high, ctx_here, tp_here),
    ]
    barrier = pltpu.get_barrier_semaphore()
    for partner in partners:
        pl.semaphore_signal(barrier, 1, device_id=partner, device_id_type=pl.DeviceIdType.MESH)
    pl.semaphore_wait(barrier, len(partners))
    first, second = pl.ds(0, rows), pl.ds(rows, rows)

    def swap_pair(sources, targets, number, partner_pair):
        copies = []
        for index in range(2):
            copy = pltpu.make_async_remote_copy(
                src_ref=sources[index],
                dst_ref=targets[index],
                send_sem=sems.at[0, 2 * number + index],
                recv_sem=sems.at[1, 2 * number + index],
                device_id=partner_pair[index],
                device_id_type=pl.DeviceIdType.MESH,
            )
            copy.start()
            copies.append(copy)
        for copy in copies:
            copy.wait()

    def each_chunk(body):
        @pl.loop(0, rows // chunk)
        def _(step):
            body(pl.ds(pl.multiple_of(step * chunk, chunk), chunk))

    swap_pair(
        [
            x_ref.at[:, :, pl.ds(1 - ctx_here, 1), first],
            x_ref.at[:, pl.ds(1 - bit_low, 1), :, second],
        ],
        [in_a1, in_b1],
        0,
        [partners[0], partners[1]],
    )

    def round_one(part):
        shifted = pl.ds(part.start + rows, chunk)
        for high in range(2):
            for other in range(2):
                stage_a[high, other, part] = (
                    x_ref[high, other, ctx_here, part] + in_a1[high, other, 0, part]
                )
                stage_b[high, other, part] = (
                    x_ref[high, bit_low, other, shifted] + in_b1[high, 0, other, part]
                )

    each_chunk(round_one)
    swap_pair(
        [stage_a.at[:, pl.ds(1 - bit_low, 1)], stage_b.at[:, pl.ds(1 - ctx_here, 1)]],
        [in_a2, in_b2],
        1,
        [partners[1], partners[0]],
    )

    def round_two(part):
        for high in range(2):
            stage_a2[high, part] = stage_a[high, bit_low, part] + in_a2[high, 0, part]
            stage_b2[high, part] = stage_b[high, ctx_here, part] + in_b2[high, 0, part]

    each_chunk(round_two)
    swap_pair(
        [stage_a2.at[pl.ds(1 - bit_high, 1)], stage_b2.at[pl.ds(1 - bit_high, 1)]],
        [in_a3, in_b3],
        2,
        [partners[2], partners[2]],
    )

    def round_three(part):
        o_ref[part] = stage_a2[bit_high, part] + in_a3[0, part]
        o_ref[pl.ds(part.start + rows, chunk)] = stage_b2[bit_high, part] + in_b3[0, part]

    each_chunk(round_three)


def halving_scatter(packed, collective_id):
    count, width = packed.shape
    rows = -(-width // (128 * 128)) * 64
    block = jnp.pad(packed, ((0, 0), (0, 2 * rows * 128 - width))).reshape(
        2, 2, 2, 2 * rows, 128
    )
    own = pl.pallas_call(
        halving_kernel,
        out_shape=jax.ShapeDtypeStruct((2 * rows, 128), jnp.float32),
        in_specs=[pl.BlockSpec(memory_space=pltpu.VMEM)],
        out_specs=pl.BlockSpec(memory_space=pltpu.VMEM),
        scratch_shapes=[
            pltpu.VMEM((2, 2, rows, 128), jnp.float32),
            pltpu.VMEM((2, rows, 128), jnp.float32),
            pltpu.VMEM((2, 2, rows, 128), jnp.float32),
            pltpu.VMEM((2, rows, 128), jnp.float32),
            pltpu.VMEM((2, 2, 1, rows, 128), jnp.float32),
            pltpu.VMEM((2, 1, rows, 128), jnp.float32),
            pltpu.VMEM((1, rows, 128), jnp.float32),
            pltpu.VMEM((2, 1, 2, rows, 128), jnp.float32),
            pltpu.VMEM((2, 1, rows, 128), jnp.float32),
            pltpu.VMEM((1, rows, 128), jnp.float32),
            pltpu.SemaphoreType.DMA((2, 6)),
        ],
        compiler_params=pltpu.CompilerParams(
            collective_id=collective_id, has_side_effects=True, vmem_limit_bytes=60 * 1024 * 1024
        ),
    )(block)
    return own.reshape(-1)[:width]

def gather_kernel(x_ref, o_ref, inbox, send_sems, recv_sems):
    fsdp_here = lax.axis_index("fsdp")
    ctx_here = lax.axis_index("ctx")
    tp_here = lax.axis_index("tp")
    ctx_count = lax.axis_size("ctx")
    count = lax.axis_size("fsdp") * ctx_count
    me = fsdp_here * ctx_count + ctx_here
    peers = []
    for offset in range(1, count):
        other = (me + offset) % count
        peers.append((other // ctx_count, other % ctx_count, tp_here))
    barrier = pltpu.get_barrier_semaphore()
    for peer in peers:
        pl.semaphore_signal(barrier, 1, device_id=peer, device_id_type=pl.DeviceIdType.MESH)
    pl.semaphore_wait(barrier, len(peers))
    copies = []
    for number, peer in enumerate(peers):
        copy = pltpu.make_async_remote_copy(
            src_ref=x_ref,
            dst_ref=inbox.at[me],
            send_sem=send_sems.at[number],
            recv_sem=recv_sems.at[me],
            device_id=peer,
            device_id_type=pl.DeviceIdType.MESH,
        )
        copy.start()
        copies.append(copy)
    o_ref[me] = x_ref[...]
    for copy in copies:
        copy.wait_send()
    for offset in range(1, count):
        source = (me + count - offset) % count
        pltpu.make_async_remote_copy(
            src_ref=x_ref,
            dst_ref=inbox.at[source],
            send_sem=send_sems.at[0],
            recv_sem=recv_sems.at[source],
            device_id=peers[0],
            device_id_type=pl.DeviceIdType.MESH,
        ).wait_recv()
        o_ref[source] = inbox[source]


def gather_shards(flat, collective_id):
    size = flat.shape[0]
    rows = -(-size // 2048) * 16
    block = jnp.pad(flat, (0, rows * 128 - size)).reshape(rows, 128)
    count = lax.axis_size("fsdp") * lax.axis_size("ctx")
    full = pl.pallas_call(
        gather_kernel,
        out_shape=jax.ShapeDtypeStruct((count, rows, 128), flat.dtype),
        in_specs=[pl.BlockSpec(memory_space=pltpu.VMEM)],
        out_specs=pl.BlockSpec(memory_space=pltpu.VMEM),
        scratch_shapes=[
            pltpu.VMEM((count, rows, 128), flat.dtype),
            pltpu.SemaphoreType.DMA((count - 1,)),
            pltpu.SemaphoreType.DMA((count,)),
        ],
        compiler_params=pltpu.CompilerParams(collective_id=collective_id, has_side_effects=True),
    )(block)
    return full.reshape(count, rows * 128)[:, :size]


def swiglu_experts(gate_up):
    return jax.nn.silu(gate_up[:, :, 0]) * gate_up[:, :, 1]


def gather_packed(pieces, axes, use_kernel=False):
    flat = jnp.concatenate([piece.reshape(-1) for piece, _ in pieces])
    if use_kernel:
        full = gather_shards(flat, 4)
    else:
        full = lax.all_gather(flat, axes, axis=0, tiled=False)
    count = full.shape[0]
    results = []
    offset = 0
    for piece, dim in pieces:
        size = piece.size
        part = full[:, offset : offset + size].reshape((count,) + piece.shape)
        offset += size
        part = jnp.moveaxis(part, 0, dim)
        shape = list(piece.shape)
        shape[dim] *= count
        results.append(part.reshape(shape))
    return results


def scatter_packed(pieces, axes, count, use_kernel=False):
    columns = []
    local_shapes = []
    for grad, dim in pieces:
        shape = grad.shape
        split = shape[:dim] + (count, shape[dim] // count) + shape[dim + 1 :]
        local_shapes.append(shape[:dim] + (shape[dim] // count,) + shape[dim + 1 :])
        part = jnp.moveaxis(grad.reshape(split), dim, 0)
        columns.append(part.reshape(count, -1))
    packed = jnp.concatenate(columns, axis=1)
    if use_kernel:
        own = halving_scatter(packed, 3)
    else:
        width = packed.shape[1]
        rows = -(-width // 1024) * 8
        packed = jnp.pad(packed, ((0, 0), (0, rows * 128 - width))).reshape(count * rows, 128)
        own = lax.psum_scatter(packed, axes, scatter_dimension=0, tiled=True).reshape(-1)
    results = []
    offset = 0
    for local_shape in local_shapes:
        size = 1
        for extent in local_shape:
            size *= extent
        results.append(own[offset : offset + size].reshape(local_shape))
        offset += size
    return results


def experts_dense(normed_two, grad_out, weights, expert_in_all, expert_down_all):
    gate_up = jnp.einsum(
        "td,edgf->etgf", normed_two, expert_in_all, preferred_element_type=jnp.float32
    )
    act, act_back = jax.vjp(swiglu_experts, gate_up)
    hidden = act.astype(jnp.bfloat16)
    outs = jnp.einsum("etf,efd->etd", hidden, expert_down_all, preferred_element_type=jnp.float32)
    weights_e = weights.T[:, :, None]
    combined = jnp.sum(weights_e * outs, axis=0)
    gate_dots = jnp.sum(outs * grad_out[None], axis=-1).T
    grad_outs = (weights_e * grad_out[None]).astype(jnp.bfloat16)
    grad_hidden = jnp.einsum(
        "etd,efd->etf", grad_outs, expert_down_all, preferred_element_type=jnp.float32
    )
    grad_gate_up = act_back(grad_hidden)[0].astype(jnp.bfloat16)
    grad_down = jnp.einsum("etf,etd->efd", hidden, grad_outs, preferred_element_type=jnp.float32)
    grad_in = jnp.einsum(
        "td,etgf->edgf", normed_two, grad_gate_up, preferred_element_type=jnp.float32
    )
    grad_rows = jnp.einsum(
        "etgf,edgf->td", grad_gate_up, expert_in_all, preferred_element_type=jnp.float32
    )
    return combined, gate_dots, grad_rows, grad_in, grad_down


def experts_routed(
    normed_two, grad_out, route_rows, gate_probs, expert_in_low, expert_down_low, capacity
):
    block_len, model_width = normed_two.shape
    experts = lax.axis_size("fsdp")
    slot_index, owner_route, filled = slot_tables(route_rows, experts, capacity)
    fill_mask = filled.astype(jnp.bfloat16)[:, None]
    route_grads = (
        (gate_probs[:, :, None] * grad_out[:, None, :])
        .astype(jnp.bfloat16)
        .reshape(2 * block_len, model_width)
    )
    send_rows = jnp.stack(
        [
            (normed_two[owner_route // 2] * fill_mask).reshape(experts, capacity, model_width),
            (route_grads[owner_route] * fill_mask).reshape(experts, capacity, model_width),
        ],
        axis=1,
    )
    exchange = lambda rows: lax.all_to_all(rows, "fsdp", split_axis=0, concat_axis=0, tiled=True)
    pair_count = lax.axis_size("tp")
    swap = lambda rows: lax.ppermute(
        rows, "tp", [(index, index + 1 - 2 * (index % 2)) for index in range(pair_count)]
    )
    half = capacity // 2
    side = lax.axis_index("tp") % 2
    mine = exchange(lax.dynamic_slice_in_dim(send_rows, side * half, half, 2))
    received_both = jnp.concatenate([mine, swap(mine)], axis=2)
    received = received_both[:, 0].reshape(experts * capacity, model_width)
    grad_received = received_both[:, 1].reshape(experts * capacity, model_width)
    gate_up = jnp.einsum("rd,dgf->rgf", received, expert_in_low, preferred_element_type=jnp.float32)
    act, act_back = jax.vjp(swiglu, gate_up)
    hidden = act.astype(jnp.bfloat16)
    outs = jnp.dot(hidden, expert_down_low, preferred_element_type=jnp.float32)
    grad_hidden = jnp.einsum(
        "rd,fd->rf", grad_received, expert_down_low, preferred_element_type=jnp.float32
    )
    grad_gate_up = act_back(grad_hidden)[0].astype(jnp.bfloat16)
    grad_in = jnp.einsum("rd,rgf->dgf", received, grad_gate_up, preferred_element_type=jnp.float32)
    grad_down = jnp.einsum("rf,rd->fd", hidden, grad_received, preferred_element_type=jnp.float32)
    grad_expert_rows = jnp.einsum(
        "rgf,dgf->rd", grad_gate_up, expert_in_low, preferred_element_type=jnp.float32
    )
    pair_sums = []
    for rows in (outs, grad_expert_rows):
        rows = rows.reshape(experts, capacity, model_width)
        pair_sums.append(rows[:, :half] + swap(rows[:, half:]))
    held = exchange(jnp.stack(pair_sums, axis=1).astype(jnp.bfloat16))
    slot_expert = slot_index // capacity
    slot_rank = slot_index % capacity
    in_side = ((slot_rank // half) == side)[:, None]
    local_slot = slot_expert * half + slot_rank % half
    picked_rows = []
    for which in range(2):
        rows = held[:, which].reshape(experts * half, model_width)[local_slot]
        picked_rows.append(
            jnp.where(in_side, rows.astype(jnp.float32), 0.0).reshape(block_len, 2, model_width)
        )
    route_out, grad_routes = picked_rows
    combined = jnp.sum(gate_probs[:, :, None] * route_out, axis=1)
    gate_dots = jnp.sum(grad_out[:, None, :] * route_out, axis=-1)
    grad_rows = jnp.sum(grad_routes, axis=1)
    return combined, gate_dots, grad_rows, grad_in, grad_down


def local(
    layer_input,
    segments,
    routes,
    cotangent,
    gains,
    attention_in,
    attention_out,
    router_weight,
    shared_in,
    shared_down,
    expert_in,
    expert_down,
    model_stats,
    head_stats,
    value_columns,
    hidden_stats,
    router_state,
    expert_model_stats,
    expert_hidden_stats,
):
    block_len = layer_input.shape[1]
    model_width = layer_input.shape[2]
    experts = router_weight.shape[1]
    dense_experts = False
    capacity = min(block_len, 4 * block_len // experts)
    ctx_index = lax.axis_index("ctx")
    tp_index = lax.axis_index("tp")
    fsdp_index = lax.axis_index("fsdp")
    shard_index = lax.axis_index(("fsdp", "ctx"))
    shard_count = lax.axis_size(("fsdp", "ctx"))
    ctx_count = lax.axis_size("ctx")
    base_pos = ctx_index * block_len
    low = lambda v: v.astype(jnp.bfloat16)
    gain_low, attn_in_low, attn_out_low, router_low = gather_packed(
        [(low(gains), 1), (low(attention_in), 0), (low(attention_out), 1), (low(router_weight), 0)],
        ("fsdp", "ctx"),
        shard_count <= 8,
    )
    later = [
        (low(shared_in), 0),
        (low(shared_down), 1),
    ]
    if dense_experts:
        later += [(low(expert_in), 0), (low(expert_down), 0)]
    later_full = gather_packed(later, ("fsdp", "ctx"))
    shared_in_low, shared_down_low = later_full[:2]
    if dense_experts:
        fe_local = expert_down.shape[1]
        expert_in_all = later_full[2].reshape(experts, model_width, 2, fe_local)
        expert_down_all = (
            later_full[3]
            .reshape(experts, ctx_count, fe_local, model_width // ctx_count)
            .transpose(0, 2, 1, 3)
            .reshape(experts, fe_local, model_width)
        )
    else:
        expert_in_low = lax.all_gather(low(expert_in), "ctx", axis=1, tiled=True)[0]
        expert_down_low = lax.all_gather(low(expert_down), "ctx", axis=2, tiled=True)[0]
    residual = layer_input[0].astype(jnp.float32)
    gain_one = gain_low[0].astype(jnp.float32)
    gain_two = gain_low[1].astype(jnp.float32)
    normed_one, norm_one_back = jax.vjp(rms_norm, residual, gain_one)
    normed_one = normed_one.astype(jnp.bfloat16)
    projected = jnp.einsum(
        "td,dgf->tgf", normed_one, attn_in_low, preferred_element_type=jnp.float32
    )
    local_cols = projected.shape[2]
    local_heads = local_cols // HD
    half_dim = HD // 2
    frequency = 10000.0 ** (-jnp.arange(half_dim, dtype=jnp.float32) / half_dim)
    angles = (base_pos + jnp.arange(block_len, dtype=jnp.int32)).astype(jnp.float32)[
        :, None
    ] * frequency[None, :]
    cosine = jnp.cos(angles)
    sine_tab = jnp.sin(angles)
    queries = rotate(projected[:, 0].reshape(block_len, local_heads, HD), cosine, sine_tab).astype(
        jnp.bfloat16
    )
    keys_own = rotate(projected[:, 1].reshape(block_len, local_heads, HD), cosine, sine_tab).astype(
        jnp.bfloat16
    )
    values_own = projected[:, 2].reshape(block_len, local_heads, HD).astype(jnp.bfloat16)
    seg_own = segments[0].astype(jnp.bfloat16)
    keys_prev, values_prev, seg_prev = from_behind((keys_own, values_own, seg_own), "ctx", 1)
    keys_ext = jnp.concatenate([keys_prev, keys_own], axis=0)
    values_ext = jnp.concatenate([values_prev, values_own], axis=0)
    seg_ext = jnp.concatenate([seg_prev, seg_own], axis=0)
    block_rows = min(512, block_len)
    block_total = block_len // block_rows
    starts = jnp.arange(block_total, dtype=jnp.int32) * block_rows

    def forward_block(start_row):
        query_rows, key_rows, value_rows, masked, allowed = block_view(
            queries, keys_ext, values_ext, seg_own, seg_ext, start_row, base_pos
        )
        row_max = jnp.max(masked, axis=-1, keepdims=True)
        exp_terms = jnp.where(allowed[None], jnp.exp(masked - row_max), 0.0)
        row_total = jnp.sum(exp_terms, axis=-1, keepdims=True)
        attn_probs = (exp_terms / row_total).astype(jnp.bfloat16)
        attended = jnp.einsum(
            "hqk,khd->qhd", attn_probs, value_rows, preferred_element_type=jnp.float32
        )
        return (attended, row_max + jnp.log(row_total))

    attended, log_totals = lax.map(forward_block, starts)
    mixed_heads = attended.reshape(block_len, local_cols).astype(jnp.bfloat16)
    attn_total = lax.psum(
        jnp.dot(mixed_heads, attn_out_low, preferred_element_type=jnp.float32), "tp"
    )
    after_attn = residual + attn_total
    normed_two, norm_two_back = jax.vjp(rms_norm, after_attn, gain_two)
    normed_two = normed_two.astype(jnp.bfloat16)
    logits = jnp.dot(normed_two, router_low, preferred_element_type=jnp.float32)
    route_rows = routes[0]
    onehot = (route_rows[:, :, None] == jnp.arange(experts, dtype=jnp.int32)[None, None, :]).astype(
        jnp.float32
    )
    picked = jnp.sum(onehot * logits[:, None, :], axis=-1)
    gate_probs = jax.nn.softmax(picked, axis=-1)
    upstream = cotangent[0]
    grad_out = upstream.astype(jnp.float32)
    if dense_experts:
        weights = jnp.sum(gate_probs[:, :, None] * onehot, axis=1)
        combined, dots_e, grad_rows, grad_expert_in, grad_expert_down = experts_dense(
            normed_two, grad_out, weights, expert_in_all, expert_down_all
        )
        gate_dots = jnp.sum(onehot * dots_e[:, None, :], axis=-1)
    else:
        combined, gate_dots, grad_rows, grad_expert_in, grad_expert_down = experts_routed(
            normed_two,
            grad_out,
            route_rows,
            gate_probs,
            expert_in_low,
            expert_down_low,
            capacity,
        )
    shared_gate_up = jnp.einsum(
        "td,dgf->tgf", normed_two, shared_in_low, preferred_element_type=jnp.float32
    )
    shared_act, shared_act_back = jax.vjp(swiglu, shared_gate_up)
    shared_hidden = shared_act.astype(jnp.bfloat16)
    shared_out = jnp.dot(shared_hidden, shared_down_low, preferred_element_type=jnp.float32)
    grad_shared_hidden = jnp.einsum(
        "td,fd->tf", upstream, shared_down_low, preferred_element_type=jnp.float32
    )
    grad_shared_gate_up = shared_act_back(grad_shared_hidden)[0].astype(jnp.bfloat16)
    partial_two = (
        jnp.einsum(
            "tgf,dgf->td", grad_shared_gate_up, shared_in_low, preferred_element_type=jnp.float32
        )
        + grad_rows
    )
    branch_total, grad_normed_part, gate_total = lax.psum(
        (shared_out + combined, partial_two, gate_dots), "tp"
    )
    layer_out = after_attn + branch_total
    grad_picked = gate_probs * (
        gate_total - jnp.sum(gate_probs * gate_total, axis=-1, keepdims=True)
    )
    grad_logits = jnp.sum(grad_picked[:, :, None] * onehot, axis=1).astype(jnp.bfloat16)
    grad_shared_in = jnp.einsum(
        "td,tgf->dgf", normed_two, grad_shared_gate_up, preferred_element_type=jnp.float32
    )
    grad_shared_down = jnp.einsum(
        "tf,td->fd", shared_hidden, upstream, preferred_element_type=jnp.float32
    )
    grad_router = jnp.einsum(
        "td,te->de", normed_two, grad_logits, preferred_element_type=jnp.float32
    )
    grad_normed_two = grad_normed_part + jnp.einsum(
        "te,de->td", grad_logits, router_low, preferred_element_type=jnp.float32
    )
    grad_after, grad_gain_two = norm_two_back(grad_normed_two)
    grad_after = grad_after + grad_out
    grad_attn_low = grad_after.astype(jnp.bfloat16)
    grad_attn_out = jnp.einsum(
        "tc,td->cd", mixed_heads, grad_attn_low, preferred_element_type=jnp.float32
    )
    first_grads = [
        (grad_attn_out, 1),
        (grad_router, 0),
        (grad_shared_in, 0),
        (grad_shared_down, 1),
        (grad_gain_two, 0),
    ]
    if dense_experts:
        fe_local = expert_down.shape[1]
        first_grads += [
            (grad_expert_in.reshape(shard_count * expert_in.shape[1], 2, fe_local), 0),
            (
                grad_expert_down.reshape(experts, fe_local, ctx_count, model_width // ctx_count)
                .transpose(0, 2, 1, 3)
                .reshape(shard_count * fe_local, model_width // ctx_count),
                0,
            ),
        ]
    if not dense_experts:
        own_expert_in = lax.psum_scatter(grad_expert_in[None], "ctx", scatter_dimension=1, tiled=True)
        own_expert_down = lax.psum_scatter(
            grad_expert_down[None], "ctx", scatter_dimension=2, tiled=True
        )
    grad_heads = (
        jnp.einsum("td,cd->tc", grad_attn_low, attn_out_low, preferred_element_type=jnp.float32)
        .astype(jnp.bfloat16)
        .reshape(block_len, local_heads, HD)
    )

    def backward_block(block_number, running):
        grad_keys, grad_values, grad_queries = running
        start_row = block_number * block_rows
        query_rows, key_rows, value_rows, masked, allowed = block_view(
            queries, keys_ext, values_ext, seg_own, seg_ext, start_row, base_pos
        )
        log_total = lax.dynamic_index_in_dim(log_totals, block_number, 0, keepdims=False)
        attn_probs = jnp.where(allowed[None], jnp.exp(masked - log_total), 0.0)
        grad_block = lax.dynamic_slice_in_dim(grad_heads, start_row, block_rows, 0)
        grad_probs = jnp.einsum(
            "qhd,khd->hqk", grad_block, value_rows, preferred_element_type=jnp.float32
        )
        inner_sum = jnp.sum(attn_probs * grad_probs, axis=-1, keepdims=True)
        grad_scores = (attn_probs * (grad_probs - inner_sum)).astype(jnp.bfloat16)
        grad_query_rows = (
            jnp.einsum("hqk,khd->qhd", grad_scores, key_rows, preferred_element_type=jnp.float32)
            * 0.125
        )
        grad_key_rows = (
            jnp.einsum("hqk,qhd->khd", grad_scores, query_rows, preferred_element_type=jnp.float32)
            * 0.125
        )
        grad_value_rows = jnp.einsum(
            "hqk,qhd->khd",
            attn_probs.astype(jnp.bfloat16),
            grad_block,
            preferred_element_type=jnp.float32,
        )
        key_offset = start_row + block_len - WINDOW
        grad_keys = lax.dynamic_update_slice_in_dim(
            grad_keys,
            lax.dynamic_slice_in_dim(grad_keys, key_offset, block_rows + WINDOW, 0) + grad_key_rows,
            key_offset,
            0,
        )
        grad_values = lax.dynamic_update_slice_in_dim(
            grad_values,
            lax.dynamic_slice_in_dim(grad_values, key_offset, block_rows + WINDOW, 0)
            + grad_value_rows,
            key_offset,
            0,
        )
        grad_queries = lax.dynamic_update_slice_in_dim(grad_queries, grad_query_rows, start_row, 0)
        return (grad_keys, grad_values, grad_queries)

    zero_ext = jnp.zeros((2 * block_len, local_heads, HD), jnp.float32)
    zero_own = jnp.zeros((block_len, local_heads, HD), jnp.float32)
    grad_keys, grad_values, grad_queries = lax.fori_loop(
        0, block_total, backward_block, (zero_ext, zero_ext, zero_own)
    )
    rim_keys, rim_values = (
        from_behind(grad_keys[:block_len].astype(jnp.bfloat16), "ctx", -1).astype(jnp.float32),
        from_behind(grad_values[:block_len].astype(jnp.bfloat16), "ctx", -1).astype(jnp.float32),
    )
    grad_keys_own = grad_keys[block_len:] + rim_keys
    grad_values_own = grad_values[block_len:] + rim_values
    grad_query_raw = rotate(grad_queries, cosine, -sine_tab)
    grad_key_raw = rotate(grad_keys_own, cosine, -sine_tab)
    grad_projected = (
        jnp.stack([grad_query_raw, grad_key_raw, grad_values_own], axis=1)
        .reshape(block_len, 3, local_cols)
        .astype(jnp.bfloat16)
    )
    grad_attn_in = jnp.einsum(
        "td,tgf->dgf", normed_one, grad_projected, preferred_element_type=jnp.float32
    )
    partial_one = jnp.einsum(
        "tgf,dgf->td", grad_projected, attn_in_low, preferred_element_type=jnp.float32
    )
    tp_one = lax.psum(partial_one, "tp")
    halving = lax.axis_size("fsdp") == 4 and ctx_count == 2
    all_own = scatter_packed(
        first_grads + [(grad_attn_in, 0)],
        ("fsdp", "ctx"),
        shard_count,
        halving,
    )
    own_attn_out, own_router, own_shared_in, own_shared_down, own_gain_two = all_own[:5]
    own_attn_in = all_own[-1]
    grad_residual, grad_gain_one = norm_one_back(tp_one + 0.0 * own_attn_in[0, 0, 0])
    input_grad = grad_after + grad_residual
    if dense_experts:
        own_expert_in = all_own[5][None]
        own_expert_down = all_own[6][None]
    lead_tp = (tp_index == 0).astype(jnp.float32)
    first_shard = (shard_index == 0).astype(jnp.float32)
    first_ctx = (ctx_index == 0).astype(jnp.float32)
    d_local = gains.shape[1]
    ff_local = shared_down.shape[0]
    fe_local = expert_down.shape[1]
    d_quarter = expert_in.shape[1]
    square_attn_in = own_attn_in * own_attn_in + TINY_SQUARE
    square_attn_out = own_attn_out * own_attn_out + TINY_SQUARE
    square_shared_in = own_shared_in * own_shared_in + TINY_SQUARE
    square_shared_down = own_shared_down * own_shared_down + TINY_SQUARE
    square_expert_in = own_expert_in[0] * own_expert_in[0] + TINY_SQUARE
    square_expert_down = own_expert_down[0] * own_expert_down[0] + TINY_SQUARE
    model_part = lax.dynamic_update_slice(
        jnp.zeros((4, D), jnp.float32),
        jnp.stack(
            [
                jnp.sum(square_attn_in, axis=(1, 2)),
                jnp.sum(square_shared_in, axis=(1, 2)),
                jnp.sum(square_attn_out, axis=0),
                jnp.sum(square_shared_down, axis=0),
            ]
        ),
        (0, shard_index * d_local),
    )
    head_part = lax.dynamic_update_slice(
        jnp.zeros((4, HH), jnp.float32),
        jnp.concatenate(
            [jnp.sum(square_attn_in, axis=0), jnp.sum(square_attn_out, axis=1)[None]], axis=0
        ),
        (0, tp_index * local_cols),
    )
    hidden_part = lax.dynamic_update_slice(
        jnp.zeros((3, FF), jnp.float32),
        jnp.concatenate(
            [jnp.sum(square_shared_in, axis=0), jnp.sum(square_shared_down, axis=1)[None]], axis=0
        ),
        (0, tp_index * ff_local),
    )
    expert_model_part = lax.dynamic_update_slice(
        jnp.zeros((experts, 2, D), jnp.float32),
        jnp.stack([jnp.sum(square_expert_in, axis=(1, 2)), jnp.sum(square_expert_down, axis=0)])[
            None
        ],
        (fsdp_index, 0, ctx_index * d_quarter),
    )
    expert_hidden_part = lax.dynamic_update_slice(
        jnp.zeros((experts, 3, FE), jnp.float32),
        jnp.concatenate(
            [jnp.sum(square_expert_in, axis=0), jnp.sum(square_expert_down, axis=1)[None]], axis=0
        )[None],
        (fsdp_index, 0, tp_index * fe_local),
    )
    scalar_part = jnp.stack(
        [
            lead_tp * jnp.sum(gains * gains),
            jnp.sum(attention_in * attention_in),
            jnp.sum(attention_out * attention_out),
            lead_tp * jnp.sum(router_weight * router_weight),
            jnp.sum(shared_in * shared_in),
            jnp.sum(shared_down * shared_down),
            jnp.sum(expert_in * expert_in),
            jnp.sum(expert_down * expert_down),
            lead_tp * jnp.sum(model_stats[2]),
            first_shard * jnp.sum(head_stats[2]),
            lead_tp * jnp.sum(model_stats[3]),
            first_shard * jnp.sum(hidden_stats[2]),
        ]
    )
    expert_old_part = lax.dynamic_update_slice(
        jnp.zeros((2, experts), jnp.float32),
        jnp.stack(
            [
                lead_tp * jnp.sum(expert_model_stats[0, 0]),
                first_ctx * jnp.sum(expert_hidden_stats[0, 2]),
            ]
        )[:, None],
        (0, fsdp_index),
    )
    global_sums = butterfly_sum(
        [
            model_part,
            head_part,
            hidden_part,
            expert_model_part,
            expert_hidden_part,
            scalar_part,
            expert_old_part,
            lead_tp * grad_gain_one,
        ],
        1,
    )
    (
        model_sum,
        head_sum,
        hidden_sum,
        expert_model_sum,
        expert_hidden_sum,
        scalar_sum,
        expert_old_sum,
        gain_one_sum,
    ) = global_sums
    own_gain_one = lax.dynamic_slice_in_dim(gain_one_sum, shard_index * d_local, d_local)
    own_gains = jnp.stack([own_gain_one, own_gain_two])
    shard_start = shard_index * d_local
    gain_state = DECAY_RATE * model_stats[0:2] + (1.0 - DECAY_RATE) * (
        own_gains * own_gains + TINY_SQUARE
    )
    update_gains = own_gains * lax.rsqrt(gain_state)
    router_new = DECAY_RATE * router_state + (1.0 - DECAY_RATE) * (
        own_router * own_router + TINY_SQUARE
    )
    update_router = own_router * lax.rsqrt(router_new)
    attn_cols_old = jnp.concatenate([head_stats[0:2], value_columns[None]], axis=0).reshape(-1)
    update_attn_in, rows_attn_in, cols_attn_in = factored_update(
        own_attn_in.reshape(d_local, 3 * local_cols),
        model_stats[2],
        attn_cols_old,
        lax.dynamic_slice_in_dim(model_sum[0], shard_start, d_local),
        lax.dynamic_slice_in_dim(head_sum[0:3], tp_index * local_cols, local_cols, 1).reshape(-1),
        D,
        3 * HH,
        scalar_sum[8],
        jnp.sum(model_sum[0]),
    )
    update_attn_out, rows_attn_out, cols_attn_out = factored_update(
        own_attn_out,
        head_stats[2],
        model_stats[4],
        lax.dynamic_slice_in_dim(head_sum[3], tp_index * local_cols, local_cols),
        lax.dynamic_slice_in_dim(model_sum[2], shard_start, d_local),
        HH,
        D,
        scalar_sum[9],
        jnp.sum(head_sum[3]),
    )
    update_shared_in, rows_shared_in, cols_shared_in = factored_update(
        own_shared_in.reshape(d_local, 2 * ff_local),
        model_stats[3],
        hidden_stats[0:2].reshape(-1),
        lax.dynamic_slice_in_dim(model_sum[1], shard_start, d_local),
        lax.dynamic_slice_in_dim(hidden_sum[0:2], tp_index * ff_local, ff_local, 1).reshape(-1),
        D,
        2 * FF,
        scalar_sum[10],
        jnp.sum(model_sum[1]),
    )
    update_shared_down, rows_shared_down, cols_shared_down = factored_update(
        own_shared_down,
        hidden_stats[2],
        model_stats[5],
        lax.dynamic_slice_in_dim(hidden_sum[2], tp_index * ff_local, ff_local),
        lax.dynamic_slice_in_dim(model_sum[3], shard_start, d_local),
        FF,
        D,
        scalar_sum[11],
        jnp.sum(hidden_sum[2]),
    )
    own_expert_model = lax.dynamic_index_in_dim(expert_model_sum, fsdp_index, 0, keepdims=False)
    own_expert_hidden = lax.dynamic_index_in_dim(expert_hidden_sum, fsdp_index, 0, keepdims=False)
    old_expert_totals = lax.dynamic_index_in_dim(expert_old_sum, fsdp_index, 1, keepdims=False)
    update_expert_in, rows_expert_in, cols_expert_in = factored_update(
        own_expert_in[0].reshape(d_quarter, 2 * fe_local),
        expert_model_stats[0, 0],
        expert_hidden_stats[0, 0:2].reshape(-1),
        lax.dynamic_slice_in_dim(own_expert_model[0], ctx_index * d_quarter, d_quarter),
        lax.dynamic_slice_in_dim(own_expert_hidden[0:2], tp_index * fe_local, fe_local, 1).reshape(
            -1
        ),
        D,
        2 * FE,
        old_expert_totals[0],
        jnp.sum(own_expert_model[0]),
    )
    update_expert_down, rows_expert_down, cols_expert_down = factored_update(
        own_expert_down[0],
        expert_hidden_stats[0, 2],
        expert_model_stats[0, 1],
        lax.dynamic_slice_in_dim(own_expert_hidden[2], tp_index * fe_local, fe_local),
        lax.dynamic_slice_in_dim(own_expert_model[1], ctx_index * d_quarter, d_quarter),
        FE,
        D,
        old_expert_totals[1],
        jnp.sum(own_expert_hidden[2]),
    )
    clip_part = jnp.stack(
        [
            lead_tp * jnp.sum(update_gains * update_gains),
            jnp.sum(update_attn_in * update_attn_in),
            jnp.sum(update_attn_out * update_attn_out),
            lead_tp * jnp.sum(update_router * update_router),
            jnp.sum(update_shared_in * update_shared_in),
            jnp.sum(update_shared_down * update_shared_down),
            jnp.sum(update_expert_in * update_expert_in),
            jnp.sum(update_expert_down * update_expert_down),
        ]
    )
    clip_total = butterfly_sum([clip_part], 2)[0]
    elements = jnp.array(
        [
            2 * D,
            D * 3 * HH,
            HH * D,
            D * experts,
            D * 2 * FF,
            FF * D,
            experts * D * 2 * FE,
            experts * FE * D,
        ],
        jnp.float32,
    )
    update_roots = jnp.sqrt(clip_total / elements)
    new_gains = apply_update(gains, update_gains, update_roots[0], scalar_sum[0], elements[0])
    new_attn_in = apply_update(
        attention_in,
        update_attn_in.reshape(attention_in.shape),
        update_roots[1],
        scalar_sum[1],
        elements[1],
    )
    new_attn_out = apply_update(
        attention_out, update_attn_out, update_roots[2], scalar_sum[2], elements[2]
    )
    new_router = apply_update(
        router_weight, update_router, update_roots[3], scalar_sum[3], elements[3]
    )
    new_shared_in = apply_update(
        shared_in,
        update_shared_in.reshape(shared_in.shape),
        update_roots[4],
        scalar_sum[4],
        elements[4],
    )
    new_shared_down = apply_update(
        shared_down, update_shared_down, update_roots[5], scalar_sum[5], elements[5]
    )
    new_expert_in = apply_update(
        expert_in,
        update_expert_in.reshape(expert_in.shape),
        update_roots[6],
        scalar_sum[6],
        elements[6],
    )
    new_expert_down = apply_update(
        expert_down,
        update_expert_down.reshape(expert_down.shape),
        update_roots[7],
        scalar_sum[7],
        elements[7],
    )
    new_model_stats = jnp.concatenate(
        [gain_state, jnp.stack([rows_attn_in, rows_shared_in, cols_attn_out, cols_shared_down])],
        axis=0,
    )
    attn_cols_new = cols_attn_in.reshape(3, local_cols)
    new_head_stats = jnp.concatenate([attn_cols_new[0:2], rows_attn_out[None]], axis=0)
    new_value_columns = attn_cols_new[2]
    new_hidden_stats = jnp.concatenate(
        [cols_shared_in.reshape(2, ff_local), rows_shared_down[None]], axis=0
    )
    new_expert_model_stats = jnp.stack([rows_expert_in, cols_expert_down])[None]
    new_expert_hidden_stats = jnp.concatenate(
        [cols_expert_in.reshape(2, fe_local), rows_expert_down[None]], axis=0
    )[None]
    return (
        layer_out.astype(jnp.bfloat16)[None],
        input_grad[None],
        own_gains,
        own_attn_in,
        own_attn_out,
        own_router,
        own_shared_in,
        own_shared_down,
        own_expert_in,
        own_expert_down,
        new_gains,
        new_attn_in,
        new_attn_out,
        new_router,
        new_shared_in,
        new_shared_down,
        new_expert_in,
        new_expert_down,
        new_model_stats,
        new_head_stats,
        new_value_columns,
        new_hidden_stats,
        router_new,
        new_expert_model_stats,
        new_expert_hidden_stats,
        update_roots,
    )


def solution(mesh):
    in_specs = (
        P("fsdp", "ctx", None),
        P("fsdp", "ctx"),
        P("fsdp", "ctx", None),
        P("fsdp", "ctx", None),
        P(None, ("fsdp", "ctx")),
        P(("fsdp", "ctx"), None, "tp"),
        P("tp", ("fsdp", "ctx")),
        P(("fsdp", "ctx"), None),
        P(("fsdp", "ctx"), None, "tp"),
        P("tp", ("fsdp", "ctx")),
        P("fsdp", "ctx", None, "tp"),
        P("fsdp", "tp", "ctx"),
        P(None, ("fsdp", "ctx")),
        P(None, "tp"),
        P("tp"),
        P(None, "tp"),
        P(("fsdp", "ctx"), None),
        P("fsdp", None, "ctx"),
        P("fsdp", None, "tp"),
    )
    out_specs = (
        P("fsdp", "ctx", None),
        P("fsdp", "ctx", None),
        P(None, ("fsdp", "ctx")),
        P(("fsdp", "ctx"), None, "tp"),
        P("tp", ("fsdp", "ctx")),
        P(("fsdp", "ctx"), None),
        P(("fsdp", "ctx"), None, "tp"),
        P("tp", ("fsdp", "ctx")),
        P("fsdp", "ctx", None, "tp"),
        P("fsdp", "tp", "ctx"),
        P(None, ("fsdp", "ctx")),
        P(("fsdp", "ctx"), None, "tp"),
        P("tp", ("fsdp", "ctx")),
        P(("fsdp", "ctx"), None),
        P(("fsdp", "ctx"), None, "tp"),
        P("tp", ("fsdp", "ctx")),
        P("fsdp", "ctx", None, "tp"),
        P("fsdp", "tp", "ctx"),
        P(None, ("fsdp", "ctx")),
        P(None, "tp"),
        P("tp"),
        P(None, "tp"),
        P(("fsdp", "ctx"), None),
        P("fsdp", None, "ctx"),
        P("fsdp", None, "tp"),
        P(),
    )
    return jax.shard_map(local, mesh=mesh, in_specs=in_specs, out_specs=out_specs, check_vma=False)
```

```python
import jax
import jax.numpy as jnp
from jax import lax
from jax.sharding import PartitionSpec as P
from jax.experimental import pallas as pl
from jax.experimental.pallas import tpu as pltpu

D = 768
HD = 64
FF = 2048
FE = 2048
WINDOW = 1024
HH = 768


EPSILON = 1e-06
TINY_SQUARE = 1e-30
SCALE_FLOOR = 0.001
DECAY_RATE = 0.5
CLIP_LIMIT = 0.5
STEP_RATE = 0.5


def from_behind(value, axis, steps):
    count = lax.axis_size(axis)
    leading, last = (max(0, -steps), min(count, count - steps))
    return lax.ppermute(value, axis, [(source, source + steps) for source in range(leading, last)])


def rms_norm(values, gain_vec):
    inv_rms = lax.rsqrt(jnp.mean(values * values, axis=-1, keepdims=True) + EPSILON)
    return values * inv_rms * gain_vec


def swiglu(gate_up):
    return jax.nn.silu(gate_up[:, 0]) * gate_up[:, 1]


def rotate(values, cosine, sine_tab):
    half_dim = values.shape[-1] // 2
    first_half = values[..., :half_dim]
    second_half = values[..., half_dim:]
    cos_b = cosine[:, None, :]
    sin_b = sine_tab[:, None, :]
    return jnp.concatenate(
        [first_half * cos_b - second_half * sin_b, second_half * cos_b + first_half * sin_b],
        axis=-1,
    )


def slot_tables(block_routes, experts, capacity):
    flat_routes = block_routes.reshape(-1)
    route_count = flat_routes.shape[0]
    onehot = (flat_routes[:, None] == jnp.arange(experts, dtype=jnp.int32)[None, :]).astype(
        jnp.int32
    )
    rank_in = jnp.sum(
        (jnp.cumsum(onehot, axis=0, dtype=jnp.int32) - 1) * onehot, axis=1, dtype=jnp.int32
    )
    slot_index = flat_routes * capacity + rank_in
    owner_route = (
        jnp.zeros((experts * capacity,), jnp.int32)
        .at[slot_index]
        .set(jnp.arange(route_count, dtype=jnp.int32))
    )
    filled = jnp.zeros((experts * capacity,), jnp.int32).at[slot_index].set(1)
    return (slot_index, owner_route, filled)


def block_view(queries, keys_ext, values_ext, seg_own, seg_ext, start_row, base_pos):
    block_len = queries.shape[0]
    block_rows = min(512, block_len)
    query_rows = lax.dynamic_slice_in_dim(queries, start_row, block_rows, 0)
    key_rows = lax.dynamic_slice_in_dim(
        keys_ext, start_row + block_len - WINDOW, block_rows + WINDOW, 0
    )
    value_rows = lax.dynamic_slice_in_dim(
        values_ext, start_row + block_len - WINDOW, block_rows + WINDOW, 0
    )
    scores = (
        jnp.einsum("qhd,khd->hqk", query_rows, key_rows, preferred_element_type=jnp.float32) * 0.125
    )
    query_pos = start_row + jnp.arange(block_rows, dtype=jnp.int32)
    key_pos = start_row - WINDOW + jnp.arange(block_rows + WINDOW, dtype=jnp.int32)
    distance = query_pos[:, None] - key_pos[None, :]
    seg_query = lax.dynamic_slice_in_dim(seg_own, start_row, block_rows, 0)
    seg_key = lax.dynamic_slice_in_dim(
        seg_ext, start_row + block_len - WINDOW, block_rows + WINDOW, 0
    )
    allowed = (
        (distance >= 0)
        & (distance < WINDOW)
        & (seg_query[:, None] == seg_key[None, :])
        & (key_pos[None, :] + base_pos >= 0)
    )
    return (query_rows, key_rows, value_rows, jnp.where(allowed[None], scores, -1e30), allowed)


def factored_update(
    grad_mat, rows_old, cols_old, row_sums, col_sums, row_total, col_total, old_total, square_total
):
    rows_new = DECAY_RATE * rows_old + (1.0 - DECAY_RATE) * row_sums / col_total
    cols_new = DECAY_RATE * cols_old + (1.0 - DECAY_RATE) * col_sums / row_total
    mean_rows = (DECAY_RATE * old_total + (1.0 - DECAY_RATE) * square_total / col_total) / row_total
    second_moment = rows_new[:, None] * cols_new[None, :] / mean_rows
    return (grad_mat * lax.rsqrt(second_moment), rows_new, cols_new)


def apply_update(weight, update, update_root, square_sum, elements):
    param_scale = jnp.maximum(SCALE_FLOOR, jnp.sqrt(square_sum / elements))
    return weight - STEP_RATE * param_scale * update / jnp.maximum(1.0, update_root / CLIP_LIMIT)


def butterfly_partners():
    partners = []
    here = [lax.axis_index(name) for name in ("fsdp", "ctx", "tp")]
    for axis_number, name in enumerate(("fsdp", "ctx", "tp")):
        size = lax.axis_size(name)
        step = 1
        while step < size:
            bit = (here[axis_number] // step) % 2
            other = list(here)
            other[axis_number] = here[axis_number] + step * (1 - 2 * bit)
            partners.append(tuple(other))
            step *= 2
    return partners


def butterfly_kernel(x_ref, o_ref, stage, inbox, send_sems, recv_sems):
    partners = butterfly_partners()
    barrier = pltpu.get_barrier_semaphore()
    for partner in partners:
        pl.semaphore_signal(
            barrier, 1, device_id=partner, device_id_type=pl.DeviceIdType.MESH
        )
    pl.semaphore_wait(barrier, len(partners))
    acc = x_ref[...]
    for round_number, partner in enumerate(partners):
        stage[round_number] = acc
        copy = pltpu.make_async_remote_copy(
            src_ref=stage.at[round_number],
            dst_ref=inbox.at[round_number],
            send_sem=send_sems.at[round_number],
            recv_sem=recv_sems.at[round_number],
            device_id=partner,
            device_id_type=pl.DeviceIdType.MESH,
        )
        copy.start()
        copy.wait()
        acc = stage[round_number] + inbox[round_number]
    o_ref[...] = acc


def butterfly_sum(values, collective_id):
    flat = jnp.concatenate([v.reshape(-1).astype(jnp.float32) for v in values])
    size = flat.shape[0]
    rows = -(-size // 1024) * 8
    block = jnp.pad(flat, (0, rows * 128 - size)).reshape(rows, 128)
    rounds = sum(
        max(1, lax.axis_size(name)).bit_length() - 1 for name in ("fsdp", "ctx", "tp")
    )
    total = pl.pallas_call(
        butterfly_kernel,
        out_shape=jax.ShapeDtypeStruct((rows, 128), jnp.float32),
        in_specs=[pl.BlockSpec(memory_space=pltpu.VMEM)],
        out_specs=pl.BlockSpec(memory_space=pltpu.VMEM),
        scratch_shapes=[
            pltpu.VMEM((rounds, rows, 128), jnp.float32),
            pltpu.VMEM((rounds, rows, 128), jnp.float32),
            pltpu.SemaphoreType.DMA((rounds,)),
            pltpu.SemaphoreType.DMA((rounds,)),
        ],
        compiler_params=pltpu.CompilerParams(collective_id=collective_id, has_side_effects=True),
    )(block).reshape(-1)
    results = []
    offset = 0
    for v in values:
        results.append(total[offset : offset + v.size].reshape(v.shape))
        offset += v.size
    return results


def halving_kernel(
    x_ref, o_ref, stage_a, stage_a2, stage_b, stage_b2, in_a1, in_a2, in_a3, in_b1, in_b2, in_b3, sems
):
    rows = o_ref.shape[0] // 2
    chunk = 64
    fsdp_here = lax.axis_index("fsdp")
    ctx_here = lax.axis_index("ctx")
    tp_here = lax.axis_index("tp")
    bit_low = fsdp_here % 2
    bit_high = (fsdp_here // 2) % 2
    partners = [
        (fsdp_here, 1 - ctx_here, tp_here),
        (fsdp_here + 1 - 2 * bit_low, ctx_here, tp_here),
        (fsdp_here + 2 - 4 * bit_high, ctx_here, tp_here),
    ]
    barrier = pltpu.get_barrier_semaphore()
    for partner in partners:
        pl.semaphore_signal(barrier, 1, device_id=partner, device_id_type=pl.DeviceIdType.MESH)
    pl.semaphore_wait(barrier, len(partners))
    first, second = pl.ds(0, rows), pl.ds(rows, rows)

    def swap_pair(sources, targets, number, partner_pair):
        copies = []
        for index in range(2):
            copy = pltpu.make_async_remote_copy(
                src_ref=sources[index],
                dst_ref=targets[index],
                send_sem=sems.at[0, 2 * number + index],
                recv_sem=sems.at[1, 2 * number + index],
                device_id=partner_pair[index],
                device_id_type=pl.DeviceIdType.MESH,
            )
            copy.start()
            copies.append(copy)
        for copy in copies:
            copy.wait()

    def each_chunk(body):
        @pl.loop(0, rows // chunk)
        def _(step):
            body(pl.ds(pl.multiple_of(step * chunk, chunk), chunk))

    swap_pair(
        [
            x_ref.at[:, :, pl.ds(1 - ctx_here, 1), first],
            x_ref.at[:, pl.ds(1 - bit_low, 1), :, second],
        ],
        [in_a1, in_b1],
        0,
        [partners[0], partners[1]],
    )

    def round_one(part):
        shifted = pl.ds(part.start + rows, chunk)
        for high in range(2):
            for other in range(2):
                stage_a[high, other, part] = (
                    x_ref[high, other, ctx_here, part] + in_a1[high, other, 0, part]
                )
                stage_b[high, other, part] = (
                    x_ref[high, bit_low, other, shifted] + in_b1[high, 0, other, part]
                )

    each_chunk(round_one)
    swap_pair(
        [stage_a.at[:, pl.ds(1 - bit_low, 1)], stage_b.at[:, pl.ds(1 - ctx_here, 1)]],
        [in_a2, in_b2],
        1,
        [partners[1], partners[0]],
    )

    def round_two(part):
        for high in range(2):
            stage_a2[high, part] = stage_a[high, bit_low, part] + in_a2[high, 0, part]
            stage_b2[high, part] = stage_b[high, ctx_here, part] + in_b2[high, 0, part]

    each_chunk(round_two)
    swap_pair(
        [stage_a2.at[pl.ds(1 - bit_high, 1)], stage_b2.at[pl.ds(1 - bit_high, 1)]],
        [in_a3, in_b3],
        2,
        [partners[2], partners[2]],
    )

    def round_three(part):
        o_ref[part] = stage_a2[bit_high, part] + in_a3[0, part]
        o_ref[pl.ds(part.start + rows, chunk)] = stage_b2[bit_high, part] + in_b3[0, part]

    each_chunk(round_three)


def halving_scatter(packed, collective_id):
    count, width = packed.shape
    rows = -(-width // (128 * 128)) * 64
    block = jnp.pad(packed, ((0, 0), (0, 2 * rows * 128 - width))).reshape(
        2, 2, 2, 2 * rows, 128
    )
    own = pl.pallas_call(
        halving_kernel,
        out_shape=jax.ShapeDtypeStruct((2 * rows, 128), jnp.float32),
        in_specs=[pl.BlockSpec(memory_space=pltpu.VMEM)],
        out_specs=pl.BlockSpec(memory_space=pltpu.VMEM),
        scratch_shapes=[
            pltpu.VMEM((2, 2, rows, 128), jnp.float32),
            pltpu.VMEM((2, rows, 128), jnp.float32),
            pltpu.VMEM((2, 2, rows, 128), jnp.float32),
            pltpu.VMEM((2, rows, 128), jnp.float32),
            pltpu.VMEM((2, 2, 1, rows, 128), jnp.float32),
            pltpu.VMEM((2, 1, rows, 128), jnp.float32),
            pltpu.VMEM((1, rows, 128), jnp.float32),
            pltpu.VMEM((2, 1, 2, rows, 128), jnp.float32),
            pltpu.VMEM((2, 1, rows, 128), jnp.float32),
            pltpu.VMEM((1, rows, 128), jnp.float32),
            pltpu.SemaphoreType.DMA((2, 6)),
        ],
        compiler_params=pltpu.CompilerParams(
            collective_id=collective_id, has_side_effects=True, vmem_limit_bytes=60 * 1024 * 1024
        ),
    )(block)
    return own.reshape(-1)[:width]

def gather_kernel(x_ref, o_ref, inbox, send_sems, recv_sems):
    fsdp_here = lax.axis_index("fsdp")
    ctx_here = lax.axis_index("ctx")
    tp_here = lax.axis_index("tp")
    ctx_count = lax.axis_size("ctx")
    count = lax.axis_size("fsdp") * ctx_count
    me = fsdp_here * ctx_count + ctx_here
    peers = []
    for offset in range(1, count):
        other = (me + offset) % count
        peers.append((other // ctx_count, other % ctx_count, tp_here))
    barrier = pltpu.get_barrier_semaphore()
    for peer in peers:
        pl.semaphore_signal(barrier, 1, device_id=peer, device_id_type=pl.DeviceIdType.MESH)
    pl.semaphore_wait(barrier, len(peers))
    copies = []
    for number, peer in enumerate(peers):
        copy = pltpu.make_async_remote_copy(
            src_ref=x_ref,
            dst_ref=inbox.at[me],
            send_sem=send_sems.at[number],
            recv_sem=recv_sems.at[me],
            device_id=peer,
            device_id_type=pl.DeviceIdType.MESH,
        )
        copy.start()
        copies.append(copy)
    o_ref[me] = x_ref[...]
    for copy in copies:
        copy.wait_send()
    for offset in range(1, count):
        source = (me + count - offset) % count
        pltpu.make_async_remote_copy(
            src_ref=x_ref,
            dst_ref=inbox.at[source],
            send_sem=send_sems.at[0],
            recv_sem=recv_sems.at[source],
            device_id=peers[0],
            device_id_type=pl.DeviceIdType.MESH,
        ).wait_recv()
        o_ref[source] = inbox[source]


def gather_shards(flat, collective_id):
    size = flat.shape[0]
    rows = -(-size // 2048) * 16
    block = jnp.pad(flat, (0, rows * 128 - size)).reshape(rows, 128)
    count = lax.axis_size("fsdp") * lax.axis_size("ctx")
    full = pl.pallas_call(
        gather_kernel,
        out_shape=jax.ShapeDtypeStruct((count, rows, 128), flat.dtype),
        in_specs=[pl.BlockSpec(memory_space=pltpu.VMEM)],
        out_specs=pl.BlockSpec(memory_space=pltpu.VMEM),
        scratch_shapes=[
            pltpu.VMEM((count, rows, 128), flat.dtype),
            pltpu.SemaphoreType.DMA((count - 1,)),
            pltpu.SemaphoreType.DMA((count,)),
        ],
        compiler_params=pltpu.CompilerParams(collective_id=collective_id, has_side_effects=True),
    )(block)
    return full.reshape(count, rows * 128)[:, :size]


def swiglu_experts(gate_up):
    return jax.nn.silu(gate_up[:, :, 0]) * gate_up[:, :, 1]


def gather_packed(pieces, axes, use_kernel=False):
    flat = jnp.concatenate([piece.reshape(-1) for piece, _ in pieces])
    if use_kernel:
        full = gather_shards(flat, 4)
    else:
        full = lax.all_gather(flat, axes, axis=0, tiled=False)
    count = full.shape[0]
    results = []
    offset = 0
    for piece, dim in pieces:
        size = piece.size
        part = full[:, offset : offset + size].reshape((count,) + piece.shape)
        offset += size
        part = jnp.moveaxis(part, 0, dim)
        shape = list(piece.shape)
        shape[dim] *= count
        results.append(part.reshape(shape))
    return results


def scatter_packed(pieces, axes, count, use_kernel=False):
    columns = []
    local_shapes = []
    for grad, dim in pieces:
        shape = grad.shape
        split = shape[:dim] + (count, shape[dim] // count) + shape[dim + 1 :]
        local_shapes.append(shape[:dim] + (shape[dim] // count,) + shape[dim + 1 :])
        part = jnp.moveaxis(grad.reshape(split), dim, 0)
        columns.append(part.reshape(count, -1))
    packed = jnp.concatenate(columns, axis=1)
    if use_kernel:
        own = halving_scatter(packed, 3)
    else:
        width = packed.shape[1]
        rows = -(-width // 1024) * 8
        packed = jnp.pad(packed, ((0, 0), (0, rows * 128 - width))).reshape(count * rows, 128)
        own = lax.psum_scatter(packed, axes, scatter_dimension=0, tiled=True).reshape(-1)
    results = []
    offset = 0
    for local_shape in local_shapes:
        size = 1
        for extent in local_shape:
            size *= extent
        results.append(own[offset : offset + size].reshape(local_shape))
        offset += size
    return results


def experts_dense(normed_two, grad_out, weights, expert_in_all, expert_down_all):
    gate_up = jnp.einsum(
        "td,edgf->etgf", normed_two, expert_in_all, preferred_element_type=jnp.float32
    )
    act, act_back = jax.vjp(swiglu_experts, gate_up)
    hidden = act.astype(jnp.bfloat16)
    outs = jnp.einsum("etf,efd->etd", hidden, expert_down_all, preferred_element_type=jnp.float32)
    weights_e = weights.T[:, :, None]
    combined = jnp.sum(weights_e * outs, axis=0)
    gate_dots = jnp.sum(outs * grad_out[None], axis=-1).T
    grad_outs = (weights_e * grad_out[None]).astype(jnp.bfloat16)
    grad_hidden = jnp.einsum(
        "etd,efd->etf", grad_outs, expert_down_all, preferred_element_type=jnp.float32
    )
    grad_gate_up = act_back(grad_hidden)[0].astype(jnp.bfloat16)
    grad_down = jnp.einsum("etf,etd->efd", hidden, grad_outs, preferred_element_type=jnp.float32)
    grad_in = jnp.einsum(
        "td,etgf->edgf", normed_two, grad_gate_up, preferred_element_type=jnp.float32
    )
    grad_rows = jnp.einsum(
        "etgf,edgf->td", grad_gate_up, expert_in_all, preferred_element_type=jnp.float32
    )
    return combined, gate_dots, grad_rows, grad_in, grad_down


def experts_routed(
    normed_two, grad_out, route_rows, gate_probs, expert_in_low, expert_down_low, capacity
):
    block_len, model_width = normed_two.shape
    experts = lax.axis_size("fsdp")
    slot_index, owner_route, filled = slot_tables(route_rows, experts, capacity)
    select = (
        (owner_route[:, None] // 2 == jnp.arange(block_len, dtype=jnp.int32)[None, :])
        & (filled[:, None] == 1)
    ).astype(jnp.bfloat16)
    token_rows = jnp.dot(select, normed_two, preferred_element_type=jnp.float32)
    grad_rows_in = jnp.dot(
        select, grad_out.astype(jnp.bfloat16), preferred_element_type=jnp.float32
    )
    slot_weights = gate_probs.reshape(-1)[owner_route][:, None]
    send_rows = jnp.stack(
        [
            token_rows.astype(jnp.bfloat16).reshape(experts, capacity, model_width),
            (slot_weights * grad_rows_in)
            .astype(jnp.bfloat16)
            .reshape(experts, capacity, model_width),
        ],
        axis=1,
    )
    exchange = lambda rows: lax.all_to_all(rows, "fsdp", split_axis=0, concat_axis=0, tiled=True)
    pair_count = lax.axis_size("tp")
    swap = lambda rows: lax.ppermute(
        rows, "tp", [(index, index + 1 - 2 * (index % 2)) for index in range(pair_count)]
    )
    half = capacity // 2
    side = lax.axis_index("tp") % 2
    mine = exchange(lax.dynamic_slice_in_dim(send_rows, side * half, half, 2))
    received_both = jnp.concatenate([mine, swap(mine)], axis=2)
    received = received_both[:, 0].reshape(experts * capacity, model_width)
    grad_received = received_both[:, 1].reshape(experts * capacity, model_width)
    gate_up = jnp.einsum("rd,dgf->rgf", received, expert_in_low, preferred_element_type=jnp.float32)
    act, act_back = jax.vjp(swiglu, gate_up)
    hidden = act.astype(jnp.bfloat16)
    outs = jnp.dot(hidden, expert_down_low, preferred_element_type=jnp.float32)
    grad_hidden = jnp.einsum(
        "rd,fd->rf", grad_received, expert_down_low, preferred_element_type=jnp.float32
    )
    grad_gate_up = act_back(grad_hidden)[0].astype(jnp.bfloat16)
    grad_in = jnp.einsum("rd,rgf->dgf", received, grad_gate_up, preferred_element_type=jnp.float32)
    grad_down = jnp.einsum("rf,rd->fd", hidden, grad_received, preferred_element_type=jnp.float32)
    grad_expert_rows = jnp.einsum(
        "rgf,dgf->rd", grad_gate_up, expert_in_low, preferred_element_type=jnp.float32
    )
    pair_sums = []
    for rows in (outs, grad_expert_rows):
        rows = rows.reshape(experts, capacity, model_width)
        pair_sums.append(rows[:, :half] + swap(rows[:, half:]))
    held = exchange(jnp.stack(pair_sums, axis=1).astype(jnp.bfloat16))
    slot_expert = slot_index // capacity
    slot_rank = slot_index % capacity
    in_side = ((slot_rank // half) == side)[:, None]
    local_slot = slot_expert * half + slot_rank % half
    pick = (
        (local_slot[:, None] == jnp.arange(experts * half, dtype=jnp.int32)[None, :]) & in_side
    ).astype(jnp.bfloat16)
    picked_rows = []
    for which in range(2):
        rows = jnp.dot(
            pick,
            held[:, which].reshape(experts * half, model_width),
            preferred_element_type=jnp.float32,
        )
        picked_rows.append(rows.reshape(block_len, 2, model_width))
    route_out, grad_routes = picked_rows
    combined = jnp.sum(gate_probs[:, :, None] * route_out, axis=1)
    gate_dots = jnp.sum(grad_out[:, None, :] * route_out, axis=-1)
    grad_rows = jnp.sum(grad_routes, axis=1)
    return combined, gate_dots, grad_rows, grad_in, grad_down


def local(
    layer_input,
    segments,
    routes,
    cotangent,
    gains,
    attention_in,
    attention_out,
    router_weight,
    shared_in,
    shared_down,
    expert_in,
    expert_down,
    model_stats,
    head_stats,
    value_columns,
    hidden_stats,
    router_state,
    expert_model_stats,
    expert_hidden_stats,
):
    block_len = layer_input.shape[1]
    model_width = layer_input.shape[2]
    experts = router_weight.shape[1]
    dense_experts = False
    capacity = min(block_len, 4 * block_len // experts)
    ctx_index = lax.axis_index("ctx")
    tp_index = lax.axis_index("tp")
    fsdp_index = lax.axis_index("fsdp")
    shard_index = lax.axis_index(("fsdp", "ctx"))
    shard_count = lax.axis_size(("fsdp", "ctx"))
    ctx_count = lax.axis_size("ctx")
    base_pos = ctx_index * block_len
    low = lambda v: v.astype(jnp.bfloat16)
    gain_low, attn_in_low, attn_out_low, router_low = gather_packed(
        [(low(gains), 1), (low(attention_in), 0), (low(attention_out), 1), (low(router_weight), 0)],
        ("fsdp", "ctx"),
        shard_count <= 8,
    )
    later = [
        (low(shared_in), 0),
        (low(shared_down), 1),
    ]
    if dense_experts:
        later += [(low(expert_in), 0), (low(expert_down), 0)]
    later_full = gather_packed(later, ("fsdp", "ctx"))
    shared_in_low, shared_down_low = later_full[:2]
    if dense_experts:
        fe_local = expert_down.shape[1]
        expert_in_all = later_full[2].reshape(experts, model_width, 2, fe_local)
        expert_down_all = (
            later_full[3]
            .reshape(experts, ctx_count, fe_local, model_width // ctx_count)
            .transpose(0, 2, 1, 3)
            .reshape(experts, fe_local, model_width)
        )
    else:
        expert_in_low = lax.all_gather(low(expert_in), "ctx", axis=1, tiled=True)[0]
        expert_down_low = lax.all_gather(low(expert_down), "ctx", axis=2, tiled=True)[0]
    residual = layer_input[0].astype(jnp.float32)
    gain_one = gain_low[0].astype(jnp.float32)
    gain_two = gain_low[1].astype(jnp.float32)
    normed_one, norm_one_back = jax.vjp(rms_norm, residual, gain_one)
    normed_one = normed_one.astype(jnp.bfloat16)
    projected = jnp.einsum(
        "td,dgf->tgf", normed_one, attn_in_low, preferred_element_type=jnp.float32
    )
    local_cols = projected.shape[2]
    local_heads = local_cols // HD
    half_dim = HD // 2
    frequency = 10000.0 ** (-jnp.arange(half_dim, dtype=jnp.float32) / half_dim)
    angles = (base_pos + jnp.arange(block_len, dtype=jnp.int32)).astype(jnp.float32)[
        :, None
    ] * frequency[None, :]
    cosine = jnp.cos(angles)
    sine_tab = jnp.sin(angles)
    queries = rotate(projected[:, 0].reshape(block_len, local_heads, HD), cosine, sine_tab).astype(
        jnp.bfloat16
    )
    keys_own = rotate(projected[:, 1].reshape(block_len, local_heads, HD), cosine, sine_tab).astype(
        jnp.bfloat16
    )
    values_own = projected[:, 2].reshape(block_len, local_heads, HD).astype(jnp.bfloat16)
    seg_own = segments[0].astype(jnp.bfloat16)
    keys_prev, values_prev, seg_prev = from_behind((keys_own, values_own, seg_own), "ctx", 1)
    keys_ext = jnp.concatenate([keys_prev, keys_own], axis=0)
    values_ext = jnp.concatenate([values_prev, values_own], axis=0)
    seg_ext = jnp.concatenate([seg_prev, seg_own], axis=0)
    block_rows = min(512, block_len)
    block_total = block_len // block_rows
    starts = jnp.arange(block_total, dtype=jnp.int32) * block_rows

    def forward_block(start_row):
        query_rows, key_rows, value_rows, masked, allowed = block_view(
            queries, keys_ext, values_ext, seg_own, seg_ext, start_row, base_pos
        )
        row_max = jnp.max(masked, axis=-1, keepdims=True)
        exp_terms = jnp.where(allowed[None], jnp.exp(masked - row_max), 0.0)
        row_total = jnp.sum(exp_terms, axis=-1, keepdims=True)
        attn_probs = (exp_terms / row_total).astype(jnp.bfloat16)
        attended = jnp.einsum(
            "hqk,khd->qhd", attn_probs, value_rows, preferred_element_type=jnp.float32
        )
        return (attended, row_max + jnp.log(row_total))

    attended, log_totals = lax.map(forward_block, starts)
    mixed_heads = attended.reshape(block_len, local_cols).astype(jnp.bfloat16)
    attn_total = lax.psum(
        jnp.dot(mixed_heads, attn_out_low, preferred_element_type=jnp.float32), "tp"
    )
    after_attn = residual + attn_total
    normed_two, norm_two_back = jax.vjp(rms_norm, after_attn, gain_two)
    normed_two = normed_two.astype(jnp.bfloat16)
    logits = jnp.dot(normed_two, router_low, preferred_element_type=jnp.float32)
    route_rows = routes[0]
    onehot = (route_rows[:, :, None] == jnp.arange(experts, dtype=jnp.int32)[None, None, :]).astype(
        jnp.float32
    )
    picked = jnp.sum(onehot * logits[:, None, :], axis=-1)
    gate_probs = jax.nn.softmax(picked, axis=-1)
    upstream = cotangent[0]
    grad_out = upstream.astype(jnp.float32)
    if dense_experts:
        weights = jnp.sum(gate_probs[:, :, None] * onehot, axis=1)
        combined, dots_e, grad_rows, grad_expert_in, grad_expert_down = experts_dense(
            normed_two, grad_out, weights, expert_in_all, expert_down_all
        )
        gate_dots = jnp.sum(onehot * dots_e[:, None, :], axis=-1)
    else:
        combined, gate_dots, grad_rows, grad_expert_in, grad_expert_down = experts_routed(
            normed_two,
            grad_out,
            route_rows,
            gate_probs,
            expert_in_low,
            expert_down_low,
            capacity,
        )
    shared_gate_up = jnp.einsum(
        "td,dgf->tgf", normed_two, shared_in_low, preferred_element_type=jnp.float32
    )
    shared_act, shared_act_back = jax.vjp(swiglu, shared_gate_up)
    shared_hidden = shared_act.astype(jnp.bfloat16)
    shared_out = jnp.dot(shared_hidden, shared_down_low, preferred_element_type=jnp.float32)
    grad_shared_hidden = jnp.einsum(
        "td,fd->tf", upstream, shared_down_low, preferred_element_type=jnp.float32
    )
    grad_shared_gate_up = shared_act_back(grad_shared_hidden)[0].astype(jnp.bfloat16)
    partial_two = (
        jnp.einsum(
            "tgf,dgf->td", grad_shared_gate_up, shared_in_low, preferred_element_type=jnp.float32
        )
        + grad_rows
    )
    branch_total, grad_normed_part, gate_total = lax.psum(
        (shared_out + combined, partial_two, gate_dots), "tp"
    )
    layer_out = after_attn + branch_total
    grad_picked = gate_probs * (
        gate_total - jnp.sum(gate_probs * gate_total, axis=-1, keepdims=True)
    )
    grad_logits = jnp.sum(grad_picked[:, :, None] * onehot, axis=1).astype(jnp.bfloat16)
    grad_shared_in = jnp.einsum(
        "td,tgf->dgf", normed_two, grad_shared_gate_up, preferred_element_type=jnp.float32
    )
    grad_shared_down = jnp.einsum(
        "tf,td->fd", shared_hidden, upstream, preferred_element_type=jnp.float32
    )
    grad_router = jnp.einsum(
        "td,te->de", normed_two, grad_logits, preferred_element_type=jnp.float32
    )
    grad_normed_two = grad_normed_part + jnp.einsum(
        "te,de->td", grad_logits, router_low, preferred_element_type=jnp.float32
    )
    grad_after, grad_gain_two = norm_two_back(grad_normed_two)
    grad_after = grad_after + grad_out
    grad_attn_low = grad_after.astype(jnp.bfloat16)
    grad_attn_out = jnp.einsum(
        "tc,td->cd", mixed_heads, grad_attn_low, preferred_element_type=jnp.float32
    )
    first_grads = [
        (grad_attn_out, 1),
        (grad_router, 0),
        (grad_shared_in, 0),
        (grad_shared_down, 1),
        (grad_gain_two, 0),
    ]
    if dense_experts:
        fe_local = expert_down.shape[1]
        first_grads += [
            (grad_expert_in.reshape(shard_count * expert_in.shape[1], 2, fe_local), 0),
            (
                grad_expert_down.reshape(experts, fe_local, ctx_count, model_width // ctx_count)
                .transpose(0, 2, 1, 3)
                .reshape(shard_count * fe_local, model_width // ctx_count),
                0,
            ),
        ]
    if not dense_experts:
        own_expert_in = lax.psum_scatter(grad_expert_in[None], "ctx", scatter_dimension=1, tiled=True)
        own_expert_down = lax.psum_scatter(
            grad_expert_down[None], "ctx", scatter_dimension=2, tiled=True
        )
    grad_heads = (
        jnp.einsum("td,cd->tc", grad_attn_low, attn_out_low, preferred_element_type=jnp.float32)
        .astype(jnp.bfloat16)
        .reshape(block_len, local_heads, HD)
    )

    def backward_block(block_number, running):
        grad_keys, grad_values, grad_queries = running
        start_row = block_number * block_rows
        query_rows, key_rows, value_rows, masked, allowed = block_view(
            queries, keys_ext, values_ext, seg_own, seg_ext, start_row, base_pos
        )
        log_total = lax.dynamic_index_in_dim(log_totals, block_number, 0, keepdims=False)
        attn_probs = jnp.where(allowed[None], jnp.exp(masked - log_total), 0.0)
        grad_block = lax.dynamic_slice_in_dim(grad_heads, start_row, block_rows, 0)
        grad_probs = jnp.einsum(
            "qhd,khd->hqk", grad_block, value_rows, preferred_element_type=jnp.float32
        )
        inner_sum = jnp.sum(attn_probs * grad_probs, axis=-1, keepdims=True)
        grad_scores = (attn_probs * (grad_probs - inner_sum)).astype(jnp.bfloat16)
        grad_query_rows = (
            jnp.einsum("hqk,khd->qhd", grad_scores, key_rows, preferred_element_type=jnp.float32)
            * 0.125
        )
        grad_key_rows = (
            jnp.einsum("hqk,qhd->khd", grad_scores, query_rows, preferred_element_type=jnp.float32)
            * 0.125
        )
        grad_value_rows = jnp.einsum(
            "hqk,qhd->khd",
            attn_probs.astype(jnp.bfloat16),
            grad_block,
            preferred_element_type=jnp.float32,
        )
        key_offset = start_row + block_len - WINDOW
        grad_keys = lax.dynamic_update_slice_in_dim(
            grad_keys,
            lax.dynamic_slice_in_dim(grad_keys, key_offset, block_rows + WINDOW, 0) + grad_key_rows,
            key_offset,
            0,
        )
        grad_values = lax.dynamic_update_slice_in_dim(
            grad_values,
            lax.dynamic_slice_in_dim(grad_values, key_offset, block_rows + WINDOW, 0)
            + grad_value_rows,
            key_offset,
            0,
        )
        grad_queries = lax.dynamic_update_slice_in_dim(grad_queries, grad_query_rows, start_row, 0)
        return (grad_keys, grad_values, grad_queries)

    zero_ext = jnp.zeros((2 * block_len, local_heads, HD), jnp.float32)
    zero_own = jnp.zeros((block_len, local_heads, HD), jnp.float32)
    grad_keys, grad_values, grad_queries = lax.fori_loop(
        0, block_total, backward_block, (zero_ext, zero_ext, zero_own)
    )
    rim_keys, rim_values = (
        from_behind(grad_keys[:block_len].astype(jnp.bfloat16), "ctx", -1).astype(jnp.float32),
        from_behind(grad_values[:block_len].astype(jnp.bfloat16), "ctx", -1).astype(jnp.float32),
    )
    grad_keys_own = grad_keys[block_len:] + rim_keys
    grad_values_own = grad_values[block_len:] + rim_values
    grad_query_raw = rotate(grad_queries, cosine, -sine_tab)
    grad_key_raw = rotate(grad_keys_own, cosine, -sine_tab)
    grad_projected = (
        jnp.stack([grad_query_raw, grad_key_raw, grad_values_own], axis=1)
        .reshape(block_len, 3, local_cols)
        .astype(jnp.bfloat16)
    )
    grad_attn_in = jnp.einsum(
        "td,tgf->dgf", normed_one, grad_projected, preferred_element_type=jnp.float32
    )
    partial_one = jnp.einsum(
        "tgf,dgf->td", grad_projected, attn_in_low, preferred_element_type=jnp.float32
    )
    tp_one = lax.psum(partial_one, "tp")
    halving = lax.axis_size("fsdp") == 4 and ctx_count == 2
    all_own = scatter_packed(
        first_grads + [(grad_attn_in, 0)],
        ("fsdp", "ctx"),
        shard_count,
        halving,
    )
    own_attn_out, own_router, own_shared_in, own_shared_down, own_gain_two = all_own[:5]
    own_attn_in = all_own[-1]
    grad_residual, grad_gain_one = norm_one_back(tp_one + 0.0 * own_attn_in[0, 0, 0])
    input_grad = grad_after + grad_residual
    if dense_experts:
        own_expert_in = all_own[5][None]
        own_expert_down = all_own[6][None]
    lead_tp = (tp_index == 0).astype(jnp.float32)
    first_shard = (shard_index == 0).astype(jnp.float32)
    first_ctx = (ctx_index == 0).astype(jnp.float32)
    d_local = gains.shape[1]
    ff_local = shared_down.shape[0]
    fe_local = expert_down.shape[1]
    d_quarter = expert_in.shape[1]
    square_attn_in = own_attn_in * own_attn_in + TINY_SQUARE
    square_attn_out = own_attn_out * own_attn_out + TINY_SQUARE
    square_shared_in = own_shared_in * own_shared_in + TINY_SQUARE
    square_shared_down = own_shared_down * own_shared_down + TINY_SQUARE
    square_expert_in = own_expert_in[0] * own_expert_in[0] + TINY_SQUARE
    square_expert_down = own_expert_down[0] * own_expert_down[0] + TINY_SQUARE
    model_part = lax.dynamic_update_slice(
        jnp.zeros((4, D), jnp.float32),
        jnp.stack(
            [
                jnp.sum(square_attn_in, axis=(1, 2)),
                jnp.sum(square_shared_in, axis=(1, 2)),
                jnp.sum(square_attn_out, axis=0),
                jnp.sum(square_shared_down, axis=0),
            ]
        ),
        (0, shard_index * d_local),
    )
    head_part = lax.dynamic_update_slice(
        jnp.zeros((4, HH), jnp.float32),
        jnp.concatenate(
            [jnp.sum(square_attn_in, axis=0), jnp.sum(square_attn_out, axis=1)[None]], axis=0
        ),
        (0, tp_index * local_cols),
    )
    hidden_part = lax.dynamic_update_slice(
        jnp.zeros((3, FF), jnp.float32),
        jnp.concatenate(
            [jnp.sum(square_shared_in, axis=0), jnp.sum(square_shared_down, axis=1)[None]], axis=0
        ),
        (0, tp_index * ff_local),
    )
    expert_model_part = lax.dynamic_update_slice(
        jnp.zeros((experts, 2, D), jnp.float32),
        jnp.stack([jnp.sum(square_expert_in, axis=(1, 2)), jnp.sum(square_expert_down, axis=0)])[
            None
        ],
        (fsdp_index, 0, ctx_index * d_quarter),
    )
    expert_hidden_part = lax.dynamic_update_slice(
        jnp.zeros((experts, 3, FE), jnp.float32),
        jnp.concatenate(
            [jnp.sum(square_expert_in, axis=0), jnp.sum(square_expert_down, axis=1)[None]], axis=0
        )[None],
        (fsdp_index, 0, tp_index * fe_local),
    )
    scalar_part = jnp.stack(
        [
            lead_tp * jnp.sum(gains * gains),
            jnp.sum(attention_in * attention_in),
            jnp.sum(attention_out * attention_out),
            lead_tp * jnp.sum(router_weight * router_weight),
            jnp.sum(shared_in * shared_in),
            jnp.sum(shared_down * shared_down),
            jnp.sum(expert_in * expert_in),
            jnp.sum(expert_down * expert_down),
            lead_tp * jnp.sum(model_stats[2]),
            first_shard * jnp.sum(head_stats[2]),
            lead_tp * jnp.sum(model_stats[3]),
            first_shard * jnp.sum(hidden_stats[2]),
        ]
    )
    expert_old_part = lax.dynamic_update_slice(
        jnp.zeros((2, experts), jnp.float32),
        jnp.stack(
            [
                lead_tp * jnp.sum(expert_model_stats[0, 0]),
                first_ctx * jnp.sum(expert_hidden_stats[0, 2]),
            ]
        )[:, None],
        (0, fsdp_index),
    )
    global_sums = butterfly_sum(
        [
            model_part,
            head_part,
            hidden_part,
            expert_model_part,
            expert_hidden_part,
            scalar_part,
            expert_old_part,
            lead_tp * grad_gain_one,
        ],
        1,
    )
    (
        model_sum,
        head_sum,
        hidden_sum,
        expert_model_sum,
        expert_hidden_sum,
        scalar_sum,
        expert_old_sum,
        gain_one_sum,
    ) = global_sums
    own_gain_one = lax.dynamic_slice_in_dim(gain_one_sum, shard_index * d_local, d_local)
    own_gains = jnp.stack([own_gain_one, own_gain_two])
    shard_start = shard_index * d_local
    gain_state = DECAY_RATE * model_stats[0:2] + (1.0 - DECAY_RATE) * (
        own_gains * own_gains + TINY_SQUARE
    )
    update_gains = own_gains * lax.rsqrt(gain_state)
    router_new = DECAY_RATE * router_state + (1.0 - DECAY_RATE) * (
        own_router * own_router + TINY_SQUARE
    )
    update_router = own_router * lax.rsqrt(router_new)
    attn_cols_old = jnp.concatenate([head_stats[0:2], value_columns[None]], axis=0).reshape(-1)
    update_attn_in, rows_attn_in, cols_attn_in = factored_update(
        own_attn_in.reshape(d_local, 3 * local_cols),
        model_stats[2],
        attn_cols_old,
        lax.dynamic_slice_in_dim(model_sum[0], shard_start, d_local),
        lax.dynamic_slice_in_dim(head_sum[0:3], tp_index * local_cols, local_cols, 1).reshape(-1),
        D,
        3 * HH,
        scalar_sum[8],
        jnp.sum(model_sum[0]),
    )
    update_attn_out, rows_attn_out, cols_attn_out = factored_update(
        own_attn_out,
        head_stats[2],
        model_stats[4],
        lax.dynamic_slice_in_dim(head_sum[3], tp_index * local_cols, local_cols),
        lax.dynamic_slice_in_dim(model_sum[2], shard_start, d_local),
        HH,
        D,
        scalar_sum[9],
        jnp.sum(head_sum[3]),
    )
    update_shared_in, rows_shared_in, cols_shared_in = factored_update(
        own_shared_in.reshape(d_local, 2 * ff_local),
        model_stats[3],
        hidden_stats[0:2].reshape(-1),
        lax.dynamic_slice_in_dim(model_sum[1], shard_start, d_local),
        lax.dynamic_slice_in_dim(hidden_sum[0:2], tp_index * ff_local, ff_local, 1).reshape(-1),
        D,
        2 * FF,
        scalar_sum[10],
        jnp.sum(model_sum[1]),
    )
    update_shared_down, rows_shared_down, cols_shared_down = factored_update(
        own_shared_down,
        hidden_stats[2],
        model_stats[5],
        lax.dynamic_slice_in_dim(hidden_sum[2], tp_index * ff_local, ff_local),
        lax.dynamic_slice_in_dim(model_sum[3], shard_start, d_local),
        FF,
        D,
        scalar_sum[11],
        jnp.sum(hidden_sum[2]),
    )
    own_expert_model = lax.dynamic_index_in_dim(expert_model_sum, fsdp_index, 0, keepdims=False)
    own_expert_hidden = lax.dynamic_index_in_dim(expert_hidden_sum, fsdp_index, 0, keepdims=False)
    old_expert_totals = lax.dynamic_index_in_dim(expert_old_sum, fsdp_index, 1, keepdims=False)
    update_expert_in, rows_expert_in, cols_expert_in = factored_update(
        own_expert_in[0].reshape(d_quarter, 2 * fe_local),
        expert_model_stats[0, 0],
        expert_hidden_stats[0, 0:2].reshape(-1),
        lax.dynamic_slice_in_dim(own_expert_model[0], ctx_index * d_quarter, d_quarter),
        lax.dynamic_slice_in_dim(own_expert_hidden[0:2], tp_index * fe_local, fe_local, 1).reshape(
            -1
        ),
        D,
        2 * FE,
        old_expert_totals[0],
        jnp.sum(own_expert_model[0]),
    )
    update_expert_down, rows_expert_down, cols_expert_down = factored_update(
        own_expert_down[0],
        expert_hidden_stats[0, 2],
        expert_model_stats[0, 1],
        lax.dynamic_slice_in_dim(own_expert_hidden[2], tp_index * fe_local, fe_local),
        lax.dynamic_slice_in_dim(own_expert_model[1], ctx_index * d_quarter, d_quarter),
        FE,
        D,
        old_expert_totals[1],
        jnp.sum(own_expert_hidden[2]),
    )
    clip_part = jnp.stack(
        [
            lead_tp * jnp.sum(update_gains * update_gains),
            jnp.sum(update_attn_in * update_attn_in),
            jnp.sum(update_attn_out * update_attn_out),
            lead_tp * jnp.sum(update_router * update_router),
            jnp.sum(update_shared_in * update_shared_in),
            jnp.sum(update_shared_down * update_shared_down),
            jnp.sum(update_expert_in * update_expert_in),
            jnp.sum(update_expert_down * update_expert_down),
        ]
    )
    clip_total = butterfly_sum([clip_part], 2)[0]
    elements = jnp.array(
        [
            2 * D,
            D * 3 * HH,
            HH * D,
            D * experts,
            D * 2 * FF,
            FF * D,
            experts * D * 2 * FE,
            experts * FE * D,
        ],
        jnp.float32,
    )
    update_roots = jnp.sqrt(clip_total / elements)
    new_gains = apply_update(gains, update_gains, update_roots[0], scalar_sum[0], elements[0])
    new_attn_in = apply_update(
        attention_in,
        update_attn_in.reshape(attention_in.shape),
        update_roots[1],
        scalar_sum[1],
        elements[1],
    )
    new_attn_out = apply_update(
        attention_out, update_attn_out, update_roots[2], scalar_sum[2], elements[2]
    )
    new_router = apply_update(
        router_weight, update_router, update_roots[3], scalar_sum[3], elements[3]
    )
    new_shared_in = apply_update(
        shared_in,
        update_shared_in.reshape(shared_in.shape),
        update_roots[4],
        scalar_sum[4],
        elements[4],
    )
    new_shared_down = apply_update(
        shared_down, update_shared_down, update_roots[5], scalar_sum[5], elements[5]
    )
    new_expert_in = apply_update(
        expert_in,
        update_expert_in.reshape(expert_in.shape),
        update_roots[6],
        scalar_sum[6],
        elements[6],
    )
    new_expert_down = apply_update(
        expert_down,
        update_expert_down.reshape(expert_down.shape),
        update_roots[7],
        scalar_sum[7],
        elements[7],
    )
    new_model_stats = jnp.concatenate(
        [gain_state, jnp.stack([rows_attn_in, rows_shared_in, cols_attn_out, cols_shared_down])],
        axis=0,
    )
    attn_cols_new = cols_attn_in.reshape(3, local_cols)
    new_head_stats = jnp.concatenate([attn_cols_new[0:2], rows_attn_out[None]], axis=0)
    new_value_columns = attn_cols_new[2]
    new_hidden_stats = jnp.concatenate(
        [cols_shared_in.reshape(2, ff_local), rows_shared_down[None]], axis=0
    )
    new_expert_model_stats = jnp.stack([rows_expert_in, cols_expert_down])[None]
    new_expert_hidden_stats = jnp.concatenate(
        [cols_expert_in.reshape(2, fe_local), rows_expert_down[None]], axis=0
    )[None]
    return (
        layer_out.astype(jnp.bfloat16)[None],
        input_grad[None],
        own_gains,
        own_attn_in,
        own_attn_out,
        own_router,
        own_shared_in,
        own_shared_down,
        own_expert_in,
        own_expert_down,
        new_gains,
        new_attn_in,
        new_attn_out,
        new_router,
        new_shared_in,
        new_shared_down,
        new_expert_in,
        new_expert_down,
        new_model_stats,
        new_head_stats,
        new_value_columns,
        new_hidden_stats,
        router_new,
        new_expert_model_stats,
        new_expert_hidden_stats,
        update_roots,
    )


def solution(mesh):
    in_specs = (
        P("fsdp", "ctx", None),
        P("fsdp", "ctx"),
        P("fsdp", "ctx", None),
        P("fsdp", "ctx", None),
        P(None, ("fsdp", "ctx")),
        P(("fsdp", "ctx"), None, "tp"),
        P("tp", ("fsdp", "ctx")),
        P(("fsdp", "ctx"), None),
        P(("fsdp", "ctx"), None, "tp"),
        P("tp", ("fsdp", "ctx")),
        P("fsdp", "ctx", None, "tp"),
        P("fsdp", "tp", "ctx"),
        P(None, ("fsdp", "ctx")),
        P(None, "tp"),
        P("tp"),
        P(None, "tp"),
        P(("fsdp", "ctx"), None),
        P("fsdp", None, "ctx"),
        P("fsdp", None, "tp"),
    )
    out_specs = (
        P("fsdp", "ctx", None),
        P("fsdp", "ctx", None),
        P(None, ("fsdp", "ctx")),
        P(("fsdp", "ctx"), None, "tp"),
        P("tp", ("fsdp", "ctx")),
        P(("fsdp", "ctx"), None),
        P(("fsdp", "ctx"), None, "tp"),
        P("tp", ("fsdp", "ctx")),
        P("fsdp", "ctx", None, "tp"),
        P("fsdp", "tp", "ctx"),
        P(None, ("fsdp", "ctx")),
        P(("fsdp", "ctx"), None, "tp"),
        P("tp", ("fsdp", "ctx")),
        P(("fsdp", "ctx"), None),
        P(("fsdp", "ctx"), None, "tp"),
        P("tp", ("fsdp", "ctx")),
        P("fsdp", "ctx", None, "tp"),
        P("fsdp", "tp", "ctx"),
        P(None, ("fsdp", "ctx")),
        P(None, "tp"),
        P("tp"),
        P(None, "tp"),
        P(("fsdp", "ctx"), None),
        P("fsdp", None, "ctx"),
        P("fsdp", None, "tp"),
        P(),
    )
    return jax.shard_map(local, mesh=mesh, in_specs=in_specs, out_specs=out_specs, check_vma=False)
```

```python
import jax
import jax.numpy as jnp
from jax import lax
from jax.sharding import PartitionSpec as P
from jax.experimental import pallas as pl
from jax.experimental.pallas import tpu as pltpu

D = 768
HD = 64
FF = 2048
FE = 2048
WINDOW = 1024
HH = 768


EPSILON = 1e-06
TINY_SQUARE = 1e-30
SCALE_FLOOR = 0.001
DECAY_RATE = 0.5
CLIP_LIMIT = 0.5
STEP_RATE = 0.5


def from_behind(value, axis, steps):
    count = lax.axis_size(axis)
    leading, last = (max(0, -steps), min(count, count - steps))
    return lax.ppermute(value, axis, [(source, source + steps) for source in range(leading, last)])


def rms_norm(values, gain_vec):
    inv_rms = lax.rsqrt(jnp.mean(values * values, axis=-1, keepdims=True) + EPSILON)
    return values * inv_rms * gain_vec


def swiglu(gate_up):
    return jax.nn.silu(gate_up[:, 0]) * gate_up[:, 1]


def rotate(values, cosine, sine_tab):
    half_dim = values.shape[-1] // 2
    first_half = values[..., :half_dim]
    second_half = values[..., half_dim:]
    cos_b = cosine[:, None, :]
    sin_b = sine_tab[:, None, :]
    return jnp.concatenate(
        [first_half * cos_b - second_half * sin_b, second_half * cos_b + first_half * sin_b],
        axis=-1,
    )


def slot_tables(block_routes, experts, capacity):
    flat_routes = block_routes.reshape(-1)
    route_count = flat_routes.shape[0]
    onehot = (flat_routes[:, None] == jnp.arange(experts, dtype=jnp.int32)[None, :]).astype(
        jnp.int32
    )
    rank_in = jnp.sum(
        (jnp.cumsum(onehot, axis=0, dtype=jnp.int32) - 1) * onehot, axis=1, dtype=jnp.int32
    )
    slot_index = flat_routes * capacity + rank_in
    owner_route = (
        jnp.zeros((experts * capacity,), jnp.int32)
        .at[slot_index]
        .set(jnp.arange(route_count, dtype=jnp.int32))
    )
    filled = jnp.zeros((experts * capacity,), jnp.int32).at[slot_index].set(1)
    return (slot_index, owner_route, filled)


def block_view(queries, keys_ext, values_ext, seg_own, seg_ext, start_row, base_pos):
    block_len = queries.shape[0]
    block_rows = min(512, block_len)
    query_rows = lax.dynamic_slice_in_dim(queries, start_row, block_rows, 0)
    key_rows = lax.dynamic_slice_in_dim(
        keys_ext, start_row + block_len - WINDOW, block_rows + WINDOW, 0
    )
    value_rows = lax.dynamic_slice_in_dim(
        values_ext, start_row + block_len - WINDOW, block_rows + WINDOW, 0
    )
    scores = (
        jnp.einsum("qhd,khd->hqk", query_rows, key_rows, preferred_element_type=jnp.float32) * 0.125
    )
    query_pos = start_row + jnp.arange(block_rows, dtype=jnp.int32)
    key_pos = start_row - WINDOW + jnp.arange(block_rows + WINDOW, dtype=jnp.int32)
    distance = query_pos[:, None] - key_pos[None, :]
    seg_query = lax.dynamic_slice_in_dim(seg_own, start_row, block_rows, 0)
    seg_key = lax.dynamic_slice_in_dim(
        seg_ext, start_row + block_len - WINDOW, block_rows + WINDOW, 0
    )
    allowed = (
        (distance >= 0)
        & (distance < WINDOW)
        & (seg_query[:, None] == seg_key[None, :])
        & (key_pos[None, :] + base_pos >= 0)
    )
    return (query_rows, key_rows, value_rows, jnp.where(allowed[None], scores, -1e30), allowed)


def factored_update(
    grad_mat, rows_old, cols_old, row_sums, col_sums, row_total, col_total, old_total, square_total
):
    rows_new = DECAY_RATE * rows_old + (1.0 - DECAY_RATE) * row_sums / col_total
    cols_new = DECAY_RATE * cols_old + (1.0 - DECAY_RATE) * col_sums / row_total
    mean_rows = (DECAY_RATE * old_total + (1.0 - DECAY_RATE) * square_total / col_total) / row_total
    second_moment = rows_new[:, None] * cols_new[None, :] / mean_rows
    return (grad_mat * lax.rsqrt(second_moment), rows_new, cols_new)


def apply_update(weight, update, update_root, square_sum, elements):
    param_scale = jnp.maximum(SCALE_FLOOR, jnp.sqrt(square_sum / elements))
    return weight - STEP_RATE * param_scale * update / jnp.maximum(1.0, update_root / CLIP_LIMIT)


def butterfly_partners():
    partners = []
    here = [lax.axis_index(name) for name in ("fsdp", "ctx", "tp")]
    for axis_number, name in enumerate(("fsdp", "ctx", "tp")):
        size = lax.axis_size(name)
        step = 1
        while step < size:
            bit = (here[axis_number] // step) % 2
            other = list(here)
            other[axis_number] = here[axis_number] + step * (1 - 2 * bit)
            partners.append(tuple(other))
            step *= 2
    return partners


def butterfly_kernel(x_ref, o_ref, stage, inbox, send_sems, recv_sems):
    partners = butterfly_partners()
    barrier = pltpu.get_barrier_semaphore()
    for partner in partners:
        pl.semaphore_signal(
            barrier, 1, device_id=partner, device_id_type=pl.DeviceIdType.MESH
        )
    pl.semaphore_wait(barrier, len(partners))
    acc = x_ref[...]
    for round_number, partner in enumerate(partners):
        stage[round_number] = acc
        copy = pltpu.make_async_remote_copy(
            src_ref=stage.at[round_number],
            dst_ref=inbox.at[round_number],
            send_sem=send_sems.at[round_number],
            recv_sem=recv_sems.at[round_number],
            device_id=partner,
            device_id_type=pl.DeviceIdType.MESH,
        )
        copy.start()
        copy.wait()
        acc = stage[round_number] + inbox[round_number]
    o_ref[...] = acc


def butterfly_sum(values, collective_id):
    flat = jnp.concatenate([v.reshape(-1).astype(jnp.float32) for v in values])
    size = flat.shape[0]
    rows = -(-size // 1024) * 8
    block = jnp.pad(flat, (0, rows * 128 - size)).reshape(rows, 128)
    rounds = sum(
        max(1, lax.axis_size(name)).bit_length() - 1 for name in ("fsdp", "ctx", "tp")
    )
    total = pl.pallas_call(
        butterfly_kernel,
        out_shape=jax.ShapeDtypeStruct((rows, 128), jnp.float32),
        in_specs=[pl.BlockSpec(memory_space=pltpu.VMEM)],
        out_specs=pl.BlockSpec(memory_space=pltpu.VMEM),
        scratch_shapes=[
            pltpu.VMEM((rounds, rows, 128), jnp.float32),
            pltpu.VMEM((rounds, rows, 128), jnp.float32),
            pltpu.SemaphoreType.DMA((rounds,)),
            pltpu.SemaphoreType.DMA((rounds,)),
        ],
        compiler_params=pltpu.CompilerParams(collective_id=collective_id, has_side_effects=True),
    )(block).reshape(-1)
    results = []
    offset = 0
    for v in values:
        results.append(total[offset : offset + v.size].reshape(v.shape))
        offset += v.size
    return results


def halving_kernel(
    x_ref, o_ref, stage_a, stage_a2, stage_b, stage_b2, in_a1, in_a2, in_a3, in_b1, in_b2, in_b3, sems
):
    rows = o_ref.shape[0] // 2
    chunk = 64
    fsdp_here = lax.axis_index("fsdp")
    ctx_here = lax.axis_index("ctx")
    tp_here = lax.axis_index("tp")
    bit_low = fsdp_here % 2
    bit_high = (fsdp_here // 2) % 2
    partners = [
        (fsdp_here, 1 - ctx_here, tp_here),
        (fsdp_here + 1 - 2 * bit_low, ctx_here, tp_here),
        (fsdp_here + 2 - 4 * bit_high, ctx_here, tp_here),
    ]
    barrier = pltpu.get_barrier_semaphore()
    for partner in partners:
        pl.semaphore_signal(barrier, 1, device_id=partner, device_id_type=pl.DeviceIdType.MESH)
    pl.semaphore_wait(barrier, len(partners))
    first, second = pl.ds(0, rows), pl.ds(rows, rows)

    def swap_pair(sources, targets, number, partner_pair):
        copies = []
        for index in range(2):
            copy = pltpu.make_async_remote_copy(
                src_ref=sources[index],
                dst_ref=targets[index],
                send_sem=sems.at[0, 2 * number + index],
                recv_sem=sems.at[1, 2 * number + index],
                device_id=partner_pair[index],
                device_id_type=pl.DeviceIdType.MESH,
            )
            copy.start()
            copies.append(copy)
        for copy in copies:
            copy.wait()

    def each_chunk(body):
        @pl.loop(0, rows // chunk)
        def _(step):
            body(pl.ds(pl.multiple_of(step * chunk, chunk), chunk))

    swap_pair(
        [
            x_ref.at[:, :, pl.ds(1 - ctx_here, 1), first],
            x_ref.at[:, pl.ds(1 - bit_low, 1), :, second],
        ],
        [in_a1, in_b1],
        0,
        [partners[0], partners[1]],
    )

    def round_one(part):
        shifted = pl.ds(part.start + rows, chunk)
        for high in range(2):
            for other in range(2):
                stage_a[high, other, part] = (
                    x_ref[high, other, ctx_here, part] + in_a1[high, other, 0, part]
                )
                stage_b[high, other, part] = (
                    x_ref[high, bit_low, other, shifted] + in_b1[high, 0, other, part]
                )

    each_chunk(round_one)
    swap_pair(
        [stage_a.at[:, pl.ds(1 - bit_low, 1)], stage_b.at[:, pl.ds(1 - ctx_here, 1)]],
        [in_a2, in_b2],
        1,
        [partners[1], partners[0]],
    )

    def round_two(part):
        for high in range(2):
            stage_a2[high, part] = stage_a[high, bit_low, part] + in_a2[high, 0, part]
            stage_b2[high, part] = stage_b[high, ctx_here, part] + in_b2[high, 0, part]

    each_chunk(round_two)
    swap_pair(
        [stage_a2.at[pl.ds(1 - bit_high, 1)], stage_b2.at[pl.ds(1 - bit_high, 1)]],
        [in_a3, in_b3],
        2,
        [partners[2], partners[2]],
    )

    def round_three(part):
        o_ref[part] = stage_a2[bit_high, part] + in_a3[0, part]
        o_ref[pl.ds(part.start + rows, chunk)] = stage_b2[bit_high, part] + in_b3[0, part]

    each_chunk(round_three)


def halving_scatter(packed, collective_id):
    count, width = packed.shape
    rows = -(-width // (128 * 128)) * 64
    block = jnp.pad(packed, ((0, 0), (0, 2 * rows * 128 - width))).reshape(
        2, 2, 2, 2 * rows, 128
    )
    own = pl.pallas_call(
        halving_kernel,
        out_shape=jax.ShapeDtypeStruct((2 * rows, 128), jnp.float32),
        in_specs=[pl.BlockSpec(memory_space=pltpu.VMEM)],
        out_specs=pl.BlockSpec(memory_space=pltpu.VMEM),
        scratch_shapes=[
            pltpu.VMEM((2, 2, rows, 128), jnp.float32),
            pltpu.VMEM((2, rows, 128), jnp.float32),
            pltpu.VMEM((2, 2, rows, 128), jnp.float32),
            pltpu.VMEM((2, rows, 128), jnp.float32),
            pltpu.VMEM((2, 2, 1, rows, 128), jnp.float32),
            pltpu.VMEM((2, 1, rows, 128), jnp.float32),
            pltpu.VMEM((1, rows, 128), jnp.float32),
            pltpu.VMEM((2, 1, 2, rows, 128), jnp.float32),
            pltpu.VMEM((2, 1, rows, 128), jnp.float32),
            pltpu.VMEM((1, rows, 128), jnp.float32),
            pltpu.SemaphoreType.DMA((2, 6)),
        ],
        compiler_params=pltpu.CompilerParams(
            collective_id=collective_id, has_side_effects=True, vmem_limit_bytes=60 * 1024 * 1024
        ),
    )(block)
    return own.reshape(-1)[:width]

def gather_kernel(x_ref, o_ref, inbox, send_sems, recv_sems):
    fsdp_here = lax.axis_index("fsdp")
    ctx_here = lax.axis_index("ctx")
    tp_here = lax.axis_index("tp")
    ctx_count = lax.axis_size("ctx")
    count = lax.axis_size("fsdp") * ctx_count
    me = fsdp_here * ctx_count + ctx_here
    peers = []
    for offset in range(1, count):
        other = (me + offset) % count
        peers.append((other // ctx_count, other % ctx_count, tp_here))
    barrier = pltpu.get_barrier_semaphore()
    for peer in peers:
        pl.semaphore_signal(barrier, 1, device_id=peer, device_id_type=pl.DeviceIdType.MESH)
    pl.semaphore_wait(barrier, len(peers))
    copies = []
    for number, peer in enumerate(peers):
        copy = pltpu.make_async_remote_copy(
            src_ref=x_ref,
            dst_ref=inbox.at[me],
            send_sem=send_sems.at[number],
            recv_sem=recv_sems.at[me],
            device_id=peer,
            device_id_type=pl.DeviceIdType.MESH,
        )
        copy.start()
        copies.append(copy)
    o_ref[me] = x_ref[...]
    for copy in copies:
        copy.wait_send()
    for offset in range(1, count):
        source = (me + count - offset) % count
        pltpu.make_async_remote_copy(
            src_ref=x_ref,
            dst_ref=inbox.at[source],
            send_sem=send_sems.at[0],
            recv_sem=recv_sems.at[source],
            device_id=peers[0],
            device_id_type=pl.DeviceIdType.MESH,
        ).wait_recv()
        o_ref[source] = inbox[source]


def gather_shards(flat, collective_id):
    size = flat.shape[0]
    rows = -(-size // 2048) * 16
    block = jnp.pad(flat, (0, rows * 128 - size)).reshape(rows, 128)
    count = lax.axis_size("fsdp") * lax.axis_size("ctx")
    full = pl.pallas_call(
        gather_kernel,
        out_shape=jax.ShapeDtypeStruct((count, rows, 128), flat.dtype),
        in_specs=[pl.BlockSpec(memory_space=pltpu.VMEM)],
        out_specs=pl.BlockSpec(memory_space=pltpu.VMEM),
        scratch_shapes=[
            pltpu.VMEM((count, rows, 128), flat.dtype),
            pltpu.SemaphoreType.DMA((count - 1,)),
            pltpu.SemaphoreType.DMA((count,)),
        ],
        compiler_params=pltpu.CompilerParams(collective_id=collective_id, has_side_effects=True),
    )(block)
    return full.reshape(count, rows * 128)[:, :size]


def swiglu_experts(gate_up):
    return jax.nn.silu(gate_up[:, :, 0]) * gate_up[:, :, 1]


def gather_packed(pieces, axes, use_kernel=False):
    flat = jnp.concatenate([piece.reshape(-1) for piece, _ in pieces])
    if use_kernel:
        full = gather_shards(flat, 4)
    else:
        full = lax.all_gather(flat, axes, axis=0, tiled=False)
    count = full.shape[0]
    results = []
    offset = 0
    for piece, dim in pieces:
        size = piece.size
        part = full[:, offset : offset + size].reshape((count,) + piece.shape)
        offset += size
        part = jnp.moveaxis(part, 0, dim)
        shape = list(piece.shape)
        shape[dim] *= count
        results.append(part.reshape(shape))
    return results


def scatter_packed(pieces, axes, count, use_kernel=False):
    columns = []
    local_shapes = []
    for grad, dim in pieces:
        shape = grad.shape
        split = shape[:dim] + (count, shape[dim] // count) + shape[dim + 1 :]
        local_shapes.append(shape[:dim] + (shape[dim] // count,) + shape[dim + 1 :])
        part = jnp.moveaxis(grad.reshape(split), dim, 0)
        columns.append(part.reshape(count, -1))
    packed = jnp.concatenate(columns, axis=1)
    if use_kernel:
        own = halving_scatter(packed, 3)
    else:
        width = packed.shape[1]
        rows = -(-width // 1024) * 8
        packed = jnp.pad(packed, ((0, 0), (0, rows * 128 - width))).reshape(count * rows, 128)
        own = lax.psum_scatter(packed, axes, scatter_dimension=0, tiled=True).reshape(-1)
    results = []
    offset = 0
    for local_shape in local_shapes:
        size = 1
        for extent in local_shape:
            size *= extent
        results.append(own[offset : offset + size].reshape(local_shape))
        offset += size
    return results


def experts_dense(normed_two, grad_out, weights, expert_in_all, expert_down_all):
    gate_up = jnp.einsum(
        "td,edgf->etgf", normed_two, expert_in_all, preferred_element_type=jnp.float32
    )
    act, act_back = jax.vjp(swiglu_experts, gate_up)
    hidden = act.astype(jnp.bfloat16)
    outs = jnp.einsum("etf,efd->etd", hidden, expert_down_all, preferred_element_type=jnp.float32)
    weights_e = weights.T[:, :, None]
    combined = jnp.sum(weights_e * outs, axis=0)
    gate_dots = jnp.sum(outs * grad_out[None], axis=-1).T
    grad_outs = (weights_e * grad_out[None]).astype(jnp.bfloat16)
    grad_hidden = jnp.einsum(
        "etd,efd->etf", grad_outs, expert_down_all, preferred_element_type=jnp.float32
    )
    grad_gate_up = act_back(grad_hidden)[0].astype(jnp.bfloat16)
    grad_down = jnp.einsum("etf,etd->efd", hidden, grad_outs, preferred_element_type=jnp.float32)
    grad_in = jnp.einsum(
        "td,etgf->edgf", normed_two, grad_gate_up, preferred_element_type=jnp.float32
    )
    grad_rows = jnp.einsum(
        "etgf,edgf->td", grad_gate_up, expert_in_all, preferred_element_type=jnp.float32
    )
    return combined, gate_dots, grad_rows, grad_in, grad_down


def experts_routed(
    normed_two, grad_out, route_rows, gate_probs, expert_in_low, expert_down_low, capacity
):
    block_len, model_width = normed_two.shape
    experts = lax.axis_size("fsdp")
    slot_index, owner_route, filled = slot_tables(route_rows, experts, capacity)
    select = (
        (owner_route[:, None] // 2 == jnp.arange(block_len, dtype=jnp.int32)[None, :])
        & (filled[:, None] == 1)
    ).astype(jnp.bfloat16)
    token_rows = jnp.dot(select, normed_two, preferred_element_type=jnp.float32)
    grad_rows_in = jnp.dot(
        select, grad_out.astype(jnp.bfloat16), preferred_element_type=jnp.float32
    )
    slot_weights = gate_probs.reshape(-1)[owner_route][:, None]
    send_rows = jnp.stack(
        [
            token_rows.astype(jnp.bfloat16).reshape(experts, capacity, model_width),
            (slot_weights * grad_rows_in)
            .astype(jnp.bfloat16)
            .reshape(experts, capacity, model_width),
        ],
        axis=1,
    )
    exchange = lambda rows: lax.all_to_all(rows, "fsdp", split_axis=0, concat_axis=0, tiled=True)
    pair_count = lax.axis_size("tp")
    swap = lambda rows: lax.ppermute(
        rows, "tp", [(index, index + 1 - 2 * (index % 2)) for index in range(pair_count)]
    )
    half = capacity // 2
    side = lax.axis_index("tp") % 2
    if pair_count == 4 and half % 2 == 0:
        quarter = half // 2
        row_side = (lax.axis_index("tp") // 2) % 2
        piece = exchange(
            lax.dynamic_slice_in_dim(send_rows, (2 * side + row_side) * quarter, quarter, 2)
        )
        other = lax.ppermute(piece, "tp", [(0, 2), (1, 3), (2, 0), (3, 1)])
        mine = lax.dynamic_slice_in_dim(
            jnp.concatenate([piece, other, piece], axis=2), row_side * quarter, half, 2
        )
    else:
        mine = exchange(lax.dynamic_slice_in_dim(send_rows, side * half, half, 2))
    received_both = jnp.concatenate([mine, swap(mine)], axis=2)
    received = received_both[:, 0].reshape(experts * capacity, model_width)
    grad_received = received_both[:, 1].reshape(experts * capacity, model_width)
    gate_up = jnp.einsum("rd,dgf->rgf", received, expert_in_low, preferred_element_type=jnp.float32)
    act, act_back = jax.vjp(swiglu, gate_up)
    hidden = act.astype(jnp.bfloat16)
    outs = jnp.dot(hidden, expert_down_low, preferred_element_type=jnp.float32)
    grad_hidden = jnp.einsum(
        "rd,fd->rf", grad_received, expert_down_low, preferred_element_type=jnp.float32
    )
    grad_gate_up = act_back(grad_hidden)[0].astype(jnp.bfloat16)
    grad_in = jnp.einsum("rd,rgf->dgf", received, grad_gate_up, preferred_element_type=jnp.float32)
    grad_down = jnp.einsum("rf,rd->fd", hidden, grad_received, preferred_element_type=jnp.float32)
    grad_expert_rows = jnp.einsum(
        "rgf,dgf->rd", grad_gate_up, expert_in_low, preferred_element_type=jnp.float32
    )
    pair_sums = []
    for rows in (outs, grad_expert_rows):
        rows = rows.reshape(experts, capacity, model_width)
        pair_sums.append(rows[:, :half] + swap(rows[:, half:]))
    held = exchange(jnp.stack(pair_sums, axis=1).astype(jnp.bfloat16))
    slot_expert = slot_index // capacity
    slot_rank = slot_index % capacity
    in_side = ((slot_rank // half) == side)[:, None]
    local_slot = slot_expert * half + slot_rank % half
    pick = (
        (local_slot[:, None] == jnp.arange(experts * half, dtype=jnp.int32)[None, :]) & in_side
    ).astype(jnp.bfloat16)
    picked_rows = []
    for which in range(2):
        rows = jnp.dot(
            pick,
            held[:, which].reshape(experts * half, model_width),
            preferred_element_type=jnp.float32,
        )
        picked_rows.append(rows.reshape(block_len, 2, model_width))
    route_out, grad_routes = picked_rows
    combined = jnp.sum(gate_probs[:, :, None] * route_out, axis=1)
    gate_dots = jnp.sum(grad_out[:, None, :] * route_out, axis=-1)
    grad_rows = jnp.sum(grad_routes, axis=1)
    return combined, gate_dots, grad_rows, grad_in, grad_down


def local(
    layer_input,
    segments,
    routes,
    cotangent,
    gains,
    attention_in,
    attention_out,
    router_weight,
    shared_in,
    shared_down,
    expert_in,
    expert_down,
    model_stats,
    head_stats,
    value_columns,
    hidden_stats,
    router_state,
    expert_model_stats,
    expert_hidden_stats,
):
    block_len = layer_input.shape[1]
    model_width = layer_input.shape[2]
    experts = router_weight.shape[1]
    dense_experts = False
    capacity = min(block_len, 4 * block_len // experts)
    ctx_index = lax.axis_index("ctx")
    tp_index = lax.axis_index("tp")
    fsdp_index = lax.axis_index("fsdp")
    shard_index = lax.axis_index(("fsdp", "ctx"))
    shard_count = lax.axis_size(("fsdp", "ctx"))
    ctx_count = lax.axis_size("ctx")
    base_pos = ctx_index * block_len
    low = lambda v: v.astype(jnp.bfloat16)
    gain_low, attn_in_low, attn_out_low, router_low = gather_packed(
        [(low(gains), 1), (low(attention_in), 0), (low(attention_out), 1), (low(router_weight), 0)],
        ("fsdp", "ctx"),
        shard_count <= 8,
    )
    later = [
        (low(shared_in), 0),
        (low(shared_down), 1),
    ]
    if dense_experts:
        later += [(low(expert_in), 0), (low(expert_down), 0)]
    later_full = gather_packed(later, ("fsdp", "ctx"))
    shared_in_low, shared_down_low = later_full[:2]
    if dense_experts:
        fe_local = expert_down.shape[1]
        expert_in_all = later_full[2].reshape(experts, model_width, 2, fe_local)
        expert_down_all = (
            later_full[3]
            .reshape(experts, ctx_count, fe_local, model_width // ctx_count)
            .transpose(0, 2, 1, 3)
            .reshape(experts, fe_local, model_width)
        )
    else:
        expert_in_low = lax.all_gather(low(expert_in), "ctx", axis=1, tiled=True)[0]
        expert_down_low = lax.all_gather(low(expert_down), "ctx", axis=2, tiled=True)[0]
    residual = layer_input[0].astype(jnp.float32)
    gain_one = gain_low[0].astype(jnp.float32)
    gain_two = gain_low[1].astype(jnp.float32)
    normed_one, norm_one_back = jax.vjp(rms_norm, residual, gain_one)
    normed_one = normed_one.astype(jnp.bfloat16)
    projected = jnp.einsum(
        "td,dgf->tgf", normed_one, attn_in_low, preferred_element_type=jnp.float32
    )
    local_cols = projected.shape[2]
    local_heads = local_cols // HD
    half_dim = HD // 2
    frequency = 10000.0 ** (-jnp.arange(half_dim, dtype=jnp.float32) / half_dim)
    angles = (base_pos + jnp.arange(block_len, dtype=jnp.int32)).astype(jnp.float32)[
        :, None
    ] * frequency[None, :]
    cosine = jnp.cos(angles)
    sine_tab = jnp.sin(angles)
    queries = rotate(projected[:, 0].reshape(block_len, local_heads, HD), cosine, sine_tab).astype(
        jnp.bfloat16
    )
    keys_own = rotate(projected[:, 1].reshape(block_len, local_heads, HD), cosine, sine_tab).astype(
        jnp.bfloat16
    )
    values_own = projected[:, 2].reshape(block_len, local_heads, HD).astype(jnp.bfloat16)
    seg_own = segments[0].astype(jnp.bfloat16)
    keys_prev, values_prev, seg_prev = from_behind((keys_own, values_own, seg_own), "ctx", 1)
    keys_ext = jnp.concatenate([keys_prev, keys_own], axis=0)
    values_ext = jnp.concatenate([values_prev, values_own], axis=0)
    seg_ext = jnp.concatenate([seg_prev, seg_own], axis=0)
    block_rows = min(512, block_len)
    block_total = block_len // block_rows
    starts = jnp.arange(block_total, dtype=jnp.int32) * block_rows

    def forward_block(start_row):
        query_rows, key_rows, value_rows, masked, allowed = block_view(
            queries, keys_ext, values_ext, seg_own, seg_ext, start_row, base_pos
        )
        row_max = jnp.max(masked, axis=-1, keepdims=True)
        exp_terms = jnp.where(allowed[None], jnp.exp(masked - row_max), 0.0)
        row_total = jnp.sum(exp_terms, axis=-1, keepdims=True)
        attn_probs = (exp_terms / row_total).astype(jnp.bfloat16)
        attended = jnp.einsum(
            "hqk,khd->qhd", attn_probs, value_rows, preferred_element_type=jnp.float32
        )
        return (attended, row_max + jnp.log(row_total))

    attended, log_totals = lax.map(forward_block, starts)
    mixed_heads = attended.reshape(block_len, local_cols).astype(jnp.bfloat16)
    attn_total = lax.psum(
        jnp.dot(mixed_heads, attn_out_low, preferred_element_type=jnp.float32), "tp"
    )
    after_attn = residual + attn_total
    normed_two, norm_two_back = jax.vjp(rms_norm, after_attn, gain_two)
    normed_two = normed_two.astype(jnp.bfloat16)
    logits = jnp.dot(normed_two, router_low, preferred_element_type=jnp.float32)
    route_rows = routes[0]
    onehot = (route_rows[:, :, None] == jnp.arange(experts, dtype=jnp.int32)[None, None, :]).astype(
        jnp.float32
    )
    picked = jnp.sum(onehot * logits[:, None, :], axis=-1)
    gate_probs = jax.nn.softmax(picked, axis=-1)
    upstream = cotangent[0]
    grad_out = upstream.astype(jnp.float32)
    if dense_experts:
        weights = jnp.sum(gate_probs[:, :, None] * onehot, axis=1)
        combined, dots_e, grad_rows, grad_expert_in, grad_expert_down = experts_dense(
            normed_two, grad_out, weights, expert_in_all, expert_down_all
        )
        gate_dots = jnp.sum(onehot * dots_e[:, None, :], axis=-1)
    else:
        combined, gate_dots, grad_rows, grad_expert_in, grad_expert_down = experts_routed(
            normed_two,
            grad_out,
            route_rows,
            gate_probs,
            expert_in_low,
            expert_down_low,
            capacity,
        )
    shared_gate_up = jnp.einsum(
        "td,dgf->tgf", normed_two, shared_in_low, preferred_element_type=jnp.float32
    )
    shared_act, shared_act_back = jax.vjp(swiglu, shared_gate_up)
    shared_hidden = shared_act.astype(jnp.bfloat16)
    shared_out = jnp.dot(shared_hidden, shared_down_low, preferred_element_type=jnp.float32)
    grad_shared_hidden = jnp.einsum(
        "td,fd->tf", upstream, shared_down_low, preferred_element_type=jnp.float32
    )
    grad_shared_gate_up = shared_act_back(grad_shared_hidden)[0].astype(jnp.bfloat16)
    partial_two = (
        jnp.einsum(
            "tgf,dgf->td", grad_shared_gate_up, shared_in_low, preferred_element_type=jnp.float32
        )
        + grad_rows
    )
    branch_total, grad_normed_part, gate_total = lax.psum(
        (shared_out + combined, partial_two, gate_dots), "tp"
    )
    layer_out = after_attn + branch_total
    grad_picked = gate_probs * (
        gate_total - jnp.sum(gate_probs * gate_total, axis=-1, keepdims=True)
    )
    grad_logits = jnp.sum(grad_picked[:, :, None] * onehot, axis=1).astype(jnp.bfloat16)
    grad_shared_in = jnp.einsum(
        "td,tgf->dgf", normed_two, grad_shared_gate_up, preferred_element_type=jnp.float32
    )
    grad_shared_down = jnp.einsum(
        "tf,td->fd", shared_hidden, upstream, preferred_element_type=jnp.float32
    )
    grad_router = jnp.einsum(
        "td,te->de", normed_two, grad_logits, preferred_element_type=jnp.float32
    )
    grad_normed_two = grad_normed_part + jnp.einsum(
        "te,de->td", grad_logits, router_low, preferred_element_type=jnp.float32
    )
    grad_after, grad_gain_two = norm_two_back(grad_normed_two)
    grad_after = grad_after + grad_out
    grad_attn_low = grad_after.astype(jnp.bfloat16)
    grad_attn_out = jnp.einsum(
        "tc,td->cd", mixed_heads, grad_attn_low, preferred_element_type=jnp.float32
    )
    first_grads = [
        (grad_attn_out, 1),
        (grad_router, 0),
        (grad_shared_in, 0),
        (grad_shared_down, 1),
        (grad_gain_two, 0),
    ]
    if dense_experts:
        fe_local = expert_down.shape[1]
        first_grads += [
            (grad_expert_in.reshape(shard_count * expert_in.shape[1], 2, fe_local), 0),
            (
                grad_expert_down.reshape(experts, fe_local, ctx_count, model_width // ctx_count)
                .transpose(0, 2, 1, 3)
                .reshape(shard_count * fe_local, model_width // ctx_count),
                0,
            ),
        ]
    if not dense_experts:
        own_expert_in = lax.psum_scatter(grad_expert_in[None], "ctx", scatter_dimension=1, tiled=True)
        own_expert_down = lax.psum_scatter(
            grad_expert_down[None], "ctx", scatter_dimension=2, tiled=True
        )
    grad_heads = (
        jnp.einsum("td,cd->tc", grad_attn_low, attn_out_low, preferred_element_type=jnp.float32)
        .astype(jnp.bfloat16)
        .reshape(block_len, local_heads, HD)
    )

    def backward_block(block_number, running):
        grad_keys, grad_values, grad_queries = running
        start_row = block_number * block_rows
        query_rows, key_rows, value_rows, masked, allowed = block_view(
            queries, keys_ext, values_ext, seg_own, seg_ext, start_row, base_pos
        )
        log_total = lax.dynamic_index_in_dim(log_totals, block_number, 0, keepdims=False)
        attn_probs = jnp.where(allowed[None], jnp.exp(masked - log_total), 0.0)
        grad_block = lax.dynamic_slice_in_dim(grad_heads, start_row, block_rows, 0)
        grad_probs = jnp.einsum(
            "qhd,khd->hqk", grad_block, value_rows, preferred_element_type=jnp.float32
        )
        inner_sum = jnp.sum(attn_probs * grad_probs, axis=-1, keepdims=True)
        grad_scores = (attn_probs * (grad_probs - inner_sum)).astype(jnp.bfloat16)
        grad_query_rows = (
            jnp.einsum("hqk,khd->qhd", grad_scores, key_rows, preferred_element_type=jnp.float32)
            * 0.125
        )
        grad_key_rows = (
            jnp.einsum("hqk,qhd->khd", grad_scores, query_rows, preferred_element_type=jnp.float32)
            * 0.125
        )
        grad_value_rows = jnp.einsum(
            "hqk,qhd->khd",
            attn_probs.astype(jnp.bfloat16),
            grad_block,
            preferred_element_type=jnp.float32,
        )
        key_offset = start_row + block_len - WINDOW
        grad_keys = lax.dynamic_update_slice_in_dim(
            grad_keys,
            lax.dynamic_slice_in_dim(grad_keys, key_offset, block_rows + WINDOW, 0) + grad_key_rows,
            key_offset,
            0,
        )
        grad_values = lax.dynamic_update_slice_in_dim(
            grad_values,
            lax.dynamic_slice_in_dim(grad_values, key_offset, block_rows + WINDOW, 0)
            + grad_value_rows,
            key_offset,
            0,
        )
        grad_queries = lax.dynamic_update_slice_in_dim(grad_queries, grad_query_rows, start_row, 0)
        return (grad_keys, grad_values, grad_queries)

    zero_ext = jnp.zeros((2 * block_len, local_heads, HD), jnp.float32)
    zero_own = jnp.zeros((block_len, local_heads, HD), jnp.float32)
    grad_keys, grad_values, grad_queries = lax.fori_loop(
        0, block_total, backward_block, (zero_ext, zero_ext, zero_own)
    )
    rim_keys, rim_values = (
        from_behind(grad_keys[:block_len].astype(jnp.bfloat16), "ctx", -1).astype(jnp.float32),
        from_behind(grad_values[:block_len].astype(jnp.bfloat16), "ctx", -1).astype(jnp.float32),
    )
    grad_keys_own = grad_keys[block_len:] + rim_keys
    grad_values_own = grad_values[block_len:] + rim_values
    grad_query_raw = rotate(grad_queries, cosine, -sine_tab)
    grad_key_raw = rotate(grad_keys_own, cosine, -sine_tab)
    grad_projected = (
        jnp.stack([grad_query_raw, grad_key_raw, grad_values_own], axis=1)
        .reshape(block_len, 3, local_cols)
        .astype(jnp.bfloat16)
    )
    grad_attn_in = jnp.einsum(
        "td,tgf->dgf", normed_one, grad_projected, preferred_element_type=jnp.float32
    )
    partial_one = jnp.einsum(
        "tgf,dgf->td", grad_projected, attn_in_low, preferred_element_type=jnp.float32
    )
    tp_one = lax.psum(partial_one, "tp")
    halving = lax.axis_size("fsdp") == 4 and ctx_count == 2
    all_own = scatter_packed(
        first_grads + [(grad_attn_in, 0)],
        ("fsdp", "ctx"),
        shard_count,
        halving,
    )
    own_attn_out, own_router, own_shared_in, own_shared_down, own_gain_two = all_own[:5]
    own_attn_in = all_own[-1]
    grad_residual, grad_gain_one = norm_one_back(tp_one + 0.0 * own_attn_in[0, 0, 0])
    input_grad = grad_after + grad_residual
    if dense_experts:
        own_expert_in = all_own[5][None]
        own_expert_down = all_own[6][None]
    lead_tp = (tp_index == 0).astype(jnp.float32)
    first_shard = (shard_index == 0).astype(jnp.float32)
    first_ctx = (ctx_index == 0).astype(jnp.float32)
    d_local = gains.shape[1]
    ff_local = shared_down.shape[0]
    fe_local = expert_down.shape[1]
    d_quarter = expert_in.shape[1]
    square_attn_in = own_attn_in * own_attn_in + TINY_SQUARE
    square_attn_out = own_attn_out * own_attn_out + TINY_SQUARE
    square_shared_in = own_shared_in * own_shared_in + TINY_SQUARE
    square_shared_down = own_shared_down * own_shared_down + TINY_SQUARE
    square_expert_in = own_expert_in[0] * own_expert_in[0] + TINY_SQUARE
    square_expert_down = own_expert_down[0] * own_expert_down[0] + TINY_SQUARE
    model_part = lax.dynamic_update_slice(
        jnp.zeros((4, D), jnp.float32),
        jnp.stack(
            [
                jnp.sum(square_attn_in, axis=(1, 2)),
                jnp.sum(square_shared_in, axis=(1, 2)),
                jnp.sum(square_attn_out, axis=0),
                jnp.sum(square_shared_down, axis=0),
            ]
        ),
        (0, shard_index * d_local),
    )
    head_part = lax.dynamic_update_slice(
        jnp.zeros((4, HH), jnp.float32),
        jnp.concatenate(
            [jnp.sum(square_attn_in, axis=0), jnp.sum(square_attn_out, axis=1)[None]], axis=0
        ),
        (0, tp_index * local_cols),
    )
    hidden_part = lax.dynamic_update_slice(
        jnp.zeros((3, FF), jnp.float32),
        jnp.concatenate(
            [jnp.sum(square_shared_in, axis=0), jnp.sum(square_shared_down, axis=1)[None]], axis=0
        ),
        (0, tp_index * ff_local),
    )
    expert_model_part = lax.dynamic_update_slice(
        jnp.zeros((experts, 2, D), jnp.float32),
        jnp.stack([jnp.sum(square_expert_in, axis=(1, 2)), jnp.sum(square_expert_down, axis=0)])[
            None
        ],
        (fsdp_index, 0, ctx_index * d_quarter),
    )
    expert_hidden_part = lax.dynamic_update_slice(
        jnp.zeros((experts, 3, FE), jnp.float32),
        jnp.concatenate(
            [jnp.sum(square_expert_in, axis=0), jnp.sum(square_expert_down, axis=1)[None]], axis=0
        )[None],
        (fsdp_index, 0, tp_index * fe_local),
    )
    scalar_part = jnp.stack(
        [
            lead_tp * jnp.sum(gains * gains),
            jnp.sum(attention_in * attention_in),
            jnp.sum(attention_out * attention_out),
            lead_tp * jnp.sum(router_weight * router_weight),
            jnp.sum(shared_in * shared_in),
            jnp.sum(shared_down * shared_down),
            jnp.sum(expert_in * expert_in),
            jnp.sum(expert_down * expert_down),
            lead_tp * jnp.sum(model_stats[2]),
            first_shard * jnp.sum(head_stats[2]),
            lead_tp * jnp.sum(model_stats[3]),
            first_shard * jnp.sum(hidden_stats[2]),
        ]
    )
    expert_old_part = lax.dynamic_update_slice(
        jnp.zeros((2, experts), jnp.float32),
        jnp.stack(
            [
                lead_tp * jnp.sum(expert_model_stats[0, 0]),
                first_ctx * jnp.sum(expert_hidden_stats[0, 2]),
            ]
        )[:, None],
        (0, fsdp_index),
    )
    global_sums = butterfly_sum(
        [
            model_part,
            head_part,
            hidden_part,
            expert_model_part,
            expert_hidden_part,
            scalar_part,
            expert_old_part,
            lead_tp * grad_gain_one,
        ],
        1,
    )
    (
        model_sum,
        head_sum,
        hidden_sum,
        expert_model_sum,
        expert_hidden_sum,
        scalar_sum,
        expert_old_sum,
        gain_one_sum,
    ) = global_sums
    own_gain_one = lax.dynamic_slice_in_dim(gain_one_sum, shard_index * d_local, d_local)
    own_gains = jnp.stack([own_gain_one, own_gain_two])
    shard_start = shard_index * d_local
    gain_state = DECAY_RATE * model_stats[0:2] + (1.0 - DECAY_RATE) * (
        own_gains * own_gains + TINY_SQUARE
    )
    update_gains = own_gains * lax.rsqrt(gain_state)
    router_new = DECAY_RATE * router_state + (1.0 - DECAY_RATE) * (
        own_router * own_router + TINY_SQUARE
    )
    update_router = own_router * lax.rsqrt(router_new)
    attn_cols_old = jnp.concatenate([head_stats[0:2], value_columns[None]], axis=0).reshape(-1)
    update_attn_in, rows_attn_in, cols_attn_in = factored_update(
        own_attn_in.reshape(d_local, 3 * local_cols),
        model_stats[2],
        attn_cols_old,
        lax.dynamic_slice_in_dim(model_sum[0], shard_start, d_local),
        lax.dynamic_slice_in_dim(head_sum[0:3], tp_index * local_cols, local_cols, 1).reshape(-1),
        D,
        3 * HH,
        scalar_sum[8],
        jnp.sum(model_sum[0]),
    )
    update_attn_out, rows_attn_out, cols_attn_out = factored_update(
        own_attn_out,
        head_stats[2],
        model_stats[4],
        lax.dynamic_slice_in_dim(head_sum[3], tp_index * local_cols, local_cols),
        lax.dynamic_slice_in_dim(model_sum[2], shard_start, d_local),
        HH,
        D,
        scalar_sum[9],
        jnp.sum(head_sum[3]),
    )
    update_shared_in, rows_shared_in, cols_shared_in = factored_update(
        own_shared_in.reshape(d_local, 2 * ff_local),
        model_stats[3],
        hidden_stats[0:2].reshape(-1),
        lax.dynamic_slice_in_dim(model_sum[1], shard_start, d_local),
        lax.dynamic_slice_in_dim(hidden_sum[0:2], tp_index * ff_local, ff_local, 1).reshape(-1),
        D,
        2 * FF,
        scalar_sum[10],
        jnp.sum(model_sum[1]),
    )
    update_shared_down, rows_shared_down, cols_shared_down = factored_update(
        own_shared_down,
        hidden_stats[2],
        model_stats[5],
        lax.dynamic_slice_in_dim(hidden_sum[2], tp_index * ff_local, ff_local),
        lax.dynamic_slice_in_dim(model_sum[3], shard_start, d_local),
        FF,
        D,
        scalar_sum[11],
        jnp.sum(hidden_sum[2]),
    )
    own_expert_model = lax.dynamic_index_in_dim(expert_model_sum, fsdp_index, 0, keepdims=False)
    own_expert_hidden = lax.dynamic_index_in_dim(expert_hidden_sum, fsdp_index, 0, keepdims=False)
    old_expert_totals = lax.dynamic_index_in_dim(expert_old_sum, fsdp_index, 1, keepdims=False)
    update_expert_in, rows_expert_in, cols_expert_in = factored_update(
        own_expert_in[0].reshape(d_quarter, 2 * fe_local),
        expert_model_stats[0, 0],
        expert_hidden_stats[0, 0:2].reshape(-1),
        lax.dynamic_slice_in_dim(own_expert_model[0], ctx_index * d_quarter, d_quarter),
        lax.dynamic_slice_in_dim(own_expert_hidden[0:2], tp_index * fe_local, fe_local, 1).reshape(
            -1
        ),
        D,
        2 * FE,
        old_expert_totals[0],
        jnp.sum(own_expert_model[0]),
    )
    update_expert_down, rows_expert_down, cols_expert_down = factored_update(
        own_expert_down[0],
        expert_hidden_stats[0, 2],
        expert_model_stats[0, 1],
        lax.dynamic_slice_in_dim(own_expert_hidden[2], tp_index * fe_local, fe_local),
        lax.dynamic_slice_in_dim(own_expert_model[1], ctx_index * d_quarter, d_quarter),
        FE,
        D,
        old_expert_totals[1],
        jnp.sum(own_expert_hidden[2]),
    )
    clip_part = jnp.stack(
        [
            lead_tp * jnp.sum(update_gains * update_gains),
            jnp.sum(update_attn_in * update_attn_in),
            jnp.sum(update_attn_out * update_attn_out),
            lead_tp * jnp.sum(update_router * update_router),
            jnp.sum(update_shared_in * update_shared_in),
            jnp.sum(update_shared_down * update_shared_down),
            jnp.sum(update_expert_in * update_expert_in),
            jnp.sum(update_expert_down * update_expert_down),
        ]
    )
    clip_total = butterfly_sum([clip_part], 2)[0]
    elements = jnp.array(
        [
            2 * D,
            D * 3 * HH,
            HH * D,
            D * experts,
            D * 2 * FF,
            FF * D,
            experts * D * 2 * FE,
            experts * FE * D,
        ],
        jnp.float32,
    )
    update_roots = jnp.sqrt(clip_total / elements)
    new_gains = apply_update(gains, update_gains, update_roots[0], scalar_sum[0], elements[0])
    new_attn_in = apply_update(
        attention_in,
        update_attn_in.reshape(attention_in.shape),
        update_roots[1],
        scalar_sum[1],
        elements[1],
    )
    new_attn_out = apply_update(
        attention_out, update_attn_out, update_roots[2], scalar_sum[2], elements[2]
    )
    new_router = apply_update(
        router_weight, update_router, update_roots[3], scalar_sum[3], elements[3]
    )
    new_shared_in = apply_update(
        shared_in,
        update_shared_in.reshape(shared_in.shape),
        update_roots[4],
        scalar_sum[4],
        elements[4],
    )
    new_shared_down = apply_update(
        shared_down, update_shared_down, update_roots[5], scalar_sum[5], elements[5]
    )
    new_expert_in = apply_update(
        expert_in,
        update_expert_in.reshape(expert_in.shape),
        update_roots[6],
        scalar_sum[6],
        elements[6],
    )
    new_expert_down = apply_update(
        expert_down,
        update_expert_down.reshape(expert_down.shape),
        update_roots[7],
        scalar_sum[7],
        elements[7],
    )
    new_model_stats = jnp.concatenate(
        [gain_state, jnp.stack([rows_attn_in, rows_shared_in, cols_attn_out, cols_shared_down])],
        axis=0,
    )
    attn_cols_new = cols_attn_in.reshape(3, local_cols)
    new_head_stats = jnp.concatenate([attn_cols_new[0:2], rows_attn_out[None]], axis=0)
    new_value_columns = attn_cols_new[2]
    new_hidden_stats = jnp.concatenate(
        [cols_shared_in.reshape(2, ff_local), rows_shared_down[None]], axis=0
    )
    new_expert_model_stats = jnp.stack([rows_expert_in, cols_expert_down])[None]
    new_expert_hidden_stats = jnp.concatenate(
        [cols_expert_in.reshape(2, fe_local), rows_expert_down[None]], axis=0
    )[None]
    return (
        layer_out.astype(jnp.bfloat16)[None],
        input_grad[None],
        own_gains,
        own_attn_in,
        own_attn_out,
        own_router,
        own_shared_in,
        own_shared_down,
        own_expert_in,
        own_expert_down,
        new_gains,
        new_attn_in,
        new_attn_out,
        new_router,
        new_shared_in,
        new_shared_down,
        new_expert_in,
        new_expert_down,
        new_model_stats,
        new_head_stats,
        new_value_columns,
        new_hidden_stats,
        router_new,
        new_expert_model_stats,
        new_expert_hidden_stats,
        update_roots,
    )


def solution(mesh):
    in_specs = (
        P("fsdp", "ctx", None),
        P("fsdp", "ctx"),
        P("fsdp", "ctx", None),
        P("fsdp", "ctx", None),
        P(None, ("fsdp", "ctx")),
        P(("fsdp", "ctx"), None, "tp"),
        P("tp", ("fsdp", "ctx")),
        P(("fsdp", "ctx"), None),
        P(("fsdp", "ctx"), None, "tp"),
        P("tp", ("fsdp", "ctx")),
        P("fsdp", "ctx", None, "tp"),
        P("fsdp", "tp", "ctx"),
        P(None, ("fsdp", "ctx")),
        P(None, "tp"),
        P("tp"),
        P(None, "tp"),
        P(("fsdp", "ctx"), None),
        P("fsdp", None, "ctx"),
        P("fsdp", None, "tp"),
    )
    out_specs = (
        P("fsdp", "ctx", None),
        P("fsdp", "ctx", None),
        P(None, ("fsdp", "ctx")),
        P(("fsdp", "ctx"), None, "tp"),
        P("tp", ("fsdp", "ctx")),
        P(("fsdp", "ctx"), None),
        P(("fsdp", "ctx"), None, "tp"),
        P("tp", ("fsdp", "ctx")),
        P("fsdp", "ctx", None, "tp"),
        P("fsdp", "tp", "ctx"),
        P(None, ("fsdp", "ctx")),
        P(("fsdp", "ctx"), None, "tp"),
        P("tp", ("fsdp", "ctx")),
        P(("fsdp", "ctx"), None),
        P(("fsdp", "ctx"), None, "tp"),
        P("tp", ("fsdp", "ctx")),
        P("fsdp", "ctx", None, "tp"),
        P("fsdp", "tp", "ctx"),
        P(None, ("fsdp", "ctx")),
        P(None, "tp"),
        P("tp"),
        P(None, "tp"),
        P(("fsdp", "ctx"), None),
        P("fsdp", None, "ctx"),
        P("fsdp", None, "tp"),
        P(),
    )
    return jax.shard_map(local, mesh=mesh, in_specs=in_specs, out_specs=out_specs, check_vma=False)
```

```python
import jax
import jax.numpy as jnp
from jax import lax
from jax.sharding import PartitionSpec as P
from jax.experimental import pallas as pl
from jax.experimental.pallas import tpu as pltpu

D = 768
HD = 64
FF = 2048
FE = 2048
WINDOW = 1024
HH = 768


EPSILON = 1e-06
TINY_SQUARE = 1e-30
SCALE_FLOOR = 0.001
DECAY_RATE = 0.5
CLIP_LIMIT = 0.5
STEP_RATE = 0.5


def from_behind(value, axis, steps):
    count = lax.axis_size(axis)
    leading, last = (max(0, -steps), min(count, count - steps))
    return lax.ppermute(value, axis, [(source, source + steps) for source in range(leading, last)])


def rms_norm(values, gain_vec):
    inv_rms = lax.rsqrt(jnp.mean(values * values, axis=-1, keepdims=True) + EPSILON)
    return values * inv_rms * gain_vec


def swiglu(gate_up):
    return jax.nn.silu(gate_up[:, 0]) * gate_up[:, 1]


def rotate(values, cosine, sine_tab):
    half_dim = values.shape[-1] // 2
    first_half = values[..., :half_dim]
    second_half = values[..., half_dim:]
    cos_b = cosine[:, None, :]
    sin_b = sine_tab[:, None, :]
    return jnp.concatenate(
        [first_half * cos_b - second_half * sin_b, second_half * cos_b + first_half * sin_b],
        axis=-1,
    )


def slot_tables(block_routes, experts, capacity):
    flat_routes = block_routes.reshape(-1)
    route_count = flat_routes.shape[0]
    onehot = (flat_routes[:, None] == jnp.arange(experts, dtype=jnp.int32)[None, :]).astype(
        jnp.int32
    )
    rank_in = jnp.sum(
        (jnp.cumsum(onehot, axis=0, dtype=jnp.int32) - 1) * onehot, axis=1, dtype=jnp.int32
    )
    slot_index = flat_routes * capacity + rank_in
    owner_route = (
        jnp.zeros((experts * capacity,), jnp.int32)
        .at[slot_index]
        .set(jnp.arange(route_count, dtype=jnp.int32))
    )
    filled = jnp.zeros((experts * capacity,), jnp.int32).at[slot_index].set(1)
    return (slot_index, owner_route, filled)


def block_view(queries, keys_ext, values_ext, seg_own, seg_ext, start_row, base_pos):
    block_len = queries.shape[0]
    block_rows = min(512, block_len)
    query_rows = lax.dynamic_slice_in_dim(queries, start_row, block_rows, 0)
    key_rows = lax.dynamic_slice_in_dim(
        keys_ext, start_row + block_len - WINDOW, block_rows + WINDOW, 0
    )
    value_rows = lax.dynamic_slice_in_dim(
        values_ext, start_row + block_len - WINDOW, block_rows + WINDOW, 0
    )
    scores = (
        jnp.einsum("qhd,khd->hqk", query_rows, key_rows, preferred_element_type=jnp.float32) * 0.125
    )
    query_pos = start_row + jnp.arange(block_rows, dtype=jnp.int32)
    key_pos = start_row - WINDOW + jnp.arange(block_rows + WINDOW, dtype=jnp.int32)
    distance = query_pos[:, None] - key_pos[None, :]
    seg_query = lax.dynamic_slice_in_dim(seg_own, start_row, block_rows, 0)
    seg_key = lax.dynamic_slice_in_dim(
        seg_ext, start_row + block_len - WINDOW, block_rows + WINDOW, 0
    )
    allowed = (
        (distance >= 0)
        & (distance < WINDOW)
        & (seg_query[:, None] == seg_key[None, :])
        & (key_pos[None, :] + base_pos >= 0)
    )
    return (query_rows, key_rows, value_rows, jnp.where(allowed[None], scores, -1e30), allowed)


def factored_update(
    grad_mat, rows_old, cols_old, row_sums, col_sums, row_total, col_total, old_total, square_total
):
    rows_new = DECAY_RATE * rows_old + (1.0 - DECAY_RATE) * row_sums / col_total
    cols_new = DECAY_RATE * cols_old + (1.0 - DECAY_RATE) * col_sums / row_total
    mean_rows = (DECAY_RATE * old_total + (1.0 - DECAY_RATE) * square_total / col_total) / row_total
    second_moment = rows_new[:, None] * cols_new[None, :] / mean_rows
    return (grad_mat * lax.rsqrt(second_moment), rows_new, cols_new)


def apply_update(weight, update, update_root, square_sum, elements):
    param_scale = jnp.maximum(SCALE_FLOOR, jnp.sqrt(square_sum / elements))
    return weight - STEP_RATE * param_scale * update / jnp.maximum(1.0, update_root / CLIP_LIMIT)


def butterfly_partners():
    partners = []
    here = [lax.axis_index(name) for name in ("fsdp", "ctx", "tp")]
    for axis_number, name in enumerate(("fsdp", "ctx", "tp")):
        size = lax.axis_size(name)
        step = 1
        while step < size:
            bit = (here[axis_number] // step) % 2
            other = list(here)
            other[axis_number] = here[axis_number] + step * (1 - 2 * bit)
            partners.append(tuple(other))
            step *= 2
    return partners


def butterfly_kernel(x_ref, o_ref, stage, inbox, send_sems, recv_sems):
    partners = butterfly_partners()
    barrier = pltpu.get_barrier_semaphore()
    for partner in partners:
        pl.semaphore_signal(
            barrier, 1, device_id=partner, device_id_type=pl.DeviceIdType.MESH
        )
    pl.semaphore_wait(barrier, len(partners))
    acc = x_ref[...]
    for round_number, partner in enumerate(partners):
        stage[round_number] = acc
        copy = pltpu.make_async_remote_copy(
            src_ref=stage.at[round_number],
            dst_ref=inbox.at[round_number],
            send_sem=send_sems.at[round_number],
            recv_sem=recv_sems.at[round_number],
            device_id=partner,
            device_id_type=pl.DeviceIdType.MESH,
        )
        copy.start()
        copy.wait()
        acc = stage[round_number] + inbox[round_number]
    o_ref[...] = acc


def butterfly_sum(values, collective_id):
    flat = jnp.concatenate([v.reshape(-1).astype(jnp.float32) for v in values])
    size = flat.shape[0]
    rows = -(-size // 1024) * 8
    block = jnp.pad(flat, (0, rows * 128 - size)).reshape(rows, 128)
    rounds = sum(
        max(1, lax.axis_size(name)).bit_length() - 1 for name in ("fsdp", "ctx", "tp")
    )
    total = pl.pallas_call(
        butterfly_kernel,
        out_shape=jax.ShapeDtypeStruct((rows, 128), jnp.float32),
        in_specs=[pl.BlockSpec(memory_space=pltpu.VMEM)],
        out_specs=pl.BlockSpec(memory_space=pltpu.VMEM),
        scratch_shapes=[
            pltpu.VMEM((rounds, rows, 128), jnp.float32),
            pltpu.VMEM((rounds, rows, 128), jnp.float32),
            pltpu.SemaphoreType.DMA((rounds,)),
            pltpu.SemaphoreType.DMA((rounds,)),
        ],
        compiler_params=pltpu.CompilerParams(collective_id=collective_id, has_side_effects=True),
    )(block).reshape(-1)
    results = []
    offset = 0
    for v in values:
        results.append(total[offset : offset + v.size].reshape(v.shape))
        offset += v.size
    return results


def halving_kernel(
    x_ref, o_ref, stage_a, stage_a2, stage_b, stage_b2, in_a1, in_a2, in_a3, in_b1, in_b2, in_b3, sems
):
    rows = o_ref.shape[0] // 2
    chunk = 64
    fsdp_here = lax.axis_index("fsdp")
    ctx_here = lax.axis_index("ctx")
    tp_here = lax.axis_index("tp")
    bit_low = fsdp_here % 2
    bit_high = (fsdp_here // 2) % 2
    partners = [
        (fsdp_here, 1 - ctx_here, tp_here),
        (fsdp_here + 1 - 2 * bit_low, ctx_here, tp_here),
        (fsdp_here + 2 - 4 * bit_high, ctx_here, tp_here),
    ]
    barrier = pltpu.get_barrier_semaphore()
    for partner in partners:
        pl.semaphore_signal(barrier, 1, device_id=partner, device_id_type=pl.DeviceIdType.MESH)
    pl.semaphore_wait(barrier, len(partners))
    first, second = pl.ds(0, rows), pl.ds(rows, rows)

    def swap_pair(sources, targets, number, partner_pair):
        copies = []
        for index in range(2):
            copy = pltpu.make_async_remote_copy(
                src_ref=sources[index],
                dst_ref=targets[index],
                send_sem=sems.at[0, 2 * number + index],
                recv_sem=sems.at[1, 2 * number + index],
                device_id=partner_pair[index],
                device_id_type=pl.DeviceIdType.MESH,
            )
            copy.start()
            copies.append(copy)
        for copy in copies:
            copy.wait()

    def each_chunk(body):
        @pl.loop(0, rows // chunk)
        def _(step):
            body(pl.ds(pl.multiple_of(step * chunk, chunk), chunk))

    swap_pair(
        [
            x_ref.at[:, :, pl.ds(1 - ctx_here, 1), first],
            x_ref.at[:, pl.ds(1 - bit_low, 1), :, second],
        ],
        [in_a1, in_b1],
        0,
        [partners[0], partners[1]],
    )

    def round_one(part):
        shifted = pl.ds(part.start + rows, chunk)
        for high in range(2):
            for other in range(2):
                stage_a[high, other, part] = (
                    x_ref[high, other, ctx_here, part] + in_a1[high, other, 0, part]
                )
                stage_b[high, other, part] = (
                    x_ref[high, bit_low, other, shifted] + in_b1[high, 0, other, part]
                )

    each_chunk(round_one)
    swap_pair(
        [stage_a.at[:, pl.ds(1 - bit_low, 1)], stage_b.at[:, pl.ds(1 - ctx_here, 1)]],
        [in_a2, in_b2],
        1,
        [partners[1], partners[0]],
    )

    def round_two(part):
        for high in range(2):
            stage_a2[high, part] = stage_a[high, bit_low, part] + in_a2[high, 0, part]
            stage_b2[high, part] = stage_b[high, ctx_here, part] + in_b2[high, 0, part]

    each_chunk(round_two)
    swap_pair(
        [stage_a2.at[pl.ds(1 - bit_high, 1)], stage_b2.at[pl.ds(1 - bit_high, 1)]],
        [in_a3, in_b3],
        2,
        [partners[2], partners[2]],
    )

    def round_three(part):
        o_ref[part] = stage_a2[bit_high, part] + in_a3[0, part]
        o_ref[pl.ds(part.start + rows, chunk)] = stage_b2[bit_high, part] + in_b3[0, part]

    each_chunk(round_three)


def halving_scatter(packed, collective_id):
    count, width = packed.shape
    rows = -(-width // (128 * 128)) * 64
    block = jnp.pad(packed, ((0, 0), (0, 2 * rows * 128 - width))).reshape(
        2, 2, 2, 2 * rows, 128
    )
    own = pl.pallas_call(
        halving_kernel,
        out_shape=jax.ShapeDtypeStruct((2 * rows, 128), jnp.float32),
        in_specs=[pl.BlockSpec(memory_space=pltpu.VMEM)],
        out_specs=pl.BlockSpec(memory_space=pltpu.VMEM),
        scratch_shapes=[
            pltpu.VMEM((2, 2, rows, 128), jnp.float32),
            pltpu.VMEM((2, rows, 128), jnp.float32),
            pltpu.VMEM((2, 2, rows, 128), jnp.float32),
            pltpu.VMEM((2, rows, 128), jnp.float32),
            pltpu.VMEM((2, 2, 1, rows, 128), jnp.float32),
            pltpu.VMEM((2, 1, rows, 128), jnp.float32),
            pltpu.VMEM((1, rows, 128), jnp.float32),
            pltpu.VMEM((2, 1, 2, rows, 128), jnp.float32),
            pltpu.VMEM((2, 1, rows, 128), jnp.float32),
            pltpu.VMEM((1, rows, 128), jnp.float32),
            pltpu.SemaphoreType.DMA((2, 6)),
        ],
        compiler_params=pltpu.CompilerParams(
            collective_id=collective_id, has_side_effects=True, vmem_limit_bytes=60 * 1024 * 1024
        ),
    )(block)
    return own.reshape(-1)[:width]

def gather_kernel(x_ref, o_ref, inbox, send_sems, recv_sems):
    fsdp_here = lax.axis_index("fsdp")
    ctx_here = lax.axis_index("ctx")
    tp_here = lax.axis_index("tp")
    ctx_count = lax.axis_size("ctx")
    count = lax.axis_size("fsdp") * ctx_count
    me = fsdp_here * ctx_count + ctx_here
    peers = []
    for offset in range(1, count):
        other = (me + offset) % count
        peers.append((other // ctx_count, other % ctx_count, tp_here))
    barrier = pltpu.get_barrier_semaphore()
    for peer in peers:
        pl.semaphore_signal(barrier, 1, device_id=peer, device_id_type=pl.DeviceIdType.MESH)
    pl.semaphore_wait(barrier, len(peers))
    copies = []
    for number, peer in enumerate(peers):
        copy = pltpu.make_async_remote_copy(
            src_ref=x_ref,
            dst_ref=inbox.at[me],
            send_sem=send_sems.at[number],
            recv_sem=recv_sems.at[me],
            device_id=peer,
            device_id_type=pl.DeviceIdType.MESH,
        )
        copy.start()
        copies.append(copy)
    o_ref[me] = x_ref[...]
    for copy in copies:
        copy.wait_send()
    for offset in range(1, count):
        source = (me + count - offset) % count
        pltpu.make_async_remote_copy(
            src_ref=x_ref,
            dst_ref=inbox.at[source],
            send_sem=send_sems.at[0],
            recv_sem=recv_sems.at[source],
            device_id=peers[0],
            device_id_type=pl.DeviceIdType.MESH,
        ).wait_recv()
        o_ref[source] = inbox[source]


def gather_shards(flat, collective_id):
    size = flat.shape[0]
    rows = -(-size // 2048) * 16
    block = jnp.pad(flat, (0, rows * 128 - size)).reshape(rows, 128)
    count = lax.axis_size("fsdp") * lax.axis_size("ctx")
    full = pl.pallas_call(
        gather_kernel,
        out_shape=jax.ShapeDtypeStruct((count, rows, 128), flat.dtype),
        in_specs=[pl.BlockSpec(memory_space=pltpu.VMEM)],
        out_specs=pl.BlockSpec(memory_space=pltpu.VMEM),
        scratch_shapes=[
            pltpu.VMEM((count, rows, 128), flat.dtype),
            pltpu.SemaphoreType.DMA((count - 1,)),
            pltpu.SemaphoreType.DMA((count,)),
        ],
        compiler_params=pltpu.CompilerParams(collective_id=collective_id, has_side_effects=True),
    )(block)
    return full.reshape(count, rows * 128)[:, :size]


def swiglu_experts(gate_up):
    return jax.nn.silu(gate_up[:, :, 0]) * gate_up[:, :, 1]


def gather_packed(pieces, axes, use_kernel=False):
    flat = jnp.concatenate([piece.reshape(-1) for piece, _ in pieces])
    if use_kernel:
        full = gather_shards(flat, 4)
    else:
        full = lax.all_gather(flat, axes, axis=0, tiled=False)
    count = full.shape[0]
    results = []
    offset = 0
    for piece, dim in pieces:
        size = piece.size
        part = full[:, offset : offset + size].reshape((count,) + piece.shape)
        offset += size
        part = jnp.moveaxis(part, 0, dim)
        shape = list(piece.shape)
        shape[dim] *= count
        results.append(part.reshape(shape))
    return results


def scatter_packed(pieces, axes, count, use_kernel=False):
    columns = []
    local_shapes = []
    for grad, dim in pieces:
        shape = grad.shape
        split = shape[:dim] + (count, shape[dim] // count) + shape[dim + 1 :]
        local_shapes.append(shape[:dim] + (shape[dim] // count,) + shape[dim + 1 :])
        part = jnp.moveaxis(grad.reshape(split), dim, 0)
        columns.append(part.reshape(count, -1))
    packed = jnp.concatenate(columns, axis=1)
    if use_kernel:
        own = halving_scatter(packed, 3)
    else:
        width = packed.shape[1]
        rows = -(-width // 1024) * 8
        packed = jnp.pad(packed, ((0, 0), (0, rows * 128 - width))).reshape(count * rows, 128)
        own = lax.psum_scatter(packed, axes, scatter_dimension=0, tiled=True).reshape(-1)
    results = []
    offset = 0
    for local_shape in local_shapes:
        size = 1
        for extent in local_shape:
            size *= extent
        results.append(own[offset : offset + size].reshape(local_shape))
        offset += size
    return results


def experts_dense(normed_two, grad_out, weights, expert_in_all, expert_down_all):
    gate_up = jnp.einsum(
        "td,edgf->etgf", normed_two, expert_in_all, preferred_element_type=jnp.float32
    )
    act, act_back = jax.vjp(swiglu_experts, gate_up)
    hidden = act.astype(jnp.bfloat16)
    outs = jnp.einsum("etf,efd->etd", hidden, expert_down_all, preferred_element_type=jnp.float32)
    weights_e = weights.T[:, :, None]
    combined = jnp.sum(weights_e * outs, axis=0)
    gate_dots = jnp.sum(outs * grad_out[None], axis=-1).T
    grad_outs = (weights_e * grad_out[None]).astype(jnp.bfloat16)
    grad_hidden = jnp.einsum(
        "etd,efd->etf", grad_outs, expert_down_all, preferred_element_type=jnp.float32
    )
    grad_gate_up = act_back(grad_hidden)[0].astype(jnp.bfloat16)
    grad_down = jnp.einsum("etf,etd->efd", hidden, grad_outs, preferred_element_type=jnp.float32)
    grad_in = jnp.einsum(
        "td,etgf->edgf", normed_two, grad_gate_up, preferred_element_type=jnp.float32
    )
    grad_rows = jnp.einsum(
        "etgf,edgf->td", grad_gate_up, expert_in_all, preferred_element_type=jnp.float32
    )
    return combined, gate_dots, grad_rows, grad_in, grad_down


def experts_routed(
    normed_two, grad_out, route_rows, gate_probs, expert_in_low, expert_down_low, capacity
):
    block_len, model_width = normed_two.shape
    experts = lax.axis_size("fsdp")
    slot_index, owner_route, filled = slot_tables(route_rows, experts, capacity)
    select = (
        (owner_route[:, None] // 2 == jnp.arange(block_len, dtype=jnp.int32)[None, :])
        & (filled[:, None] == 1)
    ).astype(jnp.bfloat16)
    token_rows = jnp.dot(select, normed_two, preferred_element_type=jnp.float32)
    grad_rows_in = jnp.dot(
        select, grad_out.astype(jnp.bfloat16), preferred_element_type=jnp.float32
    )
    slot_weights = gate_probs.reshape(-1)[owner_route][:, None]
    send_rows = jnp.stack(
        [
            token_rows.astype(jnp.bfloat16).reshape(experts, capacity, model_width),
            (slot_weights * grad_rows_in)
            .astype(jnp.bfloat16)
            .reshape(experts, capacity, model_width),
        ],
        axis=1,
    )
    exchange = lambda rows: lax.all_to_all(rows, "fsdp", split_axis=0, concat_axis=0, tiled=True)
    pair_count = lax.axis_size("tp")
    swap = lambda rows: lax.ppermute(
        rows, "tp", [(index, index + 1 - 2 * (index % 2)) for index in range(pair_count)]
    )
    half = capacity // 2
    side = lax.axis_index("tp") % 2
    def expert_block(block):
        rows_in = block[:, 0].reshape(-1, model_width)
        grads_in = block[:, 1].reshape(-1, model_width)
        gate_up = jnp.einsum(
            "rd,dgf->rgf", rows_in, expert_in_low, preferred_element_type=jnp.float32
        )
        act, act_back = jax.vjp(swiglu, gate_up)
        hidden = act.astype(jnp.bfloat16)
        outs = jnp.dot(hidden, expert_down_low, preferred_element_type=jnp.float32)
        grad_hidden = jnp.einsum(
            "rd,fd->rf", grads_in, expert_down_low, preferred_element_type=jnp.float32
        )
        grad_gate_up = act_back(grad_hidden)[0].astype(jnp.bfloat16)
        grad_in = jnp.einsum(
            "rd,rgf->dgf", rows_in, grad_gate_up, preferred_element_type=jnp.float32
        )
        grad_down = jnp.einsum("rf,rd->fd", hidden, grads_in, preferred_element_type=jnp.float32)
        grad_expert_rows = jnp.einsum(
            "rgf,dgf->rd", grad_gate_up, expert_in_low, preferred_element_type=jnp.float32
        )
        width = block.shape[2]
        return (
            [
                outs.reshape(experts, width, model_width),
                grad_expert_rows.reshape(experts, width, model_width),
            ],
            grad_in,
            grad_down,
        )

    if pair_count == 4 and half % 2 == 0:
        quarter = half // 2
        row_side = (lax.axis_index("tp") // 2) % 2
        piece = exchange(
            lax.dynamic_slice_in_dim(send_rows, (2 * side + row_side) * quarter, quarter, 2)
        )
        other = lax.ppermute(piece, "tp", [(0, 2), (1, 3), (2, 0), (3, 1)])
        results_a, grad_in_a, grad_down_a = expert_block(
            jnp.concatenate([piece, swap(piece)], axis=2)
        )
        results_b, grad_in_b, grad_down_b = expert_block(
            jnp.concatenate([other, swap(other)], axis=2)
        )
        grad_in = grad_in_a + grad_in_b
        grad_down = grad_down_a + grad_down_b
        pair_sums = []
        for rows_a, rows_b in zip(results_a, results_b):
            sum_a = rows_a[:, :quarter] + swap(rows_a[:, quarter:])
            sum_b = rows_b[:, :quarter] + swap(rows_b[:, quarter:])
            pair_sums.append(
                lax.dynamic_slice_in_dim(
                    jnp.concatenate([sum_a, sum_b, sum_a], axis=1), row_side * quarter, half, 1
                )
            )
    else:
        mine = exchange(lax.dynamic_slice_in_dim(send_rows, side * half, half, 2))
        results, grad_in, grad_down = expert_block(jnp.concatenate([mine, swap(mine)], axis=2))
        pair_sums = [rows[:, :half] + swap(rows[:, half:]) for rows in results]
    held = exchange(jnp.stack(pair_sums, axis=1).astype(jnp.bfloat16))
    slot_expert = slot_index // capacity
    slot_rank = slot_index % capacity
    in_side = ((slot_rank // half) == side)[:, None]
    local_slot = slot_expert * half + slot_rank % half
    pick = (
        (local_slot[:, None] == jnp.arange(experts * half, dtype=jnp.int32)[None, :]) & in_side
    ).astype(jnp.bfloat16)
    picked_rows = []
    for which in range(2):
        rows = jnp.dot(
            pick,
            held[:, which].reshape(experts * half, model_width),
            preferred_element_type=jnp.float32,
        )
        picked_rows.append(rows.reshape(block_len, 2, model_width))
    route_out, grad_routes = picked_rows
    combined = jnp.sum(gate_probs[:, :, None] * route_out, axis=1)
    gate_dots = jnp.sum(grad_out[:, None, :] * route_out, axis=-1)
    grad_rows = jnp.sum(grad_routes, axis=1)
    return combined, gate_dots, grad_rows, grad_in, grad_down


def local(
    layer_input,
    segments,
    routes,
    cotangent,
    gains,
    attention_in,
    attention_out,
    router_weight,
    shared_in,
    shared_down,
    expert_in,
    expert_down,
    model_stats,
    head_stats,
    value_columns,
    hidden_stats,
    router_state,
    expert_model_stats,
    expert_hidden_stats,
):
    block_len = layer_input.shape[1]
    model_width = layer_input.shape[2]
    experts = router_weight.shape[1]
    dense_experts = False
    capacity = min(block_len, 4 * block_len // experts)
    ctx_index = lax.axis_index("ctx")
    tp_index = lax.axis_index("tp")
    fsdp_index = lax.axis_index("fsdp")
    shard_index = lax.axis_index(("fsdp", "ctx"))
    shard_count = lax.axis_size(("fsdp", "ctx"))
    ctx_count = lax.axis_size("ctx")
    base_pos = ctx_index * block_len
    low = lambda v: v.astype(jnp.bfloat16)
    gain_low, attn_in_low, attn_out_low, router_low = gather_packed(
        [(low(gains), 1), (low(attention_in), 0), (low(attention_out), 1), (low(router_weight), 0)],
        ("fsdp", "ctx"),
        shard_count <= 8,
    )
    later = [
        (low(shared_in), 0),
        (low(shared_down), 1),
    ]
    if dense_experts:
        later += [(low(expert_in), 0), (low(expert_down), 0)]
    later_full = gather_packed(later, ("fsdp", "ctx"))
    shared_in_low, shared_down_low = later_full[:2]
    if dense_experts:
        fe_local = expert_down.shape[1]
        expert_in_all = later_full[2].reshape(experts, model_width, 2, fe_local)
        expert_down_all = (
            later_full[3]
            .reshape(experts, ctx_count, fe_local, model_width // ctx_count)
            .transpose(0, 2, 1, 3)
            .reshape(experts, fe_local, model_width)
        )
    else:
        expert_in_low = lax.all_gather(low(expert_in), "ctx", axis=1, tiled=True)[0]
        expert_down_low = lax.all_gather(low(expert_down), "ctx", axis=2, tiled=True)[0]
    residual = layer_input[0].astype(jnp.float32)
    gain_one = gain_low[0].astype(jnp.float32)
    gain_two = gain_low[1].astype(jnp.float32)
    normed_one, norm_one_back = jax.vjp(rms_norm, residual, gain_one)
    normed_one = normed_one.astype(jnp.bfloat16)
    projected = jnp.einsum(
        "td,dgf->tgf", normed_one, attn_in_low, preferred_element_type=jnp.float32
    )
    local_cols = projected.shape[2]
    local_heads = local_cols // HD
    half_dim = HD // 2
    frequency = 10000.0 ** (-jnp.arange(half_dim, dtype=jnp.float32) / half_dim)
    angles = (base_pos + jnp.arange(block_len, dtype=jnp.int32)).astype(jnp.float32)[
        :, None
    ] * frequency[None, :]
    cosine = jnp.cos(angles)
    sine_tab = jnp.sin(angles)
    queries = rotate(projected[:, 0].reshape(block_len, local_heads, HD), cosine, sine_tab).astype(
        jnp.bfloat16
    )
    keys_own = rotate(projected[:, 1].reshape(block_len, local_heads, HD), cosine, sine_tab).astype(
        jnp.bfloat16
    )
    values_own = projected[:, 2].reshape(block_len, local_heads, HD).astype(jnp.bfloat16)
    seg_own = segments[0].astype(jnp.bfloat16)
    keys_prev, values_prev, seg_prev = from_behind((keys_own, values_own, seg_own), "ctx", 1)
    keys_ext = jnp.concatenate([keys_prev, keys_own], axis=0)
    values_ext = jnp.concatenate([values_prev, values_own], axis=0)
    seg_ext = jnp.concatenate([seg_prev, seg_own], axis=0)
    block_rows = min(512, block_len)
    block_total = block_len // block_rows
    starts = jnp.arange(block_total, dtype=jnp.int32) * block_rows

    def forward_block(start_row):
        query_rows, key_rows, value_rows, masked, allowed = block_view(
            queries, keys_ext, values_ext, seg_own, seg_ext, start_row, base_pos
        )
        row_max = jnp.max(masked, axis=-1, keepdims=True)
        exp_terms = jnp.where(allowed[None], jnp.exp(masked - row_max), 0.0)
        row_total = jnp.sum(exp_terms, axis=-1, keepdims=True)
        attn_probs = (exp_terms / row_total).astype(jnp.bfloat16)
        attended = jnp.einsum(
            "hqk,khd->qhd", attn_probs, value_rows, preferred_element_type=jnp.float32
        )
        return (attended, row_max + jnp.log(row_total))

    attended, log_totals = lax.map(forward_block, starts)
    mixed_heads = attended.reshape(block_len, local_cols).astype(jnp.bfloat16)
    attn_total = lax.psum(
        jnp.dot(mixed_heads, attn_out_low, preferred_element_type=jnp.float32), "tp"
    )
    after_attn = residual + attn_total
    normed_two, norm_two_back = jax.vjp(rms_norm, after_attn, gain_two)
    normed_two = normed_two.astype(jnp.bfloat16)
    logits = jnp.dot(normed_two, router_low, preferred_element_type=jnp.float32)
    route_rows = routes[0]
    onehot = (route_rows[:, :, None] == jnp.arange(experts, dtype=jnp.int32)[None, None, :]).astype(
        jnp.float32
    )
    picked = jnp.sum(onehot * logits[:, None, :], axis=-1)
    gate_probs = jax.nn.softmax(picked, axis=-1)
    upstream = cotangent[0]
    grad_out = upstream.astype(jnp.float32)
    if dense_experts:
        weights = jnp.sum(gate_probs[:, :, None] * onehot, axis=1)
        combined, dots_e, grad_rows, grad_expert_in, grad_expert_down = experts_dense(
            normed_two, grad_out, weights, expert_in_all, expert_down_all
        )
        gate_dots = jnp.sum(onehot * dots_e[:, None, :], axis=-1)
    else:
        combined, gate_dots, grad_rows, grad_expert_in, grad_expert_down = experts_routed(
            normed_two,
            grad_out,
            route_rows,
            gate_probs,
            expert_in_low,
            expert_down_low,
            capacity,
        )
    shared_gate_up = jnp.einsum(
        "td,dgf->tgf", normed_two, shared_in_low, preferred_element_type=jnp.float32
    )
    shared_act, shared_act_back = jax.vjp(swiglu, shared_gate_up)
    shared_hidden = shared_act.astype(jnp.bfloat16)
    shared_out = jnp.dot(shared_hidden, shared_down_low, preferred_element_type=jnp.float32)
    grad_shared_hidden = jnp.einsum(
        "td,fd->tf", upstream, shared_down_low, preferred_element_type=jnp.float32
    )
    grad_shared_gate_up = shared_act_back(grad_shared_hidden)[0].astype(jnp.bfloat16)
    partial_two = (
        jnp.einsum(
            "tgf,dgf->td", grad_shared_gate_up, shared_in_low, preferred_element_type=jnp.float32
        )
        + grad_rows
    )
    branch_total, grad_normed_part, gate_total = lax.psum(
        (shared_out + combined, partial_two, gate_dots), "tp"
    )
    layer_out = after_attn + branch_total
    grad_picked = gate_probs * (
        gate_total - jnp.sum(gate_probs * gate_total, axis=-1, keepdims=True)
    )
    grad_logits = jnp.sum(grad_picked[:, :, None] * onehot, axis=1).astype(jnp.bfloat16)
    grad_shared_in = jnp.einsum(
        "td,tgf->dgf", normed_two, grad_shared_gate_up, preferred_element_type=jnp.float32
    )
    grad_shared_down = jnp.einsum(
        "tf,td->fd", shared_hidden, upstream, preferred_element_type=jnp.float32
    )
    grad_router = jnp.einsum(
        "td,te->de", normed_two, grad_logits, preferred_element_type=jnp.float32
    )
    grad_normed_two = grad_normed_part + jnp.einsum(
        "te,de->td", grad_logits, router_low, preferred_element_type=jnp.float32
    )
    grad_after, grad_gain_two = norm_two_back(grad_normed_two)
    grad_after = grad_after + grad_out
    grad_attn_low = grad_after.astype(jnp.bfloat16)
    grad_attn_out = jnp.einsum(
        "tc,td->cd", mixed_heads, grad_attn_low, preferred_element_type=jnp.float32
    )
    first_grads = [
        (grad_attn_out, 1),
        (grad_router, 0),
        (grad_shared_in, 0),
        (grad_shared_down, 1),
        (grad_gain_two, 0),
    ]
    if dense_experts:
        fe_local = expert_down.shape[1]
        first_grads += [
            (grad_expert_in.reshape(shard_count * expert_in.shape[1], 2, fe_local), 0),
            (
                grad_expert_down.reshape(experts, fe_local, ctx_count, model_width // ctx_count)
                .transpose(0, 2, 1, 3)
                .reshape(shard_count * fe_local, model_width // ctx_count),
                0,
            ),
        ]
    if not dense_experts:
        own_expert_in = lax.psum_scatter(grad_expert_in[None], "ctx", scatter_dimension=1, tiled=True)
        own_expert_down = lax.psum_scatter(
            grad_expert_down[None], "ctx", scatter_dimension=2, tiled=True
        )
    grad_heads = (
        jnp.einsum("td,cd->tc", grad_attn_low, attn_out_low, preferred_element_type=jnp.float32)
        .astype(jnp.bfloat16)
        .reshape(block_len, local_heads, HD)
    )

    def backward_block(block_number, running):
        grad_keys, grad_values, grad_queries = running
        start_row = block_number * block_rows
        query_rows, key_rows, value_rows, masked, allowed = block_view(
            queries, keys_ext, values_ext, seg_own, seg_ext, start_row, base_pos
        )
        log_total = lax.dynamic_index_in_dim(log_totals, block_number, 0, keepdims=False)
        attn_probs = jnp.where(allowed[None], jnp.exp(masked - log_total), 0.0)
        grad_block = lax.dynamic_slice_in_dim(grad_heads, start_row, block_rows, 0)
        grad_probs = jnp.einsum(
            "qhd,khd->hqk", grad_block, value_rows, preferred_element_type=jnp.float32
        )
        inner_sum = jnp.sum(attn_probs * grad_probs, axis=-1, keepdims=True)
        grad_scores = (attn_probs * (grad_probs - inner_sum)).astype(jnp.bfloat16)
        grad_query_rows = (
            jnp.einsum("hqk,khd->qhd", grad_scores, key_rows, preferred_element_type=jnp.float32)
            * 0.125
        )
        grad_key_rows = (
            jnp.einsum("hqk,qhd->khd", grad_scores, query_rows, preferred_element_type=jnp.float32)
            * 0.125
        )
        grad_value_rows = jnp.einsum(
            "hqk,qhd->khd",
            attn_probs.astype(jnp.bfloat16),
            grad_block,
            preferred_element_type=jnp.float32,
        )
        key_offset = start_row + block_len - WINDOW
        grad_keys = lax.dynamic_update_slice_in_dim(
            grad_keys,
            lax.dynamic_slice_in_dim(grad_keys, key_offset, block_rows + WINDOW, 0) + grad_key_rows,
            key_offset,
            0,
        )
        grad_values = lax.dynamic_update_slice_in_dim(
            grad_values,
            lax.dynamic_slice_in_dim(grad_values, key_offset, block_rows + WINDOW, 0)
            + grad_value_rows,
            key_offset,
            0,
        )
        grad_queries = lax.dynamic_update_slice_in_dim(grad_queries, grad_query_rows, start_row, 0)
        return (grad_keys, grad_values, grad_queries)

    zero_ext = jnp.zeros((2 * block_len, local_heads, HD), jnp.float32)
    zero_own = jnp.zeros((block_len, local_heads, HD), jnp.float32)
    grad_keys, grad_values, grad_queries = lax.fori_loop(
        0, block_total, backward_block, (zero_ext, zero_ext, zero_own)
    )
    rim_keys, rim_values = (
        from_behind(grad_keys[:block_len].astype(jnp.bfloat16), "ctx", -1).astype(jnp.float32),
        from_behind(grad_values[:block_len].astype(jnp.bfloat16), "ctx", -1).astype(jnp.float32),
    )
    grad_keys_own = grad_keys[block_len:] + rim_keys
    grad_values_own = grad_values[block_len:] + rim_values
    grad_query_raw = rotate(grad_queries, cosine, -sine_tab)
    grad_key_raw = rotate(grad_keys_own, cosine, -sine_tab)
    grad_projected = (
        jnp.stack([grad_query_raw, grad_key_raw, grad_values_own], axis=1)
        .reshape(block_len, 3, local_cols)
        .astype(jnp.bfloat16)
    )
    grad_attn_in = jnp.einsum(
        "td,tgf->dgf", normed_one, grad_projected, preferred_element_type=jnp.float32
    )
    partial_one = jnp.einsum(
        "tgf,dgf->td", grad_projected, attn_in_low, preferred_element_type=jnp.float32
    )
    tp_one = lax.psum(partial_one, "tp")
    halving = lax.axis_size("fsdp") == 4 and ctx_count == 2
    all_own = scatter_packed(
        first_grads + [(grad_attn_in, 0)],
        ("fsdp", "ctx"),
        shard_count,
        halving,
    )
    own_attn_out, own_router, own_shared_in, own_shared_down, own_gain_two = all_own[:5]
    own_attn_in = all_own[-1]
    grad_residual, grad_gain_one = norm_one_back(tp_one + 0.0 * own_attn_in[0, 0, 0])
    input_grad = grad_after + grad_residual
    if dense_experts:
        own_expert_in = all_own[5][None]
        own_expert_down = all_own[6][None]
    lead_tp = (tp_index == 0).astype(jnp.float32)
    first_shard = (shard_index == 0).astype(jnp.float32)
    first_ctx = (ctx_index == 0).astype(jnp.float32)
    d_local = gains.shape[1]
    ff_local = shared_down.shape[0]
    fe_local = expert_down.shape[1]
    d_quarter = expert_in.shape[1]
    square_attn_in = own_attn_in * own_attn_in + TINY_SQUARE
    square_attn_out = own_attn_out * own_attn_out + TINY_SQUARE
    square_shared_in = own_shared_in * own_shared_in + TINY_SQUARE
    square_shared_down = own_shared_down * own_shared_down + TINY_SQUARE
    square_expert_in = own_expert_in[0] * own_expert_in[0] + TINY_SQUARE
    square_expert_down = own_expert_down[0] * own_expert_down[0] + TINY_SQUARE
    model_part = lax.dynamic_update_slice(
        jnp.zeros((4, D), jnp.float32),
        jnp.stack(
            [
                jnp.sum(square_attn_in, axis=(1, 2)),
                jnp.sum(square_shared_in, axis=(1, 2)),
                jnp.sum(square_attn_out, axis=0),
                jnp.sum(square_shared_down, axis=0),
            ]
        ),
        (0, shard_index * d_local),
    )
    head_part = lax.dynamic_update_slice(
        jnp.zeros((4, HH), jnp.float32),
        jnp.concatenate(
            [jnp.sum(square_attn_in, axis=0), jnp.sum(square_attn_out, axis=1)[None]], axis=0
        ),
        (0, tp_index * local_cols),
    )
    hidden_part = lax.dynamic_update_slice(
        jnp.zeros((3, FF), jnp.float32),
        jnp.concatenate(
            [jnp.sum(square_shared_in, axis=0), jnp.sum(square_shared_down, axis=1)[None]], axis=0
        ),
        (0, tp_index * ff_local),
    )
    expert_model_part = lax.dynamic_update_slice(
        jnp.zeros((experts, 2, D), jnp.float32),
        jnp.stack([jnp.sum(square_expert_in, axis=(1, 2)), jnp.sum(square_expert_down, axis=0)])[
            None
        ],
        (fsdp_index, 0, ctx_index * d_quarter),
    )
    expert_hidden_part = lax.dynamic_update_slice(
        jnp.zeros((experts, 3, FE), jnp.float32),
        jnp.concatenate(
            [jnp.sum(square_expert_in, axis=0), jnp.sum(square_expert_down, axis=1)[None]], axis=0
        )[None],
        (fsdp_index, 0, tp_index * fe_local),
    )
    scalar_part = jnp.stack(
        [
            lead_tp * jnp.sum(gains * gains),
            jnp.sum(attention_in * attention_in),
            jnp.sum(attention_out * attention_out),
            lead_tp * jnp.sum(router_weight * router_weight),
            jnp.sum(shared_in * shared_in),
            jnp.sum(shared_down * shared_down),
            jnp.sum(expert_in * expert_in),
            jnp.sum(expert_down * expert_down),
            lead_tp * jnp.sum(model_stats[2]),
            first_shard * jnp.sum(head_stats[2]),
            lead_tp * jnp.sum(model_stats[3]),
            first_shard * jnp.sum(hidden_stats[2]),
        ]
    )
    expert_old_part = lax.dynamic_update_slice(
        jnp.zeros((2, experts), jnp.float32),
        jnp.stack(
            [
                lead_tp * jnp.sum(expert_model_stats[0, 0]),
                first_ctx * jnp.sum(expert_hidden_stats[0, 2]),
            ]
        )[:, None],
        (0, fsdp_index),
    )
    global_sums = butterfly_sum(
        [
            model_part,
            head_part,
            hidden_part,
            expert_model_part,
            expert_hidden_part,
            scalar_part,
            expert_old_part,
            lead_tp * grad_gain_one,
        ],
        1,
    )
    (
        model_sum,
        head_sum,
        hidden_sum,
        expert_model_sum,
        expert_hidden_sum,
        scalar_sum,
        expert_old_sum,
        gain_one_sum,
    ) = global_sums
    own_gain_one = lax.dynamic_slice_in_dim(gain_one_sum, shard_index * d_local, d_local)
    own_gains = jnp.stack([own_gain_one, own_gain_two])
    shard_start = shard_index * d_local
    gain_state = DECAY_RATE * model_stats[0:2] + (1.0 - DECAY_RATE) * (
        own_gains * own_gains + TINY_SQUARE
    )
    update_gains = own_gains * lax.rsqrt(gain_state)
    router_new = DECAY_RATE * router_state + (1.0 - DECAY_RATE) * (
        own_router * own_router + TINY_SQUARE
    )
    update_router = own_router * lax.rsqrt(router_new)
    attn_cols_old = jnp.concatenate([head_stats[0:2], value_columns[None]], axis=0).reshape(-1)
    update_attn_in, rows_attn_in, cols_attn_in = factored_update(
        own_attn_in.reshape(d_local, 3 * local_cols),
        model_stats[2],
        attn_cols_old,
        lax.dynamic_slice_in_dim(model_sum[0], shard_start, d_local),
        lax.dynamic_slice_in_dim(head_sum[0:3], tp_index * local_cols, local_cols, 1).reshape(-1),
        D,
        3 * HH,
        scalar_sum[8],
        jnp.sum(model_sum[0]),
    )
    update_attn_out, rows_attn_out, cols_attn_out = factored_update(
        own_attn_out,
        head_stats[2],
        model_stats[4],
        lax.dynamic_slice_in_dim(head_sum[3], tp_index * local_cols, local_cols),
        lax.dynamic_slice_in_dim(model_sum[2], shard_start, d_local),
        HH,
        D,
        scalar_sum[9],
        jnp.sum(head_sum[3]),
    )
    update_shared_in, rows_shared_in, cols_shared_in = factored_update(
        own_shared_in.reshape(d_local, 2 * ff_local),
        model_stats[3],
        hidden_stats[0:2].reshape(-1),
        lax.dynamic_slice_in_dim(model_sum[1], shard_start, d_local),
        lax.dynamic_slice_in_dim(hidden_sum[0:2], tp_index * ff_local, ff_local, 1).reshape(-1),
        D,
        2 * FF,
        scalar_sum[10],
        jnp.sum(model_sum[1]),
    )
    update_shared_down, rows_shared_down, cols_shared_down = factored_update(
        own_shared_down,
        hidden_stats[2],
        model_stats[5],
        lax.dynamic_slice_in_dim(hidden_sum[2], tp_index * ff_local, ff_local),
        lax.dynamic_slice_in_dim(model_sum[3], shard_start, d_local),
        FF,
        D,
        scalar_sum[11],
        jnp.sum(hidden_sum[2]),
    )
    own_expert_model = lax.dynamic_index_in_dim(expert_model_sum, fsdp_index, 0, keepdims=False)
    own_expert_hidden = lax.dynamic_index_in_dim(expert_hidden_sum, fsdp_index, 0, keepdims=False)
    old_expert_totals = lax.dynamic_index_in_dim(expert_old_sum, fsdp_index, 1, keepdims=False)
    update_expert_in, rows_expert_in, cols_expert_in = factored_update(
        own_expert_in[0].reshape(d_quarter, 2 * fe_local),
        expert_model_stats[0, 0],
        expert_hidden_stats[0, 0:2].reshape(-1),
        lax.dynamic_slice_in_dim(own_expert_model[0], ctx_index * d_quarter, d_quarter),
        lax.dynamic_slice_in_dim(own_expert_hidden[0:2], tp_index * fe_local, fe_local, 1).reshape(
            -1
        ),
        D,
        2 * FE,
        old_expert_totals[0],
        jnp.sum(own_expert_model[0]),
    )
    update_expert_down, rows_expert_down, cols_expert_down = factored_update(
        own_expert_down[0],
        expert_hidden_stats[0, 2],
        expert_model_stats[0, 1],
        lax.dynamic_slice_in_dim(own_expert_hidden[2], tp_index * fe_local, fe_local),
        lax.dynamic_slice_in_dim(own_expert_model[1], ctx_index * d_quarter, d_quarter),
        FE,
        D,
        old_expert_totals[1],
        jnp.sum(own_expert_hidden[2]),
    )
    clip_part = jnp.stack(
        [
            lead_tp * jnp.sum(update_gains * update_gains),
            jnp.sum(update_attn_in * update_attn_in),
            jnp.sum(update_attn_out * update_attn_out),
            lead_tp * jnp.sum(update_router * update_router),
            jnp.sum(update_shared_in * update_shared_in),
            jnp.sum(update_shared_down * update_shared_down),
            jnp.sum(update_expert_in * update_expert_in),
            jnp.sum(update_expert_down * update_expert_down),
        ]
    )
    clip_total = butterfly_sum([clip_part], 2)[0]
    elements = jnp.array(
        [
            2 * D,
            D * 3 * HH,
            HH * D,
            D * experts,
            D * 2 * FF,
            FF * D,
            experts * D * 2 * FE,
            experts * FE * D,
        ],
        jnp.float32,
    )
    update_roots = jnp.sqrt(clip_total / elements)
    new_gains = apply_update(gains, update_gains, update_roots[0], scalar_sum[0], elements[0])
    new_attn_in = apply_update(
        attention_in,
        update_attn_in.reshape(attention_in.shape),
        update_roots[1],
        scalar_sum[1],
        elements[1],
    )
    new_attn_out = apply_update(
        attention_out, update_attn_out, update_roots[2], scalar_sum[2], elements[2]
    )
    new_router = apply_update(
        router_weight, update_router, update_roots[3], scalar_sum[3], elements[3]
    )
    new_shared_in = apply_update(
        shared_in,
        update_shared_in.reshape(shared_in.shape),
        update_roots[4],
        scalar_sum[4],
        elements[4],
    )
    new_shared_down = apply_update(
        shared_down, update_shared_down, update_roots[5], scalar_sum[5], elements[5]
    )
    new_expert_in = apply_update(
        expert_in,
        update_expert_in.reshape(expert_in.shape),
        update_roots[6],
        scalar_sum[6],
        elements[6],
    )
    new_expert_down = apply_update(
        expert_down,
        update_expert_down.reshape(expert_down.shape),
        update_roots[7],
        scalar_sum[7],
        elements[7],
    )
    new_model_stats = jnp.concatenate(
        [gain_state, jnp.stack([rows_attn_in, rows_shared_in, cols_attn_out, cols_shared_down])],
        axis=0,
    )
    attn_cols_new = cols_attn_in.reshape(3, local_cols)
    new_head_stats = jnp.concatenate([attn_cols_new[0:2], rows_attn_out[None]], axis=0)
    new_value_columns = attn_cols_new[2]
    new_hidden_stats = jnp.concatenate(
        [cols_shared_in.reshape(2, ff_local), rows_shared_down[None]], axis=0
    )
    new_expert_model_stats = jnp.stack([rows_expert_in, cols_expert_down])[None]
    new_expert_hidden_stats = jnp.concatenate(
        [cols_expert_in.reshape(2, fe_local), rows_expert_down[None]], axis=0
    )[None]
    return (
        layer_out.astype(jnp.bfloat16)[None],
        input_grad[None],
        own_gains,
        own_attn_in,
        own_attn_out,
        own_router,
        own_shared_in,
        own_shared_down,
        own_expert_in,
        own_expert_down,
        new_gains,
        new_attn_in,
        new_attn_out,
        new_router,
        new_shared_in,
        new_shared_down,
        new_expert_in,
        new_expert_down,
        new_model_stats,
        new_head_stats,
        new_value_columns,
        new_hidden_stats,
        router_new,
        new_expert_model_stats,
        new_expert_hidden_stats,
        update_roots,
    )


def solution(mesh):
    in_specs = (
        P("fsdp", "ctx", None),
        P("fsdp", "ctx"),
        P("fsdp", "ctx", None),
        P("fsdp", "ctx", None),
        P(None, ("fsdp", "ctx")),
        P(("fsdp", "ctx"), None, "tp"),
        P("tp", ("fsdp", "ctx")),
        P(("fsdp", "ctx"), None),
        P(("fsdp", "ctx"), None, "tp"),
        P("tp", ("fsdp", "ctx")),
        P("fsdp", "ctx", None, "tp"),
        P("fsdp", "tp", "ctx"),
        P(None, ("fsdp", "ctx")),
        P(None, "tp"),
        P("tp"),
        P(None, "tp"),
        P(("fsdp", "ctx"), None),
        P("fsdp", None, "ctx"),
        P("fsdp", None, "tp"),
    )
    out_specs = (
        P("fsdp", "ctx", None),
        P("fsdp", "ctx", None),
        P(None, ("fsdp", "ctx")),
        P(("fsdp", "ctx"), None, "tp"),
        P("tp", ("fsdp", "ctx")),
        P(("fsdp", "ctx"), None),
        P(("fsdp", "ctx"), None, "tp"),
        P("tp", ("fsdp", "ctx")),
        P("fsdp", "ctx", None, "tp"),
        P("fsdp", "tp", "ctx"),
        P(None, ("fsdp", "ctx")),
        P(("fsdp", "ctx"), None, "tp"),
        P("tp", ("fsdp", "ctx")),
        P(("fsdp", "ctx"), None),
        P(("fsdp", "ctx"), None, "tp"),
        P("tp", ("fsdp", "ctx")),
        P("fsdp", "ctx", None, "tp"),
        P("fsdp", "tp", "ctx"),
        P(None, ("fsdp", "ctx")),
        P(None, "tp"),
        P("tp"),
        P(None, "tp"),
        P(("fsdp", "ctx"), None),
        P("fsdp", None, "ctx"),
        P("fsdp", None, "tp"),
        P(),
    )
    return jax.shard_map(local, mesh=mesh, in_specs=in_specs, out_specs=out_specs, check_vma=False)
```

```python
import jax
import jax.numpy as jnp
from jax import lax
from jax.sharding import PartitionSpec as P
from jax.experimental import pallas as pl
from jax.experimental.pallas import tpu as pltpu

D = 768
HD = 64
FF = 2048
FE = 2048
WINDOW = 1024
HH = 768


EPSILON = 1e-06
TINY_SQUARE = 1e-30
SCALE_FLOOR = 0.001
DECAY_RATE = 0.5
CLIP_LIMIT = 0.5
STEP_RATE = 0.5


def from_behind(value, axis, steps):
    count = lax.axis_size(axis)
    leading, last = (max(0, -steps), min(count, count - steps))
    return lax.ppermute(value, axis, [(source, source + steps) for source in range(leading, last)])


def rms_norm(values, gain_vec):
    inv_rms = lax.rsqrt(jnp.mean(values * values, axis=-1, keepdims=True) + EPSILON)
    return values * inv_rms * gain_vec


def swiglu(gate_up):
    return jax.nn.silu(gate_up[:, 0]) * gate_up[:, 1]


def rotate(values, cosine, sine_tab):
    half_dim = values.shape[-1] // 2
    first_half = values[..., :half_dim]
    second_half = values[..., half_dim:]
    cos_b = cosine[:, None, :]
    sin_b = sine_tab[:, None, :]
    return jnp.concatenate(
        [first_half * cos_b - second_half * sin_b, second_half * cos_b + first_half * sin_b],
        axis=-1,
    )


def slot_tables(block_routes, experts, capacity):
    flat_routes = block_routes.reshape(-1)
    route_count = flat_routes.shape[0]
    onehot = (flat_routes[:, None] == jnp.arange(experts, dtype=jnp.int32)[None, :]).astype(
        jnp.int32
    )
    rank_in = jnp.sum(
        (jnp.cumsum(onehot, axis=0, dtype=jnp.int32) - 1) * onehot, axis=1, dtype=jnp.int32
    )
    slot_index = flat_routes * capacity + rank_in
    owner_route = (
        jnp.zeros((experts * capacity,), jnp.int32)
        .at[slot_index]
        .set(jnp.arange(route_count, dtype=jnp.int32))
    )
    filled = jnp.zeros((experts * capacity,), jnp.int32).at[slot_index].set(1)
    return (slot_index, owner_route, filled)


def block_view(queries, keys_ext, values_ext, seg_own, seg_ext, start_row, base_pos):
    block_len = queries.shape[0]
    block_rows = min(512, block_len)
    query_rows = lax.dynamic_slice_in_dim(queries, start_row, block_rows, 0)
    key_rows = lax.dynamic_slice_in_dim(
        keys_ext, start_row + block_len - WINDOW, block_rows + WINDOW, 0
    )
    value_rows = lax.dynamic_slice_in_dim(
        values_ext, start_row + block_len - WINDOW, block_rows + WINDOW, 0
    )
    scores = (
        jnp.einsum("qhd,khd->hqk", query_rows, key_rows, preferred_element_type=jnp.float32) * 0.125
    )
    query_pos = start_row + jnp.arange(block_rows, dtype=jnp.int32)
    key_pos = start_row - WINDOW + jnp.arange(block_rows + WINDOW, dtype=jnp.int32)
    distance = query_pos[:, None] - key_pos[None, :]
    seg_query = lax.dynamic_slice_in_dim(seg_own, start_row, block_rows, 0)
    seg_key = lax.dynamic_slice_in_dim(
        seg_ext, start_row + block_len - WINDOW, block_rows + WINDOW, 0
    )
    allowed = (
        (distance >= 0)
        & (distance < WINDOW)
        & (seg_query[:, None] == seg_key[None, :])
        & (key_pos[None, :] + base_pos >= 0)
    )
    return (query_rows, key_rows, value_rows, jnp.where(allowed[None], scores, -1e30), allowed)


def factored_update(
    grad_mat, rows_old, cols_old, row_sums, col_sums, row_total, col_total, old_total, square_total
):
    rows_new = DECAY_RATE * rows_old + (1.0 - DECAY_RATE) * row_sums / col_total
    cols_new = DECAY_RATE * cols_old + (1.0 - DECAY_RATE) * col_sums / row_total
    mean_rows = (DECAY_RATE * old_total + (1.0 - DECAY_RATE) * square_total / col_total) / row_total
    second_moment = rows_new[:, None] * cols_new[None, :] / mean_rows
    return (grad_mat * lax.rsqrt(second_moment), rows_new, cols_new)


def apply_update(weight, update, update_root, square_sum, elements):
    param_scale = jnp.maximum(SCALE_FLOOR, jnp.sqrt(square_sum / elements))
    return weight - STEP_RATE * param_scale * update / jnp.maximum(1.0, update_root / CLIP_LIMIT)


def butterfly_partners():
    partners = []
    here = [lax.axis_index(name) for name in ("fsdp", "ctx", "tp")]
    for axis_number, name in enumerate(("fsdp", "ctx", "tp")):
        size = lax.axis_size(name)
        step = 1
        while step < size:
            bit = (here[axis_number] // step) % 2
            other = list(here)
            other[axis_number] = here[axis_number] + step * (1 - 2 * bit)
            partners.append(tuple(other))
            step *= 2
    return partners


def butterfly_kernel(x_ref, o_ref, stage, inbox, send_sems, recv_sems):
    partners = butterfly_partners()
    barrier = pltpu.get_barrier_semaphore()
    for partner in partners:
        pl.semaphore_signal(
            barrier, 1, device_id=partner, device_id_type=pl.DeviceIdType.MESH
        )
    pl.semaphore_wait(barrier, len(partners))
    acc = x_ref[...]
    for round_number, partner in enumerate(partners):
        stage[round_number] = acc
        copy = pltpu.make_async_remote_copy(
            src_ref=stage.at[round_number],
            dst_ref=inbox.at[round_number],
            send_sem=send_sems.at[round_number],
            recv_sem=recv_sems.at[round_number],
            device_id=partner,
            device_id_type=pl.DeviceIdType.MESH,
        )
        copy.start()
        copy.wait()
        acc = stage[round_number] + inbox[round_number]
    o_ref[...] = acc


def butterfly_sum(values, collective_id):
    flat = jnp.concatenate([v.reshape(-1).astype(jnp.float32) for v in values])
    size = flat.shape[0]
    rows = -(-size // 1024) * 8
    block = jnp.pad(flat, (0, rows * 128 - size)).reshape(rows, 128)
    rounds = sum(
        max(1, lax.axis_size(name)).bit_length() - 1 for name in ("fsdp", "ctx", "tp")
    )
    total = pl.pallas_call(
        butterfly_kernel,
        out_shape=jax.ShapeDtypeStruct((rows, 128), jnp.float32),
        in_specs=[pl.BlockSpec(memory_space=pltpu.VMEM)],
        out_specs=pl.BlockSpec(memory_space=pltpu.VMEM),
        scratch_shapes=[
            pltpu.VMEM((rounds, rows, 128), jnp.float32),
            pltpu.VMEM((rounds, rows, 128), jnp.float32),
            pltpu.SemaphoreType.DMA((rounds,)),
            pltpu.SemaphoreType.DMA((rounds,)),
        ],
        compiler_params=pltpu.CompilerParams(collective_id=collective_id, has_side_effects=True),
    )(block).reshape(-1)
    results = []
    offset = 0
    for v in values:
        results.append(total[offset : offset + v.size].reshape(v.shape))
        offset += v.size
    return results


def halving_kernel(
    x_ref, o_ref, stage_a, stage_a2, stage_b, stage_b2, in_a1, in_a2, in_a3, in_b1, in_b2, in_b3, sems
):
    rows = o_ref.shape[0] // 2
    chunk = 64
    fsdp_here = lax.axis_index("fsdp")
    ctx_here = lax.axis_index("ctx")
    tp_here = lax.axis_index("tp")
    bit_low = fsdp_here % 2
    bit_high = (fsdp_here // 2) % 2
    partners = [
        (fsdp_here, 1 - ctx_here, tp_here),
        (fsdp_here + 1 - 2 * bit_low, ctx_here, tp_here),
        (fsdp_here + 2 - 4 * bit_high, ctx_here, tp_here),
    ]
    barrier = pltpu.get_barrier_semaphore()
    for partner in partners:
        pl.semaphore_signal(barrier, 1, device_id=partner, device_id_type=pl.DeviceIdType.MESH)
    pl.semaphore_wait(barrier, len(partners))
    first, second = pl.ds(0, rows), pl.ds(rows, rows)

    def swap_pair(sources, targets, number, partner_pair):
        copies = []
        for index in range(2):
            copy = pltpu.make_async_remote_copy(
                src_ref=sources[index],
                dst_ref=targets[index],
                send_sem=sems.at[0, 2 * number + index],
                recv_sem=sems.at[1, 2 * number + index],
                device_id=partner_pair[index],
                device_id_type=pl.DeviceIdType.MESH,
            )
            copy.start()
            copies.append(copy)
        for copy in copies:
            copy.wait()

    def each_chunk(body):
        @pl.loop(0, rows // chunk)
        def _(step):
            body(pl.ds(pl.multiple_of(step * chunk, chunk), chunk))

    swap_pair(
        [
            x_ref.at[:, :, pl.ds(1 - ctx_here, 1), first],
            x_ref.at[:, pl.ds(1 - bit_low, 1), :, second],
        ],
        [in_a1, in_b1],
        0,
        [partners[0], partners[1]],
    )

    def round_one(part):
        shifted = pl.ds(part.start + rows, chunk)
        for high in range(2):
            for other in range(2):
                stage_a[high, other, part] = (
                    x_ref[high, other, ctx_here, part] + in_a1[high, other, 0, part]
                )
                stage_b[high, other, part] = (
                    x_ref[high, bit_low, other, shifted] + in_b1[high, 0, other, part]
                )

    each_chunk(round_one)
    swap_pair(
        [stage_a.at[:, pl.ds(1 - bit_low, 1)], stage_b.at[:, pl.ds(1 - ctx_here, 1)]],
        [in_a2, in_b2],
        1,
        [partners[1], partners[0]],
    )

    def round_two(part):
        for high in range(2):
            stage_a2[high, part] = stage_a[high, bit_low, part] + in_a2[high, 0, part]
            stage_b2[high, part] = stage_b[high, ctx_here, part] + in_b2[high, 0, part]

    each_chunk(round_two)
    swap_pair(
        [stage_a2.at[pl.ds(1 - bit_high, 1)], stage_b2.at[pl.ds(1 - bit_high, 1)]],
        [in_a3, in_b3],
        2,
        [partners[2], partners[2]],
    )

    def round_three(part):
        o_ref[part] = stage_a2[bit_high, part] + in_a3[0, part]
        o_ref[pl.ds(part.start + rows, chunk)] = stage_b2[bit_high, part] + in_b3[0, part]

    each_chunk(round_three)


def halving_scatter(packed, collective_id):
    count, width = packed.shape
    rows = -(-width // (128 * 128)) * 64
    block = jnp.pad(packed, ((0, 0), (0, 2 * rows * 128 - width))).reshape(
        2, 2, 2, 2 * rows, 128
    )
    own = pl.pallas_call(
        halving_kernel,
        out_shape=jax.ShapeDtypeStruct((2 * rows, 128), jnp.float32),
        in_specs=[pl.BlockSpec(memory_space=pltpu.VMEM)],
        out_specs=pl.BlockSpec(memory_space=pltpu.VMEM),
        scratch_shapes=[
            pltpu.VMEM((2, 2, rows, 128), jnp.float32),
            pltpu.VMEM((2, rows, 128), jnp.float32),
            pltpu.VMEM((2, 2, rows, 128), jnp.float32),
            pltpu.VMEM((2, rows, 128), jnp.float32),
            pltpu.VMEM((2, 2, 1, rows, 128), jnp.float32),
            pltpu.VMEM((2, 1, rows, 128), jnp.float32),
            pltpu.VMEM((1, rows, 128), jnp.float32),
            pltpu.VMEM((2, 1, 2, rows, 128), jnp.float32),
            pltpu.VMEM((2, 1, rows, 128), jnp.float32),
            pltpu.VMEM((1, rows, 128), jnp.float32),
            pltpu.SemaphoreType.DMA((2, 6)),
        ],
        compiler_params=pltpu.CompilerParams(
            collective_id=collective_id, has_side_effects=True, vmem_limit_bytes=60 * 1024 * 1024
        ),
    )(block)
    return own.reshape(-1)[:width]

def gather_kernel(x_ref, o_ref, inbox, send_sems, recv_sems):
    fsdp_here = lax.axis_index("fsdp")
    ctx_here = lax.axis_index("ctx")
    tp_here = lax.axis_index("tp")
    ctx_count = lax.axis_size("ctx")
    count = lax.axis_size("fsdp") * ctx_count
    me = fsdp_here * ctx_count + ctx_here
    peers = []
    for offset in range(1, count):
        other = (me + offset) % count
        peers.append((other // ctx_count, other % ctx_count, tp_here))
    barrier = pltpu.get_barrier_semaphore()
    for peer in peers:
        pl.semaphore_signal(barrier, 1, device_id=peer, device_id_type=pl.DeviceIdType.MESH)
    pl.semaphore_wait(barrier, len(peers))
    copies = []
    for number, peer in enumerate(peers):
        copy = pltpu.make_async_remote_copy(
            src_ref=x_ref,
            dst_ref=inbox.at[me],
            send_sem=send_sems.at[number],
            recv_sem=recv_sems.at[me],
            device_id=peer,
            device_id_type=pl.DeviceIdType.MESH,
        )
        copy.start()
        copies.append(copy)
    o_ref[me] = x_ref[...]
    for copy in copies:
        copy.wait_send()
    for offset in range(1, count):
        source = (me + count - offset) % count
        pltpu.make_async_remote_copy(
            src_ref=x_ref,
            dst_ref=inbox.at[source],
            send_sem=send_sems.at[0],
            recv_sem=recv_sems.at[source],
            device_id=peers[0],
            device_id_type=pl.DeviceIdType.MESH,
        ).wait_recv()
        o_ref[source] = inbox[source]


def gather_shards(flat, collective_id):
    size = flat.shape[0]
    rows = -(-size // 2048) * 16
    block = jnp.pad(flat, (0, rows * 128 - size)).reshape(rows, 128)
    count = lax.axis_size("fsdp") * lax.axis_size("ctx")
    full = pl.pallas_call(
        gather_kernel,
        out_shape=jax.ShapeDtypeStruct((count, rows, 128), flat.dtype),
        in_specs=[pl.BlockSpec(memory_space=pltpu.VMEM)],
        out_specs=pl.BlockSpec(memory_space=pltpu.VMEM),
        scratch_shapes=[
            pltpu.VMEM((count, rows, 128), flat.dtype),
            pltpu.SemaphoreType.DMA((count - 1,)),
            pltpu.SemaphoreType.DMA((count,)),
        ],
        compiler_params=pltpu.CompilerParams(collective_id=collective_id, has_side_effects=True),
    )(block)
    return full.reshape(count, rows * 128)[:, :size]


def swiglu_experts(gate_up):
    return jax.nn.silu(gate_up[:, :, 0]) * gate_up[:, :, 1]


def gather_packed(pieces, axes, use_kernel=False):
    flat = jnp.concatenate([piece.reshape(-1) for piece, _ in pieces])
    if use_kernel:
        full = gather_shards(flat, 4)
    else:
        full = lax.all_gather(flat, axes, axis=0, tiled=False)
    count = full.shape[0]
    results = []
    offset = 0
    for piece, dim in pieces:
        size = piece.size
        part = full[:, offset : offset + size].reshape((count,) + piece.shape)
        offset += size
        part = jnp.moveaxis(part, 0, dim)
        shape = list(piece.shape)
        shape[dim] *= count
        results.append(part.reshape(shape))
    return results


def scatter_packed(pieces, axes, count, use_kernel=False):
    columns = []
    local_shapes = []
    for grad, dim in pieces:
        shape = grad.shape
        split = shape[:dim] + (count, shape[dim] // count) + shape[dim + 1 :]
        local_shapes.append(shape[:dim] + (shape[dim] // count,) + shape[dim + 1 :])
        part = jnp.moveaxis(grad.reshape(split), dim, 0)
        columns.append(part.reshape(count, -1))
    packed = jnp.concatenate(columns, axis=1)
    if use_kernel:
        own = halving_scatter(packed, 3)
    else:
        width = packed.shape[1]
        rows = -(-width // 1024) * 8
        packed = jnp.pad(packed, ((0, 0), (0, rows * 128 - width))).reshape(count * rows, 128)
        own = lax.psum_scatter(packed, axes, scatter_dimension=0, tiled=True).reshape(-1)
    results = []
    offset = 0
    for local_shape in local_shapes:
        size = 1
        for extent in local_shape:
            size *= extent
        results.append(own[offset : offset + size].reshape(local_shape))
        offset += size
    return results


def experts_dense(normed_two, grad_out, weights, expert_in_all, expert_down_all):
    gate_up = jnp.einsum(
        "td,edgf->etgf", normed_two, expert_in_all, preferred_element_type=jnp.float32
    )
    act, act_back = jax.vjp(swiglu_experts, gate_up)
    hidden = act.astype(jnp.bfloat16)
    outs = jnp.einsum("etf,efd->etd", hidden, expert_down_all, preferred_element_type=jnp.float32)
    weights_e = weights.T[:, :, None]
    combined = jnp.sum(weights_e * outs, axis=0)
    gate_dots = jnp.sum(outs * grad_out[None], axis=-1).T
    grad_outs = (weights_e * grad_out[None]).astype(jnp.bfloat16)
    grad_hidden = jnp.einsum(
        "etd,efd->etf", grad_outs, expert_down_all, preferred_element_type=jnp.float32
    )
    grad_gate_up = act_back(grad_hidden)[0].astype(jnp.bfloat16)
    grad_down = jnp.einsum("etf,etd->efd", hidden, grad_outs, preferred_element_type=jnp.float32)
    grad_in = jnp.einsum(
        "td,etgf->edgf", normed_two, grad_gate_up, preferred_element_type=jnp.float32
    )
    grad_rows = jnp.einsum(
        "etgf,edgf->td", grad_gate_up, expert_in_all, preferred_element_type=jnp.float32
    )
    return combined, gate_dots, grad_rows, grad_in, grad_down


def experts_routed(
    normed_two, grad_out, route_rows, gate_probs, expert_in_low, expert_down_low, capacity, anchor
):
    block_len, model_width = normed_two.shape
    experts = lax.axis_size("fsdp")
    slot_index, owner_route, filled = slot_tables(route_rows, experts, capacity)
    select = (
        (owner_route[:, None] // 2 == jnp.arange(block_len, dtype=jnp.int32)[None, :])
        & (filled[:, None] == 1)
    ).astype(jnp.bfloat16)
    token_rows = jnp.dot(select, normed_two, preferred_element_type=jnp.float32)
    grad_rows_in = jnp.dot(
        select, grad_out.astype(jnp.bfloat16), preferred_element_type=jnp.float32
    )
    slot_weights = gate_probs.reshape(-1)[owner_route][:, None]
    send_rows = jnp.stack(
        [
            token_rows.astype(jnp.bfloat16).reshape(experts, capacity, model_width),
            (slot_weights * grad_rows_in)
            .astype(jnp.bfloat16)
            .reshape(experts, capacity, model_width),
        ],
        axis=1,
    )
    exchange = lambda rows: lax.all_to_all(rows, "fsdp", split_axis=0, concat_axis=0, tiled=True)
    pair_count = lax.axis_size("tp")
    swap = lambda rows: lax.ppermute(
        rows, "tp", [(index, index + 1 - 2 * (index % 2)) for index in range(pair_count)]
    )
    half = capacity // 2
    side = lax.axis_index("tp") % 2
    def expert_block(block):
        rows_in = block[:, 0].reshape(-1, model_width)
        grads_in = block[:, 1].reshape(-1, model_width)
        gate_up = jnp.einsum(
            "rd,dgf->rgf", rows_in, expert_in_low, preferred_element_type=jnp.float32
        )
        act, act_back = jax.vjp(swiglu, gate_up)
        hidden = act.astype(jnp.bfloat16)
        outs = jnp.dot(hidden, expert_down_low, preferred_element_type=jnp.float32)
        grad_hidden = jnp.einsum(
            "rd,fd->rf", grads_in, expert_down_low, preferred_element_type=jnp.float32
        )
        grad_gate_up = act_back(grad_hidden)[0].astype(jnp.bfloat16)
        grad_in = jnp.einsum(
            "rd,rgf->dgf", rows_in, grad_gate_up, preferred_element_type=jnp.float32
        )
        grad_down = jnp.einsum("rf,rd->fd", hidden, grads_in, preferred_element_type=jnp.float32)
        grad_expert_rows = jnp.einsum(
            "rgf,dgf->rd", grad_gate_up, expert_in_low, preferred_element_type=jnp.float32
        )
        width = block.shape[2]
        return (
            [
                outs.reshape(experts, width, model_width),
                grad_expert_rows.reshape(experts, width, model_width),
            ],
            grad_in,
            grad_down,
        )

    if pair_count == 4 and half % 2 == 0:
        quarter = half // 2
        row_side = (lax.axis_index("tp") // 2) % 2
        piece = exchange(
            lax.dynamic_slice_in_dim(send_rows, (2 * side + row_side) * quarter, quarter, 2)
        )
        other = lax.ppermute(piece, "tp", [(0, 2), (1, 3), (2, 0), (3, 1)]) + 0.0 * anchor
        results_a, grad_in_a, grad_down_a = expert_block(
            jnp.concatenate([piece, swap(piece)], axis=2)
        )
        results_b, grad_in_b, grad_down_b = expert_block(
            jnp.concatenate([other, swap(other)], axis=2)
        )
        grad_in = grad_in_a + grad_in_b
        grad_down = grad_down_a + grad_down_b
        pair_sums = []
        for rows_a, rows_b in zip(results_a, results_b):
            sum_a = rows_a[:, :quarter] + swap(rows_a[:, quarter:])
            sum_b = rows_b[:, :quarter] + swap(rows_b[:, quarter:])
            pair_sums.append(
                lax.dynamic_slice_in_dim(
                    jnp.concatenate([sum_a, sum_b, sum_a], axis=1), row_side * quarter, half, 1
                )
            )
    else:
        mine = exchange(lax.dynamic_slice_in_dim(send_rows, side * half, half, 2))
        results, grad_in, grad_down = expert_block(jnp.concatenate([mine, swap(mine)], axis=2))
        pair_sums = [rows[:, :half] + swap(rows[:, half:]) for rows in results]
    held = exchange(jnp.stack(pair_sums, axis=1).astype(jnp.bfloat16))
    slot_expert = slot_index // capacity
    slot_rank = slot_index % capacity
    in_side = ((slot_rank // half) == side)[:, None]
    local_slot = slot_expert * half + slot_rank % half
    pick = (
        (local_slot[:, None] == jnp.arange(experts * half, dtype=jnp.int32)[None, :]) & in_side
    ).astype(jnp.bfloat16)
    picked_rows = []
    for which in range(2):
        rows = jnp.dot(
            pick,
            held[:, which].reshape(experts * half, model_width),
            preferred_element_type=jnp.float32,
        )
        picked_rows.append(rows.reshape(block_len, 2, model_width))
    route_out, grad_routes = picked_rows
    combined = jnp.sum(gate_probs[:, :, None] * route_out, axis=1)
    gate_dots = jnp.sum(grad_out[:, None, :] * route_out, axis=-1)
    grad_rows = jnp.sum(grad_routes, axis=1)
    return combined, gate_dots, grad_rows, grad_in, grad_down


def local(
    layer_input,
    segments,
    routes,
    cotangent,
    gains,
    attention_in,
    attention_out,
    router_weight,
    shared_in,
    shared_down,
    expert_in,
    expert_down,
    model_stats,
    head_stats,
    value_columns,
    hidden_stats,
    router_state,
    expert_model_stats,
    expert_hidden_stats,
):
    block_len = layer_input.shape[1]
    model_width = layer_input.shape[2]
    experts = router_weight.shape[1]
    dense_experts = False
    capacity = min(block_len, 4 * block_len // experts)
    ctx_index = lax.axis_index("ctx")
    tp_index = lax.axis_index("tp")
    fsdp_index = lax.axis_index("fsdp")
    shard_index = lax.axis_index(("fsdp", "ctx"))
    shard_count = lax.axis_size(("fsdp", "ctx"))
    ctx_count = lax.axis_size("ctx")
    base_pos = ctx_index * block_len
    low = lambda v: v.astype(jnp.bfloat16)
    gain_low, attn_in_low, attn_out_low, router_low = gather_packed(
        [(low(gains), 1), (low(attention_in), 0), (low(attention_out), 1), (low(router_weight), 0)],
        ("fsdp", "ctx"),
        shard_count <= 8,
    )
    later = [
        (low(shared_in), 0),
        (low(shared_down), 1),
    ]
    if dense_experts:
        later += [(low(expert_in), 0), (low(expert_down), 0)]
    later_full = gather_packed(later, ("fsdp", "ctx"))
    shared_in_low, shared_down_low = later_full[:2]
    if dense_experts:
        fe_local = expert_down.shape[1]
        expert_in_all = later_full[2].reshape(experts, model_width, 2, fe_local)
        expert_down_all = (
            later_full[3]
            .reshape(experts, ctx_count, fe_local, model_width // ctx_count)
            .transpose(0, 2, 1, 3)
            .reshape(experts, fe_local, model_width)
        )
    else:
        expert_in_low = lax.all_gather(low(expert_in), "ctx", axis=1, tiled=True)[0]
        expert_down_low = lax.all_gather(low(expert_down), "ctx", axis=2, tiled=True)[0]
    residual = layer_input[0].astype(jnp.float32)
    gain_one = gain_low[0].astype(jnp.float32)
    gain_two = gain_low[1].astype(jnp.float32)
    normed_one, norm_one_back = jax.vjp(rms_norm, residual, gain_one)
    normed_one = normed_one.astype(jnp.bfloat16)
    projected = jnp.einsum(
        "td,dgf->tgf", normed_one, attn_in_low, preferred_element_type=jnp.float32
    )
    local_cols = projected.shape[2]
    local_heads = local_cols // HD
    half_dim = HD // 2
    frequency = 10000.0 ** (-jnp.arange(half_dim, dtype=jnp.float32) / half_dim)
    angles = (base_pos + jnp.arange(block_len, dtype=jnp.int32)).astype(jnp.float32)[
        :, None
    ] * frequency[None, :]
    cosine = jnp.cos(angles)
    sine_tab = jnp.sin(angles)
    queries = rotate(projected[:, 0].reshape(block_len, local_heads, HD), cosine, sine_tab).astype(
        jnp.bfloat16
    )
    keys_own = rotate(projected[:, 1].reshape(block_len, local_heads, HD), cosine, sine_tab).astype(
        jnp.bfloat16
    )
    values_own = projected[:, 2].reshape(block_len, local_heads, HD).astype(jnp.bfloat16)
    seg_own = segments[0].astype(jnp.bfloat16)
    keys_prev, values_prev, seg_prev = from_behind((keys_own, values_own, seg_own), "ctx", 1)
    keys_ext = jnp.concatenate([keys_prev, keys_own], axis=0)
    values_ext = jnp.concatenate([values_prev, values_own], axis=0)
    seg_ext = jnp.concatenate([seg_prev, seg_own], axis=0)
    block_rows = min(512, block_len)
    block_total = block_len // block_rows
    starts = jnp.arange(block_total, dtype=jnp.int32) * block_rows

    def forward_block(start_row):
        query_rows, key_rows, value_rows, masked, allowed = block_view(
            queries, keys_ext, values_ext, seg_own, seg_ext, start_row, base_pos
        )
        row_max = jnp.max(masked, axis=-1, keepdims=True)
        exp_terms = jnp.where(allowed[None], jnp.exp(masked - row_max), 0.0)
        row_total = jnp.sum(exp_terms, axis=-1, keepdims=True)
        attn_probs = (exp_terms / row_total).astype(jnp.bfloat16)
        attended = jnp.einsum(
            "hqk,khd->qhd", attn_probs, value_rows, preferred_element_type=jnp.float32
        )
        return (attended, row_max + jnp.log(row_total))

    attended, log_totals = lax.map(forward_block, starts)
    mixed_heads = attended.reshape(block_len, local_cols).astype(jnp.bfloat16)
    attn_total = lax.psum(
        jnp.dot(mixed_heads, attn_out_low, preferred_element_type=jnp.float32), "tp"
    )
    after_attn = residual + attn_total
    normed_two, norm_two_back = jax.vjp(rms_norm, after_attn, gain_two)
    normed_two = normed_two.astype(jnp.bfloat16)
    logits = jnp.dot(normed_two, router_low, preferred_element_type=jnp.float32)
    route_rows = routes[0]
    onehot = (route_rows[:, :, None] == jnp.arange(experts, dtype=jnp.int32)[None, None, :]).astype(
        jnp.float32
    )
    picked = jnp.sum(onehot * logits[:, None, :], axis=-1)
    gate_probs = jax.nn.softmax(picked, axis=-1)
    upstream = cotangent[0]
    grad_out = upstream.astype(jnp.float32)
    shared_gate_up = jnp.einsum(
        "td,dgf->tgf", normed_two, shared_in_low, preferred_element_type=jnp.float32
    )
    shared_act, shared_act_back = jax.vjp(swiglu, shared_gate_up)
    shared_hidden = shared_act.astype(jnp.bfloat16)
    shared_out = jnp.dot(shared_hidden, shared_down_low, preferred_element_type=jnp.float32)
    grad_shared_hidden = jnp.einsum(
        "td,fd->tf", upstream, shared_down_low, preferred_element_type=jnp.float32
    )
    grad_shared_gate_up = shared_act_back(grad_shared_hidden)[0].astype(jnp.bfloat16)
    shared_rows = jnp.einsum(
        "tgf,dgf->td", grad_shared_gate_up, shared_in_low, preferred_element_type=jnp.float32
    )
    if dense_experts:
        weights = jnp.sum(gate_probs[:, :, None] * onehot, axis=1)
        combined, dots_e, grad_rows, grad_expert_in, grad_expert_down = experts_dense(
            normed_two, grad_out, weights, expert_in_all, expert_down_all
        )
        gate_dots = jnp.sum(onehot * dots_e[:, None, :], axis=-1)
    else:
        combined, gate_dots, grad_rows, grad_expert_in, grad_expert_down = experts_routed(
            normed_two,
            grad_out,
            route_rows,
            gate_probs,
            expert_in_low,
            expert_down_low,
            capacity,
            (shared_rows[0, 0] + shared_out[0, 0]).astype(jnp.bfloat16),
        )
    partial_two = shared_rows + grad_rows
    branch_total, grad_normed_part, gate_total = lax.psum(
        (shared_out + combined, partial_two, gate_dots), "tp"
    )
    layer_out = after_attn + branch_total
    grad_picked = gate_probs * (
        gate_total - jnp.sum(gate_probs * gate_total, axis=-1, keepdims=True)
    )
    grad_logits = jnp.sum(grad_picked[:, :, None] * onehot, axis=1).astype(jnp.bfloat16)
    grad_shared_in = jnp.einsum(
        "td,tgf->dgf", normed_two, grad_shared_gate_up, preferred_element_type=jnp.float32
    )
    grad_shared_down = jnp.einsum(
        "tf,td->fd", shared_hidden, upstream, preferred_element_type=jnp.float32
    )
    grad_router = jnp.einsum(
        "td,te->de", normed_two, grad_logits, preferred_element_type=jnp.float32
    )
    grad_normed_two = grad_normed_part + jnp.einsum(
        "te,de->td", grad_logits, router_low, preferred_element_type=jnp.float32
    )
    grad_after, grad_gain_two = norm_two_back(grad_normed_two)
    grad_after = grad_after + grad_out
    grad_attn_low = grad_after.astype(jnp.bfloat16)
    grad_attn_out = jnp.einsum(
        "tc,td->cd", mixed_heads, grad_attn_low, preferred_element_type=jnp.float32
    )
    first_grads = [
        (grad_attn_out, 1),
        (grad_router, 0),
        (grad_shared_in, 0),
        (grad_shared_down, 1),
        (grad_gain_two, 0),
    ]
    if dense_experts:
        fe_local = expert_down.shape[1]
        first_grads += [
            (grad_expert_in.reshape(shard_count * expert_in.shape[1], 2, fe_local), 0),
            (
                grad_expert_down.reshape(experts, fe_local, ctx_count, model_width // ctx_count)
                .transpose(0, 2, 1, 3)
                .reshape(shard_count * fe_local, model_width // ctx_count),
                0,
            ),
        ]
    if not dense_experts:
        own_expert_in = lax.psum_scatter(grad_expert_in[None], "ctx", scatter_dimension=1, tiled=True)
        own_expert_down = lax.psum_scatter(
            grad_expert_down[None], "ctx", scatter_dimension=2, tiled=True
        )
    grad_heads = (
        jnp.einsum("td,cd->tc", grad_attn_low, attn_out_low, preferred_element_type=jnp.float32)
        .astype(jnp.bfloat16)
        .reshape(block_len, local_heads, HD)
    )

    def backward_block(block_number, running):
        grad_keys, grad_values, grad_queries = running
        start_row = block_number * block_rows
        query_rows, key_rows, value_rows, masked, allowed = block_view(
            queries, keys_ext, values_ext, seg_own, seg_ext, start_row, base_pos
        )
        log_total = lax.dynamic_index_in_dim(log_totals, block_number, 0, keepdims=False)
        attn_probs = jnp.where(allowed[None], jnp.exp(masked - log_total), 0.0)
        grad_block = lax.dynamic_slice_in_dim(grad_heads, start_row, block_rows, 0)
        grad_probs = jnp.einsum(
            "qhd,khd->hqk", grad_block, value_rows, preferred_element_type=jnp.float32
        )
        inner_sum = jnp.sum(attn_probs * grad_probs, axis=-1, keepdims=True)
        grad_scores = (attn_probs * (grad_probs - inner_sum)).astype(jnp.bfloat16)
        grad_query_rows = (
            jnp.einsum("hqk,khd->qhd", grad_scores, key_rows, preferred_element_type=jnp.float32)
            * 0.125
        )
        grad_key_rows = (
            jnp.einsum("hqk,qhd->khd", grad_scores, query_rows, preferred_element_type=jnp.float32)
            * 0.125
        )
        grad_value_rows = jnp.einsum(
            "hqk,qhd->khd",
            attn_probs.astype(jnp.bfloat16),
            grad_block,
            preferred_element_type=jnp.float32,
        )
        key_offset = start_row + block_len - WINDOW
        grad_keys = lax.dynamic_update_slice_in_dim(
            grad_keys,
            lax.dynamic_slice_in_dim(grad_keys, key_offset, block_rows + WINDOW, 0) + grad_key_rows,
            key_offset,
            0,
        )
        grad_values = lax.dynamic_update_slice_in_dim(
            grad_values,
            lax.dynamic_slice_in_dim(grad_values, key_offset, block_rows + WINDOW, 0)
            + grad_value_rows,
            key_offset,
            0,
        )
        grad_queries = lax.dynamic_update_slice_in_dim(grad_queries, grad_query_rows, start_row, 0)
        return (grad_keys, grad_values, grad_queries)

    zero_ext = jnp.zeros((2 * block_len, local_heads, HD), jnp.float32)
    zero_own = jnp.zeros((block_len, local_heads, HD), jnp.float32)
    grad_keys, grad_values, grad_queries = lax.fori_loop(
        0, block_total, backward_block, (zero_ext, zero_ext, zero_own)
    )
    rim_keys, rim_values = (
        from_behind(grad_keys[:block_len].astype(jnp.bfloat16), "ctx", -1).astype(jnp.float32),
        from_behind(grad_values[:block_len].astype(jnp.bfloat16), "ctx", -1).astype(jnp.float32),
    )
    grad_keys_own = grad_keys[block_len:] + rim_keys
    grad_values_own = grad_values[block_len:] + rim_values
    grad_query_raw = rotate(grad_queries, cosine, -sine_tab)
    grad_key_raw = rotate(grad_keys_own, cosine, -sine_tab)
    grad_projected = (
        jnp.stack([grad_query_raw, grad_key_raw, grad_values_own], axis=1)
        .reshape(block_len, 3, local_cols)
        .astype(jnp.bfloat16)
    )
    grad_attn_in = jnp.einsum(
        "td,tgf->dgf", normed_one, grad_projected, preferred_element_type=jnp.float32
    )
    partial_one = jnp.einsum(
        "tgf,dgf->td", grad_projected, attn_in_low, preferred_element_type=jnp.float32
    )
    tp_one = lax.psum(partial_one, "tp")
    halving = lax.axis_size("fsdp") == 4 and ctx_count == 2
    all_own = scatter_packed(
        first_grads + [(grad_attn_in, 0)],
        ("fsdp", "ctx"),
        shard_count,
        halving,
    )
    own_attn_out, own_router, own_shared_in, own_shared_down, own_gain_two = all_own[:5]
    own_attn_in = all_own[-1]
    grad_residual, grad_gain_one = norm_one_back(tp_one + 0.0 * own_attn_in[0, 0, 0])
    input_grad = grad_after + grad_residual
    if dense_experts:
        own_expert_in = all_own[5][None]
        own_expert_down = all_own[6][None]
    lead_tp = (tp_index == 0).astype(jnp.float32)
    first_shard = (shard_index == 0).astype(jnp.float32)
    first_ctx = (ctx_index == 0).astype(jnp.float32)
    d_local = gains.shape[1]
    ff_local = shared_down.shape[0]
    fe_local = expert_down.shape[1]
    d_quarter = expert_in.shape[1]
    square_attn_in = own_attn_in * own_attn_in + TINY_SQUARE
    square_attn_out = own_attn_out * own_attn_out + TINY_SQUARE
    square_shared_in = own_shared_in * own_shared_in + TINY_SQUARE
    square_shared_down = own_shared_down * own_shared_down + TINY_SQUARE
    square_expert_in = own_expert_in[0] * own_expert_in[0] + TINY_SQUARE
    square_expert_down = own_expert_down[0] * own_expert_down[0] + TINY_SQUARE
    model_part = lax.dynamic_update_slice(
        jnp.zeros((4, D), jnp.float32),
        jnp.stack(
            [
                jnp.sum(square_attn_in, axis=(1, 2)),
                jnp.sum(square_shared_in, axis=(1, 2)),
                jnp.sum(square_attn_out, axis=0),
                jnp.sum(square_shared_down, axis=0),
            ]
        ),
        (0, shard_index * d_local),
    )
    head_part = lax.dynamic_update_slice(
        jnp.zeros((4, HH), jnp.float32),
        jnp.concatenate(
            [jnp.sum(square_attn_in, axis=0), jnp.sum(square_attn_out, axis=1)[None]], axis=0
        ),
        (0, tp_index * local_cols),
    )
    hidden_part = lax.dynamic_update_slice(
        jnp.zeros((3, FF), jnp.float32),
        jnp.concatenate(
            [jnp.sum(square_shared_in, axis=0), jnp.sum(square_shared_down, axis=1)[None]], axis=0
        ),
        (0, tp_index * ff_local),
    )
    expert_model_part = lax.dynamic_update_slice(
        jnp.zeros((experts, 2, D), jnp.float32),
        jnp.stack([jnp.sum(square_expert_in, axis=(1, 2)), jnp.sum(square_expert_down, axis=0)])[
            None
        ],
        (fsdp_index, 0, ctx_index * d_quarter),
    )
    expert_hidden_part = lax.dynamic_update_slice(
        jnp.zeros((experts, 3, FE), jnp.float32),
        jnp.concatenate(
            [jnp.sum(square_expert_in, axis=0), jnp.sum(square_expert_down, axis=1)[None]], axis=0
        )[None],
        (fsdp_index, 0, tp_index * fe_local),
    )
    scalar_part = jnp.stack(
        [
            lead_tp * jnp.sum(gains * gains),
            jnp.sum(attention_in * attention_in),
            jnp.sum(attention_out * attention_out),
            lead_tp * jnp.sum(router_weight * router_weight),
            jnp.sum(shared_in * shared_in),
            jnp.sum(shared_down * shared_down),
            jnp.sum(expert_in * expert_in),
            jnp.sum(expert_down * expert_down),
            lead_tp * jnp.sum(model_stats[2]),
            first_shard * jnp.sum(head_stats[2]),
            lead_tp * jnp.sum(model_stats[3]),
            first_shard * jnp.sum(hidden_stats[2]),
        ]
    )
    expert_old_part = lax.dynamic_update_slice(
        jnp.zeros((2, experts), jnp.float32),
        jnp.stack(
            [
                lead_tp * jnp.sum(expert_model_stats[0, 0]),
                first_ctx * jnp.sum(expert_hidden_stats[0, 2]),
            ]
        )[:, None],
        (0, fsdp_index),
    )
    global_sums = butterfly_sum(
        [
            model_part,
            head_part,
            hidden_part,
            expert_model_part,
            expert_hidden_part,
            scalar_part,
            expert_old_part,
            lead_tp * grad_gain_one,
        ],
        1,
    )
    (
        model_sum,
        head_sum,
        hidden_sum,
        expert_model_sum,
        expert_hidden_sum,
        scalar_sum,
        expert_old_sum,
        gain_one_sum,
    ) = global_sums
    own_gain_one = lax.dynamic_slice_in_dim(gain_one_sum, shard_index * d_local, d_local)
    own_gains = jnp.stack([own_gain_one, own_gain_two])
    shard_start = shard_index * d_local
    gain_state = DECAY_RATE * model_stats[0:2] + (1.0 - DECAY_RATE) * (
        own_gains * own_gains + TINY_SQUARE
    )
    update_gains = own_gains * lax.rsqrt(gain_state)
    router_new = DECAY_RATE * router_state + (1.0 - DECAY_RATE) * (
        own_router * own_router + TINY_SQUARE
    )
    update_router = own_router * lax.rsqrt(router_new)
    attn_cols_old = jnp.concatenate([head_stats[0:2], value_columns[None]], axis=0).reshape(-1)
    update_attn_in, rows_attn_in, cols_attn_in = factored_update(
        own_attn_in.reshape(d_local, 3 * local_cols),
        model_stats[2],
        attn_cols_old,
        lax.dynamic_slice_in_dim(model_sum[0], shard_start, d_local),
        lax.dynamic_slice_in_dim(head_sum[0:3], tp_index * local_cols, local_cols, 1).reshape(-1),
        D,
        3 * HH,
        scalar_sum[8],
        jnp.sum(model_sum[0]),
    )
    update_attn_out, rows_attn_out, cols_attn_out = factored_update(
        own_attn_out,
        head_stats[2],
        model_stats[4],
        lax.dynamic_slice_in_dim(head_sum[3], tp_index * local_cols, local_cols),
        lax.dynamic_slice_in_dim(model_sum[2], shard_start, d_local),
        HH,
        D,
        scalar_sum[9],
        jnp.sum(head_sum[3]),
    )
    update_shared_in, rows_shared_in, cols_shared_in = factored_update(
        own_shared_in.reshape(d_local, 2 * ff_local),
        model_stats[3],
        hidden_stats[0:2].reshape(-1),
        lax.dynamic_slice_in_dim(model_sum[1], shard_start, d_local),
        lax.dynamic_slice_in_dim(hidden_sum[0:2], tp_index * ff_local, ff_local, 1).reshape(-1),
        D,
        2 * FF,
        scalar_sum[10],
        jnp.sum(model_sum[1]),
    )
    update_shared_down, rows_shared_down, cols_shared_down = factored_update(
        own_shared_down,
        hidden_stats[2],
        model_stats[5],
        lax.dynamic_slice_in_dim(hidden_sum[2], tp_index * ff_local, ff_local),
        lax.dynamic_slice_in_dim(model_sum[3], shard_start, d_local),
        FF,
        D,
        scalar_sum[11],
        jnp.sum(hidden_sum[2]),
    )
    own_expert_model = lax.dynamic_index_in_dim(expert_model_sum, fsdp_index, 0, keepdims=False)
    own_expert_hidden = lax.dynamic_index_in_dim(expert_hidden_sum, fsdp_index, 0, keepdims=False)
    old_expert_totals = lax.dynamic_index_in_dim(expert_old_sum, fsdp_index, 1, keepdims=False)
    update_expert_in, rows_expert_in, cols_expert_in = factored_update(
        own_expert_in[0].reshape(d_quarter, 2 * fe_local),
        expert_model_stats[0, 0],
        expert_hidden_stats[0, 0:2].reshape(-1),
        lax.dynamic_slice_in_dim(own_expert_model[0], ctx_index * d_quarter, d_quarter),
        lax.dynamic_slice_in_dim(own_expert_hidden[0:2], tp_index * fe_local, fe_local, 1).reshape(
            -1
        ),
        D,
        2 * FE,
        old_expert_totals[0],
        jnp.sum(own_expert_model[0]),
    )
    update_expert_down, rows_expert_down, cols_expert_down = factored_update(
        own_expert_down[0],
        expert_hidden_stats[0, 2],
        expert_model_stats[0, 1],
        lax.dynamic_slice_in_dim(own_expert_hidden[2], tp_index * fe_local, fe_local),
        lax.dynamic_slice_in_dim(own_expert_model[1], ctx_index * d_quarter, d_quarter),
        FE,
        D,
        old_expert_totals[1],
        jnp.sum(own_expert_hidden[2]),
    )
    clip_part = jnp.stack(
        [
            lead_tp * jnp.sum(update_gains * update_gains),
            jnp.sum(update_attn_in * update_attn_in),
            jnp.sum(update_attn_out * update_attn_out),
            lead_tp * jnp.sum(update_router * update_router),
            jnp.sum(update_shared_in * update_shared_in),
            jnp.sum(update_shared_down * update_shared_down),
            jnp.sum(update_expert_in * update_expert_in),
            jnp.sum(update_expert_down * update_expert_down),
        ]
    )
    clip_total = butterfly_sum([clip_part], 2)[0]
    elements = jnp.array(
        [
            2 * D,
            D * 3 * HH,
            HH * D,
            D * experts,
            D * 2 * FF,
            FF * D,
            experts * D * 2 * FE,
            experts * FE * D,
        ],
        jnp.float32,
    )
    update_roots = jnp.sqrt(clip_total / elements)
    new_gains = apply_update(gains, update_gains, update_roots[0], scalar_sum[0], elements[0])
    new_attn_in = apply_update(
        attention_in,
        update_attn_in.reshape(attention_in.shape),
        update_roots[1],
        scalar_sum[1],
        elements[1],
    )
    new_attn_out = apply_update(
        attention_out, update_attn_out, update_roots[2], scalar_sum[2], elements[2]
    )
    new_router = apply_update(
        router_weight, update_router, update_roots[3], scalar_sum[3], elements[3]
    )
    new_shared_in = apply_update(
        shared_in,
        update_shared_in.reshape(shared_in.shape),
        update_roots[4],
        scalar_sum[4],
        elements[4],
    )
    new_shared_down = apply_update(
        shared_down, update_shared_down, update_roots[5], scalar_sum[5], elements[5]
    )
    new_expert_in = apply_update(
        expert_in,
        update_expert_in.reshape(expert_in.shape),
        update_roots[6],
        scalar_sum[6],
        elements[6],
    )
    new_expert_down = apply_update(
        expert_down,
        update_expert_down.reshape(expert_down.shape),
        update_roots[7],
        scalar_sum[7],
        elements[7],
    )
    new_model_stats = jnp.concatenate(
        [gain_state, jnp.stack([rows_attn_in, rows_shared_in, cols_attn_out, cols_shared_down])],
        axis=0,
    )
    attn_cols_new = cols_attn_in.reshape(3, local_cols)
    new_head_stats = jnp.concatenate([attn_cols_new[0:2], rows_attn_out[None]], axis=0)
    new_value_columns = attn_cols_new[2]
    new_hidden_stats = jnp.concatenate(
        [cols_shared_in.reshape(2, ff_local), rows_shared_down[None]], axis=0
    )
    new_expert_model_stats = jnp.stack([rows_expert_in, cols_expert_down])[None]
    new_expert_hidden_stats = jnp.concatenate(
        [cols_expert_in.reshape(2, fe_local), rows_expert_down[None]], axis=0
    )[None]
    return (
        layer_out.astype(jnp.bfloat16)[None],
        input_grad[None],
        own_gains,
        own_attn_in,
        own_attn_out,
        own_router,
        own_shared_in,
        own_shared_down,
        own_expert_in,
        own_expert_down,
        new_gains,
        new_attn_in,
        new_attn_out,
        new_router,
        new_shared_in,
        new_shared_down,
        new_expert_in,
        new_expert_down,
        new_model_stats,
        new_head_stats,
        new_value_columns,
        new_hidden_stats,
        router_new,
        new_expert_model_stats,
        new_expert_hidden_stats,
        update_roots,
    )


def solution(mesh):
    in_specs = (
        P("fsdp", "ctx", None),
        P("fsdp", "ctx"),
        P("fsdp", "ctx", None),
        P("fsdp", "ctx", None),
        P(None, ("fsdp", "ctx")),
        P(("fsdp", "ctx"), None, "tp"),
        P("tp", ("fsdp", "ctx")),
        P(("fsdp", "ctx"), None),
        P(("fsdp", "ctx"), None, "tp"),
        P("tp", ("fsdp", "ctx")),
        P("fsdp", "ctx", None, "tp"),
        P("fsdp", "tp", "ctx"),
        P(None, ("fsdp", "ctx")),
        P(None, "tp"),
        P("tp"),
        P(None, "tp"),
        P(("fsdp", "ctx"), None),
        P("fsdp", None, "ctx"),
        P("fsdp", None, "tp"),
    )
    out_specs = (
        P("fsdp", "ctx", None),
        P("fsdp", "ctx", None),
        P(None, ("fsdp", "ctx")),
        P(("fsdp", "ctx"), None, "tp"),
        P("tp", ("fsdp", "ctx")),
        P(("fsdp", "ctx"), None),
        P(("fsdp", "ctx"), None, "tp"),
        P("tp", ("fsdp", "ctx")),
        P("fsdp", "ctx", None, "tp"),
        P("fsdp", "tp", "ctx"),
        P(None, ("fsdp", "ctx")),
        P(("fsdp", "ctx"), None, "tp"),
        P("tp", ("fsdp", "ctx")),
        P(("fsdp", "ctx"), None),
        P(("fsdp", "ctx"), None, "tp"),
        P("tp", ("fsdp", "ctx")),
        P("fsdp", "ctx", None, "tp"),
        P("fsdp", "tp", "ctx"),
        P(None, ("fsdp", "ctx")),
        P(None, "tp"),
        P("tp"),
        P(None, "tp"),
        P(("fsdp", "ctx"), None),
        P("fsdp", None, "ctx"),
        P("fsdp", None, "tp"),
        P(),
    )
    return jax.shard_map(local, mesh=mesh, in_specs=in_specs, out_specs=out_specs, check_vma=False)
```
